32 devices in a mesh: dp: 8 (over y, x, core), tensor: 4 (over z).
Axes of the slice: x: 2, y: 2, z: 4, core: 2. Of those that a mesh axis runs over, the one named last changes fastest.
Arguments:
- block_in: bfloat16 [8192, 768], P(('dp', 'tensor')), may hold values from -6 to 6
- source: bfloat16 [32768, 768], P(('dp', 'tensor')), may hold values from -6 to 6
- target_len: int32 [16], P('dp'), may hold values from 256 to 512, as said below
- source_len: int32 [16], P('dp'), may hold values from 512 to 2048, as said below
- targets: int32 [8192], P('dp'), may hold values from 0 to 32127
- gain_self: float32 [768], replicated, may hold values from 0.5 to 1.5
- gain_cross: float32 [768], replicated, may hold values from 0.5 to 1.5
- gain_ff: float32 [768], replicated, may hold values from 0.5 to 1.5
- gain_final: float32 [768], replicated, may hold values from 0.5 to 1.5
- self_q: bfloat16 [768, 768], P(None, 'tensor'), may hold values from -0.21875 to 0.21875
- self_k: bfloat16 [768, 768], P(None, 'tensor'), may hold values from -0.21875 to 0.21875
- self_v: bfloat16 [768, 768], P(None, 'tensor'), may hold values from -0.21875 to 0.21875
- self_o: bfloat16 [768, 768], P('tensor'), may hold values from -0.875 to 0.875
- cross_q: bfloat16 [768, 768], P(None, 'tensor'), may hold values from -0.21875 to 0.21875
- cross_k: bfloat16 [768, 768], P(None, 'tensor'), may hold values from -0.21875 to 0.21875
- cross_v: bfloat16 [768, 768], P(None, 'tensor'), may hold values from -0.21875 to 0.21875
- cross_o: bfloat16 [768, 768], P('tensor'), may hold values from -1.25 to 1.25
- ff_gate: bfloat16 [768, 2048], P(None, 'tensor'), may hold values from -0.21875 to 0.21875
- ff_up: bfloat16 [768, 2048], P(None, 'tensor'), may hold values from -0.21875 to 0.21875
- ff_down: bfloat16 [2048, 768], P('tensor'), may hold values from -0.125 to 0.125
- embed_table: bfloat16 [32128, 768], P('tensor'), may hold values from -6 to 6
Outputs:
- block_out: float32 [8192, 768], P(('dp', 'tensor'))
- token_loss: float32 [8192], P('dp')
- grad_block_in: float32 [8192, 768], P(('dp', 'tensor'))
- grad_source: float32 [32768, 768], P(('dp', 'tensor'))
- grad_gain_self: float32 [768], replicated
- grad_gain_cross: float32 [768], replicated
- grad_gain_ff: float32 [768], replicated
- grad_gain_final: float32 [768], replicated
- grad_self_q: float32 [768, 768], P('dp', 'tensor')
- grad_self_k: float32 [768, 768], P('dp', 'tensor')
- grad_self_v: float32 [768, 768], P('dp', 'tensor')
- grad_self_o: float32 [768, 768], P('tensor', 'dp')
- grad_cross_q: float32 [768, 768], P('dp', 'tensor')
- grad_cross_k: float32 [768, 768], P('dp', 'tensor')
- grad_cross_v: float32 [768, 768], P('dp', 'tensor')
- grad_cross_o: float32 [768, 768], P('tensor', 'dp')
- grad_ff_gate: float32 [768, 2048], P('dp', 'tensor')
- grad_ff_up: float32 [768, 2048], P('dp', 'tensor')
- grad_ff_down: float32 [2048, 768], P('tensor', 'dp')
- grad_embed: float32 [32128, 768], P('tensor', 'dp')
The draws below stay inside these ranges and needn't reach their ends.
Inputs may be any that keep to these rules, and one draw needn't show every extreme that they name: `target_len`: among the 2 sequences of each index of dp one has exactly 512 live target positions. `source_len`: among the 2 sequences of each index of dp one has exactly 2048 live source positions.
All inputs are finite; a program needn't handle non-finite values.
Results may differ from the reference program's by a relative error of at most 0.019.
Values may be sent and summed in bfloat16 or wider, within the bound.
A program may use at most 256 MiB of HBM per device.

```python
import math
import jax
import jax.numpy as jnp
import numpy as np
from jax import lax

D = 768
HDIM = 64
FF = 2048
VOCAB = 32128
TGT = 512
SRC = 2048
SEQS = 2
INNER = 768
NSEQ = 16
TOKENS = 8192
SOURCES = 32768


def ragged_lengths(key, lowest, longest):
    key_len, key_pick = jax.random.split(key)
    lengths = jax.random.randint(key_len, (NSEQ,), lowest, longest + 1)
    chosen = jax.random.randint(key_pick, (NSEQ // SEQS,), 0, SEQS)
    longest_slot = jnp.arange(NSEQ) % SEQS == jnp.repeat(chosen, SEQS, total_repeat_length=NSEQ)
    return jnp.where(longest_slot, longest, lengths).astype(jnp.int32)


def draw_target_len(key, part):
    return ragged_lengths(jax.random.fold_in(key, 11), TGT // 2, TGT)


def draw_source_len(key, part):
    return ragged_lengths(jax.random.fold_in(key, 23), SRC // 4, SRC)


def touch_ends(result, stream_key, low, top_value):
    index_at = [jax.random.randint(jax.random.fold_in(stream_key, axis), (), 0, length) for axis, length in enumerate(result.shape)]
    widest = result.shape.index(max(result.shape))
    neighbour = index_at[:widest] + [(index_at[widest] + 1) % result.shape[widest]] + index_at[widest + 1:]
    return result.at[tuple(index_at)].set(low).at[tuple(neighbour)].set(top_value)


def shard_levels(own_key, extent, shards, smallest, largest):
    gain, own = 1.0, jax.random.fold_in(own_key, 6)
    for position, parts in shards:
        draws = jnp.exp(jax.random.uniform(jax.random.fold_in(own, position), (parts,), jnp.float32, smallest / len(shards), largest / len(shards)))
        gain = gain * jnp.repeat(draws, extent[position] // parts).reshape([-1 if axis == position else 1 for axis in range(len(extent))])
    return gain


def rank_bounds(amount, slope):
    loads = [(1 << 20) // math.isqrt(rank ** slope) + 1 for rank in range(1, amount + 1)]
    spread = 1 + sum(loads) // (1 << 30)
    return np.cumsum(np.array([max(1, weight // spread) for weight in loads]))


def ranked(key, dims, number_of, skew):
    table = rank_bounds(number_of, skew)
    ticket = jax.random.randint(jax.random.fold_in(key, 1), dims, 0, int(table[number_of - 1]))
    rank = jnp.searchsorted(jnp.asarray(table, jnp.int32), ticket, side="right")
    return jax.random.permutation(jax.random.fold_in(key, 2), number_of)[rank].astype(jnp.int32)


def normal_values(rng, dims, width, limit, cuts=(), kind=jnp.bfloat16):
    entries = jax.random.normal(rng, dims, jnp.float32) * width
    if len(cuts) > 0:
        entries = shard_levels(rng, dims, cuts, -0.22, 0.18) * entries
    return jnp.clip(entries, min=-limit, max=limit).astype(kind)


def setup_inputs(seed: int = 0) -> dict:
    seeds = jax.random.split(jax.random.key(seed), 22)
    return {
        "block_in": normal_values(seeds[0], (TOKENS, D), 1.0, 6.0, ((0, 32),)),
        "source": normal_values(seeds[1], (SOURCES, D), 1.0, 6.0, ((0, 32),)),
        "target_len": draw_target_len(jax.random.fold_in(seeds[21], 71), 0),
        "source_len": draw_source_len(jax.random.fold_in(seeds[21], 71), 0),
        "targets": touch_ends(ranked(seeds[4], (TOKENS,), VOCAB, 2), jax.random.fold_in(seeds[4], 3), 0, VOCAB - 1).astype(jnp.int32),
        "gain_self": jnp.clip(1.0 + 0.1 * jax.random.normal(seeds[5], (D,), jnp.float32), 0.5, 1.5),
        "gain_cross": jnp.clip(1.0 + 0.1 * jax.random.normal(seeds[6], (D,), jnp.float32), 0.5, 1.5),
        "gain_ff": jnp.clip(1.0 + 0.1 * jax.random.normal(seeds[7], (D,), jnp.float32), 0.5, 1.5),
        "gain_final": jnp.clip(1.0 + 0.1 * jax.random.normal(seeds[8], (D,), jnp.float32), 0.5, 1.5),
        "self_q": normal_values(seeds[9], (D, INNER), D ** -0.5, 0.21875, ((1, 4),)),
        "self_k": normal_values(seeds[10], (D, INNER), D ** -0.5, 0.21875, ((1, 4),)),
        "self_v": normal_values(seeds[11], (D, INNER), D ** -0.5, 0.21875, ((1, 4),)),
        "self_o": normal_values(seeds[12], (INNER, D), (INNER // 16) ** -0.5, 0.875, ((0, 4),)),
        "cross_q": normal_values(seeds[13], (D, INNER), D ** -0.5, 0.21875, ((1, 4),)),
        "cross_k": normal_values(seeds[14], (D, INNER), D ** -0.5, 0.21875, ((1, 4),)),
        "cross_v": normal_values(seeds[15], (D, INNER), D ** -0.5, 0.21875, ((1, 4),)),
        "cross_o": normal_values(seeds[16], (INNER, D), (INNER // 32) ** -0.5, 1.25, ((0, 4),)),
        "ff_gate": normal_values(seeds[17], (D, FF), D ** -0.5, 0.21875, ((1, 4),)),
        "ff_up": normal_values(seeds[18], (D, FF), D ** -0.5, 0.21875, ((1, 4),)),
        "ff_down": normal_values(seeds[19], (FF, D), FF ** -0.5, 0.125, ((0, 4),)),
        "embed_table": normal_values(seeds[20], (VOCAB, D), 1.0, 6.0, ((0, 4),)),
    }


epsilon = 1e-06
highest = lax.Precision.HIGHEST

@jax.custom_vjp
def low(v):
    return lax.optimization_barrier(v.astype(jnp.bfloat16)).astype(jnp.float32)

@jax.custom_vjp
def low_back(v):
    return v

def low_keep(v):
    return (low(v), None)

def low_pass(kept, grad):
    return (grad,)

def back_keep(v):
    return (v, None)

def back_low(kept, grad):
    return (low(grad),)
low.defvjp(low_keep, low_pass)
low_back.defvjp(back_keep, back_low)

def rms_norm(values, gain_vec):
    inv_scale = lax.rsqrt(lax.optimization_barrier(jnp.mean(values * values, axis=-1, keepdims=True)) + epsilon)
    return values * inv_scale * gain_vec

def matmul(left, right):
    return jnp.dot(left, right, precision=highest, preferred_element_type=jnp.float32)

def project(row_block, weight):
    return low_back(low(matmul(row_block, weight)))

def attention(queries, key_rows, value_rows, key_mask):
    seq_count = key_mask.shape[0]
    head_count = queries.shape[1] // HDIM
    split_q = queries.reshape(seq_count, -1, head_count, HDIM)
    split_k = key_rows.reshape(seq_count, -1, head_count, HDIM)
    split_v = value_rows.reshape(seq_count, -1, head_count, HDIM)
    scores = low_back(jnp.einsum('sqhd,skhd->shqk', split_q, split_k, precision=highest) * HDIM ** (-0.5))
    scores = jnp.where(key_mask, scores, -1000000000.0)
    row_top = lax.optimization_barrier(jnp.max(scores, axis=-1, keepdims=True))
    log_total = row_top + jnp.log(lax.optimization_barrier(jnp.sum(jnp.exp(scores - row_top), axis=-1, keepdims=True)))
    attn_probs = low(jnp.exp(scores - log_total))
    output = jnp.einsum('shqk,skhd->sqhd', attn_probs, split_v, precision=highest)
    return low_back(low(output.reshape(queries.shape[0], -1)))

def group_forward(params, x_rows, src_rows, tgt_lens, src_lens, target_rows):
    gain_self, gain_cross, gain_ff, gain_final, self_q, self_k, self_v, self_o, cross_q, cross_k, cross_v, cross_o, ff_gate, ff_up, ff_down, embed_table = params
    positions = jnp.arange(TGT)
    causal = positions[None, :] <= positions[:, None]
    self_mask = causal[None, None] & (positions[None, None, None, :] < tgt_lens[:, None, None, None])
    cross_mask = jnp.arange(SRC)[None, None, None, :] < src_lens[:, None, None, None]
    valid_rows = (positions[None, :] < tgt_lens[:, None]).reshape(-1)
    normed_one = low(rms_norm(x_rows, gain_self))
    att_one = attention(project(normed_one, self_q), project(normed_one, self_k), project(normed_one, self_v), self_mask)
    hidden_one = x_rows + low_back(matmul(att_one, self_o))
    normed_two = low(rms_norm(hidden_one, gain_cross))
    att_two = attention(project(normed_two, cross_q), project(src_rows, cross_k), project(src_rows, cross_v), cross_mask)
    hidden_two = hidden_one + low_back(matmul(att_two, cross_o))
    normed_three = low(rms_norm(hidden_two, gain_ff))
    gate_pre = low_back(matmul(normed_three, ff_gate))
    up_pre = low_back(matmul(normed_three, ff_up))
    mixed_rows = low(jax.nn.gelu(gate_pre, approximate=True) * up_pre)
    block_out = hidden_two + low_back(matmul(mixed_rows, ff_down))
    normed_final = low(rms_norm(block_out, gain_final) * D ** (-0.5))
    block_size = min(512, normed_final.shape[0])

    def head_block(operand):
        row_block, target_block, valid_block = operand
        logits = low_back(jnp.einsum('rd,vd->rv', row_block, embed_table, precision=highest))
        row_top = lax.optimization_barrier(jnp.max(logits, axis=1, keepdims=True))
        log_total = row_top[:, 0] + jnp.log(lax.optimization_barrier(jnp.sum(jnp.exp(logits - row_top), axis=1)))
        picked = jnp.take_along_axis(logits, target_block[:, None], axis=1)[:, 0]
        return jnp.where(valid_block, log_total - picked, 0.0)
    token_loss = lax.map(jax.checkpoint(head_block), (normed_final.reshape(-1, block_size, D), target_rows.reshape(-1, block_size), valid_rows.reshape(-1, block_size))).reshape(-1)
    return (block_out, token_loss)

def reference(block_in, source, target_len, source_len, targets, gain_self, gain_cross, gain_ff, gain_final, self_q, self_k, self_v, self_o, cross_q, cross_k, cross_v, cross_o, ff_gate, ff_up, ff_down, embed_table):
    params = tuple((weight.astype(jnp.float32) for weight in (gain_self, gain_cross, gain_ff, gain_final, self_q, self_k, self_v, self_o, cross_q, cross_k, cross_v, cross_o, ff_gate, ff_up, ff_down, embed_table)))
    group_count = target_len.shape[0] // SEQS
    x_groups = block_in.astype(jnp.float32).reshape(group_count, SEQS * TGT, D)
    src_groups = source.astype(jnp.float32).reshape(group_count, SEQS * SRC, D)
    len_groups = target_len.reshape(group_count, SEQS)
    src_len_groups = source_len.reshape(group_count, SEQS)
    target_groups = targets.reshape(group_count, SEQS * TGT)

    def forward(weights, x_all, src_all):

        def one_group(operand):
            x_rows, src_rows, tgt_lens, src_lens, target_rows = operand
            return group_forward(weights, x_rows, src_rows, tgt_lens, src_lens, target_rows)
        outputs, losses = lax.map(jax.checkpoint(one_group), (x_all, src_all, len_groups, src_len_groups, target_groups))
        return (jnp.sum(losses), (outputs, losses))
    objective, back_fn, (block_out, token_loss) = jax.vjp(forward, params, x_groups, src_groups, has_aux=True)
    grad_params, grad_x, grad_src = back_fn(jnp.ones((), jnp.float32))
    return (block_out.reshape(-1, D), token_loss.reshape(-1), grad_x.reshape(-1, D), grad_src.reshape(-1, D), grad_params[0], grad_params[1], grad_params[2], grad_params[3], grad_params[4], grad_params[5], grad_params[6], grad_params[7], grad_params[8], grad_params[9], grad_params[10], grad_params[11], grad_params[12], grad_params[13], grad_params[14], grad_params[15])
```

```python
import jax
import jax.numpy as jnp
from jax import lax
from jax.sharding import PartitionSpec as P
from jax.experimental import pallas as pl
from jax.experimental.pallas import tpu as pltpu

D = 768
HDIM = 64
TGT = 512
SRC = 2048
F32 = jnp.float32
BF16 = jnp.bfloat16
MESH_ID = pl.DeviceIdType.MESH

epsilon = 1e-06


def normalize(values, gain_vec):
    inv_scale = lax.rsqrt(jnp.mean(values * values, axis=-1, keepdims=True) + epsilon)
    return (values * inv_scale * gain_vec, inv_scale)


def norm_back(values, inv_scale, gain_vec, grad_out):
    weighted = gain_vec * grad_out
    grad_gain = jnp.sum(grad_out * values * inv_scale, axis=0)
    grad_values = inv_scale * weighted - values * inv_scale**3 * jnp.mean(
        weighted * values, axis=-1, keepdims=True
    )
    return (grad_values, grad_gain)


def dot_nt(left, right):
    return lax.dot_general(left, right, (((1,), (1,)), ((), ())), preferred_element_type=F32)


def dot_nn(left, right):
    return lax.dot_general(left, right, (((1,), (0,)), ((), ())), preferred_element_type=F32)


def dot_tn(left, right):
    return lax.dot_general(left, right, (((0,), (0,)), ((), ())), preferred_element_type=F32)


def swap(value, axis_name, size, bit):
    return lax.ppermute(value, axis_name, [(i, i ^ bit) for i in range(size)])


def gather_kernel(*refs):
    groups = (len(refs) - 4) // 2
    ins, outs = refs[:groups], refs[groups : 2 * groups]
    send_sem, recv_sem, local_sem, core_sem = refs[2 * groups :]
    dp = lax.axis_index("dp")
    z = lax.axis_index("tensor")
    core_peer, x_peer, y_peer = (
        dp + 1 - 2 * lax.rem(dp, 2),
        dp + 2 - 4 * lax.rem(dp // 2, 2),
        dp + 4 - 8 * (dp // 4),
    )
    xy_peer = x_peer + y_peer - dp
    z_peers = []
    for j in (1, 2, 3):
        low, high = lax.rem(z, 2), z // 2
        new_low = 1 - low if j % 2 else low
        new_high = 1 - high if j // 2 else high
        z_peers.append(new_high * 2 + new_low)
    barrier = pltpu.get_barrier_semaphore()
    for other in (core_peer, x_peer, y_peer):
        pl.semaphore_signal(
            barrier, inc=1, device_id={"dp": other, "tensor": z}, device_id_type=MESH_ID
        )
    for other in z_peers:
        pl.semaphore_signal(
            barrier, inc=1, device_id={"dp": dp, "tensor": other}, device_id_type=MESH_ID
        )
    pl.semaphore_wait(barrier, 6)

    def piece(ref, shard, index, rows, start=0, count=None):
        offset = pl.multiple_of(index * rows + start, 16)
        return ref.at[shard, pl.ds(offset, rows if count is None else count)]

    def remote(src, dst, sem, target_dp, target_z):
        copy = pltpu.make_async_remote_copy(
            src_ref=src,
            dst_ref=dst,
            send_sem=send_sem.at[sem],
            recv_sem=recv_sem.at[sem],
            device_id={"dp": target_dp, "tensor": target_z},
            device_id_type=MESH_ID,
        )
        copy.start()
        return copy

    slots = 24
    z_copies, x_copies, y_copies, dx_copies, dy_copies, c_copies, own = [], [], [], [], [], [], []
    for g in range(groups):
        rows = ins[g].shape[0] // 8
        offset = pl.multiple_of(dp * rows, 16)
        z_copies.append(
            [
                remote(
                    ins[g].at[pl.ds(offset, rows)],
                    piece(outs[g], z, dp, rows),
                    g * slots + j,
                    dp,
                    z_peers[j],
                )
                for j in range(3)
            ]
        )
        copy = pltpu.make_async_copy(ins[g], outs[g].at[z], local_sem.at[g])
        copy.start()
        own.append(copy)
    for g in range(groups):
        rows = ins[g].shape[0] // 8
        xs, ys = [], []
        for j in range(3):
            z_copies[g][j].wait()
            part = piece(outs[g], z_peers[j], dp, rows)
            xs.append(remote(part, part, g * slots + 3 + j, x_peer, z))
            ys.append(remote(part, part, g * slots + 6 + j, y_peer, z))
        x_copies.append(xs)
        y_copies.append(ys)
    for g in range(groups):
        rows = ins[g].shape[0] // 8
        dxs, dys, cs = [], [], []
        for j in range(3):
            part = piece(outs[g], z_peers[j], dp, rows)
            cs.append(remote(part, part, g * slots + 15 + j, core_peer, z))
            x_copies[g][j].wait()
            part = piece(outs[g], z_peers[j], x_peer, rows, 0, rows // 2)
            dys.append(remote(part, part, g * slots + 9 + j, y_peer, z))
            y_copies[g][j].wait()
            part = piece(outs[g], z_peers[j], y_peer, rows, rows // 2, rows // 2)
            dxs.append(remote(part, part, g * slots + 12 + j, x_peer, z))
            for n, owner in enumerate((x_peer, y_peer)):
                part = piece(outs[g], z_peers[j], owner, rows)
                cs.append(remote(part, part, g * slots + 18 + 2 * j + n, core_peer, z))
        dx_copies.append(dxs)
        dy_copies.append(dys)
        c_copies.append(cs)
    for g in range(groups):
        rows = ins[g].shape[0] // 8
        for j in range(3):
            dy_copies[g][j].wait()
            dx_copies[g][j].wait()
            part = piece(outs[g], z_peers[j], xy_peer, rows)
            copy = pltpu.make_async_remote_copy(
                src_ref=part,
                dst_ref=part,
                send_sem=core_sem.at[g * 3 + j, 0],
                recv_sem=core_sem.at[g * 3 + j, 1],
                device_id={"dp": core_peer, "tensor": z},
                device_id_type=MESH_ID,
            )
            copy.start()
            c_copies[g].append(copy)
    for g in range(groups):
        own[g].wait()
        for copy in c_copies[g]:
            copy.wait()


def gather_weights(shards, dp_size):
    if dp_size != 8:
        outs = []
        for shard in shards:
            rows = shard.shape[0] // dp_size
            part = lax.dynamic_slice_in_dim(shard, lax.axis_index("dp") * rows, rows, 0)
            outs.append(
                lax.all_gather(part, ("tensor", "dp"), axis=0, tiled=True).reshape(4, -1, D)
            )
        return outs
    groups = len(shards)
    return pl.pallas_call(
        gather_kernel,
        out_shape=[jax.ShapeDtypeStruct((4,) + shard.shape, shard.dtype) for shard in shards],
        in_specs=[pl.BlockSpec(memory_space=pl.ANY)] * groups,
        out_specs=[pl.BlockSpec(memory_space=pl.ANY)] * groups,
        scratch_shapes=[
            pltpu.SemaphoreType.DMA((24 * groups,)),
            pltpu.SemaphoreType.DMA((24 * groups,)),
            pltpu.SemaphoreType.DMA((groups,)),
            pltpu.SemaphoreType.DMA((3 * groups, 2)),
        ],
        compiler_params=pltpu.CompilerParams(collective_id=0, has_side_effects=True),
    )(*shards)


def reduce_dp(grads, dp_size):
    rows = D // dp_size
    if dp_size != 8:
        return lax.psum_scatter(
            grads.astype(F32), "dp", scatter_dimension=0, tiled=True
        ).astype(BF16)
    dp = lax.axis_index("dp")
    c, x, y = lax.rem(dp, 2), lax.rem(dp // 2, 2), dp // 4

    def fold(value, axis, position, bit):
        mine = lax.dynamic_index_in_dim(value, position, axis, keepdims=False)
        other = lax.dynamic_index_in_dim(value, 1 - position, axis, keepdims=False)
        got = swap(other, "dp", dp_size, bit)
        return (mine.astype(F32) + got.astype(F32)).astype(BF16)

    value = grads.reshape((2, 2, 2, rows) + grads.shape[1:])
    value = fold(value, 2, c, 1)
    width = value.shape[-1]
    half = (width // 2 + 127) // 128 * 128
    first = fold(fold(value[..., :half], 1, x, 2), 0, y, 4)
    second = fold(fold(value[..., half:], 0, y, 4), 0, x, 2)
    return jnp.concatenate([first, second], axis=-1)


def reduce_weights(grads, dp_size):
    z = lax.axis_index("tensor")
    part = reduce_dp(grads, dp_size)
    total = lax.dynamic_index_in_dim(part, z, 1, keepdims=False).astype(F32)
    for j in (1, 2, 3):
        piece = lax.dynamic_index_in_dim(part, z ^ j, 1, keepdims=False)
        total = total + swap(piece, "tensor", 4, j).astype(F32)
    return total


def heads(rows):
    return rows.reshape(rows.shape[0], -1, HDIM)


def scores_of(queries, keys, mask):
    scores = jnp.einsum("qhd,khd->hqk", heads(queries), heads(keys), preferred_element_type=F32)
    return jnp.where(mask, scores * HDIM ** (-0.5), -1000000000.0)


def attend(queries, keys, values, mask):
    scores = scores_of(queries, keys, mask)
    top = jnp.max(scores, axis=-1, keepdims=True)
    lse = top + jnp.log(jnp.sum(jnp.exp(scores - top), axis=-1, keepdims=True))
    probs = jnp.exp(scores - lse).astype(BF16)
    out = jnp.einsum("hqk,khd->qhd", probs, heads(values), preferred_element_type=F32)
    return out.reshape(queries.shape), lse


def attend_back(queries, keys, values, mask, lse, grad_out, row_dot):
    probs = jnp.exp(scores_of(queries, keys, mask) - lse)
    grad_probs = jnp.einsum(
        "qhd,khd->hqk", heads(grad_out), heads(values), preferred_element_type=F32
    )
    if row_dot is None:
        row_dot = jnp.sum(probs * grad_probs, axis=-1, keepdims=True)
    grad_scores = (probs * (grad_probs - row_dot)).astype(BF16)
    scale = HDIM ** (-0.5)
    grad_q = jnp.einsum("hqk,khd->qhd", grad_scores, heads(keys), preferred_element_type=F32)
    grad_k = jnp.einsum("hqk,qhd->khd", grad_scores, heads(queries), preferred_element_type=F32)
    grad_v = jnp.einsum(
        "hqk,qhd->khd", probs.astype(BF16), heads(grad_out), preferred_element_type=F32
    )
    return (
        grad_q.reshape(queries.shape) * scale,
        (grad_k.reshape(keys.shape) * scale).astype(BF16),
        grad_v.reshape(values.shape).astype(BF16),
    )


def make(mesh):
    dp_size = mesh.shape["dp"]

    def on_device(
        block_in,
        source,
        target_len,
        source_len,
        targets,
        gain_self,
        gain_cross,
        gain_ff,
        gain_final,
        self_q,
        self_k,
        self_v,
        self_o,
        cross_q,
        cross_k,
        cross_v,
        cross_o,
        ff_gate,
        ff_up,
        ff_down,
        embed_table,
    ):
        z = lax.axis_index("tensor")
        half = lax.rem(z, 2)
        seq = z // 2
        rows = block_in.shape[0]
        srcs = source.shape[0]

        def pair_swap(value):
            return swap(value, "tensor", 4, 1)

        def pair_rows(own):
            other = pair_swap(own)
            return jnp.where(
                half == 0,
                jnp.concatenate([own, other], 0),
                jnp.concatenate([other, own], 0),
            )

        def own_rows(both, axis=0):
            return lax.dynamic_slice_in_dim(both, half * rows, rows, axis)

        def other_rows(both, axis=0):
            return lax.dynamic_slice_in_dim(both, (1 - half) * rows, rows, axis)

        w_self, w_cross, w_ff = gather_weights(
            [
                jnp.concatenate([self_q.T, self_k.T, self_v.T, self_o], 0),
                jnp.concatenate([cross_q.T, cross_k.T, cross_v.T, cross_o], 0),
                jnp.concatenate([ff_gate.T, ff_up.T, ff_down], 0),
            ],
            dp_size,
        )

        def part(stack, index, size):
            return stack[:, index * size : (index + 1) * size].reshape(-1, D)

        hid = self_q.shape[1]
        fhid = ff_gate.shape[1]
        sq, sk, sv, so = (part(w_self, i, hid) for i in range(4))
        cq, ck, cv, co = (part(w_cross, i, hid) for i in range(4))
        wg, wu, wd = (part(w_ff, i, fhid) for i in range(3))

        my_len = lax.dynamic_index_in_dim(target_len, seq, keepdims=False)
        my_src = lax.dynamic_index_in_dim(source_len, seq, keepdims=False)
        pos = jnp.arange(TGT)
        self_mask = ((pos[None, :] <= pos[:, None]) & (pos[None, :] < my_len))[None]
        cross_mask = (half * srcs + jnp.arange(srcs) < my_src)[None, None, :]

        x_pair = pair_rows(block_in).astype(F32)
        n1, r1 = normalize(x_pair, gain_self)
        n1 = n1.astype(BF16)
        q1 = dot_nt(n1, sq).astype(BF16)
        k1 = dot_nt(n1, sk).astype(BF16)
        v1 = dot_nt(n1, sv).astype(BF16)
        a1, lse1 = attend(q1, k1, v1, self_mask)
        a1 = a1.astype(BF16)
        h1 = x_pair + dot_nn(a1, so)
        n2, r2 = normalize(h1, gain_cross)
        n2 = n2.astype(BF16)
        q2 = dot_nt(n2, cq).astype(BF16)
        k2 = dot_nt(source, ck).astype(BF16)
        v2 = dot_nt(source, cv).astype(BF16)
        o2, lse_own = attend(q2, k2, v2, cross_mask)
        o2_other = pair_swap(other_rows(o2).astype(BF16)).astype(F32)
        lse_other = pair_swap(lse_own)
        lse2 = jnp.logaddexp(lse_own, lse_other)

        def weigh(lse_part, out_part):
            weight = own_rows(jnp.exp(lse_part - lse2), 1)[:, :, 0].T
            return (heads(out_part) * weight[:, :, None]).reshape(out_part.shape)

        a2 = weigh(lse_own, own_rows(o2)) + weigh(lse_other, o2_other)
        a2b = a2.astype(BF16)
        h1o = own_rows(h1)
        r2o = own_rows(r2)
        h2 = h1o + dot_nn(a2b, co)
        n3, r3 = normalize(h2, gain_ff)
        n3 = n3.astype(BF16)
        gate_pre = dot_nt(n3, wg)
        up_pre = dot_nt(n3, wu)
        gelu_gate, gelu_back = jax.vjp(lambda v: jax.nn.gelu(v, approximate=True), gate_pre)
        mixed = (gelu_gate * up_pre).astype(BF16)
        block_out = h2 + dot_nn(mixed, wd)
        nf, rf = normalize(block_out, gain_final)
        fin = (nf * D ** (-0.5)).astype(BF16)

        vocab = embed_table.shape[0]
        fin_all = jnp.concatenate([fin] + [swap(fin, "tensor", 4, j) for j in (1, 2, 3)], 0)

        def relative(by_block):
            return jnp.concatenate(
                [lax.dynamic_index_in_dim(by_block, z ^ j, 0, keepdims=False) for j in range(4)], 0
            )

        tgt_rel = relative(targets.reshape(4, rows))
        pos_all = jnp.arange(4 * rows)
        live = lax.rem(pos_all, TGT) < jnp.repeat(target_len, TGT, total_repeat_length=4 * rows)
        live_rel = relative(live.reshape(4, rows))
        logits = dot_nt(fin_all, embed_table)
        columns = z * vocab + jnp.arange(vocab)
        hit = columns[None, :] == tgt_rel[:, None]
        top = jnp.max(logits, axis=1)
        total = jnp.sum(jnp.exp(logits - top[:, None]), axis=1)
        picked = jnp.sum(jnp.where(hit, logits, 0.0), axis=1)
        stats = jnp.stack([top, total, picked]).reshape(3, 4, rows)
        stats = jnp.stack(
            [lax.dynamic_index_in_dim(stats, z ^ j, 1, keepdims=False) for j in range(4)], 1
        )
        gathered = jnp.stack(
            [stats] + [swap(stats, "tensor", 4, j) for j in (1, 2, 3)], 0
        ).reshape(4, 3, 4 * rows)
        g_top = jnp.max(gathered[:, 0], axis=0)
        g_total = jnp.sum(gathered[:, 1] * jnp.exp(gathered[:, 0] - g_top), axis=0)
        g_lse = g_top + jnp.log(g_total)
        token_loss = jnp.where(live, g_lse - jnp.sum(gathered[:, 2], axis=0), 0.0)
        lse_rel = relative(g_lse.reshape(4, rows))
        grad_logits = jnp.where(
            live_rel[:, None],
            jnp.exp(logits - lse_rel[:, None]) - hit.astype(F32),
            0.0,
        ).astype(BF16)
        gf_all = dot_nn(grad_logits, embed_table)
        grad_final = gf_all[:rows]
        for j in (1, 2, 3):
            grad_final = grad_final + swap(
                gf_all[j * rows : (j + 1) * rows].astype(BF16), "tensor", 4, j
            ).astype(F32)
        grad_embed = dot_tn(fin_all, grad_logits).astype(BF16)
        grad_embed = reduce_dp(grad_embed, dp_size).astype(F32).T

        def by_shard(grad):
            return grad.astype(BF16).reshape(D, 4, -1)

        g_res, gg_final = norm_back(block_out, rf, gain_final, grad_final * D ** (-0.5))
        gr = g_res.astype(BF16)
        grad_mixed = dot_nt(gr, wd)
        g_gate = gelu_back(grad_mixed * up_pre)[0].astype(BF16)
        g_up = (grad_mixed * gelu_gate).astype(BF16)
        gn3 = dot_nn(g_gate, wg) + dot_nn(g_up, wu)
        step, gg_ff = norm_back(h2, r3, gain_ff, gn3)
        g_res = g_res + step
        ff_grads = reduce_weights(
            jnp.concatenate(
                [
                    by_shard(dot_tn(n3, g_gate)),
                    by_shard(dot_tn(n3, g_up)),
                    by_shard(dot_tn(gr, mixed)),
                ],
                2,
            ),
            dp_size,
        )
        gr_own = g_res.astype(BF16)
        gr = pair_rows(gr_own)
        g_att = dot_nt(gr, co).astype(BF16)
        dot_own = jnp.sum(heads(own_rows(g_att).astype(F32)) * heads(a2), axis=-1).T[:, :, None]
        dot_other = pair_swap(dot_own)
        row_dot = jnp.where(
            half == 0,
            jnp.concatenate([dot_own, dot_other], 1),
            jnp.concatenate([dot_other, dot_own], 1),
        )
        gq, gk, gv = attend_back(q2, k2, v2, cross_mask, lse2, g_att, row_dot)
        gq = (own_rows(gq) + pair_swap(other_rows(gq).astype(BF16)).astype(F32)).astype(BF16)
        grad_source = dot_nn(gk, ck) + dot_nn(gv, cv)
        n2o = own_rows(n2)
        cross_grads = reduce_weights(
            jnp.concatenate(
                [
                    by_shard(dot_tn(n2o, gq)),
                    by_shard(dot_tn(source, gk)),
                    by_shard(dot_tn(source, gv)),
                    by_shard(dot_tn(gr_own, a2b)),
                ],
                2,
            ),
            dp_size,
        )
        step, gg_cross = norm_back(h1o, r2o, gain_cross, dot_nn(gq, cq))
        g_res = g_res + step
        gr_own = g_res.astype(BF16)
        gr = pair_rows(gr_own)
        g_att = dot_nt(gr, so).astype(BF16)
        gq, gk, gv = attend_back(q1, k1, v1, self_mask, lse1, g_att, None)
        gq, gk, gv = own_rows(gq.astype(BF16)), own_rows(gk), own_rows(gv)
        n1o = own_rows(n1)
        self_grads = reduce_weights(
            jnp.concatenate(
                [
                    by_shard(dot_tn(n1o, gq)),
                    by_shard(dot_tn(n1o, gk)),
                    by_shard(dot_tn(n1o, gv)),
                    by_shard(dot_tn(gr_own, own_rows(a1))),
                ],
                2,
            ),
            dp_size,
        )
        gn1 = dot_nn(gq, sq) + dot_nn(gk, sk) + dot_nn(gv, sv)
        step, gg_self = norm_back(own_rows(x_pair), own_rows(r1), gain_self, gn1)
        grad_block_in = g_res + step
        gains = lax.psum(jnp.stack([gg_self, gg_cross, gg_ff, gg_final]), ("dp", "tensor"))

        def cols(grads, index, size):
            return grads[:, index * size : (index + 1) * size]

        return (
            block_out,
            token_loss,
            grad_block_in,
            grad_source,
            gains[0],
            gains[1],
            gains[2],
            gains[3],
            cols(self_grads, 0, hid),
            cols(self_grads, 1, hid),
            cols(self_grads, 2, hid),
            cols(self_grads, 3, hid).T,
            cols(cross_grads, 0, hid),
            cols(cross_grads, 1, hid),
            cols(cross_grads, 2, hid),
            cols(cross_grads, 3, hid).T,
            cols(ff_grads, 0, fhid),
            cols(ff_grads, 1, fhid),
            cols(ff_grads, 2, fhid).T,
            grad_embed,
        )

    return on_device


def solution(mesh):
    rows = P(("dp", "tensor"), None)
    wide, tall = P(None, "tensor"), P("tensor", None)
    in_specs = (rows, rows) + (P("dp"),) * 3 + (P(),) * 4
    in_specs += (wide, wide, wide, tall) * 2 + (wide, wide, tall, tall)
    g_in, g_out = P("dp", "tensor"), P("tensor", "dp")
    out_specs = (rows, P("dp"), rows, rows) + (P(),) * 4
    out_specs += (g_in, g_in, g_in, g_out) * 2 + (g_in, g_in, g_out, g_out)
    return jax.shard_map(
        make(mesh), mesh=mesh, in_specs=in_specs, out_specs=out_specs, check_vma=False
    )
```

```python
import functools
import math

import jax
import jax.numpy as jnp
from jax import lax
from jax.sharding import PartitionSpec as P
from jax.experimental import pallas as pl
from jax.experimental.pallas import tpu as pltpu

D = 768
HDIM = 64
NHEAD = D // HDIM
PAIRS = NHEAD // 2
FF = 2048
TGT = 512
ROWS = 256
KEYS = 1024
CHUNK = 256
HALF_D = D // 2
VTILE = 512
F32 = jnp.float32
BF16 = jnp.bfloat16
MESH_ID = pl.DeviceIdType.MESH
VMEM_LIMIT = 56 * 2**20
NEG = -1000000000.0
SCALE = HDIM ** (-0.5)
EPS = 1e-06


def dot_nt(left, right):
    return lax.dot_general(left, right, (((1,), (1,)), ((), ())), preferred_element_type=F32)


def dot_nn(left, right):
    return lax.dot_general(left, right, (((1,), (0,)), ((), ())), preferred_element_type=F32)


def swap(value, axis_name, size, bit):
    return lax.ppermute(value, axis_name, [(i, i ^ bit) for i in range(size)])


def gather_kernel(groups, *refs):
    ins, outs = refs[:groups], refs[groups : 2 * groups]
    send_sem, recv_sem, local_sem = refs[2 * groups :]
    dp = lax.axis_index("dp")
    z = lax.axis_index("tensor")
    core_peer = dp + 1 - 2 * lax.rem(dp, 2)
    x_peer = dp + 2 - 4 * lax.rem(dp // 2, 2)
    y_peer = dp + 4 - 8 * (dp // 4)
    xy_peer = x_peer + y_peer - dp
    low, high = lax.rem(z, 2), z // 2
    z_peers = [high * 2 + 1 - low, (1 - high) * 2 + low, (1 - high) * 2 + 1 - low]
    barrier = pltpu.get_barrier_semaphore()
    for other in (core_peer, x_peer, y_peer):
        pl.semaphore_signal(
            barrier, inc=1, device_id={"dp": other, "tensor": z}, device_id_type=MESH_ID
        )
    for other in z_peers:
        pl.semaphore_signal(
            barrier, inc=1, device_id={"dp": dp, "tensor": other}, device_id_type=MESH_ID
        )
    pl.semaphore_wait(barrier, 6)

    rows, hid = 96, 192

    def piece(g, shard, owner, start=0, count=rows):
        offset = pl.multiple_of(shard * hid + lax.rem(owner, 2) * rows + start, 16)
        return outs[g].at[owner // 2, pl.ds(offset, count)]

    used = [0]

    def remote(src, dst, target_dp, target_z):
        sem = used[0]
        used[0] += 1
        copy = pltpu.make_async_remote_copy(
            src_ref=src,
            dst_ref=dst,
            send_sem=send_sem.at[sem],
            recv_sem=recv_sem.at[sem],
            device_id={"dp": target_dp, "tensor": target_z},
            device_id_type=MESH_ID,
        )
        copy.start()
        return copy

    def along_z(g):
        offset = pl.multiple_of(dp * rows, 16)
        return [
            remote(ins[g].at[pl.ds(offset, rows)], piece(g, z, dp), dp, z_peers[j])
            for j in range(3)
        ]

    z_copies, x_copies, y_copies, d_copies, c_copies, own = {}, {}, {}, {}, {}, []
    z_copies[0] = along_z(0)
    for g in range(groups):
        for m in range(4):
            copy = pltpu.make_async_copy(
                ins[g].at[pl.ds(m * hid, hid)],
                outs[g].at[m, pl.ds(pl.multiple_of(z * hid, 16), hid)],
                local_sem.at[4 * g + m],
            )
            copy.start()
            own.append(copy)
    for step in range(groups + 2):
        g = step
        if g < groups:
            for copy in z_copies[g]:
                copy.wait()
            if g + 1 < groups:
                z_copies[g + 1] = along_z(g + 1)
            x_copies[g], y_copies[g], c_copies[g] = [], [], []
            for peer in z_peers:
                part = piece(g, peer, dp)
                x_copies[g].append(remote(part, part, x_peer, z))
                y_copies[g].append(remote(part, part, y_peer, z))
                c_copies[g].append(remote(part, part, core_peer, z))
        g = step - 1
        if 0 <= g < groups:
            d_copies[g] = []
            for j, peer in enumerate(z_peers):
                x_copies[g][j].wait()
                part = piece(g, peer, x_peer, 0, rows // 2)
                d_copies[g].append(remote(part, part, y_peer, z))
                y_copies[g][j].wait()
                part = piece(g, peer, y_peer, rows // 2, rows // 2)
                d_copies[g].append(remote(part, part, x_peer, z))
                for owner in (x_peer, y_peer):
                    part = piece(g, peer, owner)
                    c_copies[g].append(remote(part, part, core_peer, z))
        g = step - 2
        if 0 <= g < groups:
            for j, peer in enumerate(z_peers):
                d_copies[g][2 * j].wait()
                d_copies[g][2 * j + 1].wait()
                part = piece(g, peer, xy_peer)
                c_copies[g].append(remote(part, part, core_peer, z))
    for copy in own:
        copy.wait()
    for g in range(groups):
        for copy in c_copies[g]:
            copy.wait()


def gather_wide(shard, dp_size):
    rows = shard.shape[0] // dp_size
    part = lax.dynamic_slice_in_dim(shard, lax.axis_index("dp") * rows, rows, 0)
    return lax.all_gather(part, ("tensor", "dp"), axis=0, tiled=True)


def gather_blocks(shards, dp_size):
    if dp_size != 8:
        return [
            gather_wide(shard, dp_size).reshape(4, 4, D // 4, D).swapaxes(0, 1).reshape(4, D, D)
            for shard in shards
        ]
    groups = len(shards)
    return pl.pallas_call(
        functools.partial(gather_kernel, groups),
        out_shape=[jax.ShapeDtypeStruct((4, D, D), BF16) for _ in shards],
        in_specs=[pl.BlockSpec(memory_space=pl.ANY)] * groups,
        out_specs=[pl.BlockSpec(memory_space=pl.ANY)] * groups,
        scratch_shapes=[
            pltpu.SemaphoreType.DMA((27 * groups,)),
            pltpu.SemaphoreType.DMA((27 * groups,)),
            pltpu.SemaphoreType.DMA((4 * groups,)),
        ],
        compiler_params=pltpu.CompilerParams(collective_id=0, has_side_effects=True),
    )(*shards)


def tile_of(width):
    return 512 if width % 512 == 0 else 384


def fold_call(body, xyz, ins, outs, width, out_specs=None):
    tile = tile_of(width)

    def spec(rows, dtype, index):
        return pl.BlockSpec((rows, tile), index)

    smem = pl.BlockSpec(memory_space=pltpu.SMEM)
    left, right = (lambda i: (0, i)), (lambda i: (0, i + width // tile))
    in_specs = [smem] + [
        spec(a.shape[0], a.dtype, right if second else left) for a, second in ins
    ]
    moved = sum(a.shape[0] * width * a.dtype.itemsize for a, _ in ins)
    moved += sum(o.size * jnp.dtype(o.dtype).itemsize for o in outs)
    rows = max(a.shape[0] for a, _ in ins)
    return pl.pallas_call(
        body,
        grid=(width // tile,),
        out_shape=outs,
        in_specs=in_specs,
        out_specs=out_specs or [spec(o.shape[0], o.dtype, left) for o in outs],
        scratch_shapes=[pltpu.VMEM((rows, tile), F32)],
        cost_estimate=pl.CostEstimate(flops=0, bytes_accessed=moved, transcendentals=0),
    )(xyz, *[a for a, _ in ins])


def block_rows(index):
    return pl.ds(pl.multiple_of(index * 96, 96), 96)


def first_fold(xyz, mine_a, got_a, mine_b, got_b, keep_a, send_a, keep_b, send_b, sum_ref):
    x, y = xyz[0], xyz[1]
    sum_ref[...] = mine_a[...] + got_a[...].astype(F32)
    for other in range(2):
        rows = slice(other * 96, (other + 1) * 96)
        keep_a[rows, :] = sum_ref[block_rows(2 * other + x), :]
        send_a[rows, :] = sum_ref[block_rows(2 * other + 1 - x), :].astype(BF16)
    sum_ref[...] = mine_b[...] + got_b[...].astype(F32)
    for other in range(2):
        rows = slice(other * 96, (other + 1) * 96)
        keep_b[rows, :] = sum_ref[block_rows(2 * y + other), :]
        send_b[rows, :] = sum_ref[block_rows(2 * (1 - y) + other), :].astype(BF16)


def second_fold(xyz, mine_a, got_a, mine_b, got_b, keep_a, send_a, keep_b, send_b, sum_ref):
    x, y = xyz[0], xyz[1]
    sum_ref[...] = mine_a[...] + got_a[...].astype(F32)
    keep_a[...] = sum_ref[block_rows(y), :]
    send_a[...] = sum_ref[block_rows(1 - y), :].astype(BF16)
    sum_ref[...] = mine_b[...] + got_b[...].astype(F32)
    keep_b[...] = sum_ref[block_rows(x), :]
    send_b[...] = sum_ref[block_rows(1 - x), :].astype(BF16)


def third_fold(xyz, mine_a, got_a, mine_b, got_b, keep, send_1, send_2, send_3, sum_ref):
    z = xyz[2]
    width = keep.shape[1]
    for m, (mine, got) in enumerate(((mine_a, got_a), (mine_b, got_b))):
        total = mine[...] + got[...].astype(F32)
        sum_ref[2 * m] = total[:, :width]
        sum_ref[2 * m + 1] = total[:, width:]
    keep[...] = sum_ref[z]
    low, high = lax.rem(z, 2), z // 2
    send_1[...] = sum_ref[2 * high + 1 - low].astype(BF16)
    send_2[...] = sum_ref[2 * (1 - high) + low].astype(BF16)
    send_3[...] = sum_ref[2 * (1 - high) + 1 - low].astype(BF16)


def last_fold(flips, keep, got_1, got_2, got_3, *outs):
    total = keep[...] + got_1[...].astype(F32) + (got_2[...].astype(F32) + got_3[...].astype(F32))
    width = keep.shape[1] // len(outs)
    for m, out in enumerate(outs):
        part = total[:, m * width : (m + 1) * width]
        out[...] = part.T if m in flips else part


def table_fold(mine, got, out):
    out[...] = (mine[...] + got[...].astype(F32)).T


class Reduction:
    def __init__(self, xyz, mine, send):
        self.xyz, self.mine, self.width = xyz, mine, mine.shape[1] // 2
        self.got = swap(send, "dp", 8, 1)

    def first(self):
        ins = [(self.mine, 0), (self.got, 0), (self.mine, 1), (self.got, 1)]
        shape = (192, self.width)
        outs = [whole(shape, F32), whole(shape, BF16)] * 2
        keep_a, send_a, keep_b, send_b = fold_call(first_fold, self.xyz, ins, outs, self.width)
        self.keeps = keep_a, keep_b
        self.gots = swap(send_a, "dp", 8, 2), swap(send_b, "dp", 8, 4)
        return send_a, send_b

    def second(self):
        (keep_a, keep_b), (got_a, got_b) = self.keeps, self.gots
        ins = [(keep_a, 0), (got_a, 0), (keep_b, 0), (got_b, 0)]
        shape = (96, self.width)
        outs = [whole(shape, F32), whole(shape, BF16)] * 2
        keep_a, send_a, keep_b, send_b = fold_call(second_fold, self.xyz, ins, outs, self.width)
        self.keeps = keep_a, keep_b
        self.gots = swap(send_a, "dp", 8, 4), swap(send_b, "dp", 8, 2)
        return send_a, send_b

    def third(self):
        (keep_a, keep_b), (got_a, got_b) = self.keeps, self.gots
        shape = (96, self.width // 2)
        keep, *sends = pl.pallas_call(
            third_fold,
            out_shape=[whole(shape, F32)] + [whole(shape, BF16)] * 3,
            in_specs=[pl.BlockSpec(memory_space=pltpu.SMEM)]
            + [pl.BlockSpec(memory_space=pltpu.VMEM)] * 4,
            out_specs=[pl.BlockSpec(memory_space=pltpu.VMEM)] * 4,
            scratch_shapes=[pltpu.VMEM((4,) + shape, F32)],
        )(self.xyz, keep_a, got_a, keep_b, got_b)
        self.keeps = keep
        self.gots = [swap(send, "tensor", 4, j + 1) for j, send in enumerate(sends)]
        return tuple(sends)

    def last(self, count, flips):
        rows, width = self.keeps.shape
        shape = (rows, width // count)
        outs = [whole(shape[::-1] if m in flips else shape, F32) for m in range(count)]
        return pl.pallas_call(functools.partial(last_fold, flips), out_shape=outs)(
            self.keeps, *self.gots
        )

    def table(self, vocab):
        parts = []
        for keep, got, start in zip(self.keeps, self.gots, (0, self.width)):
            count = min(self.width, vocab - start)
            tile = pl.BlockSpec((96, VTILE), lambda i: (0, i))
            parts.append(
                pl.pallas_call(
                    table_fold,
                    grid=(pl.cdiv(count, VTILE),),
                    out_shape=whole((count, 96), F32),
                    in_specs=[tile] * 2,
                    out_specs=pl.BlockSpec((VTILE, 96), lambda i: (i, 0)),
                )(keep, got)
            )
        return jnp.concatenate(parts, 0)


class WideReduction:
    def __init__(self, xyz, mine, send):
        self.z = xyz[2]
        both = jnp.concatenate([mine, send.astype(F32)], 0)
        self.part = lax.psum_scatter(both, "dp", scatter_dimension=0, tiled=True)

    def first(self):
        return ()

    second = third = first

    def last(self, count, flips):
        rows = self.part.shape[0]
        by_z = self.part.reshape(rows, 4, -1)
        total = lax.psum_scatter(by_z, "tensor", scatter_dimension=1, tiled=True)[:, 0]
        parts = jnp.split(total, count, axis=1)
        return [p.T if m in flips else p for m, p in enumerate(parts)]

    def table(self, vocab):
        return self.part.T


def after(value, *others):
    return lax.optimization_barrier((value,) + others)[0]


def rms_scale(values):
    return lax.rsqrt(jnp.mean(values * values, axis=-1, keepdims=True) + EPS)


def norm_back(values, inv_scale, gain, grad_out):
    weighted = gain * grad_out
    grad_gain = jnp.sum(grad_out * values * inv_scale, axis=0, keepdims=True)
    grad_values = inv_scale * weighted - values * inv_scale * inv_scale * inv_scale * jnp.mean(
        weighted * values, axis=-1, keepdims=True
    )
    return grad_values, grad_gain


def flip(value):
    return value.astype(F32).T


def lane_half(rows, which):
    lane = lax.broadcasted_iota(jnp.int32, (rows, 2 * HDIM), 1)
    return (lane >= HDIM) if which else (lane < HDIM)


def only(value, which):
    return jnp.where(lane_half(value.shape[0], which), value, jnp.zeros_like(value))


def split_rows(flat_ref, mine_ref, send_ref, core, split):
    for block in range(4):
        if split:
            first = pl.multiple_of((2 * block + core) * 96, 96)
            second = pl.multiple_of((2 * block + 1 - core) * 96, 96)
        else:
            first, second = block * 96, HALF_D + block * 96
        mine_ref[block * 96 : (block + 1) * 96, :] = flat_ref[pl.ds(first, 96), :]
        send_ref[block * 96 : (block + 1) * 96, :] = flat_ref[pl.ds(second, 96), :]


def by_shard(left_ref, rights, out_ref, first, per_shard):
    width = 192 * len(rights)
    for z in range(4):
        part = [right[:, z * 192 : (z + 1) * 192] for right in rights]
        right = jnp.concatenate(part, axis=1) if len(part) > 1 else part[0]
        start = z * per_shard + first
        out_ref[:, start : start + width] = dot_nn(left_ref[...], right).astype(out_ref.dtype)


def whole(shape, dtype):
    return jax.ShapeDtypeStruct(shape, dtype)


def local_call(body, outs, scratch, flops, *args):
    smem = pl.BlockSpec(memory_space=pltpu.SMEM)
    vmem = pl.BlockSpec(memory_space=pltpu.VMEM)
    bytes_all = sum(a.size * a.dtype.itemsize for a in args)
    bytes_all += sum(o.size * jnp.dtype(o.dtype).itemsize for o in outs)
    held = sum(math.prod(s.shape) * jnp.dtype(s.dtype).itemsize for s in scratch)
    return pl.pallas_call(
        body,
        out_shape=outs,
        in_specs=[smem] + [vmem] * (len(args) - 1),
        out_specs=[vmem] * len(outs),
        scratch_shapes=scratch,
        cost_estimate=pl.CostEstimate(
            flops=int(flops), bytes_accessed=int(bytes_all), transcendentals=0
        ),
        compiler_params=pltpu.CompilerParams(
            vmem_limit_bytes=min(VMEM_LIMIT, int(bytes_all + held + 16 * 2**20))
        ),
    )(*args)


def self_forward(
    scal, x_own, x_other, gain_self, gain_cross, w_self, w_cq,
    q_out, k_out, v_out, lse_out, att_out, h1_out, q2_out,
    x_ref, n_ref, vt_ref, ot_ref,
):
    half = scal[0]
    live = scal[1]
    own = pl.multiple_of(half * ROWS, ROWS)
    x_ref[pl.ds(own, ROWS), :] = x_own[...].astype(F32)
    x_ref[pl.ds(pl.multiple_of((1 - half) * ROWS, ROWS), ROWS), :] = x_other[...].astype(F32)
    for i in range(2):
        rows = slice(i * ROWS, (i + 1) * ROWS)
        x = x_ref[rows, :]
        n = (x * rms_scale(x) * gain_self[...]).astype(BF16)
        n_ref[rows, :] = n
        q_out[rows, :] = dot_nt(n, w_self[0]).astype(BF16)
        k_out[rows, :] = dot_nt(n, w_self[1]).astype(BF16)
        v_out[rows, :] = dot_nt(n, w_self[2]).astype(BF16)
    vt_ref[...] = dot_nt(w_self[2], n_ref[...]).astype(BF16)
    lse_out[...] = jnp.zeros_like(lse_out)
    key = lax.broadcasted_iota(jnp.int32, (TGT, TGT), 0)
    query = lax.broadcasted_iota(jnp.int32, (TGT, TGT), 1)
    seen = (key <= query) & (key < live)

    @pl.loop(0, PAIRS)
    def _(pair):
        lanes = pl.ds(pl.multiple_of(pair * 128, 128), 128)
        q_pair, k_pair = q_out[:, lanes], k_out[:, lanes]
        for which in range(2):
            head = 2 * pair + which
            feats = pl.ds(pl.multiple_of(head * HDIM, HDIM), HDIM)
            scores = jnp.where(seen, dot_nt(k_pair, only(q_pair, which)) * SCALE, NEG)
            top = jnp.max(scores, axis=0, keepdims=True)
            probs = jnp.exp(scores - top)
            total = jnp.sum(probs, axis=0, keepdims=True)
            lse_out[pl.ds(head, 1), :] = top + jnp.log(total)
            out = dot_nn(vt_ref[feats, :], probs.astype(BF16)) / total
            ot_ref[feats, :] = out

    for i in range(2):
        rows = slice(i * ROWS, (i + 1) * ROWS)
        att = flip(ot_ref[:, rows]).astype(BF16)
        n_ref[rows, :] = att
        h1 = x_ref[rows, :] + dot_nn(att, w_self[3])
        x_ref[rows, :] = h1
        n = (h1 * rms_scale(h1) * gain_cross[...]).astype(BF16)
        q2_out[rows, :] = dot_nt(n, w_cq[...]).astype(BF16)
    att_out[...] = n_ref[pl.ds(own, ROWS), :]
    h1_out[...] = x_ref[pl.ds(own, ROWS), :]


def cross_forward(
    scal, q2, source, w_ck, w_cv, k_out, v_out, own_out, send_out, lse_out, vt_ref, s_ref, ot_ref
):
    half = scal[0]
    live = scal[2] - half * KEYS
    own = pl.multiple_of(half * ROWS, ROWS)
    other = pl.multiple_of((1 - half) * ROWS, ROWS)
    for i in range(KEYS // CHUNK):
        rows = slice(i * CHUNK, (i + 1) * CHUNK)
        src = source[rows, :]
        k_out[rows, :] = dot_nt(src, w_ck[...]).astype(BF16)
        v_out[rows, :] = dot_nt(src, w_cv[...]).astype(BF16)
        vt_ref[:, rows] = dot_nt(w_cv[...], src).astype(BF16)
    lse_out[...] = jnp.zeros_like(lse_out)
    key = lax.broadcasted_iota(jnp.int32, (CHUNK, TGT), 0)

    @pl.loop(0, PAIRS)
    def _(pair):
        lanes = pl.ds(pl.multiple_of(pair * 128, 128), 128)
        q_pair = q2[:, lanes]
        for which in range(2):
            head = 2 * pair + which
            feats = pl.ds(pl.multiple_of(head * HDIM, HDIM), HDIM)
            q_one = only(q_pair, which)
            top = jnp.full((1, TGT), 2 * NEG, F32)
            for i in range(KEYS // CHUNK):
                rows = slice(i * CHUNK, (i + 1) * CHUNK)
                scores = dot_nt(k_out[rows, lanes], q_one) * SCALE
                scores = jnp.where(key < live - i * CHUNK, scores, NEG)
                s_ref[rows, :] = scores
                top = jnp.maximum(top, jnp.max(scores, axis=0, keepdims=True))
            total = jnp.zeros((1, TGT), F32)
            out = jnp.zeros((HDIM, TGT), F32)
            for i in range(KEYS // CHUNK):
                rows = slice(i * CHUNK, (i + 1) * CHUNK)
                probs = jnp.exp(s_ref[rows, :] - top)
                total = total + jnp.sum(probs, axis=0, keepdims=True)
                out = out + dot_nn(vt_ref[feats, rows], probs.astype(BF16))
            lse_out[pl.ds(head, 1), :] = top + jnp.log(total)
            ot_ref[feats, :] = out / total

    own_out[...] = ot_ref[:, pl.ds(own, ROWS)]
    send_out[...] = ot_ref[:, pl.ds(other, ROWS)].astype(BF16)


def ff_forward(
    scal, o_own, o_other, lse_own, lse_other, h1, w_co, gain_ff, gain_final, wg, wu, wd,
    out_ref, fin_ref, h2_ref, att_t_ref, att_ref, lse_ref, mix_ref,
):
    half = scal[0]
    own = pl.multiple_of(half * ROWS, ROWS)
    first, second = lse_own[...], lse_other[...]
    top = jnp.maximum(first, second)
    lse_ref[...] = top + jnp.log(jnp.exp(first - top) + jnp.exp(second - top))
    lse = lse_ref[:, pl.ds(own, ROWS)]
    w_first = jnp.exp(lse_own[:, pl.ds(own, ROWS)] - lse)
    w_second = jnp.exp(lse_other[:, pl.ds(own, ROWS)] - lse)
    for head in range(NHEAD):
        feats = slice(head * HDIM, (head + 1) * HDIM)
        att_t_ref[feats, :] = (
            o_own[feats, :] * w_first[head : head + 1, :]
            + o_other[feats, :].astype(F32) * w_second[head : head + 1, :]
        )
    att = flip(att_t_ref[...]).astype(BF16)
    att_ref[...] = att
    h2 = h1[...] + dot_nn(att, w_co[...])
    h2_ref[...] = h2
    n3 = (h2 * rms_scale(h2) * gain_ff[...]).astype(BF16)

    @pl.loop(0, FF // 512)
    def _(i):
        rows = pl.ds(pl.multiple_of(i * 512, 512), 512)
        gate = dot_nt(n3, wg[rows, :])
        up = dot_nt(n3, wu[rows, :])
        mix_ref[:, rows] = (jax.nn.gelu(gate, approximate=True) * up).astype(BF16)

    out = h2 + dot_nn(mix_ref[...], wd[...])
    out_ref[...] = out
    fin_ref[...] = (out * rms_scale(out) * gain_final[...] * D ** (-0.5)).astype(BF16)


def ff_backward(
    split, scal, gf_own, gf_1, gf_2, gf_3, block_out, h2_in, gain_ff, gain_final, wg, wu, wd,
    w_co, att_t, mine_ref, send_ref, res_ref, rows_ref, gatt_ref, dot_ref, gg_ref,
    flat_ref, nm_ref, ns_ref, gm_ref, gs_ref, gn_ref,
):
    core = scal[3]
    grad = gf_own[...] + gf_1[...].astype(F32)
    grad = grad + (gf_2[...].astype(F32) + gf_3[...].astype(F32))
    out = block_out[...]
    res, gg_final = norm_back(out, rms_scale(out), gain_final[...], grad * D ** (-0.5))
    gg_ref[0:1, :] = gg_final
    rows_b = res.astype(BF16)
    res_ref[...] = res
    flat_ref[...] = flip(rows_b).astype(BF16)
    split_rows(flat_ref, gm_ref, gs_ref, core, split)
    h2 = h2_in[...]
    scale3 = rms_scale(h2)
    n3 = (h2 * scale3 * gain_ff[...]).astype(BF16)
    flat_ref[...] = flip(n3).astype(BF16)
    split_rows(flat_ref, nm_ref, ns_ref, core, split)
    gn_ref[...] = jnp.zeros_like(gn_ref)
    const = (2.0 / 3.141592653589793) ** 0.5

    @pl.loop(0, FF // 512)
    def _(i):
        start = pl.multiple_of(i * 512, 512)
        rows = pl.ds(start, 512)
        gate = dot_nt(n3, wg[rows, :])
        up = dot_nt(n3, wu[rows, :])
        square = gate * gate
        tanh = jnp.tanh(const * (gate + 0.044715 * gate * square))
        gelu = 0.5 * gate * (1.0 + tanh)
        slope = 0.5 * (1.0 + tanh) + 0.5 * gate * (1.0 - tanh * tanh) * const * (
            1.0 + 3.0 * 0.044715 * square
        )
        grad_mixed = dot_nt(rows_b, wd[rows, :])
        g_gate = (grad_mixed * up * slope).astype(BF16)
        g_up = (grad_mixed * gelu).astype(BF16)
        mixed = (gelu * up).astype(BF16)
        gn_ref[...] += dot_nn(g_gate, wg[rows, :]) + dot_nn(g_up, wu[rows, :])
        for m, (mine, send, right) in enumerate(
            ((nm_ref, ns_ref, g_gate), (nm_ref, ns_ref, g_up), (gm_ref, gs_ref, mixed))
        ):
            cols = pl.ds(pl.multiple_of(3 * start + m * 512, 512), 512)
            mine_ref[:, cols] = dot_nn(mine[...], right)
            send_ref[:, cols] = dot_nn(send[...], right).astype(BF16)

    step, gg_ff = norm_back(h2, scale3, gain_ff[...], gn_ref[...])
    gg_ref[1:2, :] = gg_ff
    res = res_ref[...] + step
    res_ref[...] = res
    rows_b = res.astype(BF16)
    rows_ref[...] = rows_b
    gatt_ref[...] = dot_nt(rows_b, w_co[...]).astype(BF16)
    gatt_t = dot_nt(w_co[...], rows_b).astype(BF16).astype(F32)
    dot_ref[...] = jnp.zeros_like(dot_ref)
    for head in range(NHEAD):
        feats = slice(head * HDIM, (head + 1) * HDIM)
        dot_ref[head : head + 1, :] = jnp.sum(gatt_t[feats, :] * att_t[feats, :], 0, keepdims=True)


def both_halves(half, own, other, target):
    target[pl.ds(pl.multiple_of(half * ROWS, ROWS), ROWS), :] = own[...]
    target[pl.ds(pl.multiple_of((1 - half) * ROWS, ROWS), ROWS), :] = other[...]


def cross_backward(
    scal, q2, k2, v2, lse, g_own, g_other, dot_own, dot_other,
    dk_ref, dv_ref, own_out, send_out, g_ref, dot_ref, dq_ref,
):
    half = scal[0]
    live = scal[2] - half * KEYS
    own = pl.multiple_of(half * ROWS, ROWS)
    other = pl.multiple_of((1 - half) * ROWS, ROWS)
    both_halves(half, g_own, g_other, g_ref)
    dot_ref[:, pl.ds(own, ROWS)] = dot_own[...]
    dot_ref[:, pl.ds(other, ROWS)] = dot_other[...]
    key = lax.broadcasted_iota(jnp.int32, (CHUNK, TGT), 0)

    @pl.loop(0, PAIRS)
    def _(pair):
        lanes = pl.ds(pl.multiple_of(pair * 128, 128), 128)
        q_pair, g_pair = q2[:, lanes], g_ref[:, lanes]
        for i in range(KEYS // CHUNK):
            rows = slice(i * CHUNK, (i + 1) * CHUNK)
            k_part, v_part = k2[rows, lanes], v2[rows, lanes]
            k_flip = flip(k_part).astype(BF16)
            grad_k = jnp.zeros((CHUNK, 128), F32)
            grad_v = jnp.zeros((CHUNK, 128), F32)
            for which in range(2):
                head = 2 * pair + which
                feats = pl.ds(pl.multiple_of(head * HDIM, HDIM), HDIM)
                q_one, g_one = only(q_pair, which), only(g_pair, which)
                scores = dot_nt(k_part, q_one) * SCALE
                scores = jnp.where(key < live - i * CHUNK, scores, NEG)
                probs = jnp.exp(scores - lse[pl.ds(head, 1), :])
                grad_p = dot_nt(v_part, g_one)
                grad_s = (probs * (grad_p - dot_ref[pl.ds(head, 1), :])).astype(BF16)
                grad_k = grad_k + dot_nn(grad_s, q_one)
                grad_v = grad_v + dot_nn(probs.astype(BF16), g_one)
                grad_q = dot_nn(k_flip[which * HDIM : (which + 1) * HDIM, :], grad_s)
                if i == 0:
                    dq_ref[feats, :] = grad_q
                else:
                    dq_ref[feats, :] += grad_q
            dk_ref[rows, lanes] = (grad_k * SCALE).astype(BF16)
            dv_ref[rows, lanes] = grad_v.astype(BF16)

    own_out[...] = dq_ref[:, pl.ds(own, ROWS)]
    send_out[...] = dq_ref[:, pl.ds(other, ROWS)].astype(BF16)


def source_backward(
    split, scal, dk, dv, source, w_ck, w_cv, gsrc_ref, mine_ref, send_ref, flat_ref, sm_ref, ss_ref
):
    for i in range(KEYS // CHUNK):
        rows = slice(i * CHUNK, (i + 1) * CHUNK)
        gsrc_ref[rows, :] = dot_nn(dk[rows, :], w_ck[...]) + dot_nn(dv[rows, :], w_cv[...])
        flat_ref[:, rows] = flip(source[rows, :]).astype(BF16)
    split_rows(flat_ref, sm_ref, ss_ref, scal[3], split)
    rights = (dk[...], dv[...])
    by_shard(sm_ref, rights, mine_ref, 0, 384)
    by_shard(ss_ref, rights, send_ref, 0, 384)


def query_backward(
    split, scal, dq_own, dq_other, h1_in, gain_cross, w_cq, res_in, rows_in, att, w_so,
    kv_mine, kv_send, mine_ref, send_ref, res_ref, rows_ref, gatt_ref, gg_ref, flat_ref, a_ref, b_ref,
):
    core = scal[3]
    dq = (flip(dq_own[...] + dq_other[...].astype(F32)) * SCALE).astype(BF16)
    h1 = h1_in[...]
    scale2 = rms_scale(h1)
    n2 = (h1 * scale2 * gain_cross[...]).astype(BF16)
    step, gg = norm_back(h1, scale2, gain_cross[...], dot_nn(dq, w_cq[...]))
    gg_ref[...] = gg
    res = res_in[...] + step
    res_ref[...] = res
    rows_b = res.astype(BF16)
    rows_ref[...] = rows_b
    gatt_ref[...] = dot_nt(rows_b, w_so[...]).astype(BF16)
    for m, (left, right) in enumerate(((n2, dq), (rows_in[...], att[...]))):
        flat_ref[...] = flip(left).astype(BF16)
        split_rows(flat_ref, a_ref, b_ref, core, split)
        by_shard(a_ref, (right,), mine_ref, 576 * m, D)
        by_shard(b_ref, (right,), send_ref, 576 * m, D)
    for z in range(4):
        cols = slice(z * D + 192, z * D + 576)
        mine_ref[:, cols] = kv_mine[:, z * 384 : (z + 1) * 384]
        send_ref[:, cols] = kv_send[:, z * 384 : (z + 1) * 384]


def self_backward(
    split, scal, q1, k1, v1, lse, g_own, g_other, x_own, gain_self, w_self, res_in, rows_in, att,
    mine_ref, send_ref, gin_ref, gg_ref,
    g_ref, dq_ref, dk_ref, dv_ref, flat_ref, a_ref, b_ref,
):
    half = scal[0]
    live = scal[1]
    core = scal[3]
    own = pl.multiple_of(half * ROWS, ROWS)
    both_halves(half, g_own, g_other, g_ref)
    key = lax.broadcasted_iota(jnp.int32, (TGT, TGT), 0)
    query = lax.broadcasted_iota(jnp.int32, (TGT, TGT), 1)
    seen = (key <= query) & (key < live)

    @pl.loop(0, PAIRS)
    def _(pair):
        lanes = pl.ds(pl.multiple_of(pair * 128, 128), 128)
        q_pair, g_pair = q1[:, lanes], g_ref[:, lanes]
        k_pair, v_pair = k1[:, lanes], v1[:, lanes]
        k_flip = flip(k_pair).astype(BF16)
        grad_k = jnp.zeros((TGT, 128), F32)
        grad_v = jnp.zeros((TGT, 128), F32)
        for which in range(2):
            head = 2 * pair + which
            feats = pl.ds(pl.multiple_of(head * HDIM, HDIM), HDIM)
            q_one, g_one = only(q_pair, which), only(g_pair, which)
            scores = jnp.where(seen, dot_nt(k_pair, q_one) * SCALE, NEG)
            probs = jnp.exp(scores - lse[pl.ds(head, 1), :])
            grad_p = dot_nt(v_pair, g_one)
            row_dot = jnp.sum(probs * grad_p, axis=0, keepdims=True)
            grad_s = (probs * (grad_p - row_dot)).astype(BF16)
            grad_k = grad_k + dot_nn(grad_s, q_one)
            grad_v = grad_v + dot_nn(probs.astype(BF16), g_one)
            dq_ref[feats, :] = dot_nn(k_flip[which * HDIM : (which + 1) * HDIM, :], grad_s)
        dk_ref[:, lanes] = (grad_k * SCALE).astype(BF16)
        dv_ref[:, lanes] = grad_v.astype(BF16)

    dq = (flip(dq_ref[:, pl.ds(own, ROWS)]) * SCALE).astype(BF16)
    dk = dk_ref[pl.ds(own, ROWS), :]
    dv = dv_ref[pl.ds(own, ROWS), :]
    x = x_own[...].astype(F32)
    scale1 = rms_scale(x)
    n1 = (x * scale1 * gain_self[...]).astype(BF16)
    grad_n = dot_nn(dq, w_self[0]) + dot_nn(dk, w_self[1]) + dot_nn(dv, w_self[2])
    step, gg = norm_back(x, scale1, gain_self[...], grad_n)
    gg_ref[...] = gg
    gin_ref[...] = res_in[...] + step
    flat_ref[...] = flip(n1).astype(BF16)
    split_rows(flat_ref, a_ref, b_ref, core, split)
    by_shard(a_ref, (dq, dk, dv), mine_ref, 0, D)
    by_shard(b_ref, (dq, dk, dv), send_ref, 0, D)
    flat_ref[...] = flip(rows_in[...]).astype(BF16)
    split_rows(flat_ref, a_ref, b_ref, core, split)
    by_shard(a_ref, (att[...],), mine_ref, 576, D)
    by_shard(b_ref, (att[...],), send_ref, 576, D)


def logits_kernel(vocab, rows_ref, table_ref, target_ref, logits_ref, stats_ref, m_ref, s_ref, p_ref):
    tile = pl.program_id(0)
    count = rows_ref.shape[0]

    @pl.when(tile == 0)
    def _():
        m_ref[...] = jnp.full_like(m_ref, 2 * NEG)
        s_ref[...] = jnp.zeros_like(s_ref)
        p_ref[...] = jnp.zeros_like(p_ref)

    column = tile * VTILE + lax.broadcasted_iota(jnp.int32, (count, VTILE), 1)
    logits = dot_nt(rows_ref[...], table_ref[...])
    logits = jnp.where(column < vocab, logits, 2 * NEG)
    logits_ref[...] = logits
    old = m_ref[:, 0:1]
    new = jnp.maximum(old, jnp.max(logits, axis=1, keepdims=True))
    total = s_ref[:, 0:1] * jnp.exp(old - new) + jnp.sum(
        jnp.exp(logits - new), axis=1, keepdims=True
    )
    hit = jnp.where(column == target_ref[...], logits, 0.0)
    m_ref[...] = jnp.broadcast_to(new, m_ref.shape)
    s_ref[...] = jnp.broadcast_to(total, s_ref.shape)
    p_ref[...] += jnp.broadcast_to(jnp.sum(hit, axis=1, keepdims=True), p_ref.shape)

    @pl.when(tile == pl.num_programs(0) - 1)
    def _():
        lane = lax.broadcasted_iota(jnp.int32, m_ref.shape, 1)
        merged = jnp.where(lane == 0, m_ref[...], jnp.where(lane == 1, s_ref[...], p_ref[...]))
        stats_ref[...] = merged.T[0:8, :]


def head_logits(rows, table, target):
    count = rows.shape[0]
    vocab = table.shape[0]
    tiles = pl.cdiv(vocab, VTILE)
    return pl.pallas_call(
        functools.partial(logits_kernel, vocab),
        grid=(tiles,),
        out_shape=[whole((count, tiles * VTILE), F32), whole((8, count), F32)],
        in_specs=[
            pl.BlockSpec((count, D), lambda i: (0, 0)),
            pl.BlockSpec((VTILE, D), lambda i: (i, 0)),
            pl.BlockSpec((count, 1), lambda i: (0, 0)),
        ],
        out_specs=[
            pl.BlockSpec((count, VTILE), lambda i: (0, i)),
            pl.BlockSpec((8, count), lambda i: (0, 0)),
        ],
        scratch_shapes=[pltpu.VMEM((count, 128), F32)] * 3,
        cost_estimate=pl.CostEstimate(
            flops=2 * count * vocab * D, bytes_accessed=vocab * (2 * D + 4 * count), transcendentals=0
        ),
        compiler_params=pltpu.CompilerParams(vmem_limit_bytes=VMEM_LIMIT),
    )(rows, table, target)


def grads_kernel(vocab, logits_ref, table_ref, target_ref, lse_ref, live_ref, g_ref, gf_ref, acc_ref):
    tile = pl.program_id(0)
    count = logits_ref.shape[0]

    @pl.when(tile == 0)
    def _():
        acc_ref[...] = jnp.zeros_like(acc_ref)

    column = tile * VTILE + lax.broadcasted_iota(jnp.int32, (count, VTILE), 1)
    hit = jnp.where(column == target_ref[...], 1.0, 0.0)
    grad = jnp.where(live_ref[...] > 0, jnp.exp(logits_ref[...] - lse_ref[...]) - hit, 0.0)
    grad = grad.astype(BF16)
    g_ref[...] = grad
    entry = tile * VTILE + lax.broadcasted_iota(jnp.int32, (VTILE, D), 0)
    table = jnp.where(entry < vocab, table_ref[...], jnp.zeros_like(table_ref[...]))
    acc_ref[...] += dot_nn(grad, table)

    @pl.when(tile == pl.num_programs(0) - 1)
    def _():
        gf_ref[...] = acc_ref[...].astype(gf_ref.dtype)


def head_grads(logits, table, target, lse, live, dtype):
    count = logits.shape[0]
    vocab = table.shape[0]
    tiles = pl.cdiv(vocab, VTILE)
    column = pl.BlockSpec((count, 1), lambda i: (0, 0))
    return pl.pallas_call(
        functools.partial(grads_kernel, vocab),
        grid=(tiles,),
        out_shape=[whole((count, tiles * VTILE), BF16), whole((count, D), dtype)],
        in_specs=[
            pl.BlockSpec((count, VTILE), lambda i: (0, i)),
            pl.BlockSpec((VTILE, D), lambda i: (i, 0)),
            column,
            column,
            column,
        ],
        out_specs=[
            pl.BlockSpec((count, VTILE), lambda i: (0, i)),
            pl.BlockSpec((count, D), lambda i: (0, 0)),
        ],
        scratch_shapes=[pltpu.VMEM((count, D), F32)],
        cost_estimate=pl.CostEstimate(
            flops=2 * count * vocab * D, bytes_accessed=vocab * (2 * D + 6 * count), transcendentals=0
        ),
        compiler_params=pltpu.CompilerParams(vmem_limit_bytes=VMEM_LIMIT),
    )(logits, table, target, lse, live)


def table_kernel(fm_a, fm_b, fs_a, fs_b, g_a, g_b, mine_ref, send_ref):
    first, second = g_a[...], g_b[...]
    mine_ref[...] = dot_nn(fm_a[...], first) + dot_nn(fm_b[...], second)
    send_ref[...] = (dot_nn(fs_a[...], first) + dot_nn(fs_b[...], second)).astype(BF16)


def table_grads(flat_a, flat_b, g_a, g_b):
    count, width = g_a.shape
    left = pl.BlockSpec((HALF_D, count), lambda i: (0, 0))
    right = pl.BlockSpec((count, VTILE), lambda i: (0, i))
    out = pl.BlockSpec((HALF_D, VTILE), lambda i: (0, i))
    return pl.pallas_call(
        table_kernel,
        grid=(width // VTILE,),
        out_shape=[whole((HALF_D, width), F32), whole((HALF_D, width), BF16)],
        in_specs=[left] * 4 + [right] * 2,
        out_specs=[out] * 2,
        cost_estimate=pl.CostEstimate(
            flops=4 * count * width * D, bytes_accessed=width * (4 * count + 6 * HALF_D), transcendentals=0
        ),
        compiler_params=pltpu.CompilerParams(vmem_limit_bytes=VMEM_LIMIT),
    )(flat_a[0], flat_b[0], flat_a[1], flat_b[1], g_a, g_b)


def make(mesh):
    dp_size = mesh.shape["dp"]
    split = dp_size == 8

    def on_device(
        block_in,
        source,
        target_len,
        source_len,
        targets,
        gain_self,
        gain_cross,
        gain_ff,
        gain_final,
        self_q,
        self_k,
        self_v,
        self_o,
        cross_q,
        cross_k,
        cross_v,
        cross_o,
        ff_gate,
        ff_up,
        ff_down,
        embed_table,
    ):
        z = lax.axis_index("tensor")
        dp = lax.axis_index("dp")
        half = lax.rem(z, 2)
        seq = z // 2
        core = lax.rem(dp, 2)
        gain_self, gain_cross, gain_ff, gain_final = (
            g.reshape(1, D) for g in (gain_self, gain_cross, gain_ff, gain_final)
        )

        def pair_swap(value):
            return swap(value, "tensor", 4, 1)

        x_other = pair_swap(block_in)
        w_self, w_cross = gather_blocks(
            [
                jnp.concatenate([self_q.T, self_k.T, self_v.T, self_o], 0),
                jnp.concatenate([cross_q.T, cross_k.T, cross_v.T, cross_o], 0),
            ],
            dp_size,
        )
        wg = gather_wide(ff_gate.T, dp_size)
        wu = gather_wide(ff_up.T, dp_size)
        wd = gather_wide(ff_down, dp_size)
        cq, ck, cv, co = (w_cross[i] for i in range(4))
        scal = jnp.stack(
            [
                half,
                lax.dynamic_index_in_dim(target_len, seq, keepdims=False),
                lax.dynamic_index_in_dim(source_len, seq, keepdims=False),
                core,
            ]
        ).astype(jnp.int32)

        def vm(shape, dtype):
            return pltpu.VMEM(shape, dtype)

        pair = (TGT, D)
        q1, k1, v1, lse1, a1, h1, q2 = local_call(
            self_forward,
            [whole(pair, BF16)] * 3
            + [whole((16, TGT), F32), whole((ROWS, D), BF16), whole((ROWS, D), F32), whole(pair, BF16)],
            [vm(pair, F32), vm(pair, BF16), vm((D, TGT), BF16), vm((D, TGT), F32)],
            8e9,
            scal, block_in, x_other, gain_self, gain_cross, w_self, cq,
        )
        k2, v2, o_own, o_send, lse_own = local_call(
            cross_forward,
            [whole((KEYS, D), BF16)] * 2
            + [whole((D, ROWS), F32), whole((D, ROWS), BF16), whole((16, TGT), F32)],
            [vm((D, KEYS), BF16), vm((KEYS, TGT), F32), vm((D, TGT), F32)],
            15e9,
            scal, q2, source, ck, cv,
        )
        block_out, fin, h2, att_t, a2, lse2 = local_call(
            ff_forward,
            [whole((ROWS, D), F32), whole((ROWS, D), BF16), whole((ROWS, D), F32)]
            + [whole((D, ROWS), F32), whole((ROWS, D), BF16), whole((16, TGT), F32)],
            [vm((ROWS, FF), BF16)],
            3e9,
            scal, o_own, pair_swap(o_send), lse_own, pair_swap(lse_own), h1, co,
            gain_ff, gain_final, wg, wu, wd,
        )

        vocab = embed_table.shape[0]

        def block(by_block, j, axis=0):
            return lax.dynamic_index_in_dim(by_block, z ^ j, axis, keepdims=False)

        tgt_local = targets - z * vocab
        tgt_local = jnp.where((tgt_local >= 0) & (tgt_local < vocab), tgt_local, -1)
        tgt_blocks = tgt_local.reshape(4, ROWS)
        position = lax.rem(jnp.arange(4 * ROWS), TGT)
        live = position < jnp.repeat(target_len, TGT, total_repeat_length=4 * ROWS)
        live_blocks = live.astype(jnp.int32).reshape(4, ROWS)
        fin_1, fin_2, fin_3 = (swap(fin, "tensor", 4, j) for j in (1, 2, 3))
        fin_a = jnp.concatenate([fin_2, fin_3], 0)
        fin_b = jnp.concatenate([fin, fin_1], 0)

        def columns(by_block, order):
            return jnp.concatenate([block(by_block, j) for j in order], 0)[:, None]

        tgt_a, tgt_b = columns(tgt_blocks, (2, 3)), columns(tgt_blocks, (0, 1))
        logits_b, stats_b = head_logits(fin_b, embed_table, tgt_b)
        logits_a, stats_a = head_logits(fin_a, embed_table, tgt_a)
        stats = [stats_b[:, :ROWS], stats_b[:, ROWS:], stats_a[:, :ROWS], stats_a[:, ROWS:]]
        stats = jnp.stack(stats, 0)
        stats = jnp.stack([block(stats, j) for j in range(4)], 0)
        others = [stats] + [swap(stats, "tensor", 4, j) for j in (1, 2, 3)]

        def over_z(values, op):
            return op(op(values[0], values[1]), op(values[2], values[3]))

        top = over_z([s[:, 0] for s in others], jnp.maximum)
        total = over_z([s[:, 1] * jnp.exp(s[:, 0] - top) for s in others], jnp.add)
        picked = over_z([s[:, 2] for s in others], jnp.add)
        g_lse = top + jnp.log(total)
        token_loss = jnp.where(live, (g_lse - picked).reshape(-1), 0.0)
        g_a, gf_a = head_grads(
            logits_a, embed_table, tgt_a, columns(g_lse, (2, 3)), columns(live_blocks, (2, 3)), BF16
        )
        g_b, gf_b = head_grads(
            logits_b, embed_table, tgt_b, columns(g_lse, (0, 1)), columns(live_blocks, (0, 1)), F32
        )
        gf_2 = swap(gf_a[:ROWS], "tensor", 4, 2)
        gf_3 = swap(gf_a[ROWS:], "tensor", 4, 3)
        gf_1 = swap(gf_b[ROWS:].astype(BF16), "tensor", 4, 1)

        def halves(rows):
            flat = rows.T
            if not split:
                return flat[:HALF_D], flat[HALF_D:]
            flat = flat.reshape(4, 2, 96, -1)
            return tuple(
                lax.dynamic_index_in_dim(flat, i, 1, keepdims=False).reshape(HALF_D, -1)
                for i in (core, 1 - core)
            )

        reduction = Reduction if split else WideReduction
        xyz = jnp.stack([lax.rem(dp // 2, 2), dp // 4, z]).astype(jnp.int32)
        e_mine, e_send = table_grads(halves(fin_a), halves(fin_b), g_a, g_b)
        if not split:
            e_mine, e_send = e_mine[:, :vocab], e_send[:, :vocab]
        e_sum = reduction(xyz, e_mine, e_send)

        half_t = (HALF_D, ROWS)
        ff_mine, ff_send, res2, rows2, gatt, dots, gg_a = local_call(
            functools.partial(ff_backward, split),
            [whole((HALF_D, 3 * FF), F32), whole((HALF_D, 3 * FF), BF16), whole((ROWS, D), F32)]
            + [whole((ROWS, D), BF16)] * 2
            + [whole((16, ROWS), F32), whole((2, D), F32)],
            [vm((D, ROWS), BF16)] + [vm(half_t, BF16)] * 4
            + [vm((ROWS, D), F32)],
            10e9,
            scal, after(gf_b[:ROWS], e_send), gf_1, gf_2, gf_3, block_out, h2,
            gain_ff, gain_final, wg, wu, wd, co, att_t,
        )
        ff_sum = reduction(xyz, ff_mine, ff_send)
        gatt_other, dots_other = pair_swap(gatt), pair_swap(dots)
        sent = e_sum.first()
        dk2, dv2, dq_own, dq_send = local_call(
            cross_backward,
            [whole((KEYS, D), BF16)] * 2 + [whole((D, ROWS), F32), whole((D, ROWS), BF16)],
            [vm(pair, BF16), vm((16, TGT), F32), vm((D, TGT), F32)],
            20e9,
            scal, q2, k2, v2, lse2, after(gatt, *sent), gatt_other, dots, dots_other,
        )
        dq_other = pair_swap(dq_send)
        sent = ff_sum.first()
        grad_source, kv_mine, kv_send = local_call(
            functools.partial(source_backward, split),
            [whole((KEYS, D), F32), whole((HALF_D, 2 * D), F32), whole((HALF_D, 2 * D), BF16)],
            [vm((D, KEYS), BF16)] + [vm((HALF_D, KEYS), BF16)] * 2,
            5e9,
            scal, after(dk2, *sent), dv2, source, ck, cv,
        )
        sent = e_sum.second()
        c_mine, c_send, res1, rows1, gatt1, gg_b = local_call(
            functools.partial(query_backward, split),
            [whole((HALF_D, 4 * D), F32), whole((HALF_D, 4 * D), BF16), whole((ROWS, D), F32)]
            + [whole((ROWS, D), BF16)] * 2 + [whole((1, D), F32)],
            [vm((D, ROWS), BF16)] + [vm(half_t, BF16)] * 2,
            2e9,
            scal, after(dq_own, *sent), dq_other, h1, gain_cross, cq, res2, rows2, a2, w_self[3],
            kv_mine, kv_send,
        )
        c_sum = reduction(xyz, c_mine, c_send)
        gatt1_other = pair_swap(gatt1)
        sent = ff_sum.second() + c_sum.first()
        s_mine, s_send, grad_block_in, gg_c = local_call(
            functools.partial(self_backward, split),
            [whole((HALF_D, 4 * D), F32), whole((HALF_D, 4 * D), BF16)]
            + [whole((ROWS, D), F32), whole((1, D), F32)],
            [vm(pair, BF16), vm((D, TGT), F32), vm(pair, BF16), vm(pair, BF16)]
            + [vm((D, ROWS), BF16)] + [vm(half_t, BF16)] * 2,
            12e9,
            scal, q1, k1, v1, lse1, after(gatt1, *sent), gatt1_other, block_in, gain_self, w_self,
            res1, rows1, a1,
        )
        s_sum = reduction(xyz, s_mine, s_send)
        gains = jnp.concatenate([gg_a, gg_b, gg_c], 0)
        if split:
            for axis, size, bit in (("dp", 8, 1), ("tensor", 4, 1), ("dp", 8, 2), ("tensor", 4, 2), ("dp", 8, 4)):
                gains = gains + swap(gains, axis, size, bit)
        else:
            gains = lax.psum(gains, ("dp", "tensor"))
        sent = s_sum.first()
        sent = sent + ff_sum.third() + c_sum.second()
        grad_embed = e_sum.table(vocab)
        s_sum.second()
        c_sum.third()
        ff_grads = ff_sum.last(3, (2,))
        s_sum.third()
        c_grads = c_sum.last(4, (3,))
        s_grads = s_sum.last(4, (3,))

        return (
            block_out,
            token_loss,
            grad_block_in,
            grad_source,
            gains[3],
            gains[2],
            gains[1],
            gains[0],
            *s_grads,
            *c_grads,
            *ff_grads,
            grad_embed,
        )

    return on_device


def solution(mesh):
    rows = P(("dp", "tensor"), None)
    wide, tall = P(None, "tensor"), P("tensor", None)
    in_specs = (rows, rows) + (P("dp"),) * 3 + (P(),) * 4
    in_specs += (wide, wide, wide, tall) * 2 + (wide, wide, tall, tall)
    g_in, g_out = P("dp", "tensor"), P("tensor", "dp")
    out_specs = (rows, P("dp"), rows, rows) + (P(),) * 4
    out_specs += (g_in, g_in, g_in, g_out) * 2 + (g_in, g_in, g_out, g_out)
    return jax.shard_map(
        make(mesh), mesh=mesh, in_specs=in_specs, out_specs=out_specs, check_vma=False
    )
```

```python
import functools
import math

import jax
import jax.numpy as jnp
from jax import lax
from jax.sharding import PartitionSpec as P
from jax.experimental import pallas as pl
from jax.experimental.pallas import tpu as pltpu

D = 768
HDIM = 64
NHEAD = D // HDIM
PAIRS = NHEAD // 2
FF = 2048
TGT = 512
ROWS = 256
KEYS = 1024
CHUNK = 256
HALF_D = D // 2
VTILE = 512
F32 = jnp.float32
BF16 = jnp.bfloat16
MESH_ID = pl.DeviceIdType.MESH
VMEM_LIMIT = 56 * 2**20
NEG = -1000000000.0
SCALE = HDIM ** (-0.5)
EPS = 1e-06


def dot_nt(left, right):
    return lax.dot_general(left, right, (((1,), (1,)), ((), ())), preferred_element_type=F32)


def dot_nn(left, right):
    return lax.dot_general(left, right, (((1,), (0,)), ((), ())), preferred_element_type=F32)


def swap(value, axis_name, size, bit):
    return lax.ppermute(value, axis_name, [(i, i ^ bit) for i in range(size)])


class Gather:
    def __init__(self, links, refs, used):
        self.links, self.refs, self.used = links, refs, used
        self.last = []

    def piece(self, ref, shard, owner, part=None):
        if len(ref.shape) == 2:
            rows = ref.shape[0] // 32
            base = shard * 8 * rows + owner * rows
        else:
            rows = ref.shape[1] // 8
            base = shard * 2 * rows + lax.rem(owner, 2) * rows
        start, count = (0, rows) if part is None else (part * rows // 2, rows // 2)
        where = pl.ds(pl.multiple_of(base + start, 16), count)
        return ref.at[where] if len(ref.shape) == 2 else ref.at[owner // 2, where]

    def send(self, part, peer):
        send_sem, recv_sem = self.links["sems"]
        sem = self.used[0]
        self.used[0] += 1
        copy = pltpu.make_async_remote_copy(
            src_ref=part,
            dst_ref=part,
            send_sem=send_sem.at[sem],
            recv_sem=recv_sem.at[sem],
            device_id={"dp": peer[0], "tensor": peer[1]},
            device_id_type=MESH_ID,
        )
        copy.start()
        return copy

    def along_z(self):
        links = self.links
        self.z_copies = [
            self.send(self.piece(ref, links["z"], links["dp"]), peer)
            for ref in self.refs
            for peer in links["z_peers"]
        ]

    def along_xy(self):
        links = self.links
        for copy in self.z_copies:
            copy.wait()
        self.x_copies, self.y_copies = [], []
        for ref in self.refs:
            for _, shard in links["z_peers"]:
                part = self.piece(ref, shard, links["dp"])
                self.x_copies.append(self.send(part, links["x"]))
                self.y_copies.append(self.send(part, links["y"]))
                self.last.append(self.send(part, links["core"]))

    def diagonal(self):
        links = self.links
        self.d_copies = []
        at = 0
        for ref in self.refs:
            for _, shard in links["z_peers"]:
                self.x_copies[at].wait()
                self.d_copies.append(self.send(self.piece(ref, shard, links["x"][0], 0), links["y"]))
                self.y_copies[at].wait()
                self.d_copies.append(self.send(self.piece(ref, shard, links["y"][0], 1), links["x"]))
                for owner in (links["x"][0], links["y"][0]):
                    self.last.append(self.send(self.piece(ref, shard, owner), links["core"]))
                at += 1

    def finish(self):
        links = self.links
        for copy in self.d_copies:
            copy.wait()
        for ref in self.refs:
            for _, shard in links["z_peers"]:
                self.last.append(self.send(self.piece(ref, shard, links["xy"]), links["core"]))
        for copy in self.last:
            copy.wait()


def gather_wide(shard, dp_size):
    rows = shard.shape[0] // dp_size
    part = lax.dynamic_slice_in_dim(shard, lax.axis_index("dp") * rows, rows, 0)
    return lax.all_gather(part, ("tensor", "dp"), axis=0, tiled=True)


def tile_of(width):
    return 512 if width % 512 == 0 else 384


def fold_call(body, xyz, ins, outs, width, out_specs=None):
    tile = tile_of(width)

    def spec(rows, dtype, index):
        return pl.BlockSpec((rows, tile), index)

    smem = pl.BlockSpec(memory_space=pltpu.SMEM)
    left, right = (lambda i: (0, i)), (lambda i: (0, i + width // tile))
    in_specs = [smem] + [
        spec(a.shape[0], a.dtype, right if second else left) for a, second in ins
    ]
    moved = sum(a.shape[0] * width * a.dtype.itemsize for a, _ in ins)
    moved += sum(o.size * jnp.dtype(o.dtype).itemsize for o in outs)
    rows = max(a.shape[0] for a, _ in ins)
    return pl.pallas_call(
        body,
        grid=(width // tile,),
        out_shape=outs,
        in_specs=in_specs,
        out_specs=out_specs or [spec(o.shape[0], o.dtype, left) for o in outs],
        scratch_shapes=[pltpu.VMEM((rows, tile), F32)],
        cost_estimate=pl.CostEstimate(flops=0, bytes_accessed=moved, transcendentals=0),
    )(xyz, *[a for a, _ in ins])


def block_rows(index):
    return pl.ds(pl.multiple_of(index * 96, 96), 96)


def first_fold(xyz, mine_a, got_a, mine_b, got_b, keep_a, send_a, keep_b, send_b, sum_ref):
    x, y = xyz[0], xyz[1]
    sum_ref[...] = mine_a[...] + got_a[...].astype(F32)
    for other in range(2):
        rows = slice(other * 96, (other + 1) * 96)
        keep_a[rows, :] = sum_ref[block_rows(2 * other + x), :]
        send_a[rows, :] = sum_ref[block_rows(2 * other + 1 - x), :].astype(BF16)
    sum_ref[...] = mine_b[...] + got_b[...].astype(F32)
    for other in range(2):
        rows = slice(other * 96, (other + 1) * 96)
        keep_b[rows, :] = sum_ref[block_rows(2 * y + other), :]
        send_b[rows, :] = sum_ref[block_rows(2 * (1 - y) + other), :].astype(BF16)


def second_fold(xyz, mine_a, got_a, mine_b, got_b, keep_a, send_a, keep_b, send_b, sum_ref):
    x, y = xyz[0], xyz[1]
    sum_ref[...] = mine_a[...] + got_a[...].astype(F32)
    keep_a[...] = sum_ref[block_rows(y), :]
    send_a[...] = sum_ref[block_rows(1 - y), :].astype(BF16)
    sum_ref[...] = mine_b[...] + got_b[...].astype(F32)
    keep_b[...] = sum_ref[block_rows(x), :]
    send_b[...] = sum_ref[block_rows(1 - x), :].astype(BF16)


def third_fold(xyz, mine_a, got_a, mine_b, got_b, keep, send_1, send_2, send_3, sum_ref):
    z = xyz[2]
    width = keep.shape[1]
    for m, (mine, got) in enumerate(((mine_a, got_a), (mine_b, got_b))):
        total = mine[...] + got[...].astype(F32)
        sum_ref[2 * m] = total[:, :width]
        sum_ref[2 * m + 1] = total[:, width:]
    keep[...] = sum_ref[z]
    low, high = lax.rem(z, 2), z // 2
    send_1[...] = sum_ref[2 * high + 1 - low].astype(BF16)
    send_2[...] = sum_ref[2 * (1 - high) + low].astype(BF16)
    send_3[...] = sum_ref[2 * (1 - high) + 1 - low].astype(BF16)


def last_fold(flips, keep, got_1, got_2, got_3, *outs):
    total = keep[...] + got_1[...].astype(F32) + (got_2[...].astype(F32) + got_3[...].astype(F32))
    width = keep.shape[1] // len(outs)
    for m, out in enumerate(outs):
        part = total[:, m * width : (m + 1) * width]
        out[...] = part.T if m in flips else part


def table_fold(mine, got, out):
    out[...] = (mine[...] + got[...].astype(F32)).T


class Reduction:
    def __init__(self, xyz, mine, send):
        self.xyz, self.mine, self.width = xyz, mine, mine.shape[1] // 2
        self.got = swap(send, "dp", 8, 1)

    def first(self):
        ins = [(self.mine, 0), (self.got, 0), (self.mine, 1), (self.got, 1)]
        shape = (192, self.width)
        outs = [whole(shape, F32), whole(shape, BF16)] * 2
        keep_a, send_a, keep_b, send_b = fold_call(first_fold, self.xyz, ins, outs, self.width)
        self.keeps = keep_a, keep_b
        self.gots = swap(send_a, "dp", 8, 2), swap(send_b, "dp", 8, 4)
        return send_a, send_b

    def second(self):
        (keep_a, keep_b), (got_a, got_b) = self.keeps, self.gots
        ins = [(keep_a, 0), (got_a, 0), (keep_b, 0), (got_b, 0)]
        shape = (96, self.width)
        outs = [whole(shape, F32), whole(shape, BF16)] * 2
        keep_a, send_a, keep_b, send_b = fold_call(second_fold, self.xyz, ins, outs, self.width)
        self.keeps = keep_a, keep_b
        self.gots = swap(send_a, "dp", 8, 4), swap(send_b, "dp", 8, 2)
        return send_a, send_b

    def third(self):
        (keep_a, keep_b), (got_a, got_b) = self.keeps, self.gots
        shape = (96, self.width // 2)
        keep, *sends = pl.pallas_call(
            third_fold,
            out_shape=[whole(shape, F32)] + [whole(shape, BF16)] * 3,
            in_specs=[pl.BlockSpec(memory_space=pltpu.SMEM)]
            + [pl.BlockSpec(memory_space=pltpu.VMEM)] * 4,
            out_specs=[pl.BlockSpec(memory_space=pltpu.VMEM)] * 4,
            scratch_shapes=[pltpu.VMEM((4,) + shape, F32)],
        )(self.xyz, keep_a, got_a, keep_b, got_b)
        self.keeps = keep
        self.gots = [swap(send, "tensor", 4, j + 1) for j, send in enumerate(sends)]
        return tuple(sends)

    def last(self, count, flips):
        rows, width = self.keeps.shape
        shape = (rows, width // count)
        outs = [whole(shape[::-1] if m in flips else shape, F32) for m in range(count)]
        return pl.pallas_call(functools.partial(last_fold, flips), out_shape=outs)(
            self.keeps, *self.gots
        )

    def table(self, vocab):
        parts = []
        for keep, got, start in zip(self.keeps, self.gots, (0, self.width)):
            count = min(self.width, vocab - start)
            tile = pl.BlockSpec((96, VTILE), lambda i: (0, i))
            parts.append(
                pl.pallas_call(
                    table_fold,
                    grid=(pl.cdiv(count, VTILE),),
                    out_shape=whole((count, 96), F32),
                    in_specs=[tile] * 2,
                    out_specs=pl.BlockSpec((VTILE, 96), lambda i: (i, 0)),
                )(keep, got)
            )
        return jnp.concatenate(parts, 0)


class WideReduction:
    def __init__(self, xyz, mine, send):
        self.gots = ()
        both = jnp.concatenate([mine, send.astype(F32)], 0)
        self.part = lax.psum_scatter(both, "dp", scatter_dimension=0, tiled=True)

    def first(self):
        return ()

    second = third = first

    def last(self, count, flips):
        rows = self.part.shape[0]
        by_z = self.part.reshape(rows, 4, -1)
        total = lax.psum_scatter(by_z, "tensor", scatter_dimension=1, tiled=True)[:, 0]
        parts = jnp.split(total, count, axis=1)
        return [p.T if m in flips else p for m, p in enumerate(parts)]

    def table(self, vocab):
        return self.part.T


def after(value, *others):
    return lax.optimization_barrier((value,) + others)[0]


def rms_scale(values):
    return lax.rsqrt(jnp.mean(values * values, axis=-1, keepdims=True) + EPS)


def norm_back(values, inv_scale, gain, grad_out):
    weighted = gain * grad_out
    grad_gain = jnp.sum(grad_out * values * inv_scale, axis=0, keepdims=True)
    grad_values = inv_scale * weighted - values * inv_scale * inv_scale * inv_scale * jnp.mean(
        weighted * values, axis=-1, keepdims=True
    )
    return grad_values, grad_gain


def flip(value):
    return value.astype(F32).T


def lane_half(rows, which):
    lane = lax.broadcasted_iota(jnp.int32, (rows, 2 * HDIM), 1)
    return (lane >= HDIM) if which else (lane < HDIM)


def only(value, which):
    return jnp.where(lane_half(value.shape[0], which), value, jnp.zeros_like(value))


def split_rows(flat_ref, mine_ref, send_ref, core, split):
    for block in range(4):
        if split:
            first = pl.multiple_of((2 * block + core) * 96, 96)
            second = pl.multiple_of((2 * block + 1 - core) * 96, 96)
        else:
            first, second = block * 96, HALF_D + block * 96
        mine_ref[block * 96 : (block + 1) * 96, :] = flat_ref[pl.ds(first, 96), :]
        send_ref[block * 96 : (block + 1) * 96, :] = flat_ref[pl.ds(second, 96), :]


def by_shard(left_ref, rights, out_ref, first, per_shard):
    width = 192 * len(rights)
    for z in range(4):
        part = [right[:, z * 192 : (z + 1) * 192] for right in rights]
        right = jnp.concatenate(part, axis=1) if len(part) > 1 else part[0]
        start = z * per_shard + first
        out_ref[:, start : start + width] = dot_nn(left_ref[...], right).astype(out_ref.dtype)


def whole(shape, dtype):
    return jax.ShapeDtypeStruct(shape, dtype)


def local_call(body, outs, scratch, flops, *args):
    smem = pl.BlockSpec(memory_space=pltpu.SMEM)
    vmem = pl.BlockSpec(memory_space=pltpu.VMEM)
    bytes_all = sum(a.size * a.dtype.itemsize for a in args)
    bytes_all += sum(o.size * jnp.dtype(o.dtype).itemsize for o in outs)
    held = sum(math.prod(s.shape) * jnp.dtype(s.dtype).itemsize for s in scratch)
    return pl.pallas_call(
        body,
        out_shape=outs,
        in_specs=[smem] + [vmem] * (len(args) - 1),
        out_specs=[vmem] * len(outs),
        scratch_shapes=scratch,
        cost_estimate=pl.CostEstimate(
            flops=int(flops), bytes_accessed=int(bytes_all), transcendentals=0
        ),
        compiler_params=pltpu.CompilerParams(
            vmem_limit_bytes=min(VMEM_LIMIT, int(bytes_all + held + 16 * 2**20))
        ),
    )(*args)


def forward_kernel(split, *refs):
    (scal, x_own, source, gain_self, gain_cross, gain_ff, gain_final), refs = refs[:7], refs[7:]
    shards, refs = refs[: 11 if split else 5], refs[11 if split else 5 :]
    (q1, k1, v1, lse1, att1, h1_out, q2, k2, v2), refs = refs[:9], refs[9:]
    (out_ref, fin_ref, h2_ref, att_t_ref, att2, lse2), refs = refs[:6], refs[6:]
    if split:
        copies_out, refs = refs[:11], refs[11:]
        (ws, wc, wg, wu, wd), refs = refs[:5], refs[5:]
    else:
        ws, wc, wg, wu, wd = shards
    (x_other, x_ref, n_ref, vt_ref, ot_ref, s_ref, o_send, o_other, lse_own, lse_other, mix_ref), refs = (
        refs[:11],
        refs[11:],
    )
    pair_send, pair_recv = refs[:2]
    dp = lax.axis_index("dp")
    z = lax.axis_index("tensor")
    low, high = lax.rem(z, 2), z // 2
    half, live, live_src = low, scal[1], scal[2] - low * KEYS
    z_peers = [(dp, high * 2 + 1 - low)]
    peers = z_peers
    if split:
        z_peers = z_peers + [(dp, (1 - high) * 2 + low), (dp, (1 - high) * 2 + 1 - low)]
        x_peer = dp + 2 - 4 * lax.rem(dp // 2, 2)
        y_peer = dp + 4 - 8 * (dp // 4)
        links = dict(
            dp=dp,
            z=z,
            z_peers=z_peers,
            x=(x_peer, z),
            y=(y_peer, z),
            xy=x_peer + y_peer - dp,
            core=(dp + 1 - 2 * lax.rem(dp, 2), z),
            sems=refs[2:4],
        )
        out_sem = refs[4]
        peers = z_peers + [links["x"], links["y"], links["core"]]
    barrier = pltpu.get_barrier_semaphore()
    for peer in peers:
        pl.semaphore_signal(
            barrier, inc=1, device_id={"dp": peer[0], "tensor": peer[1]}, device_id_type=MESH_ID
        )

    def exchange(index, src, dst):
        copy = pltpu.make_async_remote_copy(
            src_ref=src,
            dst_ref=dst,
            send_sem=pair_send.at[index],
            recv_sem=pair_recv.at[index],
            device_id={"dp": z_peers[0][0], "tensor": z_peers[0][1]},
            device_id_type=MESH_ID,
        )
        copy.start()
        return copy

    leaving = []
    if split:
        used = [0]
        groups = [Gather(links, refs_of, used) for refs_of in ([ws], [wc], [wg], [wu], [wd])]
        of_self, of_cross, of_gate, of_up, of_down = groups
        hid, fhid = D // 4, FF // 4

        def place_block(target, first):
            rows = pl.ds(pl.multiple_of(z * hid, 16), hid)
            for m in range(3):
                target[m, rows, :] = flip(shards[first + m][...]).astype(BF16)
            target[3, rows, :] = shards[first + 3][...]

        def place_wide(target, shard, flipped):
            rows = pl.ds(pl.multiple_of(z * fhid, 16), fhid)
            target[rows, :] = flip(shard[...]).astype(BF16) if flipped else shard[...]

        def leave(first, parts):
            for i, part in enumerate(parts):
                copy = pltpu.make_async_copy(part, copies_out[first + i], out_sem.at[first + i])
                copy.start()
                leaving.append(copy)

        place_block(ws, 0)
        pl.semaphore_wait(barrier, len(peers))
        of_self.along_z()
    else:
        pl.semaphore_wait(barrier, len(peers))
    x_copy = exchange(0, x_own, x_other)
    if split:
        place_block(wc, 4)
        place_wide(wg, shards[8], True)
        place_wide(wu, shards[9], True)
        place_wide(wd, shards[10], False)
        of_self.along_xy()
        of_cross.along_z()
        of_self.diagonal()
        of_cross.along_xy()
        of_gate.along_z()
    x_copy.wait()
    own = pl.multiple_of(half * ROWS, ROWS)
    other = pl.multiple_of((1 - half) * ROWS, ROWS)
    x_ref[pl.ds(own, ROWS), :] = x_own[...].astype(F32)
    x_ref[pl.ds(other, ROWS), :] = x_other[...].astype(F32)
    lse1[...] = jnp.zeros_like(lse1)
    lse_own[...] = jnp.zeros_like(lse_own)
    if split:
        of_self.finish()
        leave(0, [ws.at[m] for m in range(4)])
    for i in range(2):
        rows = slice(i * ROWS, (i + 1) * ROWS)
        x = x_ref[rows, :]
        n = (x * rms_scale(x) * gain_self[...]).astype(BF16)
        n_ref[rows, :] = n
        q1[rows, :] = dot_nt(n, ws[0]).astype(BF16)
        k1[rows, :] = dot_nt(n, ws[1]).astype(BF16)
        v1[rows, :] = dot_nt(n, ws[2]).astype(BF16)
    vt_ref[:, :TGT] = dot_nt(ws[2], n_ref[...]).astype(BF16)
    if split:
        of_gate.along_xy()
        of_up.along_z()
    key = lax.broadcasted_iota(jnp.int32, (TGT, TGT), 0)
    query = lax.broadcasted_iota(jnp.int32, (TGT, TGT), 1)
    seen = (key <= query) & (key < live)

    def self_pairs(first, last):
        @pl.loop(first, last)
        def _(pair):
            lanes = pl.ds(pl.multiple_of(pair * 128, 128), 128)
            q_pair, k_pair = q1[:, lanes], k1[:, lanes]
            for which in range(2):
                head = 2 * pair + which
                feats = pl.ds(pl.multiple_of(head * HDIM, HDIM), HDIM)
                scores = jnp.where(seen, dot_nt(k_pair, only(q_pair, which)) * SCALE, NEG)
                top = jnp.max(scores, axis=0, keepdims=True)
                probs = jnp.exp(scores - top)
                total = jnp.sum(probs, axis=0, keepdims=True)
                lse1[pl.ds(head, 1), :] = top + jnp.log(total)
                ot_ref[feats, :] = dot_nn(vt_ref[feats, :TGT], probs.astype(BF16)) / total

    self_pairs(0, PAIRS // 2)
    if split:
        of_cross.diagonal()
    self_pairs(PAIRS // 2, PAIRS)
    if split:
        of_up.along_xy()
        of_down.along_z()
        of_gate.diagonal()
    for i in range(2):
        rows = slice(i * ROWS, (i + 1) * ROWS)
        att = flip(ot_ref[:, rows]).astype(BF16)
        n_ref[rows, :] = att
        x_ref[rows, :] = x_ref[rows, :] + dot_nn(att, ws[3])
    att1[...] = n_ref[pl.ds(own, ROWS), :]
    h1_out[...] = x_ref[pl.ds(own, ROWS), :]
    if split:
        of_cross.finish()
        leave(4, [wc.at[m] for m in range(4)])
    for i in range(2):
        rows = slice(i * ROWS, (i + 1) * ROWS)
        h1 = x_ref[rows, :]
        n = (h1 * rms_scale(h1) * gain_cross[...]).astype(BF16)
        q2[rows, :] = dot_nt(n, wc[0]).astype(BF16)
    for i in range(KEYS // CHUNK):
        rows = slice(i * CHUNK, (i + 1) * CHUNK)
        src = source[rows, :]
        k2[rows, :] = dot_nt(src, wc[1]).astype(BF16)
        v2[rows, :] = dot_nt(src, wc[2]).astype(BF16)
        vt_ref[:, rows] = dot_nt(wc[2], src).astype(BF16)
    if split:
        of_down.along_xy()
        of_up.diagonal()
        of_gate.finish()
        leave(8, [wg])
    chunk_key = lax.broadcasted_iota(jnp.int32, (CHUNK, TGT), 0)

    def cross_pairs(first, last):
        @pl.loop(first, last)
        def _(pair):
            lanes = pl.ds(pl.multiple_of(pair * 128, 128), 128)
            q_pair = q2[:, lanes]
            for which in range(2):
                head = 2 * pair + which
                feats = pl.ds(pl.multiple_of(head * HDIM, HDIM), HDIM)
                q_one = only(q_pair, which)
                top = jnp.full((1, TGT), 2 * NEG, F32)
                for i in range(KEYS // CHUNK):
                    rows = slice(i * CHUNK, (i + 1) * CHUNK)
                    scores = dot_nt(k2[rows, lanes], q_one) * SCALE
                    scores = jnp.where(chunk_key < live_src - i * CHUNK, scores, NEG)
                    s_ref[rows, :] = scores
                    top = jnp.maximum(top, jnp.max(scores, axis=0, keepdims=True))
                total = jnp.zeros((1, TGT), F32)
                out = jnp.zeros((HDIM, TGT), F32)
                for i in range(KEYS // CHUNK):
                    rows = slice(i * CHUNK, (i + 1) * CHUNK)
                    probs = jnp.exp(s_ref[rows, :] - top)
                    total = total + jnp.sum(probs, axis=0, keepdims=True)
                    out = out + dot_nn(vt_ref[feats, rows], probs.astype(BF16))
                lse_own[pl.ds(head, 1), :] = top + jnp.log(total)
                ot_ref[feats, :] = out / total

    cross_pairs(0, PAIRS // 2)
    o_send[: D // 2, :] = ot_ref[: D // 2, pl.ds(other, ROWS)].astype(BF16)
    pair_copies = [exchange(1, o_send.at[: D // 2], o_other.at[: D // 2])]
    if split:
        of_down.diagonal()
        of_up.finish()
        leave(9, [wu])
    cross_pairs(PAIRS // 2, PAIRS)
    o_send[D // 2 :, :] = ot_ref[D // 2 :, pl.ds(other, ROWS)].astype(BF16)
    pair_copies.append(exchange(2, o_send.at[D // 2 :], o_other.at[D // 2 :]))
    pair_copies.append(exchange(3, lse_own, lse_other))
    if split:
        of_down.finish()
        leave(10, [wd])
    for copy in pair_copies:
        copy.wait()

    first, second = lse_own[...], lse_other[...]
    top = jnp.maximum(first, second)
    lse2[...] = top + jnp.log(jnp.exp(first - top) + jnp.exp(second - top))
    lse = lse2[:, pl.ds(own, ROWS)]
    w_first = jnp.exp(lse_own[:, pl.ds(own, ROWS)] - lse)
    w_second = jnp.exp(lse_other[:, pl.ds(own, ROWS)] - lse)
    for head in range(NHEAD):
        feats = slice(head * HDIM, (head + 1) * HDIM)
        att_t_ref[feats, :] = (
            ot_ref[feats, pl.ds(own, ROWS)] * w_first[head : head + 1, :]
            + o_other[feats, :].astype(F32) * w_second[head : head + 1, :]
        )
    att = flip(att_t_ref[...]).astype(BF16)
    att2[...] = att
    h2 = h1_out[...] + dot_nn(att, wc[3])
    h2_ref[...] = h2
    n3 = (h2 * rms_scale(h2) * gain_ff[...]).astype(BF16)

    @pl.loop(0, FF // 512)
    def _(i):
        rows = pl.ds(pl.multiple_of(i * 512, 512), 512)
        gate = dot_nt(n3, wg[rows, :])
        up = dot_nt(n3, wu[rows, :])
        mix_ref[:, rows] = (jax.nn.gelu(gate, approximate=True) * up).astype(BF16)

    out = h2 + dot_nn(mix_ref[...], wd[...])
    out_ref[...] = out
    fin_ref[...] = (out * rms_scale(out) * gain_final[...] * D ** (-0.5)).astype(BF16)
    for copy in leaving:
        copy.wait()


def forward(split, scal, x_own, source, gains, weights):
    pair = (TGT, D)
    block = (ROWS, D)
    outs = [whole(pair, BF16)] * 3 + [whole((16, TGT), F32), whole(block, BF16), whole(block, F32)]
    outs += [whole(pair, BF16)] + [whole((KEYS, D), BF16)] * 2
    outs += [whole(block, F32), whole(block, BF16), whole(block, F32), whole((D, ROWS), F32)]
    outs += [whole(block, BF16), whole((16, TGT), F32)]
    vmem = pl.BlockSpec(memory_space=pltpu.VMEM)
    out_specs = [vmem] * len(outs)
    scratch = []
    if split:
        outs += [whole((D, D), BF16)] * 8 + [whole((FF, D), BF16)] * 3
        out_specs += [pl.BlockSpec(memory_space=pl.ANY)] * 11
        scratch += [pltpu.VMEM((4, D, D), BF16)] * 2 + [pltpu.VMEM((FF, D), BF16)] * 3
    scratch += [
        pltpu.VMEM(block, BF16),
        pltpu.VMEM(pair, F32),
        pltpu.VMEM(pair, BF16),
        pltpu.VMEM((D, KEYS), BF16),
        pltpu.VMEM((D, TGT), F32),
        pltpu.VMEM((KEYS, TGT), F32),
        pltpu.VMEM((D, ROWS), BF16),
        pltpu.VMEM((D, ROWS), BF16),
        pltpu.VMEM((16, TGT), F32),
        pltpu.VMEM((16, TGT), F32),
        pltpu.VMEM((ROWS, FF), BF16),
        pltpu.SemaphoreType.DMA((4,)),
        pltpu.SemaphoreType.DMA((4,)),
    ]
    if split:
        scratch += [pltpu.SemaphoreType.DMA((27 * 5,))] * 2 + [pltpu.SemaphoreType.DMA((11,))]
    args = (scal, x_own, source, *gains, *weights)
    return pl.pallas_call(
        functools.partial(forward_kernel, split),
        out_shape=outs,
        in_specs=[pl.BlockSpec(memory_space=pltpu.SMEM)] + [vmem] * (len(args) - 1),
        out_specs=out_specs,
        scratch_shapes=scratch,
        cost_estimate=pl.CostEstimate(
            flops=int(80e9), bytes_accessed=int(6e7), transcendentals=0
        ),
        compiler_params=pltpu.CompilerParams(
            collective_id=0, has_side_effects=True, vmem_limit_bytes=VMEM_LIMIT
        ),
    )(*args)


def ff_backward(
    split, scal, gf_own, gf_1, gf_2, gf_3, block_out, h2_in, gain_ff, gain_final, wg, wu, wd,
    w_co, att_t, mine_ref, send_ref, res_ref, rows_ref, gatt_ref, dot_ref, gg_ref,
    flat_ref, nm_ref, ns_ref, gm_ref, gs_ref, gn_ref,
):
    core = scal[3]
    grad = gf_own[...] + gf_1[...].astype(F32)
    grad = grad + (gf_2[...].astype(F32) + gf_3[...].astype(F32))
    out = block_out[...]
    res, gg_final = norm_back(out, rms_scale(out), gain_final[...], grad * D ** (-0.5))
    gg_ref[0:1, :] = gg_final
    rows_b = res.astype(BF16)
    res_ref[...] = res
    flat_ref[...] = flip(rows_b).astype(BF16)
    split_rows(flat_ref, gm_ref, gs_ref, core, split)
    h2 = h2_in[...]
    scale3 = rms_scale(h2)
    n3 = (h2 * scale3 * gain_ff[...]).astype(BF16)
    flat_ref[...] = flip(n3).astype(BF16)
    split_rows(flat_ref, nm_ref, ns_ref, core, split)
    gn_ref[...] = jnp.zeros_like(gn_ref)
    const = (2.0 / 3.141592653589793) ** 0.5

    @pl.loop(0, FF // 512)
    def _(i):
        start = pl.multiple_of(i * 512, 512)
        rows = pl.ds(start, 512)
        gate = dot_nt(n3, wg[rows, :])
        up = dot_nt(n3, wu[rows, :])
        square = gate * gate
        tanh = jnp.tanh(const * (gate + 0.044715 * gate * square))
        gelu = 0.5 * gate * (1.0 + tanh)
        slope = 0.5 * (1.0 + tanh) + 0.5 * gate * (1.0 - tanh * tanh) * const * (
            1.0 + 3.0 * 0.044715 * square
        )
        grad_mixed = dot_nt(rows_b, wd[rows, :])
        g_gate = (grad_mixed * up * slope).astype(BF16)
        g_up = (grad_mixed * gelu).astype(BF16)
        mixed = (gelu * up).astype(BF16)
        gn_ref[...] += dot_nn(g_gate, wg[rows, :]) + dot_nn(g_up, wu[rows, :])
        for m, (mine, send, right) in enumerate(
            ((nm_ref, ns_ref, g_gate), (nm_ref, ns_ref, g_up), (gm_ref, gs_ref, mixed))
        ):
            cols = pl.ds(pl.multiple_of(3 * start + m * 512, 512), 512)
            mine_ref[:, cols] = dot_nn(mine[...], right)
            send_ref[:, cols] = dot_nn(send[...], right).astype(BF16)

    step, gg_ff = norm_back(h2, scale3, gain_ff[...], gn_ref[...])
    gg_ref[1:2, :] = gg_ff
    res = res_ref[...] + step
    res_ref[...] = res
    rows_b = res.astype(BF16)
    rows_ref[...] = rows_b
    gatt_ref[...] = dot_nt(rows_b, w_co[...]).astype(BF16)
    gatt_t = dot_nt(w_co[...], rows_b).astype(BF16).astype(F32)
    dot_ref[...] = jnp.zeros_like(dot_ref)
    for head in range(NHEAD):
        feats = slice(head * HDIM, (head + 1) * HDIM)
        dot_ref[head : head + 1, :] = jnp.sum(gatt_t[feats, :] * att_t[feats, :], 0, keepdims=True)


def both_halves(half, own, other, target):
    target[pl.ds(pl.multiple_of(half * ROWS, ROWS), ROWS), :] = own[...]
    target[pl.ds(pl.multiple_of((1 - half) * ROWS, ROWS), ROWS), :] = other[...]


def cross_backward(
    scal, q2, k2, v2, lse, g_own, g_other, dot_own, dot_other,
    dk_ref, dv_ref, own_out, send_out, g_ref, dot_ref, dq_ref,
):
    half = scal[0]
    live = scal[2] - half * KEYS
    own = pl.multiple_of(half * ROWS, ROWS)
    other = pl.multiple_of((1 - half) * ROWS, ROWS)
    both_halves(half, g_own, g_other, g_ref)
    dot_ref[:, pl.ds(own, ROWS)] = dot_own[...]
    dot_ref[:, pl.ds(other, ROWS)] = dot_other[...]
    key = lax.broadcasted_iota(jnp.int32, (CHUNK, TGT), 0)

    @pl.loop(0, PAIRS)
    def _(pair):
        lanes = pl.ds(pl.multiple_of(pair * 128, 128), 128)
        q_pair, g_pair = q2[:, lanes], g_ref[:, lanes]
        for i in range(KEYS // CHUNK):
            rows = slice(i * CHUNK, (i + 1) * CHUNK)
            k_part, v_part = k2[rows, lanes], v2[rows, lanes]
            k_flip = flip(k_part).astype(BF16)
            grad_k = jnp.zeros((CHUNK, 128), F32)
            grad_v = jnp.zeros((CHUNK, 128), F32)
            for which in range(2):
                head = 2 * pair + which
                feats = pl.ds(pl.multiple_of(head * HDIM, HDIM), HDIM)
                q_one, g_one = only(q_pair, which), only(g_pair, which)
                scores = dot_nt(k_part, q_one) * SCALE
                scores = jnp.where(key < live - i * CHUNK, scores, NEG)
                probs = jnp.exp(scores - lse[pl.ds(head, 1), :])
                grad_p = dot_nt(v_part, g_one)
                grad_s = (probs * (grad_p - dot_ref[pl.ds(head, 1), :])).astype(BF16)
                grad_k = grad_k + dot_nn(grad_s, q_one)
                grad_v = grad_v + dot_nn(probs.astype(BF16), g_one)
                grad_q = dot_nn(k_flip[which * HDIM : (which + 1) * HDIM, :], grad_s)
                if i == 0:
                    dq_ref[feats, :] = grad_q
                else:
                    dq_ref[feats, :] += grad_q
            dk_ref[rows, lanes] = (grad_k * SCALE).astype(BF16)
            dv_ref[rows, lanes] = grad_v.astype(BF16)

    own_out[...] = dq_ref[:, pl.ds(own, ROWS)]
    send_out[...] = dq_ref[:, pl.ds(other, ROWS)].astype(BF16)


def source_backward(
    split, scal, dk, dv, source, w_ck, w_cv, gsrc_ref, mine_ref, send_ref, flat_ref, sm_ref, ss_ref
):
    for i in range(KEYS // CHUNK):
        rows = slice(i * CHUNK, (i + 1) * CHUNK)
        gsrc_ref[rows, :] = dot_nn(dk[rows, :], w_ck[...]) + dot_nn(dv[rows, :], w_cv[...])
        flat_ref[:, rows] = flip(source[rows, :]).astype(BF16)
    split_rows(flat_ref, sm_ref, ss_ref, scal[3], split)
    rights = (dk[...], dv[...])
    by_shard(sm_ref, rights, mine_ref, 0, 384)
    by_shard(ss_ref, rights, send_ref, 0, 384)


def query_backward(
    split, scal, dq_own, dq_other, h1_in, gain_cross, w_cq, res_in, rows_in, att, w_so,
    kv_mine, kv_send, mine_ref, send_ref, res_ref, rows_ref, gatt_ref, gg_ref, flat_ref, a_ref, b_ref,
):
    core = scal[3]
    dq = (flip(dq_own[...] + dq_other[...].astype(F32)) * SCALE).astype(BF16)
    h1 = h1_in[...]
    scale2 = rms_scale(h1)
    n2 = (h1 * scale2 * gain_cross[...]).astype(BF16)
    step, gg = norm_back(h1, scale2, gain_cross[...], dot_nn(dq, w_cq[...]))
    gg_ref[...] = gg
    res = res_in[...] + step
    res_ref[...] = res
    rows_b = res.astype(BF16)
    rows_ref[...] = rows_b
    gatt_ref[...] = dot_nt(rows_b, w_so[...]).astype(BF16)
    for m, (left, right) in enumerate(((n2, dq), (rows_in[...], att[...]))):
        flat_ref[...] = flip(left).astype(BF16)
        split_rows(flat_ref, a_ref, b_ref, core, split)
        by_shard(a_ref, (right,), mine_ref, 576 * m, D)
        by_shard(b_ref, (right,), send_ref, 576 * m, D)
    for z in range(4):
        cols = slice(z * D + 192, z * D + 576)
        mine_ref[:, cols] = kv_mine[:, z * 384 : (z + 1) * 384]
        send_ref[:, cols] = kv_send[:, z * 384 : (z + 1) * 384]


def self_backward(
    split, scal, q1, k1, v1, lse, g_own, g_other, x_own, gain_self, w_q, w_k, w_v, res_in, rows_in, att,
    mine_ref, send_ref, gin_ref, gg_ref,
    g_ref, dq_ref, dk_ref, dv_ref, flat_ref, a_ref, b_ref,
):
    half = scal[0]
    live = scal[1]
    core = scal[3]
    own = pl.multiple_of(half * ROWS, ROWS)
    both_halves(half, g_own, g_other, g_ref)
    key = lax.broadcasted_iota(jnp.int32, (TGT, TGT), 0)
    query = lax.broadcasted_iota(jnp.int32, (TGT, TGT), 1)
    seen = (key <= query) & (key < live)

    @pl.loop(0, PAIRS)
    def _(pair):
        lanes = pl.ds(pl.multiple_of(pair * 128, 128), 128)
        q_pair, g_pair = q1[:, lanes], g_ref[:, lanes]
        k_pair, v_pair = k1[:, lanes], v1[:, lanes]
        k_flip = flip(k_pair).astype(BF16)
        grad_k = jnp.zeros((TGT, 128), F32)
        grad_v = jnp.zeros((TGT, 128), F32)
        for which in range(2):
            head = 2 * pair + which
            feats = pl.ds(pl.multiple_of(head * HDIM, HDIM), HDIM)
            q_one, g_one = only(q_pair, which), only(g_pair, which)
            scores = jnp.where(seen, dot_nt(k_pair, q_one) * SCALE, NEG)
            probs = jnp.exp(scores - lse[pl.ds(head, 1), :])
            grad_p = dot_nt(v_pair, g_one)
            row_dot = jnp.sum(probs * grad_p, axis=0, keepdims=True)
            grad_s = (probs * (grad_p - row_dot)).astype(BF16)
            grad_k = grad_k + dot_nn(grad_s, q_one)
            grad_v = grad_v + dot_nn(probs.astype(BF16), g_one)
            dq_ref[feats, :] = dot_nn(k_flip[which * HDIM : (which + 1) * HDIM, :], grad_s)
        dk_ref[:, lanes] = (grad_k * SCALE).astype(BF16)
        dv_ref[:, lanes] = grad_v.astype(BF16)

    dq = (flip(dq_ref[:, pl.ds(own, ROWS)]) * SCALE).astype(BF16)
    dk = dk_ref[pl.ds(own, ROWS), :]
    dv = dv_ref[pl.ds(own, ROWS), :]
    x = x_own[...].astype(F32)
    scale1 = rms_scale(x)
    n1 = (x * scale1 * gain_self[...]).astype(BF16)
    grad_n = dot_nn(dq, w_q[...]) + dot_nn(dk, w_k[...]) + dot_nn(dv, w_v[...])
    step, gg = norm_back(x, scale1, gain_self[...], grad_n)
    gg_ref[...] = gg
    gin_ref[...] = res_in[...] + step
    flat_ref[...] = flip(n1).astype(BF16)
    split_rows(flat_ref, a_ref, b_ref, core, split)
    by_shard(a_ref, (dq, dk, dv), mine_ref, 0, D)
    by_shard(b_ref, (dq, dk, dv), send_ref, 0, D)
    flat_ref[...] = flip(rows_in[...]).astype(BF16)
    split_rows(flat_ref, a_ref, b_ref, core, split)
    by_shard(a_ref, (att[...],), mine_ref, 576, D)
    by_shard(b_ref, (att[...],), send_ref, 576, D)


def logits_kernel(vocab, rows_ref, table_ref, target_ref, logits_ref, stats_ref, m_ref, s_ref, p_ref):
    tile = pl.program_id(0)
    count = rows_ref.shape[0]

    @pl.when(tile == 0)
    def _():
        m_ref[...] = jnp.full_like(m_ref, 2 * NEG)
        s_ref[...] = jnp.zeros_like(s_ref)
        p_ref[...] = jnp.zeros_like(p_ref)

    column = tile * VTILE + lax.broadcasted_iota(jnp.int32, (count, VTILE), 1)
    logits = dot_nt(rows_ref[...], table_ref[...])
    logits = jnp.where(column < vocab, logits, 2 * NEG)
    logits_ref[...] = logits
    old = m_ref[:, 0:1]
    new = jnp.maximum(old, jnp.max(logits, axis=1, keepdims=True))
    total = s_ref[:, 0:1] * jnp.exp(old - new) + jnp.sum(
        jnp.exp(logits - new), axis=1, keepdims=True
    )
    hit = jnp.where(column == target_ref[...], logits, 0.0)
    m_ref[...] = jnp.broadcast_to(new, m_ref.shape)
    s_ref[...] = jnp.broadcast_to(total, s_ref.shape)
    p_ref[...] += jnp.broadcast_to(jnp.sum(hit, axis=1, keepdims=True), p_ref.shape)

    @pl.when(tile == pl.num_programs(0) - 1)
    def _():
        lane = lax.broadcasted_iota(jnp.int32, m_ref.shape, 1)
        merged = jnp.where(lane == 0, m_ref[...], jnp.where(lane == 1, s_ref[...], p_ref[...]))
        stats_ref[...] = merged.T[0:8, :]


def head_logits(rows, table, target):
    count = rows.shape[0]
    vocab = table.shape[0]
    tiles = pl.cdiv(vocab, VTILE)
    return pl.pallas_call(
        functools.partial(logits_kernel, vocab),
        grid=(tiles,),
        out_shape=[whole((count, tiles * VTILE), F32), whole((8, count), F32)],
        in_specs=[
            pl.BlockSpec((count, D), lambda i: (0, 0)),
            pl.BlockSpec((VTILE, D), lambda i: (i, 0)),
            pl.BlockSpec((count, 1), lambda i: (0, 0)),
        ],
        out_specs=[
            pl.BlockSpec((count, VTILE), lambda i: (0, i)),
            pl.BlockSpec((8, count), lambda i: (0, 0)),
        ],
        scratch_shapes=[pltpu.VMEM((count, 128), F32)] * 3,
        cost_estimate=pl.CostEstimate(
            flops=2 * count * vocab * D, bytes_accessed=vocab * (2 * D + 4 * count), transcendentals=0
        ),
        compiler_params=pltpu.CompilerParams(vmem_limit_bytes=VMEM_LIMIT),
    )(rows, table, target)


def grads_kernel(vocab, logits_ref, table_ref, target_ref, lse_ref, live_ref, g_ref, gf_ref, acc_ref):
    tile = pl.program_id(0)
    count = logits_ref.shape[0]

    @pl.when(tile == 0)
    def _():
        acc_ref[...] = jnp.zeros_like(acc_ref)

    column = tile * VTILE + lax.broadcasted_iota(jnp.int32, (count, VTILE), 1)
    hit = jnp.where(column == target_ref[...], 1.0, 0.0)
    grad = jnp.where(live_ref[...] > 0, jnp.exp(logits_ref[...] - lse_ref[...]) - hit, 0.0)
    grad = grad.astype(BF16)
    g_ref[...] = grad
    entry = tile * VTILE + lax.broadcasted_iota(jnp.int32, (VTILE, D), 0)
    table = jnp.where(entry < vocab, table_ref[...], jnp.zeros_like(table_ref[...]))
    acc_ref[...] += dot_nn(grad, table)

    @pl.when(tile == pl.num_programs(0) - 1)
    def _():
        gf_ref[...] = acc_ref[...].astype(gf_ref.dtype)


def head_grads(logits, table, target, lse, live, dtype):
    count = logits.shape[0]
    vocab = table.shape[0]
    tiles = pl.cdiv(vocab, VTILE)
    column = pl.BlockSpec((count, 1), lambda i: (0, 0))
    return pl.pallas_call(
        functools.partial(grads_kernel, vocab),
        grid=(tiles,),
        out_shape=[whole((count, tiles * VTILE), BF16), whole((count, D), dtype)],
        in_specs=[
            pl.BlockSpec((count, VTILE), lambda i: (0, i)),
            pl.BlockSpec((VTILE, D), lambda i: (i, 0)),
            column,
            column,
            column,
        ],
        out_specs=[
            pl.BlockSpec((count, VTILE), lambda i: (0, i)),
            pl.BlockSpec((count, D), lambda i: (0, 0)),
        ],
        scratch_shapes=[pltpu.VMEM((count, D), F32)],
        cost_estimate=pl.CostEstimate(
            flops=2 * count * vocab * D, bytes_accessed=vocab * (2 * D + 6 * count), transcendentals=0
        ),
        compiler_params=pltpu.CompilerParams(vmem_limit_bytes=VMEM_LIMIT),
    )(logits, table, target, lse, live)


def table_kernel(fm_a, fm_b, fs_a, fs_b, g_a, g_b, mine_ref, send_ref):
    first, second = g_a[...], g_b[...]
    mine_ref[...] = dot_nn(fm_a[...], first) + dot_nn(fm_b[...], second)
    send_ref[...] = (dot_nn(fs_a[...], first) + dot_nn(fs_b[...], second)).astype(BF16)


def table_grads(flat_a, flat_b, g_a, g_b):
    count, width = g_a.shape
    left = pl.BlockSpec((HALF_D, count), lambda i: (0, 0))
    right = pl.BlockSpec((count, VTILE), lambda i: (0, i))
    out = pl.BlockSpec((HALF_D, VTILE), lambda i: (0, i))
    return pl.pallas_call(
        table_kernel,
        grid=(width // VTILE,),
        out_shape=[whole((HALF_D, width), F32), whole((HALF_D, width), BF16)],
        in_specs=[left] * 4 + [right] * 2,
        out_specs=[out] * 2,
        cost_estimate=pl.CostEstimate(
            flops=4 * count * width * D, bytes_accessed=width * (4 * count + 6 * HALF_D), transcendentals=0
        ),
        compiler_params=pltpu.CompilerParams(vmem_limit_bytes=VMEM_LIMIT),
    )(flat_a[0], flat_b[0], flat_a[1], flat_b[1], g_a, g_b)


def make(mesh):
    dp_size = mesh.shape["dp"]
    split = dp_size == 8

    def on_device(
        block_in,
        source,
        target_len,
        source_len,
        targets,
        gain_self,
        gain_cross,
        gain_ff,
        gain_final,
        self_q,
        self_k,
        self_v,
        self_o,
        cross_q,
        cross_k,
        cross_v,
        cross_o,
        ff_gate,
        ff_up,
        ff_down,
        embed_table,
    ):
        z = lax.axis_index("tensor")
        dp = lax.axis_index("dp")
        half = lax.rem(z, 2)
        seq = z // 2
        core = lax.rem(dp, 2)
        gain_self, gain_cross, gain_ff, gain_final = (
            g.reshape(1, D) for g in (gain_self, gain_cross, gain_ff, gain_final)
        )

        def pair_swap(value):
            return swap(value, "tensor", 4, 1)

        scal = jnp.stack(
            [
                half,
                lax.dynamic_index_in_dim(target_len, seq, keepdims=False),
                lax.dynamic_index_in_dim(source_len, seq, keepdims=False),
                core,
            ]
        ).astype(jnp.int32)

        def vm(shape, dtype):
            return pltpu.VMEM(shape, dtype)

        pair = (TGT, D)
        weights = (
            self_q, self_k, self_v, self_o, cross_q, cross_k, cross_v, cross_o, ff_gate, ff_up, ff_down,
        )
        if not split:
            wide = [gather_wide(w if i in (3, 7, 10) else w.T, dp_size) for i, w in enumerate(weights)]
            sq, sk, sv, so, cq, ck, cv, co, wg, wu, wd = wide
            weights = jnp.stack([sq, sk, sv, so]), jnp.stack([cq, ck, cv, co]), wg, wu, wd
        gains = gain_self, gain_cross, gain_ff, gain_final
        results = forward(split, scal, block_in, source, gains, weights)
        q1, k1, v1, lse1, a1, h1, q2, k2, v2, block_out, fin, h2, att_t, a2, lse2 = results[:15]
        if split:
            sq, sk, sv, so, cq, ck, cv, co, wg, wu, wd = results[15:]

        vocab = embed_table.shape[0]

        def block(by_block, j, axis=0):
            return lax.dynamic_index_in_dim(by_block, z ^ j, axis, keepdims=False)

        tgt_local = targets - z * vocab
        tgt_local = jnp.where((tgt_local >= 0) & (tgt_local < vocab), tgt_local, -1)
        tgt_blocks = tgt_local.reshape(4, ROWS)
        position = lax.rem(jnp.arange(4 * ROWS), TGT)
        live = position < jnp.repeat(target_len, TGT, total_repeat_length=4 * ROWS)
        live_blocks = live.astype(jnp.int32).reshape(4, ROWS)
        fin_1, fin_2, fin_3 = (swap(fin, "tensor", 4, j) for j in (1, 2, 3))
        fin_a = jnp.concatenate([fin_2, fin_3], 0)
        fin_b = jnp.concatenate([fin, fin_1], 0)

        def columns(by_block, order):
            return jnp.concatenate([block(by_block, j) for j in order], 0)[:, None]

        tgt_a, tgt_b = columns(tgt_blocks, (2, 3)), columns(tgt_blocks, (0, 1))
        logits_b, stats_b = head_logits(fin_b, embed_table, tgt_b)
        logits_a, stats_a = head_logits(fin_a, embed_table, tgt_a)
        stats = [stats_b[:, :ROWS], stats_b[:, ROWS:], stats_a[:, :ROWS], stats_a[:, ROWS:]]
        stats = jnp.stack(stats, 0)
        stats = jnp.stack([block(stats, j) for j in range(4)], 0)
        others = [stats] + [swap(stats, "tensor", 4, j) for j in (1, 2, 3)]

        def over_z(values, op):
            return op(op(values[0], values[1]), op(values[2], values[3]))

        top = over_z([s[:, 0] for s in others], jnp.maximum)
        total = over_z([s[:, 1] * jnp.exp(s[:, 0] - top) for s in others], jnp.add)
        picked = over_z([s[:, 2] for s in others], jnp.add)
        g_lse = top + jnp.log(total)
        token_loss = jnp.where(live, (g_lse - picked).reshape(-1), 0.0)
        g_a, gf_a = head_grads(
            logits_a, embed_table, tgt_a, columns(g_lse, (2, 3)), columns(live_blocks, (2, 3)), BF16
        )
        gf_2 = swap(gf_a[:ROWS], "tensor", 4, 2)
        g_b, gf_b = head_grads(
            logits_b, embed_table, tgt_b, columns(g_lse, (0, 1)), columns(live_blocks, (0, 1)), F32
        )
        g_b, gf_b, gf_2, gf_a = lax.optimization_barrier((g_b, gf_b, gf_2, gf_a))
        gf_3 = swap(gf_a[ROWS:], "tensor", 4, 3)
        gf_1 = swap(gf_b[ROWS:].astype(BF16), "tensor", 4, 1)

        def halves(rows):
            flat = rows.T
            if not split:
                return flat[:HALF_D], flat[HALF_D:]
            flat = flat.reshape(4, 2, 96, -1)
            return tuple(
                lax.dynamic_index_in_dim(flat, i, 1, keepdims=False).reshape(HALF_D, -1)
                for i in (core, 1 - core)
            )

        reduction = Reduction if split else WideReduction
        xyz = jnp.stack([lax.rem(dp // 2, 2), dp // 4, z]).astype(jnp.int32)
        e_mine, e_send = table_grads(halves(fin_a), halves(fin_b), g_a, g_b)
        if not split:
            e_mine, e_send = e_mine[:, :vocab], e_send[:, :vocab]
        e_mine, e_send, gf_1, gf_3 = lax.optimization_barrier((e_mine, e_send, gf_1, gf_3))
        e_sum = reduction(xyz, e_mine, e_send)

        half_t = (HALF_D, ROWS)
        ff_mine, ff_send, res2, rows2, gatt, dots, gg_a = local_call(
            functools.partial(ff_backward, split),
            [whole((HALF_D, 3 * FF), F32), whole((HALF_D, 3 * FF), BF16), whole((ROWS, D), F32)]
            + [whole((ROWS, D), BF16)] * 2
            + [whole((16, ROWS), F32), whole((2, D), F32)],
            [vm((D, ROWS), BF16)] + [vm(half_t, BF16)] * 4
            + [vm((ROWS, D), F32)],
            10e9,
            scal, after(gf_b[:ROWS], e_send), gf_1, gf_2, gf_3, block_out, h2,
            gain_ff, gain_final, wg, wu, wd, co, att_t,
        )
        ff_sum = reduction(xyz, ff_mine, ff_send)
        gatt_other, dots_other = pair_swap(gatt), pair_swap(dots)
        sent = e_sum.first()
        dk2, dv2, dq_own, dq_send = local_call(
            cross_backward,
            [whole((KEYS, D), BF16)] * 2 + [whole((D, ROWS), F32), whole((D, ROWS), BF16)],
            [vm(pair, BF16), vm((16, TGT), F32), vm((D, TGT), F32)],
            20e9,
            scal, q2, k2, v2, lse2, after(gatt, *sent), gatt_other, dots, dots_other,
        )
        dq_other = pair_swap(dq_send)
        dk2, *e_sum.gots = lax.optimization_barrier((dk2, *e_sum.gots))
        sent = ff_sum.first()
        grad_source, kv_mine, kv_send = local_call(
            functools.partial(source_backward, split),
            [whole((KEYS, D), F32), whole((HALF_D, 2 * D), F32), whole((HALF_D, 2 * D), BF16)],
            [vm((D, KEYS), BF16)] + [vm((HALF_D, KEYS), BF16)] * 2,
            5e9,
            scal, after(dk2, *sent), dv2, source, ck, cv,
        )
        sent = e_sum.second()
        c_mine, c_send, res1, rows1, gatt1, gg_b = local_call(
            functools.partial(query_backward, split),
            [whole((HALF_D, 4 * D), F32), whole((HALF_D, 4 * D), BF16), whole((ROWS, D), F32)]
            + [whole((ROWS, D), BF16)] * 2 + [whole((1, D), F32)],
            [vm((D, ROWS), BF16)] + [vm(half_t, BF16)] * 2,
            2e9,
            scal, after(dq_own, *sent), dq_other, h1, gain_cross, cq, res2, rows2, a2, so,
            kv_mine, kv_send,
        )
        c_sum = reduction(xyz, c_mine, c_send)
        gatt1_other = pair_swap(gatt1)
        sent = ff_sum.second() + c_sum.first()
        s_mine, s_send, grad_block_in, gg_c = local_call(
            functools.partial(self_backward, split),
            [whole((HALF_D, 4 * D), F32), whole((HALF_D, 4 * D), BF16)]
            + [whole((ROWS, D), F32), whole((1, D), F32)],
            [vm(pair, BF16), vm((D, TGT), F32), vm(pair, BF16), vm(pair, BF16)]
            + [vm((D, ROWS), BF16)] + [vm(half_t, BF16)] * 2,
            12e9,
            scal, q1, k1, v1, lse1, after(gatt1, *sent), gatt1_other, block_in, gain_self, sq, sk, sv,
            res1, rows1, a1,
        )
        flying = (*e_sum.gots, *ff_sum.gots, *c_sum.gots)
        s_mine, s_send, *flying = lax.optimization_barrier((s_mine, s_send, *flying))
        if split:
            e_sum.gots, ff_sum.gots, c_sum.gots = flying[:2], flying[2:4], flying[4:]
        s_sum = reduction(xyz, s_mine, s_send)
        gains = jnp.concatenate([gg_a, gg_b, gg_c], 0)
        if split:
            for axis, size, bit in (("dp", 8, 1), ("tensor", 4, 1), ("dp", 8, 2), ("tensor", 4, 2), ("dp", 8, 4)):
                gains = gains + swap(gains, axis, size, bit)
        else:
            gains = lax.psum(gains, ("dp", "tensor"))
        sent = s_sum.first()
        sent = sent + ff_sum.third() + c_sum.second()
        grad_embed = e_sum.table(vocab)
        s_sum.second()
        c_sum.third()
        ff_grads = ff_sum.last(3, (2,))
        s_sum.third()
        c_grads = c_sum.last(4, (3,))
        s_grads = s_sum.last(4, (3,))

        return (
            block_out,
            token_loss,
            grad_block_in,
            grad_source,
            gains[3],
            gains[2],
            gains[1],
            gains[0],
            *s_grads,
            *c_grads,
            *ff_grads,
            grad_embed,
        )

    return on_device


def solution(mesh):
    rows = P(("dp", "tensor"), None)
    wide, tall = P(None, "tensor"), P("tensor", None)
    in_specs = (rows, rows) + (P("dp"),) * 3 + (P(),) * 4
    in_specs += (wide, wide, wide, tall) * 2 + (wide, wide, tall, tall)
    g_in, g_out = P("dp", "tensor"), P("tensor", "dp")
    out_specs = (rows, P("dp"), rows, rows) + (P(),) * 4
    out_specs += (g_in, g_in, g_in, g_out) * 2 + (g_in, g_in, g_out, g_out)
    return jax.shard_map(
        make(mesh), mesh=mesh, in_specs=in_specs, out_specs=out_specs, check_vma=False
    )
```

```python
import functools
import math

import jax
import jax.numpy as jnp
from jax import lax
from jax.sharding import PartitionSpec as P
from jax.experimental import pallas as pl
from jax.experimental.pallas import tpu as pltpu

D = 768
HDIM = 64
NHEAD = D // HDIM
PAIRS = NHEAD // 2
FF = 2048
TGT = 512
ROWS = 256
KEYS = 1024
CHUNK = 256
HALF_D = D // 2
VTILE = 512
HTILE = 1024
F32 = jnp.float32
BF16 = jnp.bfloat16
MESH_ID = pl.DeviceIdType.MESH
VMEM_LIMIT = 56 * 2**20
NEG = -1000000000.0
SCALE = HDIM ** (-0.5)
EPS = 1e-06


def dot_nt(left, right):
    return lax.dot_general(left, right, (((1,), (1,)), ((), ())), preferred_element_type=F32)


def dot_nn(left, right):
    return lax.dot_general(left, right, (((1,), (0,)), ((), ())), preferred_element_type=F32)


def swap(value, axis_name, size, bit):
    return lax.ppermute(value, axis_name, [(i, i ^ bit) for i in range(size)])


class Gather:
    def __init__(self, links, refs, used):
        self.links, self.refs, self.used = links, refs, used
        self.last = []

    def piece(self, ref, shard, owner, part=None):
        if len(ref.shape) == 2:
            rows = ref.shape[0] // 32
            base = shard * 8 * rows + owner * rows
        else:
            rows = ref.shape[1] // 8
            base = shard * 2 * rows + lax.rem(owner, 2) * rows
        start, count = (0, rows) if part is None else (part * rows // 2, rows // 2)
        where = pl.ds(pl.multiple_of(base + start, 16), count)
        return ref.at[where] if len(ref.shape) == 2 else ref.at[owner // 2, where]

    def send(self, part, peer):
        send_sem, recv_sem = self.links["sems"]
        sem = self.used[0]
        self.used[0] += 1
        copy = pltpu.make_async_remote_copy(
            src_ref=part,
            dst_ref=part,
            send_sem=send_sem.at[sem],
            recv_sem=recv_sem.at[sem],
            device_id={"dp": peer[0], "tensor": peer[1]},
            device_id_type=MESH_ID,
        )
        copy.start()
        return copy

    def along_z(self):
        links = self.links
        self.z_copies = [
            self.send(self.piece(ref, links["z"], links["dp"]), peer)
            for ref in self.refs
            for peer in links["z_peers"]
        ]

    def along_xy(self):
        links = self.links
        for copy in self.z_copies:
            copy.wait()
        self.x_copies, self.y_copies = [], []
        for ref in self.refs:
            for _, shard in links["z_peers"]:
                part = self.piece(ref, shard, links["dp"])
                self.x_copies.append(self.send(part, links["x"]))
                self.y_copies.append(self.send(part, links["y"]))
                self.last.append(self.send(part, links["core"]))

    def diagonal(self):
        links = self.links
        self.d_copies = []
        at = 0
        for ref in self.refs:
            for _, shard in links["z_peers"]:
                self.x_copies[at].wait()
                self.d_copies.append(self.send(self.piece(ref, shard, links["x"][0], 0), links["y"]))
                self.y_copies[at].wait()
                self.d_copies.append(self.send(self.piece(ref, shard, links["y"][0], 1), links["x"]))
                for owner in (links["x"][0], links["y"][0]):
                    self.last.append(self.send(self.piece(ref, shard, owner), links["core"]))
                at += 1

    def finish(self):
        links = self.links
        for copy in self.d_copies:
            copy.wait()
        for ref in self.refs:
            for _, shard in links["z_peers"]:
                self.last.append(self.send(self.piece(ref, shard, links["xy"]), links["core"]))
        for copy in self.last:
            copy.wait()


def gather_wide(shard, dp_size):
    rows = shard.shape[0] // dp_size
    part = lax.dynamic_slice_in_dim(shard, lax.axis_index("dp") * rows, rows, 0)
    return lax.all_gather(part, ("tensor", "dp"), axis=0, tiled=True)


def tile_of(width):
    return 512 if width % 512 == 0 else 384


def fold_call(body, xyz, ins, outs, width, out_specs=None):
    tile = tile_of(width)

    def spec(rows, dtype, index):
        return pl.BlockSpec((rows, tile), index)

    smem = pl.BlockSpec(memory_space=pltpu.SMEM)
    left, right = (lambda i: (0, i)), (lambda i: (0, i + width // tile))
    in_specs = [smem] + [
        spec(a.shape[0], a.dtype, right if second else left) for a, second in ins
    ]
    moved = sum(a.shape[0] * width * a.dtype.itemsize for a, _ in ins)
    moved += sum(o.size * jnp.dtype(o.dtype).itemsize for o in outs)
    rows = max(a.shape[0] for a, _ in ins)
    return pl.pallas_call(
        body,
        grid=(width // tile,),
        out_shape=outs,
        in_specs=in_specs,
        out_specs=out_specs or [spec(o.shape[0], o.dtype, left) for o in outs],
        scratch_shapes=[pltpu.VMEM((rows, tile), F32)],
        cost_estimate=pl.CostEstimate(flops=0, bytes_accessed=moved, transcendentals=0),
    )(xyz, *[a for a, _ in ins])


def block_rows(index):
    return pl.ds(pl.multiple_of(index * 96, 96), 96)


def first_fold(xyz, mine_a, got_a, mine_b, got_b, keep_a, send_a, keep_b, send_b, sum_ref):
    x, y = xyz[0], xyz[1]
    sum_ref[...] = mine_a[...] + got_a[...].astype(F32)
    for other in range(2):
        rows = slice(other * 96, (other + 1) * 96)
        keep_a[rows, :] = sum_ref[block_rows(2 * other + x), :]
        send_a[rows, :] = sum_ref[block_rows(2 * other + 1 - x), :].astype(BF16)
    sum_ref[...] = mine_b[...] + got_b[...].astype(F32)
    for other in range(2):
        rows = slice(other * 96, (other + 1) * 96)
        keep_b[rows, :] = sum_ref[block_rows(2 * y + other), :]
        send_b[rows, :] = sum_ref[block_rows(2 * (1 - y) + other), :].astype(BF16)


def second_fold(xyz, mine_a, got_a, mine_b, got_b, keep_a, send_a, keep_b, send_b, sum_ref):
    x, y = xyz[0], xyz[1]
    sum_ref[...] = mine_a[...] + got_a[...].astype(F32)
    keep_a[...] = sum_ref[block_rows(y), :]
    send_a[...] = sum_ref[block_rows(1 - y), :].astype(BF16)
    sum_ref[...] = mine_b[...] + got_b[...].astype(F32)
    keep_b[...] = sum_ref[block_rows(x), :]
    send_b[...] = sum_ref[block_rows(1 - x), :].astype(BF16)


def third_fold(xyz, mine_a, got_a, mine_b, got_b, keep, send_1, send_2, send_3, sum_ref):
    z = xyz[2]
    width = keep.shape[1]
    for m, (mine, got) in enumerate(((mine_a, got_a), (mine_b, got_b))):
        total = mine[...] + got[...].astype(F32)
        sum_ref[2 * m] = total[:, :width]
        sum_ref[2 * m + 1] = total[:, width:]
    keep[...] = sum_ref[z]
    low, high = lax.rem(z, 2), z // 2
    send_1[...] = sum_ref[2 * high + 1 - low].astype(BF16)
    send_2[...] = sum_ref[2 * (1 - high) + low].astype(BF16)
    send_3[...] = sum_ref[2 * (1 - high) + 1 - low].astype(BF16)


def last_fold(flips, keep, got_1, got_2, got_3, *outs):
    total = keep[...] + got_1[...].astype(F32) + (got_2[...].astype(F32) + got_3[...].astype(F32))
    width = keep.shape[1] // len(outs)
    for m, out in enumerate(outs):
        part = total[:, m * width : (m + 1) * width]
        out[...] = part.T if m in flips else part


def table_fold(mine, got, out):
    out[...] = (mine[...] + got[...].astype(F32)).T


class Reduction:
    def __init__(self, xyz, mine, send):
        self.xyz, self.mine, self.width = xyz, mine, mine.shape[1] // 2
        self.got = swap(send, "dp", 8, 1)

    def first(self):
        ins = [(self.mine, 0), (self.got, 0), (self.mine, 1), (self.got, 1)]
        shape = (192, self.width)
        outs = [whole(shape, F32), whole(shape, BF16)] * 2
        keep_a, send_a, keep_b, send_b = fold_call(first_fold, self.xyz, ins, outs, self.width)
        self.keeps = keep_a, keep_b
        self.gots = swap(send_a, "dp", 8, 2), swap(send_b, "dp", 8, 4)
        return send_a, send_b

    def second(self):
        (keep_a, keep_b), (got_a, got_b) = self.keeps, self.gots
        ins = [(keep_a, 0), (got_a, 0), (keep_b, 0), (got_b, 0)]
        shape = (96, self.width)
        outs = [whole(shape, F32), whole(shape, BF16)] * 2
        keep_a, send_a, keep_b, send_b = fold_call(second_fold, self.xyz, ins, outs, self.width)
        self.keeps = keep_a, keep_b
        self.gots = swap(send_a, "dp", 8, 4), swap(send_b, "dp", 8, 2)
        return send_a, send_b

    def third(self):
        (keep_a, keep_b), (got_a, got_b) = self.keeps, self.gots
        shape = (96, self.width // 2)
        keep, *sends = pl.pallas_call(
            third_fold,
            out_shape=[whole(shape, F32)] + [whole(shape, BF16)] * 3,
            in_specs=[pl.BlockSpec(memory_space=pltpu.SMEM)]
            + [pl.BlockSpec(memory_space=pltpu.VMEM)] * 4,
            out_specs=[pl.BlockSpec(memory_space=pltpu.VMEM)] * 4,
            scratch_shapes=[pltpu.VMEM((4,) + shape, F32)],
        )(self.xyz, keep_a, got_a, keep_b, got_b)
        self.keeps = keep
        self.gots = [swap(send, "tensor", 4, j + 1) for j, send in enumerate(sends)]
        return tuple(sends)

    def last(self, count, flips):
        rows, width = self.keeps.shape
        shape = (rows, width // count)
        outs = [whole(shape[::-1] if m in flips else shape, F32) for m in range(count)]
        return pl.pallas_call(functools.partial(last_fold, flips), out_shape=outs)(
            self.keeps, *self.gots
        )

    def table(self, vocab):
        parts = []
        for keep, got, start in zip(self.keeps, self.gots, (0, self.width)):
            count = min(self.width, vocab - start)
            tile = pl.BlockSpec((96, VTILE), lambda i: (0, i))
            parts.append(
                pl.pallas_call(
                    table_fold,
                    grid=(pl.cdiv(count, VTILE),),
                    out_shape=whole((count, 96), F32),
                    in_specs=[tile] * 2,
                    out_specs=pl.BlockSpec((VTILE, 96), lambda i: (i, 0)),
                )(keep, got)
            )
        return jnp.concatenate(parts, 0)


class WideReduction:
    def __init__(self, xyz, mine, send):
        self.gots = ()
        both = jnp.concatenate([mine, send.astype(F32)], 0)
        self.part = lax.psum_scatter(both, "dp", scatter_dimension=0, tiled=True)

    def first(self):
        return ()

    second = third = first

    def last(self, count, flips):
        rows = self.part.shape[0]
        by_z = self.part.reshape(rows, 4, -1)
        total = lax.psum_scatter(by_z, "tensor", scatter_dimension=1, tiled=True)[:, 0]
        parts = jnp.split(total, count, axis=1)
        return [p.T if m in flips else p for m, p in enumerate(parts)]

    def table(self, vocab):
        return self.part.T


def after(value, *others):
    return lax.optimization_barrier((value,) + others)[0]


def rms_scale(values):
    return lax.rsqrt(jnp.mean(values * values, axis=-1, keepdims=True) + EPS)


def norm_back(values, inv_scale, gain, grad_out):
    weighted = gain * grad_out
    grad_gain = jnp.sum(grad_out * values * inv_scale, axis=0, keepdims=True)
    grad_values = inv_scale * weighted - values * inv_scale * inv_scale * inv_scale * jnp.mean(
        weighted * values, axis=-1, keepdims=True
    )
    return grad_values, grad_gain


def flip(value):
    return value.astype(F32).T


def lane_half(rows, which):
    lane = lax.broadcasted_iota(jnp.int32, (rows, 2 * HDIM), 1)
    return (lane >= HDIM) if which else (lane < HDIM)


def only(value, which):
    return jnp.where(lane_half(value.shape[0], which), value, jnp.zeros_like(value))


def split_rows(flat_ref, mine_ref, send_ref, core, split):
    for block in range(4):
        if split:
            first = pl.multiple_of((2 * block + core) * 96, 96)
            second = pl.multiple_of((2 * block + 1 - core) * 96, 96)
        else:
            first, second = block * 96, HALF_D + block * 96
        mine_ref[block * 96 : (block + 1) * 96, :] = flat_ref[pl.ds(first, 96), :]
        send_ref[block * 96 : (block + 1) * 96, :] = flat_ref[pl.ds(second, 96), :]


def by_shard(left_ref, rights, out_ref, first, per_shard):
    width = 192 * len(rights)
    for z in range(4):
        part = [right[:, z * 192 : (z + 1) * 192] for right in rights]
        right = jnp.concatenate(part, axis=1) if len(part) > 1 else part[0]
        start = z * per_shard + first
        out_ref[:, start : start + width] = dot_nn(left_ref[...], right).astype(out_ref.dtype)


def whole(shape, dtype):
    return jax.ShapeDtypeStruct(shape, dtype)


def local_call(body, outs, scratch, flops, *args):
    smem = pl.BlockSpec(memory_space=pltpu.SMEM)
    vmem = pl.BlockSpec(memory_space=pltpu.VMEM)
    bytes_all = sum(a.size * a.dtype.itemsize for a in args)
    bytes_all += sum(o.size * jnp.dtype(o.dtype).itemsize for o in outs)
    held = sum(math.prod(s.shape) * jnp.dtype(s.dtype).itemsize for s in scratch)
    return pl.pallas_call(
        body,
        out_shape=outs,
        in_specs=[smem] + [vmem] * (len(args) - 1),
        out_specs=[vmem] * len(outs),
        scratch_shapes=scratch,
        cost_estimate=pl.CostEstimate(
            flops=int(flops), bytes_accessed=int(bytes_all), transcendentals=0
        ),
        compiler_params=pltpu.CompilerParams(
            vmem_limit_bytes=min(VMEM_LIMIT, int(bytes_all + held + 16 * 2**20))
        ),
    )(*args)


def forward_kernel(split, *refs):
    (scal, x_own, source, gain_self, gain_cross, gain_ff, gain_final), refs = refs[:7], refs[7:]
    shards, refs = refs[: 11 if split else 5], refs[11 if split else 5 :]
    (q1, k1, v1, lse1, att1, h1_out, q2, k2, v2), refs = refs[:9], refs[9:]
    (out_ref, fin_ref, h2_ref, att_t_ref, att2, lse2), refs = refs[:6], refs[6:]
    if split:
        copies_out, refs = refs[:11], refs[11:]
        (ws, wc, wg, wu, wd), refs = refs[:5], refs[5:]
    else:
        ws, wc, wg, wu, wd = shards
    (x_other, x_ref, n_ref, vt_ref, ot_ref, s_ref, o_send, o_other, lse_own, lse_other, mix_ref), refs = (
        refs[:11],
        refs[11:],
    )
    pair_send, pair_recv = refs[:2]
    dp = lax.axis_index("dp")
    z = lax.axis_index("tensor")
    low, high = lax.rem(z, 2), z // 2
    half, live, live_src = low, scal[1], scal[2] - low * KEYS
    z_peers = [(dp, high * 2 + 1 - low)]
    peers = z_peers
    if split:
        z_peers = z_peers + [(dp, (1 - high) * 2 + low), (dp, (1 - high) * 2 + 1 - low)]
        x_peer = dp + 2 - 4 * lax.rem(dp // 2, 2)
        y_peer = dp + 4 - 8 * (dp // 4)
        links = dict(
            dp=dp,
            z=z,
            z_peers=z_peers,
            x=(x_peer, z),
            y=(y_peer, z),
            xy=x_peer + y_peer - dp,
            core=(dp + 1 - 2 * lax.rem(dp, 2), z),
            sems=refs[2:4],
        )
        out_sem = refs[4]
        peers = z_peers + [links["x"], links["y"], links["core"]]
    barrier = pltpu.get_barrier_semaphore()
    for peer in peers:
        pl.semaphore_signal(
            barrier, inc=1, device_id={"dp": peer[0], "tensor": peer[1]}, device_id_type=MESH_ID
        )

    def exchange(index, src, dst):
        copy = pltpu.make_async_remote_copy(
            src_ref=src,
            dst_ref=dst,
            send_sem=pair_send.at[index],
            recv_sem=pair_recv.at[index],
            device_id={"dp": z_peers[0][0], "tensor": z_peers[0][1]},
            device_id_type=MESH_ID,
        )
        copy.start()
        return copy

    leaving = []
    if split:
        used = [0]
        groups = [Gather(links, refs_of, used) for refs_of in ([ws], [wc], [wg], [wu], [wd])]
        of_self, of_cross, of_gate, of_up, of_down = groups
        hid, fhid = D // 4, FF // 4

        def place_block(target, first):
            rows = pl.ds(pl.multiple_of(z * hid, 16), hid)
            for m in range(3):
                target[m, rows, :] = flip(shards[first + m][...]).astype(BF16)
            target[3, rows, :] = shards[first + 3][...]

        def place_wide(target, shard, flipped):
            rows = pl.ds(pl.multiple_of(z * fhid, 16), fhid)
            target[rows, :] = flip(shard[...]).astype(BF16) if flipped else shard[...]

        def leave(first, parts):
            for i, part in enumerate(parts):
                copy = pltpu.make_async_copy(part, copies_out[first + i], out_sem.at[first + i])
                copy.start()
                leaving.append(copy)

        place_block(ws, 0)
        pl.semaphore_wait(barrier, len(peers))
        of_self.along_z()
    else:
        pl.semaphore_wait(barrier, len(peers))
    x_copy = exchange(0, x_own, x_other)
    if split:
        place_block(wc, 4)
        place_wide(wg, shards[8], True)
        place_wide(wu, shards[9], True)
        place_wide(wd, shards[10], False)
        of_self.along_xy()
        of_cross.along_z()
        of_self.diagonal()
        of_cross.along_xy()
        of_gate.along_z()
    x_copy.wait()
    own = pl.multiple_of(half * ROWS, ROWS)
    other = pl.multiple_of((1 - half) * ROWS, ROWS)
    x_ref[pl.ds(own, ROWS), :] = x_own[...].astype(F32)
    x_ref[pl.ds(other, ROWS), :] = x_other[...].astype(F32)
    lse1[...] = jnp.zeros_like(lse1)
    lse_own[...] = jnp.zeros_like(lse_own)
    if split:
        of_self.finish()
        leave(0, [ws.at[m] for m in range(4)])
    for i in range(2):
        rows = slice(i * ROWS, (i + 1) * ROWS)
        x = x_ref[rows, :]
        n = (x * rms_scale(x) * gain_self[...]).astype(BF16)
        n_ref[rows, :] = n
        q1[rows, :] = dot_nt(n, ws[0]).astype(BF16)
        k1[rows, :] = dot_nt(n, ws[1]).astype(BF16)
        v1[rows, :] = dot_nt(n, ws[2]).astype(BF16)
    vt_ref[:, :TGT] = dot_nt(ws[2], n_ref[...]).astype(BF16)
    if split:
        of_gate.along_xy()
        of_up.along_z()
    key = lax.broadcasted_iota(jnp.int32, (TGT, TGT), 0)
    query = lax.broadcasted_iota(jnp.int32, (TGT, TGT), 1)
    seen = (key <= query) & (key < live)

    def self_pairs(first, last):
        @pl.loop(first, last)
        def _(pair):
            lanes = pl.ds(pl.multiple_of(pair * 128, 128), 128)
            q_pair, k_pair = q1[:, lanes], k1[:, lanes]
            for which in range(2):
                head = 2 * pair + which
                feats = pl.ds(pl.multiple_of(head * HDIM, HDIM), HDIM)
                scores = jnp.where(seen, dot_nt(k_pair, only(q_pair, which)) * SCALE, NEG)
                top = jnp.max(scores, axis=0, keepdims=True)
                probs = jnp.exp(scores - top)
                total = jnp.sum(probs, axis=0, keepdims=True)
                lse1[pl.ds(head, 1), :] = top + jnp.log(total)
                ot_ref[feats, :] = dot_nn(vt_ref[feats, :TGT], probs.astype(BF16)) / total

    self_pairs(0, PAIRS // 2)
    if split:
        of_cross.diagonal()
    self_pairs(PAIRS // 2, PAIRS)
    if split:
        of_up.along_xy()
        of_down.along_z()
        of_gate.diagonal()
    for i in range(2):
        rows = slice(i * ROWS, (i + 1) * ROWS)
        att = flip(ot_ref[:, rows]).astype(BF16)
        n_ref[rows, :] = att
        x_ref[rows, :] = x_ref[rows, :] + dot_nn(att, ws[3])
    att1[...] = n_ref[pl.ds(own, ROWS), :]
    h1_out[...] = x_ref[pl.ds(own, ROWS), :]
    if split:
        of_cross.finish()
        leave(4, [wc.at[m] for m in range(4)])
    for i in range(2):
        rows = slice(i * ROWS, (i + 1) * ROWS)
        h1 = x_ref[rows, :]
        n = (h1 * rms_scale(h1) * gain_cross[...]).astype(BF16)
        q2[rows, :] = dot_nt(n, wc[0]).astype(BF16)
    for i in range(KEYS // CHUNK):
        rows = slice(i * CHUNK, (i + 1) * CHUNK)
        src = source[rows, :]
        k2[rows, :] = dot_nt(src, wc[1]).astype(BF16)
        v2[rows, :] = dot_nt(src, wc[2]).astype(BF16)
        vt_ref[:, rows] = dot_nt(wc[2], src).astype(BF16)
    if split:
        of_down.along_xy()
        of_up.diagonal()
        of_gate.finish()
        leave(8, [wg])
    chunk_key = lax.broadcasted_iota(jnp.int32, (CHUNK, TGT), 0)

    def cross_pairs(first, last):
        @pl.loop(first, last)
        def _(pair):
            lanes = pl.ds(pl.multiple_of(pair * 128, 128), 128)
            q_pair = q2[:, lanes]
            for which in range(2):
                head = 2 * pair + which
                feats = pl.ds(pl.multiple_of(head * HDIM, HDIM), HDIM)
                q_one = only(q_pair, which)
                top = jnp.full((1, TGT), 2 * NEG, F32)
                for i in range(KEYS // CHUNK):
                    rows = slice(i * CHUNK, (i + 1) * CHUNK)
                    scores = dot_nt(k2[rows, lanes], q_one) * SCALE
                    scores = jnp.where(chunk_key < live_src - i * CHUNK, scores, NEG)
                    s_ref[rows, :] = scores
                    top = jnp.maximum(top, jnp.max(scores, axis=0, keepdims=True))
                total = jnp.zeros((1, TGT), F32)
                out = jnp.zeros((HDIM, TGT), F32)
                for i in range(KEYS // CHUNK):
                    rows = slice(i * CHUNK, (i + 1) * CHUNK)
                    probs = jnp.exp(s_ref[rows, :] - top)
                    total = total + jnp.sum(probs, axis=0, keepdims=True)
                    out = out + dot_nn(vt_ref[feats, rows], probs.astype(BF16))
                lse_own[pl.ds(head, 1), :] = top + jnp.log(total)
                ot_ref[feats, :] = out / total

    cross_pairs(0, PAIRS // 2)
    o_send[: D // 2, :] = ot_ref[: D // 2, pl.ds(other, ROWS)].astype(BF16)
    pair_copies = [exchange(1, o_send.at[: D // 2], o_other.at[: D // 2])]
    if split:
        of_down.diagonal()
        of_up.finish()
        leave(9, [wu])
    cross_pairs(PAIRS // 2, PAIRS)
    o_send[D // 2 :, :] = ot_ref[D // 2 :, pl.ds(other, ROWS)].astype(BF16)
    pair_copies.append(exchange(2, o_send.at[D // 2 :], o_other.at[D // 2 :]))
    pair_copies.append(exchange(3, lse_own, lse_other))
    if split:
        of_down.finish()
        leave(10, [wd])
    for copy in pair_copies:
        copy.wait()

    first, second = lse_own[...], lse_other[...]
    top = jnp.maximum(first, second)
    lse2[...] = top + jnp.log(jnp.exp(first - top) + jnp.exp(second - top))
    lse = lse2[:, pl.ds(own, ROWS)]
    w_first = jnp.exp(lse_own[:, pl.ds(own, ROWS)] - lse)
    w_second = jnp.exp(lse_other[:, pl.ds(own, ROWS)] - lse)
    for head in range(NHEAD):
        feats = slice(head * HDIM, (head + 1) * HDIM)
        att_t_ref[feats, :] = (
            ot_ref[feats, pl.ds(own, ROWS)] * w_first[head : head + 1, :]
            + o_other[feats, :].astype(F32) * w_second[head : head + 1, :]
        )
    att = flip(att_t_ref[...]).astype(BF16)
    att2[...] = att
    h2 = h1_out[...] + dot_nn(att, wc[3])
    h2_ref[...] = h2
    n3 = (h2 * rms_scale(h2) * gain_ff[...]).astype(BF16)

    @pl.loop(0, FF // 512)
    def _(i):
        rows = pl.ds(pl.multiple_of(i * 512, 512), 512)
        gate = dot_nt(n3, wg[rows, :])
        up = dot_nt(n3, wu[rows, :])
        mix_ref[:, rows] = (jax.nn.gelu(gate, approximate=True) * up).astype(BF16)

    out = h2 + dot_nn(mix_ref[...], wd[...])
    out_ref[...] = out
    fin_ref[...] = (out * rms_scale(out) * gain_final[...] * D ** (-0.5)).astype(BF16)
    for copy in leaving:
        copy.wait()


def forward(split, scal, x_own, source, gains, weights):
    pair = (TGT, D)
    block = (ROWS, D)
    outs = [whole(pair, BF16)] * 3 + [whole((16, TGT), F32), whole(block, BF16), whole(block, F32)]
    outs += [whole(pair, BF16)] + [whole((KEYS, D), BF16)] * 2
    outs += [whole(block, F32), whole(block, BF16), whole(block, F32), whole((D, ROWS), F32)]
    outs += [whole(block, BF16), whole((16, TGT), F32)]
    vmem = pl.BlockSpec(memory_space=pltpu.VMEM)
    out_specs = [vmem] * len(outs)
    scratch = []
    if split:
        outs += [whole((D, D), BF16)] * 8 + [whole((FF, D), BF16)] * 3
        out_specs += [pl.BlockSpec(memory_space=pl.ANY)] * 11
        scratch += [pltpu.VMEM((4, D, D), BF16)] * 2 + [pltpu.VMEM((FF, D), BF16)] * 3
    scratch += [
        pltpu.VMEM(block, BF16),
        pltpu.VMEM(pair, F32),
        pltpu.VMEM(pair, BF16),
        pltpu.VMEM((D, KEYS), BF16),
        pltpu.VMEM((D, TGT), F32),
        pltpu.VMEM((KEYS, TGT), F32),
        pltpu.VMEM((D, ROWS), BF16),
        pltpu.VMEM((D, ROWS), BF16),
        pltpu.VMEM((16, TGT), F32),
        pltpu.VMEM((16, TGT), F32),
        pltpu.VMEM((ROWS, FF), BF16),
        pltpu.SemaphoreType.DMA((4,)),
        pltpu.SemaphoreType.DMA((4,)),
    ]
    if split:
        scratch += [pltpu.SemaphoreType.DMA((27 * 5,))] * 2 + [pltpu.SemaphoreType.DMA((11,))]
    args = (scal, x_own, source, *gains, *weights)
    return pl.pallas_call(
        functools.partial(forward_kernel, split),
        out_shape=outs,
        in_specs=[pl.BlockSpec(memory_space=pltpu.SMEM)] + [vmem] * (len(args) - 1),
        out_specs=out_specs,
        scratch_shapes=scratch,
        cost_estimate=pl.CostEstimate(
            flops=int(80e9), bytes_accessed=int(6e7), transcendentals=0
        ),
        compiler_params=pltpu.CompilerParams(
            collective_id=0, has_side_effects=True, vmem_limit_bytes=VMEM_LIMIT
        ),
    )(*args)


def ff_backward(
    split, scal, gf_own, gf_1, gf_2, gf_3, block_out, h2_in, gain_ff, gain_final, wg, wu, wd,
    w_co, att_t, mine_ref, send_ref, res_ref, rows_ref, gatt_ref, dot_ref, gg_ref,
    flat_ref, nm_ref, ns_ref, gm_ref, gs_ref, gn_ref,
):
    core = scal[3]
    grad = gf_own[...] + gf_1[...].astype(F32)
    grad = grad + (gf_2[...].astype(F32) + gf_3[...].astype(F32))
    out = block_out[...]
    res, gg_final = norm_back(out, rms_scale(out), gain_final[...], grad * D ** (-0.5))
    gg_ref[0:1, :] = gg_final
    rows_b = res.astype(BF16)
    res_ref[...] = res
    flat_ref[...] = flip(rows_b).astype(BF16)
    split_rows(flat_ref, gm_ref, gs_ref, core, split)
    h2 = h2_in[...]
    scale3 = rms_scale(h2)
    n3 = (h2 * scale3 * gain_ff[...]).astype(BF16)
    flat_ref[...] = flip(n3).astype(BF16)
    split_rows(flat_ref, nm_ref, ns_ref, core, split)
    gn_ref[...] = jnp.zeros_like(gn_ref)
    const = (2.0 / 3.141592653589793) ** 0.5

    @pl.loop(0, FF // 512)
    def _(i):
        start = pl.multiple_of(i * 512, 512)
        rows = pl.ds(start, 512)
        gate = dot_nt(n3, wg[rows, :])
        up = dot_nt(n3, wu[rows, :])
        square = gate * gate
        tanh = jnp.tanh(const * (gate + 0.044715 * gate * square))
        gelu = 0.5 * gate * (1.0 + tanh)
        slope = 0.5 * (1.0 + tanh) + 0.5 * gate * (1.0 - tanh * tanh) * const * (
            1.0 + 3.0 * 0.044715 * square
        )
        grad_mixed = dot_nt(rows_b, wd[rows, :])
        g_gate = (grad_mixed * up * slope).astype(BF16)
        g_up = (grad_mixed * gelu).astype(BF16)
        mixed = (gelu * up).astype(BF16)
        gn_ref[...] += dot_nn(g_gate, wg[rows, :]) + dot_nn(g_up, wu[rows, :])
        for m, (mine, send, right) in enumerate(
            ((nm_ref, ns_ref, g_gate), (nm_ref, ns_ref, g_up), (gm_ref, gs_ref, mixed))
        ):
            cols = pl.ds(pl.multiple_of(3 * start + m * 512, 512), 512)
            mine_ref[:, cols] = dot_nn(mine[...], right)
            send_ref[:, cols] = dot_nn(send[...], right).astype(BF16)

    step, gg_ff = norm_back(h2, scale3, gain_ff[...], gn_ref[...])
    gg_ref[1:2, :] = gg_ff
    res = res_ref[...] + step
    res_ref[...] = res
    rows_b = res.astype(BF16)
    rows_ref[...] = rows_b
    gatt_ref[...] = dot_nt(rows_b, w_co[...]).astype(BF16)
    gatt_t = dot_nt(w_co[...], rows_b).astype(BF16).astype(F32)
    dot_ref[...] = jnp.zeros_like(dot_ref)
    for head in range(NHEAD):
        feats = slice(head * HDIM, (head + 1) * HDIM)
        dot_ref[head : head + 1, :] = jnp.sum(gatt_t[feats, :] * att_t[feats, :], 0, keepdims=True)


def both_halves(half, own, other, target):
    target[pl.ds(pl.multiple_of(half * ROWS, ROWS), ROWS), :] = own[...]
    target[pl.ds(pl.multiple_of((1 - half) * ROWS, ROWS), ROWS), :] = other[...]


def cross_backward(
    scal, q2, k2, v2, lse, g_own, g_other, dot_own, dot_other,
    dk_ref, dv_ref, own_out, send_out, g_ref, dot_ref, dq_ref,
):
    half = scal[0]
    live = scal[2] - half * KEYS
    own = pl.multiple_of(half * ROWS, ROWS)
    other = pl.multiple_of((1 - half) * ROWS, ROWS)
    both_halves(half, g_own, g_other, g_ref)
    dot_ref[:, pl.ds(own, ROWS)] = dot_own[...]
    dot_ref[:, pl.ds(other, ROWS)] = dot_other[...]
    key = lax.broadcasted_iota(jnp.int32, (CHUNK, TGT), 0)

    @pl.loop(0, PAIRS)
    def _(pair):
        lanes = pl.ds(pl.multiple_of(pair * 128, 128), 128)
        q_pair, g_pair = q2[:, lanes], g_ref[:, lanes]
        for i in range(KEYS // CHUNK):
            rows = slice(i * CHUNK, (i + 1) * CHUNK)
            k_part, v_part = k2[rows, lanes], v2[rows, lanes]
            k_flip = flip(k_part).astype(BF16)
            grad_k = jnp.zeros((CHUNK, 128), F32)
            grad_v = jnp.zeros((CHUNK, 128), F32)
            for which in range(2):
                head = 2 * pair + which
                feats = pl.ds(pl.multiple_of(head * HDIM, HDIM), HDIM)
                q_one, g_one = only(q_pair, which), only(g_pair, which)
                scores = dot_nt(k_part, q_one) * SCALE
                scores = jnp.where(key < live - i * CHUNK, scores, NEG)
                probs = jnp.exp(scores - lse[pl.ds(head, 1), :])
                grad_p = dot_nt(v_part, g_one)
                grad_s = (probs * (grad_p - dot_ref[pl.ds(head, 1), :])).astype(BF16)
                grad_k = grad_k + dot_nn(grad_s, q_one)
                grad_v = grad_v + dot_nn(probs.astype(BF16), g_one)
                grad_q = dot_nn(k_flip[which * HDIM : (which + 1) * HDIM, :], grad_s)
                if i == 0:
                    dq_ref[feats, :] = grad_q
                else:
                    dq_ref[feats, :] += grad_q
            dk_ref[rows, lanes] = (grad_k * SCALE).astype(BF16)
            dv_ref[rows, lanes] = grad_v.astype(BF16)

    own_out[...] = dq_ref[:, pl.ds(own, ROWS)]
    send_out[...] = dq_ref[:, pl.ds(other, ROWS)].astype(BF16)


def source_backward(
    split, scal, dk, dv, source, w_ck, w_cv, gsrc_ref, mine_ref, send_ref, flat_ref, sm_ref, ss_ref
):
    for i in range(KEYS // CHUNK):
        rows = slice(i * CHUNK, (i + 1) * CHUNK)
        gsrc_ref[rows, :] = dot_nn(dk[rows, :], w_ck[...]) + dot_nn(dv[rows, :], w_cv[...])
        flat_ref[:, rows] = flip(source[rows, :]).astype(BF16)
    split_rows(flat_ref, sm_ref, ss_ref, scal[3], split)
    rights = (dk[...], dv[...])
    by_shard(sm_ref, rights, mine_ref, 0, 384)
    by_shard(ss_ref, rights, send_ref, 0, 384)


def query_backward(
    split, scal, dq_own, dq_other, h1_in, gain_cross, w_cq, res_in, rows_in, att, w_so,
    kv_mine, kv_send, mine_ref, send_ref, res_ref, rows_ref, gatt_ref, gg_ref, flat_ref, a_ref, b_ref,
):
    core = scal[3]
    dq = (flip(dq_own[...] + dq_other[...].astype(F32)) * SCALE).astype(BF16)
    h1 = h1_in[...]
    scale2 = rms_scale(h1)
    n2 = (h1 * scale2 * gain_cross[...]).astype(BF16)
    step, gg = norm_back(h1, scale2, gain_cross[...], dot_nn(dq, w_cq[...]))
    gg_ref[...] = gg
    res = res_in[...] + step
    res_ref[...] = res
    rows_b = res.astype(BF16)
    rows_ref[...] = rows_b
    gatt_ref[...] = dot_nt(rows_b, w_so[...]).astype(BF16)
    for m, (left, right) in enumerate(((n2, dq), (rows_in[...], att[...]))):
        flat_ref[...] = flip(left).astype(BF16)
        split_rows(flat_ref, a_ref, b_ref, core, split)
        by_shard(a_ref, (right,), mine_ref, 576 * m, D)
        by_shard(b_ref, (right,), send_ref, 576 * m, D)
    for z in range(4):
        cols = slice(z * D + 192, z * D + 576)
        mine_ref[:, cols] = kv_mine[:, z * 384 : (z + 1) * 384]
        send_ref[:, cols] = kv_send[:, z * 384 : (z + 1) * 384]


def self_backward(
    split, scal, q1, k1, v1, lse, g_own, g_other, x_own, gain_self, w_q, w_k, w_v, res_in, rows_in, att,
    mine_ref, send_ref, gin_ref, gg_ref,
    g_ref, dq_ref, dk_ref, dv_ref, flat_ref, a_ref, b_ref,
):
    half = scal[0]
    live = scal[1]
    core = scal[3]
    own = pl.multiple_of(half * ROWS, ROWS)
    both_halves(half, g_own, g_other, g_ref)
    key = lax.broadcasted_iota(jnp.int32, (TGT, TGT), 0)
    query = lax.broadcasted_iota(jnp.int32, (TGT, TGT), 1)
    seen = (key <= query) & (key < live)

    @pl.loop(0, PAIRS)
    def _(pair):
        lanes = pl.ds(pl.multiple_of(pair * 128, 128), 128)
        q_pair, g_pair = q1[:, lanes], g_ref[:, lanes]
        k_pair, v_pair = k1[:, lanes], v1[:, lanes]
        k_flip = flip(k_pair).astype(BF16)
        grad_k = jnp.zeros((TGT, 128), F32)
        grad_v = jnp.zeros((TGT, 128), F32)
        for which in range(2):
            head = 2 * pair + which
            feats = pl.ds(pl.multiple_of(head * HDIM, HDIM), HDIM)
            q_one, g_one = only(q_pair, which), only(g_pair, which)
            scores = jnp.where(seen, dot_nt(k_pair, q_one) * SCALE, NEG)
            probs = jnp.exp(scores - lse[pl.ds(head, 1), :])
            grad_p = dot_nt(v_pair, g_one)
            row_dot = jnp.sum(probs * grad_p, axis=0, keepdims=True)
            grad_s = (probs * (grad_p - row_dot)).astype(BF16)
            grad_k = grad_k + dot_nn(grad_s, q_one)
            grad_v = grad_v + dot_nn(probs.astype(BF16), g_one)
            dq_ref[feats, :] = dot_nn(k_flip[which * HDIM : (which + 1) * HDIM, :], grad_s)
        dk_ref[:, lanes] = (grad_k * SCALE).astype(BF16)
        dv_ref[:, lanes] = grad_v.astype(BF16)

    dq = (flip(dq_ref[:, pl.ds(own, ROWS)]) * SCALE).astype(BF16)
    dk = dk_ref[pl.ds(own, ROWS), :]
    dv = dv_ref[pl.ds(own, ROWS), :]
    x = x_own[...].astype(F32)
    scale1 = rms_scale(x)
    n1 = (x * scale1 * gain_self[...]).astype(BF16)
    grad_n = dot_nn(dq, w_q[...]) + dot_nn(dk, w_k[...]) + dot_nn(dv, w_v[...])
    step, gg = norm_back(x, scale1, gain_self[...], grad_n)
    gg_ref[...] = gg
    gin_ref[...] = res_in[...] + step
    flat_ref[...] = flip(n1).astype(BF16)
    split_rows(flat_ref, a_ref, b_ref, core, split)
    by_shard(a_ref, (dq, dk, dv), mine_ref, 0, D)
    by_shard(b_ref, (dq, dk, dv), send_ref, 0, D)
    flat_ref[...] = flip(rows_in[...]).astype(BF16)
    split_rows(flat_ref, a_ref, b_ref, core, split)
    by_shard(a_ref, (att[...],), mine_ref, 576, D)
    by_shard(b_ref, (att[...],), send_ref, 576, D)


def logits_kernel(vocab, flat_ref, table_ref, target_ref, logits_ref, stats_ref):
    tile = pl.program_id(0)

    @pl.when(tile == 0)
    def _():
        row = lax.broadcasted_iota(jnp.int32, stats_ref.shape, 0)
        stats_ref[...] = jnp.where(row == 0, 2 * NEG, 0.0)

    logits = dot_nn(table_ref[...], flat_ref[...])
    entry = tile * HTILE + lax.broadcasted_iota(jnp.int32, logits.shape, 0)
    logits = jnp.where(entry < vocab, logits, 2 * NEG)
    logits_ref[...] = logits
    old = stats_ref[0:1, :]
    new = jnp.maximum(old, jnp.max(logits, axis=0, keepdims=True))
    stats_ref[1:2, :] = stats_ref[1:2, :] * jnp.exp(old - new) + jnp.sum(
        jnp.exp(logits - new), axis=0, keepdims=True
    )
    stats_ref[0:1, :] = new
    hit = jnp.where(entry == target_ref[...], logits, 0.0)
    stats_ref[2:3, :] += jnp.sum(hit, axis=0, keepdims=True)


def head_logits(flat, table, target):
    count = flat.shape[1]
    vocab = table.shape[0]
    tiles = pl.cdiv(vocab, HTILE)
    return pl.pallas_call(
        functools.partial(logits_kernel, vocab),
        grid=(tiles,),
        out_shape=[whole((tiles * HTILE, count), F32), whole((8, count), F32)],
        in_specs=[
            pl.BlockSpec((D, count), lambda i: (0, 0)),
            pl.BlockSpec((HTILE, D), lambda i: (i, 0)),
            pl.BlockSpec((1, count), lambda i: (0, 0)),
        ],
        out_specs=[
            pl.BlockSpec((HTILE, count), lambda i: (i, 0)),
            pl.BlockSpec((8, count), lambda i: (0, 0)),
        ],
        cost_estimate=pl.CostEstimate(
            flops=2 * count * vocab * D, bytes_accessed=vocab * (2 * D + 4 * count), transcendentals=0
        ),
        compiler_params=pltpu.CompilerParams(vmem_limit_bytes=VMEM_LIMIT // 2),
    )(flat, table, target)


def grads_kernel(vocab, logits_ref, table_ref, target_ref, lse_ref, live_ref, g_ref, gf_ref, acc_ref):
    tile = pl.program_id(0)

    @pl.when(tile == 0)
    def _():
        acc_ref[...] = jnp.zeros_like(acc_ref)

    entry = tile * HTILE + lax.broadcasted_iota(jnp.int32, logits_ref.shape, 0)
    hit = jnp.where(entry == target_ref[...], 1.0, 0.0)
    grad = jnp.where(live_ref[...] > 0, jnp.exp(logits_ref[...] - lse_ref[...]) - hit, 0.0)
    grad = grad.astype(BF16)
    g_ref[...] = grad
    entry = tile * HTILE + lax.broadcasted_iota(jnp.int32, (HTILE, D), 0)
    table = jnp.where(entry < vocab, table_ref[...], jnp.zeros_like(table_ref[...]))
    acc_ref[...] += lax.dot_general(
        grad, table, (((0,), (0,)), ((), ())), preferred_element_type=F32
    )

    @pl.when(tile == pl.num_programs(0) - 1)
    def _():
        gf_ref[...] = acc_ref[...].astype(gf_ref.dtype)


def head_grads(logits, table, target, lse, live, dtype):
    count = logits.shape[1]
    vocab = table.shape[0]
    tiles = pl.cdiv(vocab, HTILE)
    row = pl.BlockSpec((1, count), lambda i: (0, 0))
    return pl.pallas_call(
        functools.partial(grads_kernel, vocab),
        grid=(tiles,),
        out_shape=[whole((tiles * HTILE, count), BF16), whole((count, D), dtype)],
        in_specs=[
            pl.BlockSpec((HTILE, count), lambda i: (i, 0)),
            pl.BlockSpec((HTILE, D), lambda i: (i, 0)),
            row,
            row,
            row,
        ],
        out_specs=[
            pl.BlockSpec((HTILE, count), lambda i: (i, 0)),
            pl.BlockSpec((count, D), lambda i: (0, 0)),
        ],
        scratch_shapes=[pltpu.VMEM((count, D), F32)],
        cost_estimate=pl.CostEstimate(
            flops=2 * count * vocab * D, bytes_accessed=vocab * (2 * D + 6 * count), transcendentals=0
        ),
        compiler_params=pltpu.CompilerParams(vmem_limit_bytes=VMEM_LIMIT // 2),
    )(logits, table, target, lse, live)


def table_kernel(fm_a, fm_b, fs_a, fs_b, g_a, g_b, mine_ref, send_ref):
    first, second = g_a[...], g_b[...]
    mine_ref[...] = dot_nt(fm_a[...], first) + dot_nt(fm_b[...], second)
    send_ref[...] = (dot_nt(fs_a[...], first) + dot_nt(fs_b[...], second)).astype(BF16)


def table_grads(flat_a, flat_b, g_a, g_b):
    width, count = g_a.shape
    left = pl.BlockSpec((HALF_D, count), lambda i: (0, 0))
    right = pl.BlockSpec((HTILE, count), lambda i: (i, 0))
    out = pl.BlockSpec((HALF_D, HTILE), lambda i: (0, i))
    return pl.pallas_call(
        table_kernel,
        grid=(width // HTILE,),
        out_shape=[whole((HALF_D, width), F32), whole((HALF_D, width), BF16)],
        in_specs=[left] * 4 + [right] * 2,
        out_specs=[out] * 2,
        cost_estimate=pl.CostEstimate(
            flops=4 * count * width * D, bytes_accessed=width * (4 * count + 6 * HALF_D), transcendentals=0
        ),
        compiler_params=pltpu.CompilerParams(vmem_limit_bytes=VMEM_LIMIT),
    )(flat_a[0], flat_b[0], flat_a[1], flat_b[1], g_a, g_b)


def make(mesh):
    dp_size = mesh.shape["dp"]
    split = dp_size == 8

    def on_device(
        block_in,
        source,
        target_len,
        source_len,
        targets,
        gain_self,
        gain_cross,
        gain_ff,
        gain_final,
        self_q,
        self_k,
        self_v,
        self_o,
        cross_q,
        cross_k,
        cross_v,
        cross_o,
        ff_gate,
        ff_up,
        ff_down,
        embed_table,
    ):
        z = lax.axis_index("tensor")
        dp = lax.axis_index("dp")
        half = lax.rem(z, 2)
        seq = z // 2
        core = lax.rem(dp, 2)
        gain_self, gain_cross, gain_ff, gain_final = (
            g.reshape(1, D) for g in (gain_self, gain_cross, gain_ff, gain_final)
        )

        def pair_swap(value):
            return swap(value, "tensor", 4, 1)

        scal = jnp.stack(
            [
                half,
                lax.dynamic_index_in_dim(target_len, seq, keepdims=False),
                lax.dynamic_index_in_dim(source_len, seq, keepdims=False),
                core,
            ]
        ).astype(jnp.int32)

        def vm(shape, dtype):
            return pltpu.VMEM(shape, dtype)

        pair = (TGT, D)
        weights = (
            self_q, self_k, self_v, self_o, cross_q, cross_k, cross_v, cross_o, ff_gate, ff_up, ff_down,
        )
        if not split:
            wide = [gather_wide(w if i in (3, 7, 10) else w.T, dp_size) for i, w in enumerate(weights)]
            sq, sk, sv, so, cq, ck, cv, co, wg, wu, wd = wide
            weights = jnp.stack([sq, sk, sv, so]), jnp.stack([cq, ck, cv, co]), wg, wu, wd
        gains = gain_self, gain_cross, gain_ff, gain_final
        results = forward(split, scal, block_in, source, gains, weights)
        q1, k1, v1, lse1, a1, h1, q2, k2, v2, block_out, fin, h2, att_t, a2, lse2 = results[:15]
        if split:
            sq, sk, sv, so, cq, ck, cv, co, wg, wu, wd = results[15:]

        vocab = embed_table.shape[0]

        def block(by_block, j, axis=0):
            return lax.dynamic_index_in_dim(by_block, z ^ j, axis, keepdims=False)

        tgt_local = targets - z * vocab
        tgt_local = jnp.where((tgt_local >= 0) & (tgt_local < vocab), tgt_local, -1)
        tgt_blocks = tgt_local.reshape(4, ROWS)
        position = lax.rem(jnp.arange(4 * ROWS), TGT)
        live = position < jnp.repeat(target_len, TGT, total_repeat_length=4 * ROWS)
        live_blocks = live.astype(jnp.int32).reshape(4, ROWS)
        fin_1, fin_2, fin_3 = (swap(fin, "tensor", 4, j) for j in (1, 2, 3))
        fin_a = jnp.concatenate([fin_2, fin_3], 0).T
        fin_b = jnp.concatenate([fin, fin_1], 0).T

        def columns(by_block, order):
            return jnp.concatenate([block(by_block, j) for j in order], 0)[None, :]

        tgt_a, tgt_b = columns(tgt_blocks, (2, 3)), columns(tgt_blocks, (0, 1))
        logits_b, stats_b = head_logits(fin_b, embed_table, tgt_b)
        logits_a, stats_a = head_logits(fin_a, embed_table, tgt_a)
        stats = [stats_b[:, :ROWS], stats_b[:, ROWS:], stats_a[:, :ROWS], stats_a[:, ROWS:]]
        stats = jnp.stack(stats, 0)
        stats = jnp.stack([block(stats, j) for j in range(4)], 0)
        others = [stats] + [swap(stats, "tensor", 4, j) for j in (1, 2, 3)]

        def over_z(values, op):
            return op(op(values[0], values[1]), op(values[2], values[3]))

        top = over_z([s[:, 0] for s in others], jnp.maximum)
        total = over_z([s[:, 1] * jnp.exp(s[:, 0] - top) for s in others], jnp.add)
        picked = over_z([s[:, 2] for s in others], jnp.add)
        g_lse = top + jnp.log(total)
        token_loss = jnp.where(live, (g_lse - picked).reshape(-1), 0.0)
        g_a, gf_a = head_grads(
            logits_a, embed_table, tgt_a, columns(g_lse, (2, 3)), columns(live_blocks, (2, 3)), BF16
        )
        gf_2 = swap(gf_a[:ROWS], "tensor", 4, 2)
        g_b, gf_b = head_grads(
            logits_b, embed_table, tgt_b, columns(g_lse, (0, 1)), columns(live_blocks, (0, 1)), F32
        )
        g_b, gf_b, gf_2, gf_a = lax.optimization_barrier((g_b, gf_b, gf_2, gf_a))
        gf_3 = swap(gf_a[ROWS:], "tensor", 4, 3)
        gf_1 = swap(gf_b[ROWS:].astype(BF16), "tensor", 4, 1)

        def halves(flat):
            if not split:
                return flat[:HALF_D], flat[HALF_D:]
            flat = flat.reshape(4, 2, 96, -1)
            return tuple(
                lax.dynamic_index_in_dim(flat, i, 1, keepdims=False).reshape(HALF_D, -1)
                for i in (core, 1 - core)
            )

        reduction = Reduction if split else WideReduction
        xyz = jnp.stack([lax.rem(dp // 2, 2), dp // 4, z]).astype(jnp.int32)
        e_mine, e_send = table_grads(halves(fin_a), halves(fin_b), g_a, g_b)
        if not split:
            e_mine, e_send = e_mine[:, :vocab], e_send[:, :vocab]
        e_mine, e_send, gf_1, gf_3 = lax.optimization_barrier((e_mine, e_send, gf_1, gf_3))
        e_sum = reduction(xyz, e_mine, e_send)

        half_t = (HALF_D, ROWS)
        ff_mine, ff_send, res2, rows2, gatt, dots, gg_a = local_call(
            functools.partial(ff_backward, split),
            [whole((HALF_D, 3 * FF), F32), whole((HALF_D, 3 * FF), BF16), whole((ROWS, D), F32)]
            + [whole((ROWS, D), BF16)] * 2
            + [whole((16, ROWS), F32), whole((2, D), F32)],
            [vm((D, ROWS), BF16)] + [vm(half_t, BF16)] * 4
            + [vm((ROWS, D), F32)],
            10e9,
            scal, after(gf_b[:ROWS], e_send), gf_1, gf_2, gf_3, block_out, h2,
            gain_ff, gain_final, wg, wu, wd, co, att_t,
        )
        ff_sum = reduction(xyz, ff_mine, ff_send)
        gatt_other, dots_other = pair_swap(gatt), pair_swap(dots)
        sent = e_sum.first()
        dk2, dv2, dq_own, dq_send = local_call(
            cross_backward,
            [whole((KEYS, D), BF16)] * 2 + [whole((D, ROWS), F32), whole((D, ROWS), BF16)],
            [vm(pair, BF16), vm((16, TGT), F32), vm((D, TGT), F32)],
            20e9,
            scal, q2, k2, v2, lse2, after(gatt, *sent), gatt_other, dots, dots_other,
        )
        dq_other = pair_swap(dq_send)
        dk2, *e_sum.gots = lax.optimization_barrier((dk2, *e_sum.gots))
        sent = ff_sum.first()
        grad_source, kv_mine, kv_send = local_call(
            functools.partial(source_backward, split),
            [whole((KEYS, D), F32), whole((HALF_D, 2 * D), F32), whole((HALF_D, 2 * D), BF16)],
            [vm((D, KEYS), BF16)] + [vm((HALF_D, KEYS), BF16)] * 2,
            5e9,
            scal, after(dk2, *sent), dv2, source, ck, cv,
        )
        sent = e_sum.second()
        c_mine, c_send, res1, rows1, gatt1, gg_b = local_call(
            functools.partial(query_backward, split),
            [whole((HALF_D, 4 * D), F32), whole((HALF_D, 4 * D), BF16), whole((ROWS, D), F32)]
            + [whole((ROWS, D), BF16)] * 2 + [whole((1, D), F32)],
            [vm((D, ROWS), BF16)] + [vm(half_t, BF16)] * 2,
            2e9,
            scal, after(dq_own, *sent), dq_other, h1, gain_cross, cq, res2, rows2, a2, so,
            kv_mine, kv_send,
        )
        c_sum = reduction(xyz, c_mine, c_send)
        gatt1_other = pair_swap(gatt1)
        sent = ff_sum.second() + c_sum.first()
        s_mine, s_send, grad_block_in, gg_c = local_call(
            functools.partial(self_backward, split),
            [whole((HALF_D, 4 * D), F32), whole((HALF_D, 4 * D), BF16)]
            + [whole((ROWS, D), F32), whole((1, D), F32)],
            [vm(pair, BF16), vm((D, TGT), F32), vm(pair, BF16), vm(pair, BF16)]
            + [vm((D, ROWS), BF16)] + [vm(half_t, BF16)] * 2,
            12e9,
            scal, q1, k1, v1, lse1, after(gatt1, *sent), gatt1_other, block_in, gain_self, sq, sk, sv,
            res1, rows1, a1,
        )
        flying = (*e_sum.gots, *ff_sum.gots, *c_sum.gots)
        s_mine, s_send, *flying = lax.optimization_barrier((s_mine, s_send, *flying))
        if split:
            e_sum.gots, ff_sum.gots, c_sum.gots = flying[:2], flying[2:4], flying[4:]
        s_sum = reduction(xyz, s_mine, s_send)
        gains = jnp.concatenate([gg_a, gg_b, gg_c], 0)
        if split:
            for axis, size, bit in (("dp", 8, 1), ("tensor", 4, 1), ("dp", 8, 2), ("tensor", 4, 2), ("dp", 8, 4)):
                gains = gains + swap(gains, axis, size, bit)
        else:
            gains = lax.psum(gains, ("dp", "tensor"))
        sent = s_sum.first()
        sent = sent + ff_sum.third() + c_sum.second()
        grad_embed = e_sum.table(vocab)
        s_sum.second()
        c_sum.third()
        ff_grads = ff_sum.last(3, (2,))
        s_sum.third()
        c_grads = c_sum.last(4, (3,))
        s_grads = s_sum.last(4, (3,))

        return (
            block_out,
            token_loss,
            grad_block_in,
            grad_source,
            gains[3],
            gains[2],
            gains[1],
            gains[0],
            *s_grads,
            *c_grads,
            *ff_grads,
            grad_embed,
        )

    return on_device


def solution(mesh):
    rows = P(("dp", "tensor"), None)
    wide, tall = P(None, "tensor"), P("tensor", None)
    in_specs = (rows, rows) + (P("dp"),) * 3 + (P(),) * 4
    in_specs += (wide, wide, wide, tall) * 2 + (wide, wide, tall, tall)
    g_in, g_out = P("dp", "tensor"), P("tensor", "dp")
    out_specs = (rows, P("dp"), rows, rows) + (P(),) * 4
    out_specs += (g_in, g_in, g_in, g_out) * 2 + (g_in, g_in, g_out, g_out)
    return jax.shard_map(
        make(mesh), mesh=mesh, in_specs=in_specs, out_specs=out_specs, check_vma=False
    )
```

```python
import functools
import math

import jax
import jax.numpy as jnp
from jax import lax
from jax.sharding import PartitionSpec as P
from jax.experimental import pallas as pl
from jax.experimental.pallas import tpu as pltpu

D = 768
HDIM = 64
NHEAD = D // HDIM
PAIRS = NHEAD // 2
FF = 2048
TGT = 512
ROWS = 256
KEYS = 1024
CHUNK = 256
HALF_D = D // 2
VTILE = 512
HTILE = 1024
F32 = jnp.float32
BF16 = jnp.bfloat16
MESH_ID = pl.DeviceIdType.MESH
VMEM_LIMIT = 56 * 2**20
FUSED_LIMIT = 62 * 2**20
NEG = -1000000000.0
SCALE = HDIM ** (-0.5)
EPS = 1e-06


def dot_nt(left, right):
    return lax.dot_general(left, right, (((1,), (1,)), ((), ())), preferred_element_type=F32)


def dot_nn(left, right):
    return lax.dot_general(left, right, (((1,), (0,)), ((), ())), preferred_element_type=F32)


def swap(value, axis_name, size, bit):
    return lax.ppermute(value, axis_name, [(i, i ^ bit) for i in range(size)])


class Gather:
    def __init__(self, links, refs, used):
        self.links, self.refs, self.used = links, refs, used
        self.last = []

    def piece(self, ref, shard, owner, part=None):
        if len(ref.shape) == 2:
            rows = ref.shape[0] // 32
            base = shard * 8 * rows + owner * rows
        else:
            rows = ref.shape[1] // 8
            base = shard * 2 * rows + lax.rem(owner, 2) * rows
        start, count = (0, rows) if part is None else (part * rows // 2, rows // 2)
        where = pl.ds(pl.multiple_of(base + start, 16), count)
        return ref.at[where] if len(ref.shape) == 2 else ref.at[owner // 2, where]

    def send(self, part, peer):
        send_sem, recv_sem = self.links["sems"]
        sem = self.used[0]
        self.used[0] += 1
        copy = pltpu.make_async_remote_copy(
            src_ref=part,
            dst_ref=part,
            send_sem=send_sem.at[sem],
            recv_sem=recv_sem.at[sem],
            device_id={"dp": peer[0], "tensor": peer[1]},
            device_id_type=MESH_ID,
        )
        copy.start()
        return copy

    def along_z(self):
        links = self.links
        self.z_copies = [
            self.send(self.piece(ref, links["z"], links["dp"]), peer)
            for ref in self.refs
            for peer in links["z_peers"]
        ]

    def along_xy(self):
        links = self.links
        for copy in self.z_copies:
            copy.wait()
        self.x_copies, self.y_copies = [], []
        for ref in self.refs:
            for _, shard in links["z_peers"]:
                part = self.piece(ref, shard, links["dp"])
                self.x_copies.append(self.send(part, links["x"]))
                self.y_copies.append(self.send(part, links["y"]))
                self.last.append(self.send(part, links["core"]))

    def diagonal(self):
        links = self.links
        self.d_copies = []
        at = 0
        for ref in self.refs:
            for _, shard in links["z_peers"]:
                self.x_copies[at].wait()
                self.d_copies.append(self.send(self.piece(ref, shard, links["x"][0], 0), links["y"]))
                self.y_copies[at].wait()
                self.d_copies.append(self.send(self.piece(ref, shard, links["y"][0], 1), links["x"]))
                for owner in (links["x"][0], links["y"][0]):
                    self.last.append(self.send(self.piece(ref, shard, owner), links["core"]))
                at += 1

    def finish(self):
        links = self.links
        for copy in self.d_copies:
            copy.wait()
        for ref in self.refs:
            for _, shard in links["z_peers"]:
                self.last.append(self.send(self.piece(ref, shard, links["xy"]), links["core"]))
        for copy in self.last:
            copy.wait()


def gather_wide(shard, dp_size):
    rows = shard.shape[0] // dp_size
    part = lax.dynamic_slice_in_dim(shard, lax.axis_index("dp") * rows, rows, 0)
    return lax.all_gather(part, ("tensor", "dp"), axis=0, tiled=True)


def block_rows(index):
    return pl.ds(pl.multiple_of(index * 96, 96), 96)


class Comm:
    def __init__(self, send_sem, recv_sem):
        self.send_sem, self.recv_sem, self.used = send_sem, recv_sem, 0
        dp, z = lax.axis_index("dp"), lax.axis_index("tensor")
        self.z = z
        self.c, self.x, self.y = lax.rem(dp, 2), lax.rem(dp // 2, 2), dp // 4
        low, high = lax.rem(z, 2), z // 2
        self.core_peer = (dp + 1 - 2 * self.c, z)
        self.x_peer = (dp + 2 - 4 * self.x, z)
        self.y_peer = (dp + 4 - 8 * self.y, z)
        self.z_shards = (high * 2 + 1 - low, (1 - high) * 2 + low, (1 - high) * 2 + 1 - low)
        self.z_peers = [(dp, shard) for shard in self.z_shards]

    def barrier(self):
        barrier = pltpu.get_barrier_semaphore()
        peers = [self.core_peer, self.x_peer, self.y_peer] + self.z_peers
        for peer in peers:
            pl.semaphore_signal(
                barrier, inc=1, device_id={"dp": peer[0], "tensor": peer[1]}, device_id_type=MESH_ID
            )
        pl.semaphore_wait(barrier, len(peers))

    def copy(self, src, dst, peer, index):
        return pltpu.make_async_remote_copy(
            src_ref=src,
            dst_ref=dst,
            send_sem=self.send_sem.at[index],
            recv_sem=self.recv_sem.at[index],
            device_id={"dp": peer[0], "tensor": peer[1]},
            device_id_type=MESH_ID,
        )

    def reserve(self, count):
        self.used += count
        return self.used - count

    def send(self, src, dst, peer):
        copy = self.copy(src, dst, peer, self.reserve(1))
        copy.start()
        return copy


def fold_one(comm, mine, got, keep, send, is_right):
    for other in range(2):
        rows = slice(other * 96, (other + 1) * 96)
        along_x, along_y = 2 * other + comm.x, 2 * comm.y + other
        stay = along_x * (1 - is_right) + along_y * is_right
        along_x, along_y = 2 * other + 1 - comm.x, 2 * (1 - comm.y) + other
        leave = along_x * (1 - is_right) + along_y * is_right
        stay, leave = block_rows(stay), block_rows(leave)
        keep[rows, :] = mine[stay, :] + got[stay, :].astype(F32)
        send[rows, :] = (mine[leave, :] + got[leave, :].astype(F32)).astype(BF16)


def fold_two(comm, mine, got, keep, send):
    for side, bit in enumerate((comm.y, comm.x)):
        stay, leave = block_rows(bit), block_rows(1 - bit)
        keep[side] = mine[side, stay, :] + got[side, stay, :].astype(F32)
        send[side] = (mine[side, leave, :] + got[side, leave, :].astype(F32)).astype(BF16)


class Flow:
    def __init__(self, comm, one, two, three):
        self.comm, self.one, self.two, self.three = comm, one, two, three
        self.copies = []

    def wait(self):
        for copy in self.copies:
            copy.wait()

    def from_core(self, mine, send, got):
        comm = self.comm
        self.copies = [comm.send(send, got, comm.core_peer)]
        self.mine, self.got = mine, got

    def fold_first(self):
        self.wait()
        keep, send, _ = self.one
        width = keep.shape[2]
        for side in range(2):
            cols = pl.ds(side * width, width)
            fold_one(
                self.comm, self.mine.at[:, cols], self.got.at[:, cols], keep.at[side], send.at[side], side
            )

    def send_first(self):
        comm = self.comm
        _, send, recv = self.one
        self.copies = [
            comm.send(send.at[0], recv.at[0], comm.x_peer),
            comm.send(send.at[1], recv.at[1], comm.y_peer),
        ]

    def fold_second(self):
        self.wait()
        fold_two(self.comm, self.one[0], self.one[2], self.two[0], self.two[1])

    def send_second(self):
        comm = self.comm
        _, send, recv = self.two
        self.copies = [
            comm.send(send.at[0], recv.at[0], comm.y_peer),
            comm.send(send.at[1], recv.at[1], comm.x_peer),
        ]

    def fold_third(self, shard_ref):
        self.wait()
        comm = self.comm
        (keep, _, recv), (keep3, send3, recv3) = self.two, self.three
        width = keep3.shape[1]
        for side in range(2):
            total = keep[side] + recv[side].astype(F32)
            shard_ref[2 * side, :, :width] = total[:, :width]
            shard_ref[2 * side + 1, :, :width] = total[:, width:]
        keep3[...] = shard_ref[comm.z, :, :width]
        self.copies = []
        for j, shard in enumerate(comm.z_shards):
            send3[j] = shard_ref[shard, :, :width].astype(BF16)
            self.copies.append(comm.send(send3.at[j], recv3.at[j], comm.z_peers[j]))

    def finish(self, outs, flipped, turn_ref):
        self.wait()
        keep, _, recv = self.three
        width = keep.shape[1] // len(outs)
        for m, out in enumerate(outs):
            cols = slice(m * width, (m + 1) * width)
            part = keep[:, cols] + recv[0, :, cols].astype(F32)
            part = part + (recv[1, :, cols].astype(F32) + recv[2, :, cols].astype(F32))
            if m == flipped:
                turn_ref[:, :width] = part
                out[...] = turn_ref[:, :width].T
            else:
                out[...] = part


class WideReduction:
    def __init__(self, z, mine, send):
        both = jnp.concatenate([mine, send.astype(F32)], 0)
        self.part = lax.psum_scatter(both, "dp", scatter_dimension=0, tiled=True)

    def last(self, count, flips):
        rows = self.part.shape[0]
        by_z = self.part.reshape(rows, 4, -1)
        total = lax.psum_scatter(by_z, "tensor", scatter_dimension=1, tiled=True)[:, 0]
        parts = jnp.split(total, count, axis=1)
        return [p.T if m in flips else p for m, p in enumerate(parts)]

    def table(self, vocab):
        return self.part.T


def rms_scale(values):
    return lax.rsqrt(jnp.mean(values * values, axis=-1, keepdims=True) + EPS)


def spots(scal, split):
    if split:
        half, core = lax.rem(lax.axis_index("tensor"), 2), lax.rem(lax.axis_index("dp"), 2)
    else:
        half, core = scal[0], scal[3]
    return half, scal[1], scal[2] - half * KEYS, core


def norm_back(values, inv_scale, gain, grad_out):
    weighted = gain * grad_out
    grad_gain = jnp.sum(grad_out * values * inv_scale, axis=0, keepdims=True)
    grad_values = inv_scale * weighted - values * inv_scale * inv_scale * inv_scale * jnp.mean(
        weighted * values, axis=-1, keepdims=True
    )
    return grad_values, grad_gain


def flip(value):
    return value.astype(F32).T


def lane_half(rows, which):
    lane = lax.broadcasted_iota(jnp.int32, (rows, 2 * HDIM), 1)
    return (lane >= HDIM) if which else (lane < HDIM)


def only(value, which):
    return jnp.where(lane_half(value.shape[0], which), value, jnp.zeros_like(value))


def split_rows(flat_ref, mine_ref, send_ref, core, split):
    for block in range(4):
        if split:
            first = pl.multiple_of((2 * block + core) * 96, 96)
            second = pl.multiple_of((2 * block + 1 - core) * 96, 96)
        else:
            first, second = block * 96, HALF_D + block * 96
        mine_ref[block * 96 : (block + 1) * 96, :] = flat_ref[pl.ds(first, 96), :]
        send_ref[block * 96 : (block + 1) * 96, :] = flat_ref[pl.ds(second, 96), :]


def by_shard(left_ref, rights, out_ref, first, per_shard):
    width = 192 * len(rights)
    for z in range(4):
        part = [right[:, z * 192 : (z + 1) * 192] for right in rights]
        right = jnp.concatenate(part, axis=1) if len(part) > 1 else part[0]
        start = z * per_shard + first
        out_ref[:, start : start + width] = dot_nn(left_ref[...], right).astype(out_ref.dtype)


def whole(shape, dtype):
    return jax.ShapeDtypeStruct(shape, dtype)


def local_call(body, outs, scratch, flops, *args):
    smem = pl.BlockSpec(memory_space=pltpu.SMEM)
    vmem = pl.BlockSpec(memory_space=pltpu.VMEM)
    bytes_all = sum(a.size * a.dtype.itemsize for a in args)
    bytes_all += sum(o.size * jnp.dtype(o.dtype).itemsize for o in outs)
    held = sum(math.prod(s.shape) * jnp.dtype(s.dtype).itemsize for s in scratch)
    return pl.pallas_call(
        body,
        out_shape=outs,
        in_specs=[smem] + [vmem] * (len(args) - 1),
        out_specs=[vmem] * len(outs),
        scratch_shapes=scratch,
        cost_estimate=pl.CostEstimate(
            flops=int(flops), bytes_accessed=int(bytes_all), transcendentals=0
        ),
        compiler_params=pltpu.CompilerParams(
            vmem_limit_bytes=min(VMEM_LIMIT, int(bytes_all + held + 16 * 2**20))
        ),
    )(*args)


def forward_kernel(split, *refs):
    (scal, x_own, source, gain_self, gain_cross, gain_ff, gain_final), refs = refs[:7], refs[7:]
    shards, refs = refs[: 11 if split else 5], refs[11 if split else 5 :]
    (q1, k1, v1, lse1, att1, h1_out, q2, k2, v2), refs = refs[:9], refs[9:]
    (out_ref, fin_ref, h2_ref, att_t_ref, att2, lse2), refs = refs[:6], refs[6:]
    if split:
        copies_out, refs = refs[:11], refs[11:]
        (ws, wc, wg, wu, wd), refs = refs[:5], refs[5:]
    else:
        ws, wc, wg, wu, wd = shards
    (x_other, x_ref, n_ref, vt_ref, ot_ref, s_ref, o_send, o_other, lse_own, lse_other, mix_ref), refs = (
        refs[:11],
        refs[11:],
    )
    pair_send, pair_recv = refs[:2]
    dp = lax.axis_index("dp")
    z = lax.axis_index("tensor")
    low, high = lax.rem(z, 2), z // 2
    half, live, live_src = low, scal[1], scal[2] - low * KEYS
    z_peers = [(dp, high * 2 + 1 - low)]
    peers = z_peers
    if split:
        z_peers = z_peers + [(dp, (1 - high) * 2 + low), (dp, (1 - high) * 2 + 1 - low)]
        x_peer = dp + 2 - 4 * lax.rem(dp // 2, 2)
        y_peer = dp + 4 - 8 * (dp // 4)
        links = dict(
            dp=dp,
            z=z,
            z_peers=z_peers,
            x=(x_peer, z),
            y=(y_peer, z),
            xy=x_peer + y_peer - dp,
            core=(dp + 1 - 2 * lax.rem(dp, 2), z),
            sems=refs[2:4],
        )
        out_sem = refs[4]
        peers = z_peers + [links["x"], links["y"], links["core"]]
    barrier = pltpu.get_barrier_semaphore()
    for peer in peers:
        pl.semaphore_signal(
            barrier, inc=1, device_id={"dp": peer[0], "tensor": peer[1]}, device_id_type=MESH_ID
        )

    def exchange(index, src, dst):
        copy = pltpu.make_async_remote_copy(
            src_ref=src,
            dst_ref=dst,
            send_sem=pair_send.at[index],
            recv_sem=pair_recv.at[index],
            device_id={"dp": z_peers[0][0], "tensor": z_peers[0][1]},
            device_id_type=MESH_ID,
        )
        copy.start()
        return copy

    leaving = []
    if split:
        used = [0]
        groups = [Gather(links, refs_of, used) for refs_of in ([ws], [wc], [wg], [wu], [wd])]
        of_self, of_cross, of_gate, of_up, of_down = groups
        hid, fhid = D // 4, FF // 4

        def place_block(target, first):
            rows = pl.ds(pl.multiple_of(z * hid, 16), hid)
            for m in range(3):
                target[m, rows, :] = flip(shards[first + m][...]).astype(BF16)
            target[3, rows, :] = shards[first + 3][...]

        def place_wide(target, shard, flipped):
            rows = pl.ds(pl.multiple_of(z * fhid, 16), fhid)
            target[rows, :] = flip(shard[...]).astype(BF16) if flipped else shard[...]

        def leave(first, parts):
            for i, part in enumerate(parts):
                copy = pltpu.make_async_copy(part, copies_out[first + i], out_sem.at[first + i])
                copy.start()
                leaving.append(copy)

        place_block(ws, 0)
        pl.semaphore_wait(barrier, len(peers))
        of_self.along_z()
    else:
        pl.semaphore_wait(barrier, len(peers))
    x_copy = exchange(0, x_own, x_other)
    if split:
        place_block(wc, 4)
        place_wide(wg, shards[8], True)
        place_wide(wu, shards[9], True)
        place_wide(wd, shards[10], False)
        of_self.along_xy()
        of_cross.along_z()
        of_self.diagonal()
        of_cross.along_xy()
        of_gate.along_z()
    x_copy.wait()
    own = pl.multiple_of(half * ROWS, ROWS)
    other = pl.multiple_of((1 - half) * ROWS, ROWS)
    x_ref[pl.ds(own, ROWS), :] = x_own[...].astype(F32)
    x_ref[pl.ds(other, ROWS), :] = x_other[...].astype(F32)
    lse1[...] = jnp.zeros_like(lse1)
    lse_own[...] = jnp.zeros_like(lse_own)
    if split:
        of_self.finish()
        leave(0, [ws.at[m] for m in range(4)])
    for i in range(2):
        rows = slice(i * ROWS, (i + 1) * ROWS)
        x = x_ref[rows, :]
        n = (x * rms_scale(x) * gain_self[...]).astype(BF16)
        n_ref[rows, :] = n
        q1[rows, :] = dot_nt(n, ws[0]).astype(BF16)
        k1[rows, :] = dot_nt(n, ws[1]).astype(BF16)
        v1[rows, :] = dot_nt(n, ws[2]).astype(BF16)
    vt_ref[:, :TGT] = dot_nt(ws[2], n_ref[...]).astype(BF16)
    if split:
        of_gate.along_xy()
        of_up.along_z()
    key = lax.broadcasted_iota(jnp.int32, (TGT, TGT), 0)
    query = lax.broadcasted_iota(jnp.int32, (TGT, TGT), 1)
    seen = (key <= query) & (key < live)

    def self_pairs(first, last):
        @pl.loop(first, last)
        def _(pair):
            lanes = pl.ds(pl.multiple_of(pair * 128, 128), 128)
            q_pair, k_pair = q1[:, lanes], k1[:, lanes]
            for which in range(2):
                head = 2 * pair + which
                feats = pl.ds(pl.multiple_of(head * HDIM, HDIM), HDIM)
                scores = jnp.where(seen, dot_nt(k_pair, only(q_pair, which)) * SCALE, NEG)
                top = jnp.max(scores, axis=0, keepdims=True)
                probs = jnp.exp(scores - top)
                total = jnp.sum(probs, axis=0, keepdims=True)
                lse1[pl.ds(head, 1), :] = top + jnp.log(total)
                ot_ref[feats, :] = dot_nn(vt_ref[feats, :TGT], probs.astype(BF16)) / total

    self_pairs(0, PAIRS // 2)
    if split:
        of_cross.diagonal()
    self_pairs(PAIRS // 2, PAIRS)
    if split:
        of_up.along_xy()
        of_down.along_z()
        of_gate.diagonal()
    for i in range(2):
        rows = slice(i * ROWS, (i + 1) * ROWS)
        att = flip(ot_ref[:, rows]).astype(BF16)
        n_ref[rows, :] = att
        x_ref[rows, :] = x_ref[rows, :] + dot_nn(att, ws[3])
    att1[...] = n_ref[pl.ds(own, ROWS), :]
    h1_out[...] = x_ref[pl.ds(own, ROWS), :]
    if split:
        of_cross.finish()
        leave(4, [wc.at[m] for m in range(4)])
    for i in range(2):
        rows = slice(i * ROWS, (i + 1) * ROWS)
        h1 = x_ref[rows, :]
        n = (h1 * rms_scale(h1) * gain_cross[...]).astype(BF16)
        q2[rows, :] = dot_nt(n, wc[0]).astype(BF16)
    for i in range(KEYS // CHUNK):
        rows = slice(i * CHUNK, (i + 1) * CHUNK)
        src = source[rows, :]
        k2[rows, :] = dot_nt(src, wc[1]).astype(BF16)
        v2[rows, :] = dot_nt(src, wc[2]).astype(BF16)
        vt_ref[:, rows] = dot_nt(wc[2], src).astype(BF16)
    if split:
        of_down.along_xy()
        of_up.diagonal()
        of_gate.finish()
        leave(8, [wg])
    chunk_key = lax.broadcasted_iota(jnp.int32, (CHUNK, TGT), 0)

    def cross_pairs(first, last):
        @pl.loop(first, last)
        def _(pair):
            lanes = pl.ds(pl.multiple_of(pair * 128, 128), 128)
            q_pair = q2[:, lanes]
            for which in range(2):
                head = 2 * pair + which
                feats = pl.ds(pl.multiple_of(head * HDIM, HDIM), HDIM)
                q_one = only(q_pair, which)
                top = jnp.full((1, TGT), 2 * NEG, F32)
                for i in range(KEYS // CHUNK):
                    rows = slice(i * CHUNK, (i + 1) * CHUNK)
                    scores = dot_nt(k2[rows, lanes], q_one) * SCALE
                    scores = jnp.where(chunk_key < live_src - i * CHUNK, scores, NEG)
                    s_ref[rows, :] = scores
                    top = jnp.maximum(top, jnp.max(scores, axis=0, keepdims=True))
                total = jnp.zeros((1, TGT), F32)
                out = jnp.zeros((HDIM, TGT), F32)
                for i in range(KEYS // CHUNK):
                    rows = slice(i * CHUNK, (i + 1) * CHUNK)
                    probs = jnp.exp(s_ref[rows, :] - top)
                    total = total + jnp.sum(probs, axis=0, keepdims=True)
                    out = out + dot_nn(vt_ref[feats, rows], probs.astype(BF16))
                lse_own[pl.ds(head, 1), :] = top + jnp.log(total)
                ot_ref[feats, :] = out / total

    cross_pairs(0, PAIRS // 2)
    o_send[: D // 2, :] = ot_ref[: D // 2, pl.ds(other, ROWS)].astype(BF16)
    pair_copies = [exchange(1, o_send.at[: D // 2], o_other.at[: D // 2])]
    if split:
        of_down.diagonal()
        of_up.finish()
        leave(9, [wu])
    cross_pairs(PAIRS // 2, PAIRS)
    o_send[D // 2 :, :] = ot_ref[D // 2 :, pl.ds(other, ROWS)].astype(BF16)
    pair_copies.append(exchange(2, o_send.at[D // 2 :], o_other.at[D // 2 :]))
    pair_copies.append(exchange(3, lse_own, lse_other))
    if split:
        of_down.finish()
        leave(10, [wd])
    for copy in pair_copies:
        copy.wait()

    first, second = lse_own[...], lse_other[...]
    top = jnp.maximum(first, second)
    lse2[...] = top + jnp.log(jnp.exp(first - top) + jnp.exp(second - top))
    lse = lse2[:, pl.ds(own, ROWS)]
    w_first = jnp.exp(lse_own[:, pl.ds(own, ROWS)] - lse)
    w_second = jnp.exp(lse_other[:, pl.ds(own, ROWS)] - lse)
    for head in range(NHEAD):
        feats = slice(head * HDIM, (head + 1) * HDIM)
        att_t_ref[feats, :] = (
            ot_ref[feats, pl.ds(own, ROWS)] * w_first[head : head + 1, :]
            + o_other[feats, :].astype(F32) * w_second[head : head + 1, :]
        )
    att = flip(att_t_ref[...]).astype(BF16)
    att2[...] = att
    h2 = h1_out[...] + dot_nn(att, wc[3])
    h2_ref[...] = h2
    n3 = (h2 * rms_scale(h2) * gain_ff[...]).astype(BF16)

    @pl.loop(0, FF // 512)
    def _(i):
        rows = pl.ds(pl.multiple_of(i * 512, 512), 512)
        gate = dot_nt(n3, wg[rows, :])
        up = dot_nt(n3, wu[rows, :])
        mix_ref[:, rows] = (jax.nn.gelu(gate, approximate=True) * up).astype(BF16)

    out = h2 + dot_nn(mix_ref[...], wd[...])
    out_ref[...] = out
    fin_ref[...] = (out * rms_scale(out) * gain_final[...] * D ** (-0.5)).astype(BF16)
    for copy in leaving:
        copy.wait()


def forward(split, scal, x_own, source, gains, weights):
    pair = (TGT, D)
    block = (ROWS, D)
    outs = [whole(pair, BF16)] * 3 + [whole((16, TGT), F32), whole(block, BF16), whole(block, F32)]
    outs += [whole(pair, BF16)] + [whole((KEYS, D), BF16)] * 2
    outs += [whole(block, F32), whole(block, BF16), whole(block, F32), whole((D, ROWS), F32)]
    outs += [whole(block, BF16), whole((16, TGT), F32)]
    vmem = pl.BlockSpec(memory_space=pltpu.VMEM)
    out_specs = [vmem] * len(outs)
    scratch = []
    if split:
        outs += [whole((D, D), BF16)] * 8 + [whole((FF, D), BF16)] * 3
        out_specs += [pl.BlockSpec(memory_space=pl.ANY)] * 11
        scratch += [pltpu.VMEM((4, D, D), BF16)] * 2 + [pltpu.VMEM((FF, D), BF16)] * 3
    scratch += [
        pltpu.VMEM(block, BF16),
        pltpu.VMEM(pair, F32),
        pltpu.VMEM(pair, BF16),
        pltpu.VMEM((D, KEYS), BF16),
        pltpu.VMEM((D, TGT), F32),
        pltpu.VMEM((KEYS, TGT), F32),
        pltpu.VMEM((D, ROWS), BF16),
        pltpu.VMEM((D, ROWS), BF16),
        pltpu.VMEM((16, TGT), F32),
        pltpu.VMEM((16, TGT), F32),
        pltpu.VMEM((ROWS, FF), BF16),
        pltpu.SemaphoreType.DMA((4,)),
        pltpu.SemaphoreType.DMA((4,)),
    ]
    if split:
        scratch += [pltpu.SemaphoreType.DMA((27 * 5,))] * 2 + [pltpu.SemaphoreType.DMA((11,))]
    args = (scal, x_own, source, *gains, *weights)
    return pl.pallas_call(
        functools.partial(forward_kernel, split),
        out_shape=outs,
        in_specs=[pl.BlockSpec(memory_space=pltpu.SMEM)] + [vmem] * (len(args) - 1),
        out_specs=out_specs,
        scratch_shapes=scratch,
        cost_estimate=pl.CostEstimate(
            flops=int(80e9), bytes_accessed=int(6e7), transcendentals=0
        ),
        compiler_params=pltpu.CompilerParams(
            collective_id=0, has_side_effects=True, vmem_limit_bytes=VMEM_LIMIT
        ),
    )(*args)


def ff_backward(
    split, scal, gf_own, gf_1, gf_2, gf_3, block_out, h2_in, gain_ff, gain_final, wg, wu, wd,
    w_co, att_t, mine_ref, send_ref, res_ref, rows_ref, gatt_ref, dot_ref, gg_ref,
    flat_ref, flat_2, nm_ref, ns_ref, gm_ref, gs_ref, gn_ref,
):
    core = scal[3]
    grad = gf_own[...] + gf_1[...].astype(F32)
    grad = grad + (gf_2[...].astype(F32) + gf_3[...].astype(F32))
    out = block_out[...]
    res, gg_final = norm_back(out, rms_scale(out), gain_final[...], grad * D ** (-0.5))
    gg_ref[0:1, :] = gg_final
    rows_b = res.astype(BF16)
    res_ref[...] = res
    rows_ref[...] = rows_b
    flat_ref[...] = flip(rows_ref[...]).astype(BF16)
    split_rows(flat_ref, gm_ref, gs_ref, core, split)
    h2 = h2_in[...]
    scale3 = rms_scale(h2)
    n3 = (h2 * scale3 * gain_ff[...]).astype(BF16)
    rows_ref[...] = n3
    flat_2[...] = flip(rows_ref[...]).astype(BF16)
    split_rows(flat_2, nm_ref, ns_ref, core, split)
    gn_ref[...] = jnp.zeros_like(gn_ref)
    const = (2.0 / 3.141592653589793) ** 0.5

    @pl.loop(0, FF // 512)
    def _(i):
        start = pl.multiple_of(i * 512, 512)
        rows = pl.ds(start, 512)
        gate = dot_nt(n3, wg[rows, :])
        up = dot_nt(n3, wu[rows, :])
        square = gate * gate
        tanh = jnp.tanh(const * (gate + 0.044715 * gate * square))
        gelu = 0.5 * gate * (1.0 + tanh)
        slope = 0.5 * (1.0 + tanh) + 0.5 * gate * (1.0 - tanh * tanh) * const * (
            1.0 + 3.0 * 0.044715 * square
        )
        grad_mixed = dot_nt(rows_b, wd[rows, :])
        g_gate = (grad_mixed * up * slope).astype(BF16)
        g_up = (grad_mixed * gelu).astype(BF16)
        mixed = (gelu * up).astype(BF16)
        gn_ref[...] += dot_nn(g_gate, wg[rows, :]) + dot_nn(g_up, wu[rows, :])
        for m, (mine, send, right) in enumerate(
            ((nm_ref, ns_ref, g_gate), (nm_ref, ns_ref, g_up), (gm_ref, gs_ref, mixed))
        ):
            cols = pl.ds(pl.multiple_of(3 * start + m * 512, 512), 512)
            mine_ref[:, cols] = dot_nn(mine[...], right)
            send_ref[:, cols] = dot_nn(send[...], right).astype(BF16)

    step, gg_ff = norm_back(h2, scale3, gain_ff[...], gn_ref[...])
    gg_ref[1:2, :] = gg_ff
    res = res_ref[...] + step
    res_ref[...] = res
    rows_b = res.astype(BF16)
    rows_ref[...] = rows_b
    gatt_ref[...] = dot_nt(rows_b, w_co[...]).astype(BF16)
    gatt_t = dot_nt(w_co[...], rows_b).astype(BF16).astype(F32)
    dot_ref[...] = jnp.zeros_like(dot_ref)
    for head in range(NHEAD):
        feats = slice(head * HDIM, (head + 1) * HDIM)
        dot_ref[head : head + 1, :] = jnp.sum(gatt_t[feats, :] * att_t[feats, :], 0, keepdims=True)


def both_halves(half, own, other, target):
    target[pl.ds(pl.multiple_of(half * ROWS, ROWS), ROWS), :] = own[...]
    target[pl.ds(pl.multiple_of((1 - half) * ROWS, ROWS), ROWS), :] = other[...]


def cross_backward(
    split, scal, q2, k2, v2, lse, g_own, g_other, dot_own, dot_other,
    dk_ref, dv_ref, own_out, send_out, g_ref, dot_ref, dq_ref,
):
    half, _, live, _ = spots(scal, split)
    own = pl.multiple_of(half * ROWS, ROWS)
    other = pl.multiple_of((1 - half) * ROWS, ROWS)
    both_halves(half, g_own, g_other, g_ref)
    dot_ref[:, pl.ds(own, ROWS)] = dot_own[...]
    dot_ref[:, pl.ds(other, ROWS)] = dot_other[...]
    key = lax.broadcasted_iota(jnp.int32, (CHUNK, TGT), 0)

    @pl.loop(0, PAIRS)
    def _(pair):
        lanes = pl.ds(pl.multiple_of(pair * 128, 128), 128)
        q_pair, g_pair = q2[:, lanes], g_ref[:, lanes]
        for i in range(KEYS // CHUNK):
            rows = slice(i * CHUNK, (i + 1) * CHUNK)
            k_part, v_part = k2[rows, lanes], v2[rows, lanes]
            k_flip = flip(k_part).astype(BF16)
            grad_k = jnp.zeros((CHUNK, 128), F32)
            grad_v = jnp.zeros((CHUNK, 128), F32)
            for which in range(2):
                head = 2 * pair + which
                feats = pl.ds(pl.multiple_of(head * HDIM, HDIM), HDIM)
                q_one, g_one = only(q_pair, which), only(g_pair, which)
                scores = dot_nt(k_part, q_one) * SCALE
                scores = jnp.where(key < live - i * CHUNK, scores, NEG)
                probs = jnp.exp(scores - lse[pl.ds(head, 1), :])
                grad_p = dot_nt(v_part, g_one)
                grad_s = (probs * (grad_p - dot_ref[pl.ds(head, 1), :])).astype(BF16)
                grad_k = grad_k + dot_nn(grad_s, q_one)
                grad_v = grad_v + dot_nn(probs.astype(BF16), g_one)
                grad_q = dot_nn(k_flip[which * HDIM : (which + 1) * HDIM, :], grad_s)
                if i == 0:
                    dq_ref[feats, :] = grad_q
                else:
                    dq_ref[feats, :] += grad_q
            dk_ref[rows, lanes] = (grad_k * SCALE).astype(BF16)
            dv_ref[rows, lanes] = grad_v.astype(BF16)

    own_out[...] = dq_ref[:, pl.ds(own, ROWS)]
    send_out[...] = dq_ref[:, pl.ds(other, ROWS)].astype(BF16)


def source_backward(
    split, scal, dk, dv, source, w_ck, w_cv, gsrc_ref, mine_ref, send_ref, flat_ref, sm_ref, ss_ref
):
    for i in range(KEYS // CHUNK):
        rows = slice(i * CHUNK, (i + 1) * CHUNK)
        gsrc_ref[rows, :] = dot_nn(dk[rows, :], w_ck[...]) + dot_nn(dv[rows, :], w_cv[...])
        flat_ref[:, rows] = flip(source[rows, :]).astype(BF16)
    split_rows(flat_ref, sm_ref, ss_ref, spots(scal, split)[3], split)
    rights = (dk[...], dv[...])
    first, per_shard = (192, D) if split else (0, 384)
    by_shard(sm_ref, rights, mine_ref, first, per_shard)
    by_shard(ss_ref, rights, send_ref, first, per_shard)


def query_backward(
    split, scal, dq_own, dq_other, h1_in, gain_cross, w_cq, res_in, rows_in, att, w_so,
    kv_mine, kv_send, mine_ref, send_ref, res_ref, rows_ref, gatt_ref, gg_ref, flat_ref, flat_2, a_ref, b_ref, turn_ref,
):
    core = spots(scal, split)[3]
    turn_ref[...] = dq_own[...] + dq_other[...].astype(F32)
    dq = (turn_ref[...].T * SCALE).astype(BF16)
    h1 = h1_in[...]
    scale2 = rms_scale(h1)
    rows_ref[...] = (h1 * scale2 * gain_cross[...]).astype(BF16)
    flat_ref[...] = flip(rows_ref[...]).astype(BF16)
    split_rows(flat_ref, a_ref, b_ref, core, split)
    by_shard(a_ref, (dq,), mine_ref, 0, D)
    by_shard(b_ref, (dq,), send_ref, 0, D)
    step, gg = norm_back(h1, scale2, gain_cross[...], dot_nn(dq, w_cq[...]))
    gg_ref[...] = gg
    res = res_in[...] + step
    res_ref[...] = res
    rows_b = res.astype(BF16)
    rows_ref[...] = rows_b
    gatt_ref[...] = dot_nt(rows_b, w_so[...]).astype(BF16)
    flat_2[...] = flip(rows_in[...]).astype(BF16)
    split_rows(flat_2, a_ref, b_ref, core, split)
    by_shard(a_ref, (att[...],), mine_ref, 576, D)
    by_shard(b_ref, (att[...],), send_ref, 576, D)
    for z in range(0 if split else 4):
        cols = slice(z * D + 192, z * D + 576)
        mine_ref[:, cols] = kv_mine[:, z * 384 : (z + 1) * 384]
        send_ref[:, cols] = kv_send[:, z * 384 : (z + 1) * 384]


def self_backward(
    split, scal, q1, k1, v1, lse, g_own, g_other, x_own, gain_self, w_q, w_k, w_v, res_in, rows_in, att,
    mine_ref, send_ref, gin_ref, gg_ref,
    g_ref, dq_ref, dk_ref, dv_ref, flat_ref, flat_2, a_ref, b_ref,
):
    half, live, _, core = spots(scal, split)
    own = pl.multiple_of(half * ROWS, ROWS)
    both_halves(half, g_own, g_other, g_ref)
    key = lax.broadcasted_iota(jnp.int32, (TGT, TGT), 0)
    query = lax.broadcasted_iota(jnp.int32, (TGT, TGT), 1)
    seen = (key <= query) & (key < live)

    @pl.loop(0, PAIRS)
    def _(pair):
        lanes = pl.ds(pl.multiple_of(pair * 128, 128), 128)
        q_pair, g_pair = q1[:, lanes], g_ref[:, lanes]
        k_pair, v_pair = k1[:, lanes], v1[:, lanes]
        k_flip = flip(k_pair).astype(BF16)
        grad_k = jnp.zeros((TGT, 128), F32)
        grad_v = jnp.zeros((TGT, 128), F32)
        for which in range(2):
            head = 2 * pair + which
            feats = pl.ds(pl.multiple_of(head * HDIM, HDIM), HDIM)
            q_one, g_one = only(q_pair, which), only(g_pair, which)
            scores = jnp.where(seen, dot_nt(k_pair, q_one) * SCALE, NEG)
            probs = jnp.exp(scores - lse[pl.ds(head, 1), :])
            grad_p = dot_nt(v_pair, g_one)
            row_dot = jnp.sum(probs * grad_p, axis=0, keepdims=True)
            grad_s = (probs * (grad_p - row_dot)).astype(BF16)
            grad_k = grad_k + dot_nn(grad_s, q_one)
            grad_v = grad_v + dot_nn(probs.astype(BF16), g_one)
            dq_ref[feats, :] = dot_nn(k_flip[which * HDIM : (which + 1) * HDIM, :], grad_s)
        dk_ref[:, lanes] = (grad_k * SCALE).astype(BF16)
        dv_ref[:, lanes] = grad_v.astype(BF16)

    dq = (flip(dq_ref[:, pl.ds(own, ROWS)]) * SCALE).astype(BF16)
    dk = dk_ref[pl.ds(own, ROWS), :]
    dv = dv_ref[pl.ds(own, ROWS), :]
    x = x_own[...].astype(F32)
    scale1 = rms_scale(x)
    grad_n = dot_nn(dq, w_q[...]) + dot_nn(dk, w_k[...]) + dot_nn(dv, w_v[...])
    step, gg = norm_back(x, scale1, gain_self[...], grad_n)
    gg_ref[...] = gg
    gin_ref[...] = res_in[...] + step
    g_ref[:ROWS, :] = (x * scale1 * gain_self[...]).astype(BF16)
    flat_ref[...] = flip(g_ref[:ROWS, :]).astype(BF16)
    split_rows(flat_ref, a_ref, b_ref, core, split)
    by_shard(a_ref, (dq, dk, dv), mine_ref, 0, D)
    by_shard(b_ref, (dq, dk, dv), send_ref, 0, D)
    flat_2[...] = flip(rows_in[...]).astype(BF16)
    split_rows(flat_2, a_ref, b_ref, core, split)
    by_shard(a_ref, (att[...],), mine_ref, 576, D)
    by_shard(b_ref, (att[...],), send_ref, 576, D)


def table_ff_kernel(*refs):
    (scal, g_a, g_b, fm_a, fm_b, fs_a, fs_b, gf_a, gf_b, gf_2), refs = refs[:10], refs[10:]
    (block_out, h2_in, gain_ff, gain_final, wg, wu, wd, w_co, att_t), refs = refs[:9], refs[9:]
    (e_keep, e_send, f_keep, f_send, res_ref, rows_ref), refs = refs[:6], refs[6:]
    (gatt_ref, gatt_other, dot_ref, dot_other, gg_ref), refs = refs[:5], refs[5:]
    (ga_ring, gb_ring, w_ring, mine_ring, send_ring, got, e_keep1, e_send1, e_recv1), refs = (
        refs[:9],
        refs[9:],
    )
    (flat_ref, flat_2, nm_ref, ns_ref, gm_ref, gs_ref, gn_ref, gf_send, gf_recv), refs = refs[:9], refs[9:]
    send_sem, recv_sem, load_sem, w_sem = refs
    comm = Comm(send_sem, recv_sem)
    core = comm.c

    def load(step):
        tile = lax.rem(step, 2) * 4 + step // 2
        rows = pl.ds(pl.multiple_of(tile * HTILE, HTILE), HTILE)
        slot = lax.rem(step, 2)
        return [
            pltpu.make_async_copy(src.at[rows], dst.at[slot], load_sem.at[slot, i])
            for i, (src, dst) in enumerate(((g_a, ga_ring), (g_b, gb_ring)))
        ]

    def load_weights(step):
        shard = lax.rem(step, 2) * 2 + step // 2
        rows = pl.ds(pl.multiple_of(shard * 512, 512), 512)
        slot = lax.rem(step, 2)
        return [
            pltpu.make_async_copy(src.at[rows], w_ring.at[slot, i], w_sem.at[slot, i])
            for i, src in enumerate((wg, wu, wd))
        ]

    for copy in load(0) + load_weights(0):
        copy.start()
    comm.barrier()
    gf_send[...] = gf_b[ROWS:, :].astype(BF16)
    gf_copies = [
        comm.send(gf_send, gf_recv.at[0], comm.z_peers[0]),
        comm.send(gf_a.at[ROWS:], gf_recv.at[1], comm.z_peers[2]),
    ]
    e_core, e_line, f_core = comm.reserve(8), comm.reserve(8), comm.reserve(4)

    def core_copy(step):
        tile = lax.rem(step, 2) * 4 + step // 2
        return comm.copy(
            send_ring.at[lax.rem(step, 2), pl.ds(0, 2)],
            got.at[pl.ds(2 * tile, 2)],
            comm.core_peer,
            e_core + step,
        )

    def line_copy(step):
        side, column = lax.rem(step, 2), step // 2
        cols = pl.ds(pl.multiple_of(column * HTILE, HTILE), HTILE)
        peer = comm.x_peer[0] * (1 - side) + comm.y_peer[0] * side
        return comm.copy(
            e_send1.at[side, :, cols], e_recv1.at[side, :, cols], (peer, comm.z), e_line + step
        )

    @pl.loop(0, 9)
    def _(step):
        @pl.when(step < 8)
        def _():
            slot = lax.rem(step, 2)
            for copy in load(step):
                copy.wait()

            @pl.when(step < 7)
            def _():
                for copy in load(step + 1):
                    copy.start()

            @pl.when(step >= 2)
            def _():
                core_copy(step - 2).wait_send()

            for part in range(2):
                rows = slice(part * 512, (part + 1) * 512)
                first, second = ga_ring[slot, rows, :], gb_ring[slot, rows, :]
                mine_ring[slot, part] = dot_nt(fm_a[...], first) + dot_nt(fm_b[...], second)
                send_ring[slot, part] = (
                    dot_nt(fs_a[...], first) + dot_nt(fs_b[...], second)
                ).astype(BF16)
            core_copy(step).start()

        @pl.when(step > 0)
        def _():
            last = step - 1
            slot, side = lax.rem(last, 2), lax.rem(last, 2)
            tile = side * 4 + last // 2
            core_copy(last).wait_recv()
            for part in range(2):
                start = pl.multiple_of((last // 2) * HTILE + part * 512, 512)
                cols = pl.ds(start, 512)
                fold_one(
                    comm,
                    mine_ring.at[slot, part],
                    got.at[2 * tile + part],
                    e_keep1.at[side, :, cols],
                    e_send1.at[side, :, cols],
                    side,
                )
            line_copy(last).start()

    for step in (6, 7):
        core_copy(step).wait_send()
    for copy in gf_copies:
        copy.wait()

    grad = gf_b[:ROWS, :] + gf_recv[0].astype(F32)
    grad = grad + (gf_2[...].astype(F32) + gf_recv[1].astype(F32))
    out = block_out[...]
    res, gg_final = norm_back(out, rms_scale(out), gain_final[...], grad * D ** (-0.5))
    gg_ref[0:1, :] = gg_final
    res_ref[...] = res
    gatt_ref[...] = res.astype(BF16)
    flat_ref[...] = flip(gatt_ref[...]).astype(BF16)
    split_rows(flat_ref, gm_ref, gs_ref, core, True)
    h2 = h2_in[...]
    rows_ref[...] = (h2 * rms_scale(h2) * gain_ff[...]).astype(BF16)
    flat_2[...] = flip(rows_ref[...]).astype(BF16)
    split_rows(flat_2, nm_ref, ns_ref, core, True)
    gn_ref[...] = jnp.zeros_like(gn_ref)

    def ff_copy(step):
        return comm.copy(
            send_ring.at[lax.rem(step, 2)],
            got.at[pl.ds(3 * step, 3)],
            comm.core_peer,
            f_core + step,
        )

    @pl.loop(0, 5)
    def _(step):
        @pl.when(step < 4)
        def _():
            slot = lax.rem(step, 2)
            for copy in load_weights(step):
                copy.wait()

            @pl.when(step < 3)
            def _():
                for copy in load_weights(step + 1):
                    copy.start()

            @pl.when(step >= 2)
            def _():
                ff_copy(step - 2).wait_send()

            g_gate, g_up, mixed = ff_block(rows_ref, gatt_ref, gn_ref, w_ring.at[slot])
            for m, (mine, send, right) in enumerate(
                ((nm_ref, ns_ref, g_gate), (nm_ref, ns_ref, g_up), (gm_ref, gs_ref, mixed))
            ):
                mine_ring[slot, m] = dot_nn(mine[...], right)
                send_ring[slot, m] = dot_nn(send[...], right).astype(BF16)
            ff_copy(step).start()

        @pl.when(step > 0)
        def _():
            last = step - 1
            slot, side = lax.rem(last, 2), lax.rem(last, 2)
            ff_copy(last).wait_recv()
            for m in range(3):
                cols = pl.ds(pl.multiple_of((last // 2) * 1536 + m * 512, 512), 512)
                fold_one(
                    comm,
                    mine_ring.at[slot, m],
                    got.at[3 * last + m],
                    f_keep.at[side, :, cols],
                    f_send.at[side, :, cols],
                    side,
                )

    step, gg_ff = norm_back(h2_in[...], rms_scale(h2_in[...]), gain_ff[...], gn_ref[...])
    gg_ref[1:2, :] = gg_ff
    res = res_ref[...] + step
    res_ref[...] = res
    rows_b = res.astype(BF16)
    rows_ref[...] = rows_b
    gatt_ref[...] = dot_nt(rows_b, w_co[...]).astype(BF16)
    gatt_t = dot_nt(w_co[...], rows_b).astype(BF16).astype(F32)
    dot_ref[...] = jnp.zeros_like(dot_ref)
    for head in range(NHEAD):
        feats = slice(head * HDIM, (head + 1) * HDIM)
        dot_ref[head : head + 1, :] = jnp.sum(gatt_t[feats, :] * att_t[feats, :], 0, keepdims=True)
    pair_copies = [
        comm.send(gatt_ref, gatt_other, comm.z_peers[0]),
        comm.send(dot_ref, dot_other, comm.z_peers[0]),
    ]
    for step in (2, 3):
        ff_copy(step).wait_send()
    for step in range(8):
        line_copy(step).wait()
    fold_two(comm, e_keep1, e_recv1, e_keep, e_send)
    for copy in pair_copies:
        copy.wait()


def ff_block(n3_ref, grad_ref, gn_ref, weights):
    const = (2.0 / 3.141592653589793) ** 0.5
    wg, wu, wd = weights[0], weights[1], weights[2]
    n3 = n3_ref[...]
    gate = dot_nt(n3, wg)
    up = dot_nt(n3, wu)
    square = gate * gate
    tanh = jnp.tanh(const * (gate + 0.044715 * gate * square))
    gelu = 0.5 * gate * (1.0 + tanh)
    slope = 0.5 * (1.0 + tanh) + 0.5 * gate * (1.0 - tanh * tanh) * const * (
        1.0 + 3.0 * 0.044715 * square
    )
    grad_mixed = dot_nt(grad_ref[...], wd)
    g_gate = (grad_mixed * up * slope).astype(BF16)
    g_up = (grad_mixed * gelu).astype(BF16)
    gn_ref[...] += dot_nn(g_gate, wg) + dot_nn(g_up, wu)
    return g_gate, g_up, (gelu * up).astype(BF16)


def cross_kernel(*refs):
    (scal, q2, k2, v2, lse2, g_own, g_other, dot_own, dot_oth, source), refs = refs[:10], refs[10:]
    (w_ck, w_cv, w_cq, w_so, h1, gain_cross, res_in, rows_in, att), refs = refs[:9], refs[9:]
    (e_send, f_keep, f_send), refs = refs[:3], refs[3:]
    (gsrc, res_ref, rows_ref, gatt1, gatt1_other, gg_ref), refs = refs[:6], refs[6:]
    (c_keep, c_send, f_keep2, f_send2, e_recv), refs = refs[:5], refs[5:]
    (g_ref, dot_ref, dq_ref, dk_ref, dv_ref, flat_ref, sm_ref, ss_ref), refs = refs[:8], refs[8:]
    (mine, send, got, f_recv, own_ref, go_ref, come_ref, flat2, a_ref, b_ref), refs = (
        refs[:10],
        refs[10:],
    )
    comm = Comm(*refs)
    comm.barrier()
    ff = Flow(comm, (f_keep, f_send, f_recv), (f_keep2, f_send2, None), None)
    ff.send_first()
    e_copies = [
        comm.send(e_send.at[0], e_recv.at[0], comm.y_peer),
        comm.send(e_send.at[1], e_recv.at[1], comm.x_peer),
    ]
    cross_backward(
        True, scal, q2, k2, v2, lse2, g_own, g_other, dot_own, dot_oth,
        dk_ref, dv_ref, own_ref, go_ref, g_ref, dot_ref, dq_ref,
    )
    dq_copy = comm.send(go_ref, come_ref, comm.z_peers[0])
    source_backward(
        True, scal, dk_ref, dv_ref, source, w_ck, w_cv, gsrc, mine, send, flat_ref, sm_ref, ss_ref
    )
    dq_copy.wait()
    query_backward(
        True, scal, own_ref, come_ref, h1, gain_cross, w_cq, res_in, rows_in, att, w_so,
        None, None, mine, send, res_ref, rows_ref, gatt1, gg_ref, flat2, go_ref, a_ref, b_ref, dq_ref.at[:, :ROWS],
    )
    pair_copy = comm.send(gatt1, gatt1_other, comm.z_peers[0])
    cross = Flow(comm, (c_keep, c_send, None), None, None)
    cross.from_core(mine, send, got)
    cross.fold_first()
    ff.fold_second()
    pair_copy.wait()
    for copy in e_copies:
        copy.wait()


def self_kernel(vocab, *refs):
    (scal, q1, k1, v1, lse1, g_own, g_other, x_own, gain_self, w_q, w_k, w_v), refs = (
        refs[:12],
        refs[12:],
    )
    (res_in, rows_in, att, gg_a, gg_b), refs = refs[:5], refs[5:]
    (e_keep, e_recv, f_keep, f_send, c_keep, c_send), refs = refs[:6], refs[6:]
    (gin_ref, gains_ref, e_out), refs = refs[:3], refs[3:]
    s_outs, c_outs, f_outs, refs = refs[:4], refs[4:8], refs[8:11], refs[11:]
    (g_ref, dq_ref, dk_ref, dv_ref, flat_ref, flat_2, a_ref, b_ref, gain_ref), refs = refs[:9], refs[9:]
    (mine, send, got, shard_ref, f_recv), refs = refs[:5], refs[5:]
    f_three, (c_recv1, c_keep2, c_send2, c_recv2), refs = refs[:3], refs[3:7], refs[7:]
    c_three, s_one, s_two, s_three, refs = refs[:3], refs[3:6], refs[6:9], refs[9:12], refs[12:]
    gain_send, gain_recv, turn_ref, refs = refs[0], refs[1], refs[2], refs[3:]
    comm = Comm(*refs)
    comm.barrier()
    cross = Flow(comm, (c_keep, c_send, c_recv1), (c_keep2, c_send2, c_recv2), c_three)
    ff = Flow(comm, None, (f_keep, f_send, f_recv), f_three)
    own = Flow(comm, s_one, s_two, s_three)
    ff.send_second()
    cross.send_first()
    self_backward(
        True, scal, q1, k1, v1, lse1, g_own, g_other, x_own, gain_self, w_q, w_k, w_v,
        res_in, rows_in, att, mine, send, gin_ref, gain_ref,
        g_ref, dq_ref, dk_ref, dv_ref, flat_ref, flat_2, a_ref, b_ref,
    )
    own.from_core(mine, send, got)
    gains_ref[...] = jnp.zeros_like(gains_ref)
    gains_ref[0:2, :] = gg_a[...]
    gains_ref[2:3, :] = gg_b[...]
    gains_ref[3:4, :] = gain_ref[...]

    def gain_step(step, peer):
        gain_send[step] = gains_ref[...]
        return comm.send(gain_send.at[step], gain_recv.at[step], peer)

    def gain_done(step, copy):
        copy.wait()
        gains_ref[...] = gains_ref[...] + gain_recv[step]

    copy = gain_step(0, comm.core_peer)
    own.fold_first()
    own.send_first()
    gain_done(0, copy)
    copy = gain_step(1, comm.z_peers[0])
    ff.fold_third(shard_ref)
    cross.fold_second()
    cross.send_second()
    gain_done(1, copy)
    copy = gain_step(2, comm.x_peer)
    width = e_keep.shape[2]
    for start in range(0, vocab, 512):
        side, column = start // width, start % width
        count = min(512, vocab - start)
        cols = slice(column, column + 512)
        turn_ref[...] = e_keep[side, :, cols] + e_recv[side, :, cols].astype(F32)
        e_out[start : start + count, :] = turn_ref[...].T[:count, :]
    gain_done(2, copy)
    copy = gain_step(3, comm.y_peer)
    own.fold_second()
    own.send_second()
    cross.fold_third(shard_ref)
    gain_done(3, copy)
    copy = gain_step(4, comm.z_peers[1])
    ff.finish(f_outs, 2, turn_ref)
    own.fold_third(shard_ref)
    gain_done(4, copy)
    cross.finish(c_outs, 3, turn_ref)
    own.finish(s_outs, 3, turn_ref)


def fused_call(body, collective_id, ins, outs, scratch, copies, flops):
    hbm, vmem = pl.BlockSpec(memory_space=pl.ANY), pl.BlockSpec(memory_space=pltpu.VMEM)
    moved = sum(a.size * a.dtype.itemsize for a, _ in ins)
    return pl.pallas_call(
        body,
        out_shape=[shape for shape, _ in outs],
        in_specs=[pl.BlockSpec(memory_space=pltpu.SMEM)] + [hbm if far else vmem for _, far in ins[1:]],
        out_specs=[hbm if far else vmem for _, far in outs],
        scratch_shapes=scratch(copies),
        cost_estimate=pl.CostEstimate(
            flops=int(flops), bytes_accessed=int(moved), transcendentals=0
        ),
        compiler_params=pltpu.CompilerParams(
            collective_id=collective_id, has_side_effects=True, vmem_limit_bytes=FUSED_LIMIT
        ),
    )(*[a for a, _ in ins])


def fused_backward(
    scal, flats_a, flats_b, g_a, g_b, gf_a, gf_b, gf_2, saved, weights, gains, block_in, source, vocab
):
    (q1, k1, v1, lse1, a1, h1, q2, k2, v2, block_out, h2, att_t, a2, lse2) = saved
    (sq, sk, sv, so, cq, ck, cv, co, wg, wu, wd) = weights
    gain_self, gain_cross, gain_ff, gain_final = gains

    def vm(*shape, dtype=BF16):
        return pltpu.VMEM(shape, dtype)

    def sems(copies):
        return [pltpu.SemaphoreType.DMA((copies,))] * 2

    def near(*arrays):
        return [(a, False) for a in arrays]

    def far(*arrays):
        return [(a, True) for a in arrays]

    block, pair = (ROWS, D), (TGT, D)
    half_t = (HALF_D, ROWS)
    e_half, f_half, c_half = 4096, 3 * FF // 2, 2 * D

    def scratch_1(copies):
        return [
            vm(2, HTILE, TGT), vm(2, HTILE, TGT), vm(2, 3, 512, D), vm(2, 3, HALF_D, 512, dtype=F32),
            vm(2, 3, HALF_D, 512), vm(16, HALF_D, 512), vm(2, 192, e_half, dtype=F32),
            vm(2, 192, e_half), vm(2, 192, e_half), vm(D, ROWS), vm(D, ROWS),
            vm(*half_t), vm(*half_t), vm(*half_t), vm(*half_t), vm(*block, dtype=F32),
            vm(*block), vm(2, *block), *sems(copies),
            pltpu.SemaphoreType.DMA((2, 2)), pltpu.SemaphoreType.DMA((2, 3)),
        ]

    outs = near(
        whole((2, 96, e_half), F32), whole((2, 96, e_half), BF16),
        whole((2, 192, f_half), F32), whole((2, 192, f_half), BF16),
        whole(block, F32), whole(block, BF16), whole(block, BF16), whole(block, BF16),
        whole((16, ROWS), F32), whole((16, ROWS), F32), whole((2, D), F32),
    )
    e_keep, e_send, f_keep, f_send, res2, rows2, gatt, gatt_o, dots, dots_o, gg_a = fused_call(
        table_ff_kernel, 1,
        near(scal) + far(g_a, g_b)
        + near(flats_a[0], flats_b[0], flats_a[1], flats_b[1], gf_a, gf_b, gf_2)
        + near(block_out, h2, gain_ff, gain_final) + far(wg, wu, wd) + near(co, att_t),
        outs, scratch_1, 24, 40e9,
    )

    def scratch_2(copies):
        return [
            vm(*pair), vm(16, TGT, dtype=F32), vm(D, TGT, dtype=F32), vm(KEYS, D), vm(KEYS, D),
            vm(D, KEYS), vm(HALF_D, KEYS), vm(HALF_D, KEYS),
            vm(HALF_D, 4 * D, dtype=F32), vm(HALF_D, 4 * D), vm(HALF_D, 4 * D),
            vm(2, 192, f_half), vm(D, ROWS, dtype=F32), vm(D, ROWS), vm(D, ROWS),
            vm(D, ROWS), vm(*half_t), vm(*half_t), *sems(copies),
        ]

    outs = near(
        whole((KEYS, D), F32), whole(block, F32), whole(block, BF16), whole(block, BF16),
        whole(block, BF16), whole((1, D), F32),
        whole((2, 192, c_half), F32), whole((2, 192, c_half), BF16),
        whole((2, 96, f_half), F32), whole((2, 96, f_half), BF16),
    ) + far(whole((2, 96, e_half), BF16))
    (
        grad_source, res1, rows1, gatt1, gatt1_o, gg_b, c_keep, c_send, f_keep, f_send, e_recv,
    ) = fused_call(
        cross_kernel, 2,
        near(scal, q2, k2, v2, lse2, gatt, gatt_o, dots, dots_o, source, ck, cv, cq, so)
        + near(h1, gain_cross, res2, rows2, a2) + far(e_send) + near(f_keep) + far(f_send),
        outs, scratch_2, 8, 40e9,
    )

    def scratch_3(copies):
        def three(width):
            return [vm(96, width, dtype=F32), vm(3, 96, width), vm(3, 96, width)]

        def two(width):
            return [vm(2, 96, width, dtype=F32), vm(2, 96, width), vm(2, 96, width)]

        return [
            vm(*pair), vm(D, TGT, dtype=F32), vm(*pair), vm(*pair), vm(D, ROWS), vm(D, ROWS),
            vm(*half_t), vm(*half_t), vm(1, D, dtype=F32),
            vm(HALF_D, 4 * D, dtype=F32), vm(HALF_D, 4 * D), vm(HALF_D, 4 * D),
            vm(4, 96, f_half // 2, dtype=F32), vm(2, 96, f_half), *three(f_half // 2),
            vm(2, 192, c_half), *two(c_half), *three(c_half // 2),
            vm(2, 192, c_half, dtype=F32), vm(2, 192, c_half), vm(2, 192, c_half),
            *two(c_half), *three(c_half // 2),
            vm(5, 8, D, dtype=F32), vm(5, 8, D, dtype=F32), vm(96, 512, dtype=F32), *sems(copies),
        ]

    wide, tall = whole((96, 192), F32), whole((192, 96), F32)
    ff_wide, ff_tall = whole((96, 512), F32), whole((512, 96), F32)
    outs = near(
        whole(block, F32), whole((8, D), F32), whole((vocab, 96), F32),
        wide, wide, wide, tall, wide, wide, wide, tall, ff_wide, ff_wide, ff_tall,
    )
    grad_in, gain_sums, grad_embed, *grads = fused_call(
        functools.partial(self_kernel, vocab), 3,
        near(scal, q1, k1, v1, lse1, gatt1, gatt1_o, block_in, gain_self, sq, sk, sv)
        + near(res1, rows1, a1, gg_a, gg_b, e_keep, e_recv, f_keep) + far(f_send)
        + near(c_keep) + far(c_send),
        outs, scratch_3, 32, 20e9,
    )
    return grad_in, grad_source, gain_sums, grads, grad_embed


def logits_kernel(vocab, flat_ref, table_ref, target_ref, logits_ref, stats_ref):
    tile = pl.program_id(0)

    @pl.when(tile == 0)
    def _():
        row = lax.broadcasted_iota(jnp.int32, stats_ref.shape, 0)
        stats_ref[...] = jnp.where(row == 0, 2 * NEG, 0.0)

    logits = dot_nn(table_ref[...], flat_ref[...])
    entry = tile * HTILE + lax.broadcasted_iota(jnp.int32, logits.shape, 0)
    logits = jnp.where(entry < vocab, logits, 2 * NEG)
    logits_ref[...] = logits
    old = stats_ref[0:1, :]
    new = jnp.maximum(old, jnp.max(logits, axis=0, keepdims=True))
    stats_ref[1:2, :] = stats_ref[1:2, :] * jnp.exp(old - new) + jnp.sum(
        jnp.exp(logits - new), axis=0, keepdims=True
    )
    stats_ref[0:1, :] = new
    hit = jnp.where(entry == target_ref[...], logits, 0.0)
    stats_ref[2:3, :] += jnp.sum(hit, axis=0, keepdims=True)


def head_logits(flat, table, target):
    count = flat.shape[1]
    vocab = table.shape[0]
    tiles = pl.cdiv(vocab, HTILE)
    return pl.pallas_call(
        functools.partial(logits_kernel, vocab),
        grid=(tiles,),
        out_shape=[whole((tiles * HTILE, count), F32), whole((8, count), F32)],
        in_specs=[
            pl.BlockSpec((D, count), lambda i: (0, 0)),
            pl.BlockSpec((HTILE, D), lambda i: (i, 0)),
            pl.BlockSpec((1, count), lambda i: (0, 0)),
        ],
        out_specs=[
            pl.BlockSpec((HTILE, count), lambda i: (i, 0)),
            pl.BlockSpec((8, count), lambda i: (0, 0)),
        ],
        cost_estimate=pl.CostEstimate(
            flops=2 * count * vocab * D, bytes_accessed=vocab * (2 * D + 4 * count), transcendentals=0
        ),
        compiler_params=pltpu.CompilerParams(vmem_limit_bytes=VMEM_LIMIT // 2),
    )(flat, table, target)


def grads_kernel(vocab, logits_ref, table_ref, target_ref, lse_ref, live_ref, g_ref, gf_ref, acc_ref):
    tile = pl.program_id(0)

    @pl.when(tile == 0)
    def _():
        acc_ref[...] = jnp.zeros_like(acc_ref)

    entry = tile * HTILE + lax.broadcasted_iota(jnp.int32, logits_ref.shape, 0)
    hit = jnp.where(entry == target_ref[...], 1.0, 0.0)
    grad = jnp.where(live_ref[...] > 0, jnp.exp(logits_ref[...] - lse_ref[...]) - hit, 0.0)
    grad = grad.astype(BF16)
    g_ref[...] = grad
    entry = tile * HTILE + lax.broadcasted_iota(jnp.int32, (HTILE, D), 0)
    table = jnp.where(entry < vocab, table_ref[...], jnp.zeros_like(table_ref[...]))
    acc_ref[...] += lax.dot_general(
        grad, table, (((0,), (0,)), ((), ())), preferred_element_type=F32
    )

    @pl.when(tile == pl.num_programs(0) - 1)
    def _():
        gf_ref[...] = acc_ref[...].astype(gf_ref.dtype)


def head_grads(logits, table, target, lse, live, dtype):
    count = logits.shape[1]
    vocab = table.shape[0]
    tiles = pl.cdiv(vocab, HTILE)
    row = pl.BlockSpec((1, count), lambda i: (0, 0))
    return pl.pallas_call(
        functools.partial(grads_kernel, vocab),
        grid=(tiles,),
        out_shape=[whole((tiles * HTILE, count), BF16), whole((count, D), dtype)],
        in_specs=[
            pl.BlockSpec((HTILE, count), lambda i: (i, 0)),
            pl.BlockSpec((HTILE, D), lambda i: (i, 0)),
            row,
            row,
            row,
        ],
        out_specs=[
            pl.BlockSpec((HTILE, count), lambda i: (i, 0)),
            pl.BlockSpec((count, D), lambda i: (0, 0)),
        ],
        scratch_shapes=[pltpu.VMEM((count, D), F32)],
        cost_estimate=pl.CostEstimate(
            flops=2 * count * vocab * D, bytes_accessed=vocab * (2 * D + 6 * count), transcendentals=0
        ),
        compiler_params=pltpu.CompilerParams(vmem_limit_bytes=VMEM_LIMIT // 2),
    )(logits, table, target, lse, live)


def table_kernel(fm_a, fm_b, fs_a, fs_b, g_a, g_b, mine_ref, send_ref):
    first, second = g_a[...], g_b[...]
    mine_ref[...] = dot_nt(fm_a[...], first) + dot_nt(fm_b[...], second)
    send_ref[...] = (dot_nt(fs_a[...], first) + dot_nt(fs_b[...], second)).astype(BF16)


def table_grads(flat_a, flat_b, g_a, g_b):
    width, count = g_a.shape
    left = pl.BlockSpec((HALF_D, count), lambda i: (0, 0))
    right = pl.BlockSpec((HTILE, count), lambda i: (i, 0))
    out = pl.BlockSpec((HALF_D, HTILE), lambda i: (0, i))
    return pl.pallas_call(
        table_kernel,
        grid=(width // HTILE,),
        out_shape=[whole((HALF_D, width), F32), whole((HALF_D, width), BF16)],
        in_specs=[left] * 4 + [right] * 2,
        out_specs=[out] * 2,
        cost_estimate=pl.CostEstimate(
            flops=4 * count * width * D, bytes_accessed=width * (4 * count + 6 * HALF_D), transcendentals=0
        ),
        compiler_params=pltpu.CompilerParams(vmem_limit_bytes=VMEM_LIMIT),
    )(flat_a[0], flat_b[0], flat_a[1], flat_b[1], g_a, g_b)


def make(mesh):
    dp_size = mesh.shape["dp"]
    split = dp_size == 8

    def on_device(
        block_in,
        source,
        target_len,
        source_len,
        targets,
        gain_self,
        gain_cross,
        gain_ff,
        gain_final,
        self_q,
        self_k,
        self_v,
        self_o,
        cross_q,
        cross_k,
        cross_v,
        cross_o,
        ff_gate,
        ff_up,
        ff_down,
        embed_table,
    ):
        z = lax.axis_index("tensor")
        dp = lax.axis_index("dp")
        half = lax.rem(z, 2)
        seq = z // 2
        core = lax.rem(dp, 2)
        gain_self, gain_cross, gain_ff, gain_final = (
            g.reshape(1, D) for g in (gain_self, gain_cross, gain_ff, gain_final)
        )

        def pair_swap(value):
            return swap(value, "tensor", 4, 1)

        scal = jnp.stack(
            [
                half,
                lax.dynamic_index_in_dim(target_len, seq, keepdims=False),
                lax.dynamic_index_in_dim(source_len, seq, keepdims=False),
                core,
            ]
        ).astype(jnp.int32)

        def vm(shape, dtype):
            return pltpu.VMEM(shape, dtype)

        pair = (TGT, D)
        weights = (
            self_q, self_k, self_v, self_o, cross_q, cross_k, cross_v, cross_o, ff_gate, ff_up, ff_down,
        )
        if not split:
            wide = [gather_wide(w if i in (3, 7, 10) else w.T, dp_size) for i, w in enumerate(weights)]
            sq, sk, sv, so, cq, ck, cv, co, wg, wu, wd = wide
            weights = jnp.stack([sq, sk, sv, so]), jnp.stack([cq, ck, cv, co]), wg, wu, wd
        gains = gain_self, gain_cross, gain_ff, gain_final
        results = forward(split, scal, block_in, source, gains, weights)
        q1, k1, v1, lse1, a1, h1, q2, k2, v2, block_out, fin, h2, att_t, a2, lse2 = results[:15]
        if split:
            sq, sk, sv, so, cq, ck, cv, co, wg, wu, wd = results[15:]

        vocab = embed_table.shape[0]

        def block(by_block, j, axis=0):
            return lax.dynamic_index_in_dim(by_block, z ^ j, axis, keepdims=False)

        tgt_local = targets - z * vocab
        tgt_local = jnp.where((tgt_local >= 0) & (tgt_local < vocab), tgt_local, -1)
        tgt_blocks = tgt_local.reshape(4, ROWS)
        position = lax.rem(jnp.arange(4 * ROWS), TGT)
        live = position < jnp.repeat(target_len, TGT, total_repeat_length=4 * ROWS)
        live_blocks = live.astype(jnp.int32).reshape(4, ROWS)
        fin_1, fin_2, fin_3 = (swap(fin, "tensor", 4, j) for j in (1, 2, 3))
        fin_a = jnp.concatenate([fin_2, fin_3], 0).T
        fin_b = jnp.concatenate([fin, fin_1], 0).T

        def columns(by_block, order):
            return jnp.concatenate([block(by_block, j) for j in order], 0)[None, :]

        tgt_a, tgt_b = columns(tgt_blocks, (2, 3)), columns(tgt_blocks, (0, 1))
        logits_b, stats_b = head_logits(fin_b, embed_table, tgt_b)
        logits_a, stats_a = head_logits(fin_a, embed_table, tgt_a)
        stats = [stats_b[:, :ROWS], stats_b[:, ROWS:], stats_a[:, :ROWS], stats_a[:, ROWS:]]
        stats = jnp.stack(stats, 0)
        stats = jnp.stack([block(stats, j) for j in range(4)], 0)
        others = [stats] + [swap(stats, "tensor", 4, j) for j in (1, 2, 3)]

        def over_z(values, op):
            return op(op(values[0], values[1]), op(values[2], values[3]))

        top = over_z([s[:, 0] for s in others], jnp.maximum)
        total = over_z([s[:, 1] * jnp.exp(s[:, 0] - top) for s in others], jnp.add)
        picked = over_z([s[:, 2] for s in others], jnp.add)
        g_lse = top + jnp.log(total)
        token_loss = jnp.where(live, (g_lse - picked).reshape(-1), 0.0)
        g_a, gf_a = head_grads(
            logits_a, embed_table, tgt_a, columns(g_lse, (2, 3)), columns(live_blocks, (2, 3)), BF16
        )
        gf_2 = swap(gf_a[:ROWS], "tensor", 4, 2)
        g_b, gf_b = head_grads(
            logits_b, embed_table, tgt_b, columns(g_lse, (0, 1)), columns(live_blocks, (0, 1)), F32
        )
        g_b, gf_b, gf_2, gf_a = lax.optimization_barrier((g_b, gf_b, gf_2, gf_a))
        def halves(flat):
            if not split:
                return flat[:HALF_D], flat[HALF_D:]
            flat = flat.reshape(4, 2, 96, -1)
            return tuple(
                lax.dynamic_index_in_dim(flat, i, 1, keepdims=False).reshape(HALF_D, -1)
                for i in (core, 1 - core)
            )

        if split:
            saved = (q1, k1, v1, lse1, a1, h1, q2, k2, v2, block_out, h2, att_t, a2, lse2)
            grad_block_in, grad_source, gains, grads, grad_embed = fused_backward(
                scal, halves(fin_a), halves(fin_b), g_a, g_b, gf_a, gf_b, gf_2, saved,
                (sq, sk, sv, so, cq, ck, cv, co, wg, wu, wd),
                (gain_self, gain_cross, gain_ff, gain_final), block_in, source, vocab,
            )
            return (
                block_out, token_loss, grad_block_in, grad_source,
                gains[3], gains[2], gains[1], gains[0], *grads, grad_embed,
            )

        gf_3 = swap(gf_a[ROWS:], "tensor", 4, 3)
        gf_1 = swap(gf_b[ROWS:].astype(BF16), "tensor", 4, 1)
        e_mine, e_send = table_grads(halves(fin_a), halves(fin_b), g_a, g_b)
        e_sum = WideReduction(z, e_mine[:, :vocab], e_send[:, :vocab])

        half_t = (HALF_D, ROWS)
        ff_mine, ff_send, res2, rows2, gatt, dots, gg_a = local_call(
            functools.partial(ff_backward, split),
            [whole((HALF_D, 3 * FF), F32), whole((HALF_D, 3 * FF), BF16), whole((ROWS, D), F32)]
            + [whole((ROWS, D), BF16)] * 2
            + [whole((16, ROWS), F32), whole((2, D), F32)],
            [vm((D, ROWS), BF16)] * 2 + [vm(half_t, BF16)] * 4
            + [vm((ROWS, D), F32)],
            10e9,
            scal, gf_b[:ROWS], gf_1, gf_2, gf_3, block_out, h2,
            gain_ff, gain_final, wg, wu, wd, co, att_t,
        )
        ff_sum = WideReduction(z, ff_mine, ff_send)
        gatt_other, dots_other = pair_swap(gatt), pair_swap(dots)
        dk2, dv2, dq_own, dq_send = local_call(
            functools.partial(cross_backward, split),
            [whole((KEYS, D), BF16)] * 2 + [whole((D, ROWS), F32), whole((D, ROWS), BF16)],
            [vm(pair, BF16), vm((16, TGT), F32), vm((D, TGT), F32)],
            20e9,
            scal, q2, k2, v2, lse2, gatt, gatt_other, dots, dots_other,
        )
        dq_other = pair_swap(dq_send)
        grad_source, kv_mine, kv_send = local_call(
            functools.partial(source_backward, split),
            [whole((KEYS, D), F32), whole((HALF_D, 2 * D), F32), whole((HALF_D, 2 * D), BF16)],
            [vm((D, KEYS), BF16)] + [vm((HALF_D, KEYS), BF16)] * 2,
            5e9,
            scal, dk2, dv2, source, ck, cv,
        )
        c_mine, c_send, res1, rows1, gatt1, gg_b = local_call(
            functools.partial(query_backward, split),
            [whole((HALF_D, 4 * D), F32), whole((HALF_D, 4 * D), BF16), whole((ROWS, D), F32)]
            + [whole((ROWS, D), BF16)] * 2 + [whole((1, D), F32)],
            [vm((D, ROWS), BF16)] * 2 + [vm(half_t, BF16)] * 2 + [vm((D, ROWS), F32)],
            2e9,
            scal, dq_own, dq_other, h1, gain_cross, cq, res2, rows2, a2, so,
            kv_mine, kv_send,
        )
        c_sum = WideReduction(z, c_mine, c_send)
        gatt1_other = pair_swap(gatt1)
        s_mine, s_send, grad_block_in, gg_c = local_call(
            functools.partial(self_backward, split),
            [whole((HALF_D, 4 * D), F32), whole((HALF_D, 4 * D), BF16)]
            + [whole((ROWS, D), F32), whole((1, D), F32)],
            [vm(pair, BF16), vm((D, TGT), F32), vm(pair, BF16), vm(pair, BF16)]
            + [vm((D, ROWS), BF16)] * 2 + [vm(half_t, BF16)] * 2,
            12e9,
            scal, q1, k1, v1, lse1, gatt1, gatt1_other, block_in, gain_self, sq, sk, sv,
            res1, rows1, a1,
        )
        s_sum = WideReduction(z, s_mine, s_send)
        gains = jnp.concatenate([gg_a, gg_b, gg_c], 0)
        gains = lax.psum(gains, ("dp", "tensor"))
        grad_embed = e_sum.table(vocab)
        ff_grads = ff_sum.last(3, (2,))
        c_grads = c_sum.last(4, (3,))
        s_grads = s_sum.last(4, (3,))

        return (
            block_out,
            token_loss,
            grad_block_in,
            grad_source,
            gains[3],
            gains[2],
            gains[1],
            gains[0],
            *s_grads,
            *c_grads,
            *ff_grads,
            grad_embed,
        )

    return on_device


def solution(mesh):
    rows = P(("dp", "tensor"), None)
    wide, tall = P(None, "tensor"), P("tensor", None)
    in_specs = (rows, rows) + (P("dp"),) * 3 + (P(),) * 4
    in_specs += (wide, wide, wide, tall) * 2 + (wide, wide, tall, tall)
    g_in, g_out = P("dp", "tensor"), P("tensor", "dp")
    out_specs = (rows, P("dp"), rows, rows) + (P(),) * 4
    out_specs += (g_in, g_in, g_in, g_out) * 2 + (g_in, g_in, g_out, g_out)
    return jax.shard_map(
        make(mesh), mesh=mesh, in_specs=in_specs, out_specs=out_specs, check_vma=False
    )
```

```python
import functools
import math

import jax
import jax.numpy as jnp
from jax import lax
from jax.sharding import PartitionSpec as P
from jax.experimental import pallas as pl
from jax.experimental.pallas import tpu as pltpu

D = 768
HDIM = 64
NHEAD = D // HDIM
PAIRS = NHEAD // 2
FF = 2048
TGT = 512
ROWS = 256
KEYS = 1024
CHUNK = 256
HALF_D = D // 2
VTILE = 512
HTILE = 1024
F32 = jnp.float32
BF16 = jnp.bfloat16
MESH_ID = pl.DeviceIdType.MESH
VMEM_LIMIT = 56 * 2**20
FUSED_LIMIT = 62 * 2**20
NEG = -1000000000.0
SCALE = HDIM ** (-0.5)
EPS = 1e-06


def dot_nt(left, right):
    return lax.dot_general(left, right, (((1,), (1,)), ((), ())), preferred_element_type=F32)


def dot_nn(left, right):
    return lax.dot_general(left, right, (((1,), (0,)), ((), ())), preferred_element_type=F32)


def swap(value, axis_name, size, bit):
    return lax.ppermute(value, axis_name, [(i, i ^ bit) for i in range(size)])


class Gather:
    def __init__(self, links, refs, used):
        self.links, self.refs, self.used = links, refs, used
        self.last = []

    def piece(self, ref, shard, owner, part=None):
        if len(ref.shape) == 2:
            rows = ref.shape[0] // 32
            base = shard * 8 * rows + owner * rows
        else:
            rows = ref.shape[1] // 8
            base = shard * 2 * rows + lax.rem(owner, 2) * rows
        start, count = (0, rows) if part is None else (part * rows // 2, rows // 2)
        where = pl.ds(pl.multiple_of(base + start, 16), count)
        return ref.at[where] if len(ref.shape) == 2 else ref.at[owner // 2, where]

    def send(self, part, peer):
        send_sem, recv_sem = self.links["sems"]
        sem = self.used[0]
        self.used[0] += 1
        copy = pltpu.make_async_remote_copy(
            src_ref=part,
            dst_ref=part,
            send_sem=send_sem.at[sem],
            recv_sem=recv_sem.at[sem],
            device_id={"dp": peer[0], "tensor": peer[1]},
            device_id_type=MESH_ID,
        )
        copy.start()
        return copy

    def along_z(self):
        links = self.links
        self.z_copies = [
            self.send(self.piece(ref, links["z"], links["dp"]), peer)
            for ref in self.refs
            for peer in links["z_peers"]
        ]

    def along_xy(self):
        links = self.links
        for copy in self.z_copies:
            copy.wait()
        self.x_copies, self.y_copies = [], []
        for ref in self.refs:
            for _, shard in links["z_peers"]:
                part = self.piece(ref, shard, links["dp"])
                self.x_copies.append(self.send(part, links["x"]))
                self.y_copies.append(self.send(part, links["y"]))
                self.last.append(self.send(part, links["core"]))

    def diagonal(self):
        links = self.links
        self.d_copies = []
        at = 0
        for ref in self.refs:
            for _, shard in links["z_peers"]:
                self.x_copies[at].wait()
                self.d_copies.append(self.send(self.piece(ref, shard, links["x"][0], 0), links["y"]))
                self.y_copies[at].wait()
                self.d_copies.append(self.send(self.piece(ref, shard, links["y"][0], 1), links["x"]))
                for owner in (links["x"][0], links["y"][0]):
                    self.last.append(self.send(self.piece(ref, shard, owner), links["core"]))
                at += 1

    def finish(self):
        links = self.links
        for copy in self.d_copies:
            copy.wait()
        for ref in self.refs:
            for _, shard in links["z_peers"]:
                self.last.append(self.send(self.piece(ref, shard, links["xy"]), links["core"]))
        for copy in self.last:
            copy.wait()


def gather_wide(shard, dp_size):
    rows = shard.shape[0] // dp_size
    part = lax.dynamic_slice_in_dim(shard, lax.axis_index("dp") * rows, rows, 0)
    return lax.all_gather(part, ("tensor", "dp"), axis=0, tiled=True)


def block_rows(index):
    return pl.ds(pl.multiple_of(index * 96, 96), 96)


class Comm:
    def __init__(self, send_sem, recv_sem):
        self.send_sem, self.recv_sem, self.used = send_sem, recv_sem, 0
        dp, z = lax.axis_index("dp"), lax.axis_index("tensor")
        self.z = z
        self.c, self.x, self.y = lax.rem(dp, 2), lax.rem(dp // 2, 2), dp // 4
        low, high = lax.rem(z, 2), z // 2
        self.core_peer = (dp + 1 - 2 * self.c, z)
        self.x_peer = (dp + 2 - 4 * self.x, z)
        self.y_peer = (dp + 4 - 8 * self.y, z)
        self.z_shards = (high * 2 + 1 - low, (1 - high) * 2 + low, (1 - high) * 2 + 1 - low)
        self.z_peers = [(dp, shard) for shard in self.z_shards]

    def barrier(self):
        barrier = pltpu.get_barrier_semaphore()
        peers = [self.core_peer, self.x_peer, self.y_peer] + self.z_peers
        for peer in peers:
            pl.semaphore_signal(
                barrier, inc=1, device_id={"dp": peer[0], "tensor": peer[1]}, device_id_type=MESH_ID
            )
        pl.semaphore_wait(barrier, len(peers))

    def copy(self, src, dst, peer, index):
        return pltpu.make_async_remote_copy(
            src_ref=src,
            dst_ref=dst,
            send_sem=self.send_sem.at[index],
            recv_sem=self.recv_sem.at[index],
            device_id={"dp": peer[0], "tensor": peer[1]},
            device_id_type=MESH_ID,
        )

    def reserve(self, count):
        self.used += count
        return self.used - count

    def send(self, src, dst, peer):
        copy = self.copy(src, dst, peer, self.reserve(1))
        copy.start()
        return copy


def fold_one(comm, mine, got, keep, send, is_right):
    for other in range(2):
        rows = slice(other * 96, (other + 1) * 96)
        along_x, along_y = 2 * other + comm.x, 2 * comm.y + other
        stay = along_x * (1 - is_right) + along_y * is_right
        along_x, along_y = 2 * other + 1 - comm.x, 2 * (1 - comm.y) + other
        leave = along_x * (1 - is_right) + along_y * is_right
        stay, leave = block_rows(stay), block_rows(leave)
        keep[rows, :] = mine[stay, :] + got[stay, :].astype(F32)
        send[rows, :] = (mine[leave, :] + got[leave, :].astype(F32)).astype(BF16)


def fold_two(comm, mine, got, keep, send):
    for side, bit in enumerate((comm.y, comm.x)):
        stay, leave = block_rows(bit), block_rows(1 - bit)
        keep[side] = mine[side, stay, :] + got[side, stay, :].astype(F32)
        send[side] = (mine[side, leave, :] + got[side, leave, :].astype(F32)).astype(BF16)


class Flow:
    def __init__(self, comm, one, two, three):
        self.comm, self.one, self.two, self.three = comm, one, two, three
        self.copies = []

    def wait(self):
        for copy in self.copies:
            copy.wait()

    def from_core(self, mine, send, got):
        comm = self.comm
        self.copies = [comm.send(send, got, comm.core_peer)]
        self.mine, self.got = mine, got

    def fold_first(self):
        self.wait()
        keep, send, _ = self.one
        width = keep.shape[2]
        for side in range(2):
            cols = pl.ds(side * width, width)
            fold_one(
                self.comm, self.mine.at[:, cols], self.got.at[:, cols], keep.at[side], send.at[side], side
            )

    def send_first(self):
        comm = self.comm
        _, send, recv = self.one
        self.copies = [
            comm.send(send.at[0], recv.at[0], comm.x_peer),
            comm.send(send.at[1], recv.at[1], comm.y_peer),
        ]

    def fold_second(self):
        self.wait()
        fold_two(self.comm, self.one[0], self.one[2], self.two[0], self.two[1])

    def send_second(self):
        comm = self.comm
        _, send, recv = self.two
        self.copies = [
            comm.send(send.at[0], recv.at[0], comm.y_peer),
            comm.send(send.at[1], recv.at[1], comm.x_peer),
        ]

    def fold_third(self, shard_ref):
        self.wait()
        comm = self.comm
        (keep, _, recv), (keep3, send3, recv3) = self.two, self.three
        width = keep3.shape[1]
        for side in range(2):
            total = keep[side] + recv[side].astype(F32)
            shard_ref[2 * side, :, :width] = total[:, :width]
            shard_ref[2 * side + 1, :, :width] = total[:, width:]
        keep3[...] = shard_ref[comm.z, :, :width]
        self.copies = []
        for j, shard in enumerate(comm.z_shards):
            send3[j] = shard_ref[shard, :, :width].astype(BF16)
            self.copies.append(comm.send(send3.at[j], recv3.at[j], comm.z_peers[j]))


def finish_kernel(vocab, e_keep, e_recv, f_keep, f_recv, c_keep, c_recv, s_keep, s_recv, gin, *refs):
    e_out, gin_out, refs, turn_ref = refs[0], refs[1], refs[2:-1], refs[-1]
    gin_out[...] = gin[...]
    width = e_keep.shape[2]
    for side in range(2):
        count = min(width, vocab - side * width)
        e_out[:, side * width : side * width + count] = e_keep[side, :, :count] + e_recv[
            side, :, :count
        ].astype(F32)
    for keep, recv, outs in ((f_keep, f_recv, refs[8:]), (c_keep, c_recv, refs[4:8]), (s_keep, s_recv, refs[:4])):
        width = keep.shape[1] // len(outs)
        for m, out in enumerate(outs):
            cols = slice(m * width, (m + 1) * width)
            part = keep[:, cols] + recv[0, :, cols].astype(F32)
            part = part + (recv[1, :, cols].astype(F32) + recv[2, :, cols].astype(F32))
            if out.shape[0] == 96:
                out[...] = part
            else:
                turn_ref[...] = part
                out[...] = turn_ref[...].T


class WideReduction:
    def __init__(self, z, mine, send):
        both = jnp.concatenate([mine, send.astype(F32)], 0)
        self.part = lax.psum_scatter(both, "dp", scatter_dimension=0, tiled=True)

    def last(self, count, flips):
        rows = self.part.shape[0]
        by_z = self.part.reshape(rows, 4, -1)
        total = lax.psum_scatter(by_z, "tensor", scatter_dimension=1, tiled=True)[:, 0]
        parts = jnp.split(total, count, axis=1)
        return [p.T if m in flips else p for m, p in enumerate(parts)]

    def table(self, vocab):
        return self.part.T


def rms_scale(values):
    return lax.rsqrt(jnp.mean(values * values, axis=-1, keepdims=True) + EPS)


def spots(scal, split):
    if split:
        z = lax.axis_index("tensor")
        half, core = lax.rem(z, 2), lax.rem(lax.axis_index("dp"), 2)
        return half, scal[z // 2], scal[2 + z // 2] - half * KEYS, core
    half, core = scal[0], scal[3]
    return half, scal[1], scal[2] - half * KEYS, core


def norm_back(values, inv_scale, gain, grad_out):
    weighted = gain * grad_out
    grad_gain = jnp.sum(grad_out * values * inv_scale, axis=0, keepdims=True)
    grad_values = inv_scale * weighted - values * inv_scale * inv_scale * inv_scale * jnp.mean(
        weighted * values, axis=-1, keepdims=True
    )
    return grad_values, grad_gain


def flip(value):
    return value.astype(F32).T


def lane_half(rows, which):
    lane = lax.broadcasted_iota(jnp.int32, (rows, 2 * HDIM), 1)
    return (lane >= HDIM) if which else (lane < HDIM)


def only(value, which):
    return jnp.where(lane_half(value.shape[0], which), value, jnp.zeros_like(value))


def split_rows(flat_ref, mine_ref, send_ref, core, split):
    for block in range(4):
        if split:
            first = pl.multiple_of((2 * block + core) * 96, 96)
            second = pl.multiple_of((2 * block + 1 - core) * 96, 96)
        else:
            first, second = block * 96, HALF_D + block * 96
        mine_ref[block * 96 : (block + 1) * 96, :] = flat_ref[pl.ds(first, 96), :]
        send_ref[block * 96 : (block + 1) * 96, :] = flat_ref[pl.ds(second, 96), :]


def by_shard(left_ref, rights, out_ref, first, per_shard):
    width = 192 * len(rights)
    for z in range(4):
        part = [right[:, z * 192 : (z + 1) * 192] for right in rights]
        right = jnp.concatenate(part, axis=1) if len(part) > 1 else part[0]
        start = z * per_shard + first
        out_ref[:, start : start + width] = dot_nn(left_ref[...], right).astype(out_ref.dtype)


def whole(shape, dtype):
    return jax.ShapeDtypeStruct(shape, dtype)


def local_call(body, outs, scratch, flops, *args):
    smem = pl.BlockSpec(memory_space=pltpu.SMEM)
    vmem = pl.BlockSpec(memory_space=pltpu.VMEM)
    bytes_all = sum(a.size * a.dtype.itemsize for a in args)
    bytes_all += sum(o.size * jnp.dtype(o.dtype).itemsize for o in outs)
    held = sum(math.prod(s.shape) * jnp.dtype(s.dtype).itemsize for s in scratch)
    return pl.pallas_call(
        body,
        out_shape=outs,
        in_specs=[smem] + [vmem] * (len(args) - 1),
        out_specs=[vmem] * len(outs),
        scratch_shapes=scratch,
        cost_estimate=pl.CostEstimate(
            flops=int(flops), bytes_accessed=int(bytes_all), transcendentals=0
        ),
        compiler_params=pltpu.CompilerParams(
            vmem_limit_bytes=min(VMEM_LIMIT, int(bytes_all + held + 16 * 2**20))
        ),
    )(*args)


def forward_kernel(split, *refs):
    (scal, x_own, source, gains), refs = refs[:4], refs[4:]
    gain_self, gain_cross, gain_ff, gain_final = (gains.at[i : i + 1] for i in range(4))
    shards, refs = refs[: 11 if split else 5], refs[11 if split else 5 :]
    (q1, k1, v1, lse1, att1, h1_out, q2, k2, v2), refs = refs[:9], refs[9:]
    (out_ref, fin_ref, h2_ref, att_t_ref, att2, lse2), refs = refs[:6], refs[6:]
    if split:
        copies_out, refs = refs[:11], refs[11:]
        (ws, wc, wg, wu, wd), refs = refs[:5], refs[5:]
    else:
        ws, wc, wg, wu, wd = shards
    (x_other, x_ref, n_ref, vt_ref, ot_ref, s_ref, o_send, o_other, lse_own, lse_other, mix_ref), refs = (
        refs[:11],
        refs[11:],
    )
    pair_send, pair_recv = refs[:2]
    dp = lax.axis_index("dp")
    z = lax.axis_index("tensor")
    low, high = lax.rem(z, 2), z // 2
    half = low
    live = scal[high] if split else scal[1]
    live_src = (scal[2 + high] if split else scal[2]) - low * KEYS
    z_peers = [(dp, high * 2 + 1 - low)]
    peers = z_peers
    if split:
        z_peers = z_peers + [(dp, (1 - high) * 2 + low), (dp, (1 - high) * 2 + 1 - low)]
        x_peer = dp + 2 - 4 * lax.rem(dp // 2, 2)
        y_peer = dp + 4 - 8 * (dp // 4)
        links = dict(
            dp=dp,
            z=z,
            z_peers=z_peers,
            x=(x_peer, z),
            y=(y_peer, z),
            xy=x_peer + y_peer - dp,
            core=(dp + 1 - 2 * lax.rem(dp, 2), z),
            sems=refs[2:4],
        )
        out_sem = refs[4]
        peers = z_peers + [links["x"], links["y"], links["core"]]
    barrier = pltpu.get_barrier_semaphore()
    for peer in peers:
        pl.semaphore_signal(
            barrier, inc=1, device_id={"dp": peer[0], "tensor": peer[1]}, device_id_type=MESH_ID
        )

    def exchange(index, src, dst):
        copy = pltpu.make_async_remote_copy(
            src_ref=src,
            dst_ref=dst,
            send_sem=pair_send.at[index],
            recv_sem=pair_recv.at[index],
            device_id={"dp": z_peers[0][0], "tensor": z_peers[0][1]},
            device_id_type=MESH_ID,
        )
        copy.start()
        return copy

    leaving = []
    if split:
        used = [0]
        groups = [Gather(links, refs_of, used) for refs_of in ([ws], [wc], [wg], [wu], [wd])]
        of_self, of_cross, of_gate, of_up, of_down = groups
        hid, fhid = D // 4, FF // 4

        def place_block(target, first):
            rows = pl.ds(pl.multiple_of(z * hid, 16), hid)
            for m in range(3):
                target[m, rows, :] = shards[first + m][...]
            target[3, rows, :] = shards[first + 3][...]

        def place_wide(target, shard, flipped):
            rows = pl.ds(pl.multiple_of(z * fhid, 16), fhid)
            target[rows, :] = flip(shard[...]).astype(BF16) if flipped else shard[...]

        def leave(first, parts):
            for i, part in enumerate(parts):
                copy = pltpu.make_async_copy(part, copies_out[first + i], out_sem.at[first + i])
                copy.start()
                leaving.append(copy)

        place_block(ws, 0)
        pl.semaphore_wait(barrier, len(peers))
        of_self.along_z()
    else:
        pl.semaphore_wait(barrier, len(peers))
    x_copy = exchange(0, x_own, x_other)
    if split:
        place_block(wc, 4)
        place_wide(wg, shards[8], True)
        place_wide(wu, shards[9], True)
        place_wide(wd, shards[10], False)
        of_self.along_xy()
        of_cross.along_z()
        of_self.diagonal()
        of_cross.along_xy()
        of_gate.along_z()
    x_copy.wait()
    own = pl.multiple_of(half * ROWS, ROWS)
    other = pl.multiple_of((1 - half) * ROWS, ROWS)
    x_ref[pl.ds(own, ROWS), :] = x_own[...].astype(F32)
    x_ref[pl.ds(other, ROWS), :] = x_other[...].astype(F32)
    lse1[...] = jnp.zeros_like(lse1)
    lse_own[...] = jnp.zeros_like(lse_own)
    if split:
        of_self.finish()
        leave(0, [ws.at[m] for m in range(4)])
    for i in range(2):
        rows = slice(i * ROWS, (i + 1) * ROWS)
        x = x_ref[rows, :]
        n = (x * rms_scale(x) * gain_self[...]).astype(BF16)
        n_ref[rows, :] = n
        q1[rows, :] = dot_nt(n, ws[0]).astype(BF16)
        k1[rows, :] = dot_nt(n, ws[1]).astype(BF16)
        v1[rows, :] = dot_nt(n, ws[2]).astype(BF16)
    vt_ref[:, :TGT] = dot_nt(ws[2], n_ref[...]).astype(BF16)
    if split:
        of_gate.along_xy()
        of_up.along_z()
    key = lax.broadcasted_iota(jnp.int32, (TGT, TGT), 0)
    query = lax.broadcasted_iota(jnp.int32, (TGT, TGT), 1)
    seen = (key <= query) & (key < live)

    def self_pairs(first, last):
        @pl.loop(first, last)
        def _(pair):
            lanes = pl.ds(pl.multiple_of(pair * 128, 128), 128)
            q_pair, k_pair = q1[:, lanes], k1[:, lanes]
            for which in range(2):
                head = 2 * pair + which
                feats = pl.ds(pl.multiple_of(head * HDIM, HDIM), HDIM)
                scores = jnp.where(seen, dot_nt(k_pair, only(q_pair, which)) * SCALE, NEG)
                top = jnp.max(scores, axis=0, keepdims=True)
                probs = jnp.exp(scores - top)
                total = jnp.sum(probs, axis=0, keepdims=True)
                lse1[pl.ds(head, 1), :] = top + jnp.log(total)
                ot_ref[feats, :] = dot_nn(vt_ref[feats, :TGT], probs.astype(BF16)) / total

    self_pairs(0, PAIRS // 2)
    if split:
        of_cross.diagonal()
    self_pairs(PAIRS // 2, PAIRS)
    if split:
        of_up.along_xy()
        of_down.along_z()
        of_gate.diagonal()
    for i in range(2):
        rows = slice(i * ROWS, (i + 1) * ROWS)
        att = flip(ot_ref[:, rows]).astype(BF16)
        n_ref[rows, :] = att
        x_ref[rows, :] = x_ref[rows, :] + dot_nn(att, ws[3])
    att1[...] = n_ref[pl.ds(own, ROWS), :]
    h1_out[...] = x_ref[pl.ds(own, ROWS), :]
    if split:
        of_cross.finish()
        leave(4, [wc.at[m] for m in range(4)])
    for i in range(2):
        rows = slice(i * ROWS, (i + 1) * ROWS)
        h1 = x_ref[rows, :]
        n = (h1 * rms_scale(h1) * gain_cross[...]).astype(BF16)
        q2[rows, :] = dot_nt(n, wc[0]).astype(BF16)
    for i in range(KEYS // CHUNK):
        rows = slice(i * CHUNK, (i + 1) * CHUNK)
        src = source[rows, :]
        k2[rows, :] = dot_nt(src, wc[1]).astype(BF16)
        v2[rows, :] = dot_nt(src, wc[2]).astype(BF16)
        vt_ref[:, rows] = dot_nt(wc[2], src).astype(BF16)
    if split:
        of_down.along_xy()
        of_up.diagonal()
        of_gate.finish()
        leave(8, [wg])
    chunk_key = lax.broadcasted_iota(jnp.int32, (CHUNK, TGT), 0)

    def cross_pairs(first, last):
        @pl.loop(first, last)
        def _(pair):
            lanes = pl.ds(pl.multiple_of(pair * 128, 128), 128)
            q_pair = q2[:, lanes]
            for which in range(2):
                head = 2 * pair + which
                feats = pl.ds(pl.multiple_of(head * HDIM, HDIM), HDIM)
                q_one = only(q_pair, which)
                top = jnp.full((1, TGT), 2 * NEG, F32)
                for i in range(KEYS // CHUNK):
                    rows = slice(i * CHUNK, (i + 1) * CHUNK)
                    scores = dot_nt(k2[rows, lanes], q_one) * SCALE
                    scores = jnp.where(chunk_key < live_src - i * CHUNK, scores, NEG)
                    s_ref[rows, :] = scores
                    top = jnp.maximum(top, jnp.max(scores, axis=0, keepdims=True))
                total = jnp.zeros((1, TGT), F32)
                out = jnp.zeros((HDIM, TGT), F32)
                for i in range(KEYS // CHUNK):
                    rows = slice(i * CHUNK, (i + 1) * CHUNK)
                    probs = jnp.exp(s_ref[rows, :] - top)
                    total = total + jnp.sum(probs, axis=0, keepdims=True)
                    out = out + dot_nn(vt_ref[feats, rows], probs.astype(BF16))
                lse_own[pl.ds(head, 1), :] = top + jnp.log(total)
                ot_ref[feats, :] = out / total

    cross_pairs(0, PAIRS // 2)
    o_send[: D // 2, :] = ot_ref[: D // 2, pl.ds(other, ROWS)].astype(BF16)
    pair_copies = [exchange(1, o_send.at[: D // 2], o_other.at[: D // 2])]
    if split:
        of_down.diagonal()
        of_up.finish()
        leave(9, [wu])
    cross_pairs(PAIRS // 2, PAIRS)
    o_send[D // 2 :, :] = ot_ref[D // 2 :, pl.ds(other, ROWS)].astype(BF16)
    pair_copies.append(exchange(2, o_send.at[D // 2 :], o_other.at[D // 2 :]))
    pair_copies.append(exchange(3, lse_own, lse_other))
    if split:
        of_down.finish()
        leave(10, [wd])
    for copy in pair_copies:
        copy.wait()

    first, second = lse_own[...], lse_other[...]
    top = jnp.maximum(first, second)
    lse2[...] = top + jnp.log(jnp.exp(first - top) + jnp.exp(second - top))
    lse = lse2[:, pl.ds(own, ROWS)]
    w_first = jnp.exp(lse_own[:, pl.ds(own, ROWS)] - lse)
    w_second = jnp.exp(lse_other[:, pl.ds(own, ROWS)] - lse)
    for head in range(NHEAD):
        feats = slice(head * HDIM, (head + 1) * HDIM)
        att_t_ref[feats, :] = (
            ot_ref[feats, pl.ds(own, ROWS)] * w_first[head : head + 1, :]
            + o_other[feats, :].astype(F32) * w_second[head : head + 1, :]
        )
    att = flip(att_t_ref[...]).astype(BF16)
    att2[...] = att
    h2 = h1_out[...] + dot_nn(att, wc[3])
    h2_ref[...] = h2
    n3 = (h2 * rms_scale(h2) * gain_ff[...]).astype(BF16)

    @pl.loop(0, FF // 512)
    def _(i):
        rows = pl.ds(pl.multiple_of(i * 512, 512), 512)
        gate = dot_nt(n3, wg[rows, :])
        up = dot_nt(n3, wu[rows, :])
        mix_ref[:, rows] = (jax.nn.gelu(gate, approximate=True) * up).astype(BF16)

    out = h2 + dot_nn(mix_ref[...], wd[...])
    out_ref[...] = out
    x_ref[:ROWS, :] = out * rms_scale(out) * gain_final[...] * D ** (-0.5)
    fin_ref[...] = x_ref[:ROWS, :].T.astype(BF16)
    for copy in leaving:
        copy.wait()


def forward(split, scal, x_own, source, gains, weights):
    pair = (TGT, D)
    block = (ROWS, D)
    outs = [whole(pair, BF16)] * 3 + [whole((16, TGT), F32), whole(block, BF16), whole(block, F32)]
    outs += [whole(pair, BF16)] + [whole((KEYS, D), BF16)] * 2
    outs += [whole(block, F32), whole((D, ROWS), BF16), whole(block, F32), whole((D, ROWS), F32)]
    outs += [whole(block, BF16), whole((16, TGT), F32)]
    vmem = pl.BlockSpec(memory_space=pltpu.VMEM)
    out_specs = [vmem] * len(outs)
    scratch = []
    if split:
        outs += [whole((D, D), BF16)] * 8 + [whole((FF, D), BF16)] * 3
        out_specs += [pl.BlockSpec(memory_space=pl.ANY)] * 11
        scratch += [pltpu.VMEM((4, D, D), BF16)] * 2 + [pltpu.VMEM((FF, D), BF16)] * 3
    scratch += [
        pltpu.VMEM(block, BF16),
        pltpu.VMEM(pair, F32),
        pltpu.VMEM(pair, BF16),
        pltpu.VMEM((D, KEYS), BF16),
        pltpu.VMEM((D, TGT), F32),
        pltpu.VMEM((KEYS, TGT), F32),
        pltpu.VMEM((D, ROWS), BF16),
        pltpu.VMEM((D, ROWS), BF16),
        pltpu.VMEM((16, TGT), F32),
        pltpu.VMEM((16, TGT), F32),
        pltpu.VMEM((ROWS, FF), BF16),
        pltpu.SemaphoreType.DMA((4,)),
        pltpu.SemaphoreType.DMA((4,)),
    ]
    if split:
        scratch += [pltpu.SemaphoreType.DMA((27 * 5,))] * 2 + [pltpu.SemaphoreType.DMA((11,))]
    args = (scal, x_own, source, gains, *weights)
    return pl.pallas_call(
        functools.partial(forward_kernel, split),
        out_shape=outs,
        in_specs=[pl.BlockSpec(memory_space=pltpu.SMEM)] + [vmem] * (len(args) - 1),
        out_specs=out_specs,
        scratch_shapes=scratch,
        cost_estimate=pl.CostEstimate(
            flops=int(80e9), bytes_accessed=int(6e7), transcendentals=0
        ),
        compiler_params=pltpu.CompilerParams(
            collective_id=0, has_side_effects=True, vmem_limit_bytes=VMEM_LIMIT
        ),
    )(*args)


def ff_backward(
    split, scal, gf_own, gf_1, gf_2, gf_3, block_out, h2_in, gain_ff, gain_final, wg, wu, wd,
    w_co, att_t, mine_ref, send_ref, res_ref, rows_ref, gatt_ref, dot_ref, gg_ref,
    flat_ref, flat_2, nm_ref, ns_ref, gm_ref, gs_ref, gn_ref,
):
    core = scal[3]
    grad = gf_own[...] + gf_1[...].astype(F32)
    grad = grad + (gf_2[...].astype(F32) + gf_3[...].astype(F32))
    out = block_out[...]
    res, gg_final = norm_back(out, rms_scale(out), gain_final[...], grad * D ** (-0.5))
    gg_ref[0:1, :] = gg_final
    rows_b = res.astype(BF16)
    res_ref[...] = res
    rows_ref[...] = rows_b
    flat_ref[...] = flip(rows_ref[...]).astype(BF16)
    split_rows(flat_ref, gm_ref, gs_ref, core, split)
    h2 = h2_in[...]
    scale3 = rms_scale(h2)
    n3 = (h2 * scale3 * gain_ff[...]).astype(BF16)
    rows_ref[...] = n3
    flat_2[...] = flip(rows_ref[...]).astype(BF16)
    split_rows(flat_2, nm_ref, ns_ref, core, split)
    gn_ref[...] = jnp.zeros_like(gn_ref)
    const = (2.0 / 3.141592653589793) ** 0.5

    @pl.loop(0, FF // 512)
    def _(i):
        start = pl.multiple_of(i * 512, 512)
        rows = pl.ds(start, 512)
        gate = dot_nt(n3, wg[rows, :])
        up = dot_nt(n3, wu[rows, :])
        square = gate * gate
        tanh = jnp.tanh(const * (gate + 0.044715 * gate * square))
        gelu = 0.5 * gate * (1.0 + tanh)
        slope = 0.5 * (1.0 + tanh) + 0.5 * gate * (1.0 - tanh * tanh) * const * (
            1.0 + 3.0 * 0.044715 * square
        )
        grad_mixed = dot_nt(rows_b, wd[rows, :])
        g_gate = (grad_mixed * up * slope).astype(BF16)
        g_up = (grad_mixed * gelu).astype(BF16)
        mixed = (gelu * up).astype(BF16)
        gn_ref[...] += dot_nn(g_gate, wg[rows, :]) + dot_nn(g_up, wu[rows, :])
        for m, (mine, send, right) in enumerate(
            ((nm_ref, ns_ref, g_gate), (nm_ref, ns_ref, g_up), (gm_ref, gs_ref, mixed))
        ):
            cols = pl.ds(pl.multiple_of(3 * start + m * 512, 512), 512)
            mine_ref[:, cols] = dot_nn(mine[...], right)
            send_ref[:, cols] = dot_nn(send[...], right).astype(BF16)

    step, gg_ff = norm_back(h2, scale3, gain_ff[...], gn_ref[...])
    gg_ref[1:2, :] = gg_ff
    res = res_ref[...] + step
    res_ref[...] = res
    rows_b = res.astype(BF16)
    rows_ref[...] = rows_b
    gatt_ref[...] = dot_nt(rows_b, w_co[...]).astype(BF16)
    gatt_t = dot_nt(w_co[...], rows_b).astype(BF16).astype(F32)
    dot_ref[...] = jnp.zeros_like(dot_ref)
    for head in range(NHEAD):
        feats = slice(head * HDIM, (head + 1) * HDIM)
        dot_ref[head : head + 1, :] = jnp.sum(gatt_t[feats, :] * att_t[feats, :], 0, keepdims=True)


def both_halves(half, own, other, target):
    target[pl.ds(pl.multiple_of(half * ROWS, ROWS), ROWS), :] = own[...]
    target[pl.ds(pl.multiple_of((1 - half) * ROWS, ROWS), ROWS), :] = other[...]


def cross_backward(
    split, scal, q2, k2, v2, lse, g_own, g_other, dot_own, dot_other,
    dk_ref, dv_ref, own_out, send_out, g_ref, dot_ref, dq_ref,
):
    half, _, live, _ = spots(scal, split)
    own = pl.multiple_of(half * ROWS, ROWS)
    other = pl.multiple_of((1 - half) * ROWS, ROWS)
    both_halves(half, g_own, g_other, g_ref)
    dot_ref[:, pl.ds(own, ROWS)] = dot_own[...]
    dot_ref[:, pl.ds(other, ROWS)] = dot_other[...]
    key = lax.broadcasted_iota(jnp.int32, (CHUNK, TGT), 0)

    @pl.loop(0, PAIRS)
    def _(pair):
        lanes = pl.ds(pl.multiple_of(pair * 128, 128), 128)
        q_pair, g_pair = q2[:, lanes], g_ref[:, lanes]
        for i in range(KEYS // CHUNK):
            rows = slice(i * CHUNK, (i + 1) * CHUNK)
            k_part, v_part = k2[rows, lanes], v2[rows, lanes]
            k_flip = flip(k_part).astype(BF16)
            grad_k = jnp.zeros((CHUNK, 128), F32)
            grad_v = jnp.zeros((CHUNK, 128), F32)
            for which in range(2):
                head = 2 * pair + which
                feats = pl.ds(pl.multiple_of(head * HDIM, HDIM), HDIM)
                q_one, g_one = only(q_pair, which), only(g_pair, which)
                scores = dot_nt(k_part, q_one) * SCALE
                scores = jnp.where(key < live - i * CHUNK, scores, NEG)
                probs = jnp.exp(scores - lse[pl.ds(head, 1), :])
                grad_p = dot_nt(v_part, g_one)
                grad_s = (probs * (grad_p - dot_ref[pl.ds(head, 1), :])).astype(BF16)
                grad_k = grad_k + dot_nn(grad_s, q_one)
                grad_v = grad_v + dot_nn(probs.astype(BF16), g_one)
                grad_q = dot_nn(k_flip[which * HDIM : (which + 1) * HDIM, :], grad_s)
                if i == 0:
                    dq_ref[feats, :] = grad_q
                else:
                    dq_ref[feats, :] += grad_q
            dk_ref[rows, lanes] = (grad_k * SCALE).astype(BF16)
            dv_ref[rows, lanes] = grad_v.astype(BF16)

    own_out[...] = dq_ref[:, pl.ds(own, ROWS)]
    send_out[...] = dq_ref[:, pl.ds(other, ROWS)].astype(BF16)


def source_backward(
    split, scal, dk, dv, source, w_ck, w_cv, gsrc_ref, mine_ref, send_ref, flat_ref, sm_ref, ss_ref
):
    for i in range(KEYS // CHUNK):
        rows = slice(i * CHUNK, (i + 1) * CHUNK)
        gsrc_ref[rows, :] = dot_nn(dk[rows, :], w_ck[...]) + dot_nn(dv[rows, :], w_cv[...])
        flat_ref[:, rows] = flip(source[rows, :]).astype(BF16)
    split_rows(flat_ref, sm_ref, ss_ref, spots(scal, split)[3], split)
    rights = (dk[...], dv[...])
    first, per_shard = (192, D) if split else (0, 384)
    by_shard(sm_ref, rights, mine_ref, first, per_shard)
    by_shard(ss_ref, rights, send_ref, first, per_shard)


def query_backward(
    split, scal, dq_own, dq_other, h1_in, gain_cross, w_cq, res_in, rows_in, att, w_so,
    kv_mine, kv_send, mine_ref, send_ref, res_ref, rows_ref, gatt_ref, gg_ref, flat_ref, flat_2, a_ref, b_ref, turn_ref,
):
    core = spots(scal, split)[3]
    turn_ref[...] = dq_own[...] + dq_other[...].astype(F32)
    dq = (turn_ref[...].T * SCALE).astype(BF16)
    h1 = h1_in[...]
    scale2 = rms_scale(h1)
    rows_ref[...] = (h1 * scale2 * gain_cross[...]).astype(BF16)
    flat_ref[...] = flip(rows_ref[...]).astype(BF16)
    split_rows(flat_ref, a_ref, b_ref, core, split)
    by_shard(a_ref, (dq,), mine_ref, 0, D)
    by_shard(b_ref, (dq,), send_ref, 0, D)
    step, gg = norm_back(h1, scale2, gain_cross[...], dot_nn(dq, w_cq[...]))
    gg_ref[...] = gg
    res = res_in[...] + step
    res_ref[...] = res
    rows_b = res.astype(BF16)
    rows_ref[...] = rows_b
    gatt_ref[...] = dot_nt(rows_b, w_so[...]).astype(BF16)
    flat_2[...] = flip(rows_in[...]).astype(BF16)
    split_rows(flat_2, a_ref, b_ref, core, split)
    by_shard(a_ref, (att[...],), mine_ref, 576, D)
    by_shard(b_ref, (att[...],), send_ref, 576, D)
    for z in range(0 if split else 4):
        cols = slice(z * D + 192, z * D + 576)
        mine_ref[:, cols] = kv_mine[:, z * 384 : (z + 1) * 384]
        send_ref[:, cols] = kv_send[:, z * 384 : (z + 1) * 384]


def self_backward(
    split, scal, q1, k1, v1, lse, g_own, g_other, x_own, gain_self, w_q, w_k, w_v, res_in, rows_in, att,
    mine_ref, send_ref, gin_ref, gg_ref,
    g_ref, dq_ref, dk_ref, dv_ref, flat_ref, flat_2, a_ref, b_ref,
):
    half, live, _, core = spots(scal, split)
    own = pl.multiple_of(half * ROWS, ROWS)
    both_halves(half, g_own, g_other, g_ref)
    key = lax.broadcasted_iota(jnp.int32, (TGT, TGT), 0)
    query = lax.broadcasted_iota(jnp.int32, (TGT, TGT), 1)
    seen = (key <= query) & (key < live)

    @pl.loop(0, PAIRS)
    def _(pair):
        lanes = pl.ds(pl.multiple_of(pair * 128, 128), 128)
        q_pair, g_pair = q1[:, lanes], g_ref[:, lanes]
        k_pair, v_pair = k1[:, lanes], v1[:, lanes]
        k_flip = flip(k_pair).astype(BF16)
        grad_k = jnp.zeros((TGT, 128), F32)
        grad_v = jnp.zeros((TGT, 128), F32)
        for which in range(2):
            head = 2 * pair + which
            feats = pl.ds(pl.multiple_of(head * HDIM, HDIM), HDIM)
            q_one, g_one = only(q_pair, which), only(g_pair, which)
            scores = jnp.where(seen, dot_nt(k_pair, q_one) * SCALE, NEG)
            probs = jnp.exp(scores - lse[pl.ds(head, 1), :])
            grad_p = dot_nt(v_pair, g_one)
            row_dot = jnp.sum(probs * grad_p, axis=0, keepdims=True)
            grad_s = (probs * (grad_p - row_dot)).astype(BF16)
            grad_k = grad_k + dot_nn(grad_s, q_one)
            grad_v = grad_v + dot_nn(probs.astype(BF16), g_one)
            dq_ref[feats, :] = dot_nn(k_flip[which * HDIM : (which + 1) * HDIM, :], grad_s)
        dk_ref[:, lanes] = (grad_k * SCALE).astype(BF16)
        dv_ref[:, lanes] = grad_v.astype(BF16)

    dq = (flip(dq_ref[:, pl.ds(own, ROWS)]) * SCALE).astype(BF16)
    dk = dk_ref[pl.ds(own, ROWS), :]
    dv = dv_ref[pl.ds(own, ROWS), :]
    x = x_own[...].astype(F32)
    scale1 = rms_scale(x)
    grad_n = dot_nn(dq, w_q[...]) + dot_nn(dk, w_k[...]) + dot_nn(dv, w_v[...])
    step, gg = norm_back(x, scale1, gain_self[...], grad_n)
    gg_ref[...] = gg
    gin_ref[...] = res_in[...] + step
    g_ref[:ROWS, :] = (x * scale1 * gain_self[...]).astype(BF16)
    flat_ref[...] = flip(g_ref[:ROWS, :]).astype(BF16)
    split_rows(flat_ref, a_ref, b_ref, core, split)
    by_shard(a_ref, (dq, dk, dv), mine_ref, 0, D)
    by_shard(b_ref, (dq, dk, dv), send_ref, 0, D)
    flat_2[...] = flip(rows_in[...]).astype(BF16)
    split_rows(flat_2, a_ref, b_ref, core, split)
    by_shard(a_ref, (att[...],), mine_ref, 576, D)
    by_shard(b_ref, (att[...],), send_ref, 576, D)


def table_ff_kernel(*refs):
    (scal, g_a, g_b, fin_a, fin_b, gf_sum, gf_3), refs = refs[:7], refs[7:]
    (block_out, h2_in, gains, wg, wu, wd, w_co, att_t), refs = refs[:8], refs[8:]
    gain_ff, gain_final = gains.at[2:3], gains.at[3:4]
    (e_keep, e_send, f_keep, f_send, res_ref, rows_ref), refs = refs[:6], refs[6:]
    (gatt_ref, gatt_other, dot_ref, dot_other, gg_ref), refs = refs[:5], refs[5:]
    (ga_ring, gb_ring, w_ring, mine_ring, send_ring, got, e_keep1, e_send1, e_recv1), refs = (
        refs[:9],
        refs[9:],
    )
    (flat_ref, flat_2, nm_ref, ns_ref, gm_ref, gs_ref, gn_ref, gf_recv), refs = refs[:8], refs[8:]
    (fm_a, fm_b, fs_a, fs_b), refs = refs[:4], refs[4:]
    send_sem, recv_sem, load_sem, w_sem = refs
    comm = Comm(send_sem, recv_sem)
    core = comm.c

    def load(step):
        tile = lax.rem(step, 2) * 4 + step // 2
        rows = pl.ds(pl.multiple_of(tile * HTILE, HTILE), HTILE)
        slot = lax.rem(step, 2)
        return [
            pltpu.make_async_copy(src.at[rows], dst.at[slot], load_sem.at[slot, i])
            for i, (src, dst) in enumerate(((g_a, ga_ring), (g_b, gb_ring)))
        ]

    def load_weights(step):
        shard = lax.rem(step, 2) * 2 + step // 2
        rows = pl.ds(pl.multiple_of(shard * 512, 512), 512)
        slot = lax.rem(step, 2)
        return [
            pltpu.make_async_copy(src.at[rows], w_ring.at[slot, i], w_sem.at[slot, i])
            for i, src in enumerate((wg, wu, wd))
        ]

    for copy in load(0) + load_weights(0):
        copy.start()
    comm.barrier()
    gf_copies = [comm.send(gf_3, gf_recv, comm.z_peers[2])]
    split_rows(fin_a, fm_a, fs_a, core, True)
    split_rows(fin_b, fm_b, fs_b, core, True)
    e_core, e_line, f_core = comm.reserve(8), comm.reserve(8), comm.reserve(4)

    def core_copy(step):
        tile = lax.rem(step, 2) * 4 + step // 2
        return comm.copy(
            send_ring.at[lax.rem(step, 2), pl.ds(0, 2)],
            got.at[pl.ds(2 * tile, 2)],
            comm.core_peer,
            e_core + step,
        )

    def line_copy(step):
        side, column = lax.rem(step, 2), step // 2
        cols = pl.ds(pl.multiple_of(column * HTILE, HTILE), HTILE)
        peer = comm.x_peer[0] * (1 - side) + comm.y_peer[0] * side
        return comm.copy(
            e_send1.at[side, :, cols], e_recv1.at[side, :, cols], (peer, comm.z), e_line + step
        )

    @pl.loop(0, 9)
    def _(step):
        @pl.when(step < 8)
        def _():
            slot = lax.rem(step, 2)
            for copy in load(step):
                copy.wait()

            @pl.when(step < 7)
            def _():
                for copy in load(step + 1):
                    copy.start()

            @pl.when(step >= 2)
            def _():
                core_copy(step - 2).wait_send()

            for part in range(2):
                rows = slice(part * 512, (part + 1) * 512)
                first, second = ga_ring[slot, rows, :], gb_ring[slot, rows, :]
                mine_ring[slot, part] = dot_nt(fm_a[...], first) + dot_nt(fm_b[...], second)
                send_ring[slot, part] = (
                    dot_nt(fs_a[...], first) + dot_nt(fs_b[...], second)
                ).astype(BF16)
            core_copy(step).start()

        @pl.when(step > 0)
        def _():
            last = step - 1
            slot, side = lax.rem(last, 2), lax.rem(last, 2)
            tile = side * 4 + last // 2
            core_copy(last).wait_recv()
            for part in range(2):
                start = pl.multiple_of((last // 2) * HTILE + part * 512, 512)
                cols = pl.ds(start, 512)
                fold_one(
                    comm,
                    mine_ring.at[slot, part],
                    got.at[2 * tile + part],
                    e_keep1.at[side, :, cols],
                    e_send1.at[side, :, cols],
                    side,
                )
            line_copy(last).start()

    for step in (6, 7):
        core_copy(step).wait_send()
    for copy in gf_copies:
        copy.wait()

    grad = gf_sum[...] + gf_recv[...].astype(F32)
    out = block_out[...]
    res, gg_final = norm_back(out, rms_scale(out), gain_final[...], grad * D ** (-0.5))
    gg_ref[0:1, :] = gg_final
    res_ref[...] = res
    gatt_ref[...] = res.astype(BF16)
    flat_ref[...] = flip(gatt_ref[...]).astype(BF16)
    split_rows(flat_ref, gm_ref, gs_ref, core, True)
    h2 = h2_in[...]
    rows_ref[...] = (h2 * rms_scale(h2) * gain_ff[...]).astype(BF16)
    flat_2[...] = flip(rows_ref[...]).astype(BF16)
    split_rows(flat_2, nm_ref, ns_ref, core, True)
    gn_ref[...] = jnp.zeros_like(gn_ref)

    def ff_copy(step):
        return comm.copy(
            send_ring.at[lax.rem(step, 2)],
            got.at[pl.ds(3 * step, 3)],
            comm.core_peer,
            f_core + step,
        )

    @pl.loop(0, 5)
    def _(step):
        @pl.when(step < 4)
        def _():
            slot = lax.rem(step, 2)
            for copy in load_weights(step):
                copy.wait()

            @pl.when(step < 3)
            def _():
                for copy in load_weights(step + 1):
                    copy.start()

            @pl.when(step >= 2)
            def _():
                ff_copy(step - 2).wait_send()

            g_gate, g_up, mixed = ff_block(rows_ref, gatt_ref, gn_ref, w_ring.at[slot])
            for m, (mine, send, right) in enumerate(
                ((nm_ref, ns_ref, g_gate), (nm_ref, ns_ref, g_up), (gm_ref, gs_ref, mixed))
            ):
                mine_ring[slot, m] = dot_nn(mine[...], right)
                send_ring[slot, m] = dot_nn(send[...], right).astype(BF16)
            ff_copy(step).start()

        @pl.when(step > 0)
        def _():
            last = step - 1
            slot, side = lax.rem(last, 2), lax.rem(last, 2)
            ff_copy(last).wait_recv()
            for m in range(3):
                cols = pl.ds(pl.multiple_of((last // 2) * 1536 + m * 512, 512), 512)
                fold_one(
                    comm,
                    mine_ring.at[slot, m],
                    got.at[3 * last + m],
                    f_keep.at[side, :, cols],
                    f_send.at[side, :, cols],
                    side,
                )

    step, gg_ff = norm_back(h2_in[...], rms_scale(h2_in[...]), gain_ff[...], gn_ref[...])
    gg_ref[1:2, :] = gg_ff
    res = res_ref[...] + step
    res_ref[...] = res
    rows_b = res.astype(BF16)
    rows_ref[...] = rows_b
    gatt_ref[...] = dot_nt(rows_b, w_co[...]).astype(BF16)
    gatt_t = dot_nt(w_co[...], rows_b).astype(BF16).astype(F32)
    dot_ref[...] = jnp.zeros_like(dot_ref)
    for head in range(NHEAD):
        feats = slice(head * HDIM, (head + 1) * HDIM)
        dot_ref[head : head + 1, :] = jnp.sum(gatt_t[feats, :] * att_t[feats, :], 0, keepdims=True)
    pair_copies = [
        comm.send(gatt_ref, gatt_other, comm.z_peers[0]),
        comm.send(dot_ref, dot_other, comm.z_peers[0]),
    ]
    for step in (2, 3):
        ff_copy(step).wait_send()
    for step in range(8):
        line_copy(step).wait()
    fold_two(comm, e_keep1, e_recv1, e_keep, e_send)
    for copy in pair_copies:
        copy.wait()


def ff_block(n3_ref, grad_ref, gn_ref, weights):
    const = (2.0 / 3.141592653589793) ** 0.5
    wg, wu, wd = weights[0], weights[1], weights[2]
    n3 = n3_ref[...]
    gate = dot_nt(n3, wg)
    up = dot_nt(n3, wu)
    square = gate * gate
    tanh = jnp.tanh(const * (gate + 0.044715 * gate * square))
    gelu = 0.5 * gate * (1.0 + tanh)
    slope = 0.5 * (1.0 + tanh) + 0.5 * gate * (1.0 - tanh * tanh) * const * (
        1.0 + 3.0 * 0.044715 * square
    )
    grad_mixed = dot_nt(grad_ref[...], wd)
    g_gate = (grad_mixed * up * slope).astype(BF16)
    g_up = (grad_mixed * gelu).astype(BF16)
    gn_ref[...] += dot_nn(g_gate, wg) + dot_nn(g_up, wu)
    return g_gate, g_up, (gelu * up).astype(BF16)


def cross_kernel(*refs):
    (scal, q2, k2, v2, lse2, g_own, g_other, dot_own, dot_oth, source), refs = refs[:10], refs[10:]
    (w_ck, w_cv, w_cq, w_so, h1, gains, res_in, rows_in, att), refs = refs[:9], refs[9:]
    gain_cross = gains.at[1:2]
    (e_send, f_keep, f_send), refs = refs[:3], refs[3:]
    (gsrc, res_ref, rows_ref, gatt1, gatt1_other, gg_ref), refs = refs[:6], refs[6:]
    (c_keep, c_send, f_keep2, f_send2, e_recv), refs = refs[:5], refs[5:]
    (g_ref, dot_ref, dq_ref, dk_ref, dv_ref, flat_ref, sm_ref, ss_ref), refs = refs[:8], refs[8:]
    (mine, send, got, f_recv, own_ref, go_ref, come_ref, flat2, a_ref, b_ref), refs = (
        refs[:10],
        refs[10:],
    )
    comm = Comm(*refs)
    comm.barrier()
    ff = Flow(comm, (f_keep, f_send, f_recv), (f_keep2, f_send2, None), None)
    ff.send_first()
    e_copies = [
        comm.send(e_send.at[0], e_recv.at[0], comm.y_peer),
        comm.send(e_send.at[1], e_recv.at[1], comm.x_peer),
    ]
    cross_backward(
        True, scal, q2, k2, v2, lse2, g_own, g_other, dot_own, dot_oth,
        dk_ref, dv_ref, own_ref, go_ref, g_ref, dot_ref, dq_ref,
    )
    dq_copy = comm.send(go_ref, come_ref, comm.z_peers[0])
    source_backward(
        True, scal, dk_ref, dv_ref, source, w_ck, w_cv, gsrc, mine, send, flat_ref, sm_ref, ss_ref
    )
    dq_copy.wait()
    query_backward(
        True, scal, own_ref, come_ref, h1, gain_cross, w_cq, res_in, rows_in, att, w_so,
        None, None, mine, send, res_ref, rows_ref, gatt1, gg_ref, flat2, go_ref, a_ref, b_ref, dq_ref.at[:, :ROWS],
    )
    pair_copy = comm.send(gatt1, gatt1_other, comm.z_peers[0])
    cross = Flow(comm, (c_keep, c_send, None), None, None)
    cross.from_core(mine, send, got)
    cross.fold_first()
    ff.fold_second()
    pair_copy.wait()
    for copy in e_copies:
        copy.wait()


def self_kernel(*refs):
    (scal, q1, k1, v1, lse1, g_own, g_other, x_own, gains, w_q, w_k, w_v), refs = (
        refs[:12],
        refs[12:],
    )
    gain_self = gains.at[0:1]
    (res_in, rows_in, att, gg_a, gg_b), refs = refs[:5], refs[5:]
    (f_keep, f_send, c_keep, c_send), refs = refs[:4], refs[4:]
    (gin_ref, gains_ref, f_keep3, f_recv3, c_keep3, c_recv3, s_keep3, s_recv3), refs = refs[:8], refs[8:]
    (g_ref, dq_ref, dk_ref, dv_ref, flat_ref, flat_2, a_ref, b_ref, gain_ref), refs = refs[:9], refs[9:]
    (mine, send, got, shard_ref, f_recv), refs = refs[:5], refs[5:]
    (c_recv1, c_keep2, c_send2, c_recv2), refs = refs[:4], refs[4:]
    s_one, s_two, refs = refs[:3], refs[3:6], refs[6:]
    (f_send3, c_send3, s_send3, gain_send, gain_recv), refs = refs[:5], refs[5:]
    f_three = f_keep3, f_send3, f_recv3
    c_three = c_keep3, c_send3, c_recv3
    s_three = s_keep3, s_send3, s_recv3
    comm = Comm(*refs)
    comm.barrier()
    cross = Flow(comm, (c_keep, c_send, c_recv1), (c_keep2, c_send2, c_recv2), c_three)
    ff = Flow(comm, None, (f_keep, f_send, f_recv), f_three)
    own = Flow(comm, s_one, s_two, s_three)
    ff.send_second()
    cross.send_first()
    self_backward(
        True, scal, q1, k1, v1, lse1, g_own, g_other, x_own, gain_self, w_q, w_k, w_v,
        res_in, rows_in, att, mine, send, gin_ref, gain_ref,
        g_ref, dq_ref, dk_ref, dv_ref, flat_ref, flat_2, a_ref, b_ref,
    )
    own.from_core(mine, send, got)
    gains_ref[...] = jnp.zeros_like(gains_ref)
    gains_ref[0:2, :] = gg_a[...]
    gains_ref[2:3, :] = gg_b[...]
    gains_ref[3:4, :] = gain_ref[...]

    def gain_step(step, peer):
        gain_send[step] = gains_ref[...]
        return comm.send(gain_send.at[step], gain_recv.at[step], peer)

    def gain_done(step, copy):
        copy.wait()
        gains_ref[...] = gains_ref[...] + gain_recv[step]

    copy = gain_step(0, comm.core_peer)
    own.fold_first()
    own.send_first()
    gain_done(0, copy)
    copy = gain_step(1, comm.z_peers[0])
    ff.fold_third(shard_ref)
    cross.fold_second()
    cross.send_second()
    gain_done(1, copy)
    copy = gain_step(2, comm.x_peer)
    gain_done(2, copy)
    copy = gain_step(3, comm.y_peer)
    own.fold_second()
    own.send_second()
    cross.fold_third(shard_ref)
    gain_done(3, copy)
    copy = gain_step(4, comm.z_peers[1])
    ff.wait()
    own.fold_third(shard_ref)
    gain_done(4, copy)
    cross.wait()
    own.wait()


def head_kernel(vocab, *refs):
    (lens, fin_own, table, targets), refs = refs[:4], refs[4:]
    (g_a, g_b, gf_sum, gf_3, loss_ref, fin_a, fin_b), refs = refs[:7], refs[7:]
    (e_ref, l_ref, fin_recv, stats, stats_recv, ring, acc_ref, gf_send, gf_recv), refs = (
        refs[:9],
        refs[9:],
    )
    send_sem, recv_sem, e_sem, ring_sem = refs
    comm = Comm(send_sem, recv_sem)
    z = comm.z
    shards = (z,) + comm.z_shards
    load = pltpu.make_async_copy(table, e_ref.at[:vocab], e_sem.at[0])
    load.start()
    barrier = pltpu.get_barrier_semaphore()
    for peer in comm.z_peers:
        pl.semaphore_signal(
            barrier, inc=1, device_id={"dp": peer[0], "tensor": peer[1]}, device_id_type=MESH_ID
        )
    pl.semaphore_wait(barrier, 3)
    fin_copies = [comm.send(fin_own, fin_recv.at[j], comm.z_peers[j]) for j in range(3)]
    padded = e_ref.shape[0]
    if padded > vocab:
        e_ref[vocab:, :] = jnp.zeros((padded - vocab, D), BF16)
    load.wait()
    tiles = padded // HTILE
    local = []
    for shard in shards:
        target = targets[pl.ds(shard, 1), :] - z * vocab
        local.append(jnp.where(target < vocab, target, -1))
    entry = lax.broadcasted_iota(jnp.int32, (HTILE, ROWS), 0)

    for i in range(4):
        if i > 0:
            fin_copies[i - 1].wait()
        fin = fin_own if i == 0 else fin_recv.at[i - 1]
        lanes = slice((i % 2) * ROWS, (i % 2 + 1) * ROWS)
        (fin_b if i < 2 else fin_a)[:, lanes] = fin[...]
        row = lax.broadcasted_iota(jnp.int32, (8, ROWS), 0)
        stats[i] = jnp.where(row == 0, 2 * NEG, 0.0)

        @pl.loop(0, tiles)
        def _(tile):
            start = pl.multiple_of(tile * HTILE, HTILE)
            logits = dot_nn(e_ref[pl.ds(start, HTILE), :], fin[...])
            logits = jnp.where(entry < vocab - start, logits, 2 * NEG)
            l_ref[i, pl.ds(start, HTILE), :] = logits
            old = stats[i, 0:1, :]
            new = jnp.maximum(old, jnp.max(logits, axis=0, keepdims=True))
            stats[i, 1:2, :] = stats[i, 1:2, :] * jnp.exp(old - new) + jnp.sum(
                jnp.exp(logits - new), axis=0, keepdims=True
            )
            stats[i, 0:1, :] = new
            hit = jnp.where(entry == local[i] - start, logits, 0.0)
            stats[i, 2:3, :] += jnp.sum(hit, axis=0, keepdims=True)

    copies = [comm.send(stats, stats_recv.at[j], comm.z_peers[j]) for j in range(3)]
    for copy in copies:
        copy.wait()

    def over_z(values, op):
        return op(op(values[0], values[1]), op(values[2], values[3]))

    lse, live = [], []
    for i in range(4):
        parts = [stats.at[i]] + [stats_recv.at[k - 1, i ^ k] for k in (1, 2, 3)]
        top = over_z([p[0:1, :] for p in parts], jnp.maximum)
        total = over_z([p[1:2, :] * jnp.exp(p[0:1, :] - top) for p in parts], jnp.add)
        picked = over_z([p[2:3, :] for p in parts], jnp.add)
        lse.append(top + jnp.log(total))
        lane = lax.broadcasted_iota(jnp.int32, (1, ROWS), 1)
        live.append(lax.rem(shards[i], 2) * ROWS + lane < lens[shards[i] // 2])
        loss_ref[pl.ds(shards[i], 1), :] = jnp.where(live[i], lse[i] - picked, 0.0)

    gf_copies = []
    for i in (2, 1, 3, 0):
        target = g_b if i < 2 else g_a
        acc_ref[...] = jnp.zeros_like(acc_ref)

        def leave(tile):
            rows = pl.ds(pl.multiple_of(tile * HTILE, HTILE), HTILE)
            slot = lax.rem(tile, 2)
            return pltpu.make_async_copy(
                ring.at[slot], target.at[rows, pl.ds((i % 2) * ROWS, ROWS)], ring_sem.at[slot]
            )

        @pl.loop(0, tiles)
        def _(tile):
            start = pl.multiple_of(tile * HTILE, HTILE)

            @pl.when(tile >= 2)
            def _():
                leave(tile - 2).wait()

            hit = jnp.where(entry == local[i] - start, 1.0, 0.0)
            grad = jnp.exp(l_ref[i, pl.ds(start, HTILE), :] - lse[i]) - hit
            grad = jnp.where(live[i], grad, 0.0).astype(BF16)
            ring[lax.rem(tile, 2)] = grad
            leave(tile).start()
            acc_ref[...] += lax.dot_general(
                grad, e_ref[pl.ds(start, HTILE), :], (((0,), (0,)), ((), ())), preferred_element_type=F32
            )

        for tile in (tiles - 2, tiles - 1):
            leave(tile).wait()
        if i == 3:
            gf_3[...] = acc_ref[...].astype(BF16)
        elif i > 0:
            gf_send[i - 1] = acc_ref[...].astype(BF16)
            gf_copies.append(comm.send(gf_send.at[i - 1], gf_recv.at[i - 1], comm.z_peers[i - 1]))
    for copy in gf_copies:
        copy.wait()
    gf_sum[...] = acc_ref[...] + (gf_recv[0].astype(F32) + gf_recv[1].astype(F32))


def fused_head(lens, fin_t, table, targets):
    vocab = table.shape[0]
    padded = pl.cdiv(vocab, HTILE) * HTILE
    hbm, vmem = pl.BlockSpec(memory_space=pl.ANY), pl.BlockSpec(memory_space=pltpu.VMEM)
    grad = whole((padded, TGT), BF16)
    block = (ROWS, D)
    return pl.pallas_call(
        functools.partial(head_kernel, vocab),
        out_shape=[
            grad, grad, whole(block, F32), whole(block, BF16), whole((4, ROWS), F32),
            whole((D, TGT), BF16), whole((D, TGT), BF16),
        ],
        in_specs=[pl.BlockSpec(memory_space=pltpu.SMEM), vmem, hbm, vmem],
        out_specs=[hbm, hbm] + [vmem] * 5,
        scratch_shapes=[
            pltpu.VMEM((padded, D), BF16),
            pltpu.VMEM((4, padded, ROWS), F32),
            pltpu.VMEM((3, D, ROWS), BF16),
            pltpu.VMEM((4, 8, ROWS), F32),
            pltpu.VMEM((3, 4, 8, ROWS), F32),
            pltpu.VMEM((2, HTILE, ROWS), BF16),
            pltpu.VMEM(block, F32),
            pltpu.VMEM((2,) + block, BF16),
            pltpu.VMEM((2,) + block, BF16),
            pltpu.SemaphoreType.DMA((8,)),
            pltpu.SemaphoreType.DMA((8,)),
            pltpu.SemaphoreType.DMA((1,)),
            pltpu.SemaphoreType.DMA((2,)),
        ],
        compiler_params=pltpu.CompilerParams(
            collective_id=4, has_side_effects=True, vmem_limit_bytes=FUSED_LIMIT
        ),
    )(lens, fin_t, table, targets)


def fused_call(body, collective_id, ins, outs, scratch, copies, flops):
    hbm, vmem = pl.BlockSpec(memory_space=pl.ANY), pl.BlockSpec(memory_space=pltpu.VMEM)
    moved = sum(a.size * a.dtype.itemsize for a, _ in ins)
    return pl.pallas_call(
        body,
        out_shape=[shape for shape, _ in outs],
        in_specs=[pl.BlockSpec(memory_space=pltpu.SMEM)] + [hbm if far else vmem for _, far in ins[1:]],
        out_specs=[hbm if far else vmem for _, far in outs],
        scratch_shapes=scratch(copies),
        cost_estimate=pl.CostEstimate(
            flops=int(flops), bytes_accessed=int(moved), transcendentals=0
        ),
        compiler_params=pltpu.CompilerParams(
            collective_id=collective_id, has_side_effects=True, vmem_limit_bytes=FUSED_LIMIT
        ),
    )(*[a for a, _ in ins])


def fused_backward(
    scal, fin_a, fin_b, g_a, g_b, gf_sum, gf_3, saved, weights, gains, block_in, source, vocab
):
    (q1, k1, v1, lse1, a1, h1, q2, k2, v2, block_out, h2, att_t, a2, lse2) = saved
    (sq, sk, sv, so, cq, ck, cv, co, wg, wu, wd) = weights

    def vm(*shape, dtype=BF16):
        return pltpu.VMEM(shape, dtype)

    def sems(copies):
        return [pltpu.SemaphoreType.DMA((copies,))] * 2

    def near(*arrays):
        return [(a, False) for a in arrays]

    def far(*arrays):
        return [(a, True) for a in arrays]

    block, pair = (ROWS, D), (TGT, D)
    half_t = (HALF_D, ROWS)
    e_half, f_half, c_half = 4096, 3 * FF // 2, 2 * D

    def scratch_1(copies):
        return [
            vm(2, HTILE, TGT), vm(2, HTILE, TGT), vm(2, 3, 512, D), vm(2, 3, HALF_D, 512, dtype=F32),
            vm(2, 3, HALF_D, 512), vm(16, HALF_D, 512), vm(2, 192, e_half, dtype=F32),
            vm(2, 192, e_half), vm(2, 192, e_half), vm(D, ROWS), vm(D, ROWS),
            vm(*half_t), vm(*half_t), vm(*half_t), vm(*half_t), vm(*block, dtype=F32),
            vm(*block), *[vm(HALF_D, TGT)] * 4, *sems(copies),
            pltpu.SemaphoreType.DMA((2, 2)), pltpu.SemaphoreType.DMA((2, 3)),
        ]

    outs = near(
        whole((2, 96, e_half), F32), whole((2, 96, e_half), BF16),
        whole((2, 192, f_half), F32), whole((2, 192, f_half), BF16),
        whole(block, F32), whole(block, BF16), whole(block, BF16), whole(block, BF16),
        whole((16, ROWS), F32), whole((16, ROWS), F32), whole((2, D), F32),
    )
    e_keep, e_send, f_keep, f_send, res2, rows2, gatt, gatt_o, dots, dots_o, gg_a = fused_call(
        table_ff_kernel, 1,
        near(scal) + far(g_a, g_b) + near(fin_a, fin_b, gf_sum, gf_3)
        + near(block_out, h2, gains) + far(wg, wu, wd) + near(co, att_t),
        outs, scratch_1, 24, 40e9,
    )

    def scratch_2(copies):
        return [
            vm(*pair), vm(16, TGT, dtype=F32), vm(D, TGT, dtype=F32), vm(KEYS, D), vm(KEYS, D),
            vm(D, KEYS), vm(HALF_D, KEYS), vm(HALF_D, KEYS),
            vm(HALF_D, 4 * D, dtype=F32), vm(HALF_D, 4 * D), vm(HALF_D, 4 * D),
            vm(2, 192, f_half), vm(D, ROWS, dtype=F32), vm(D, ROWS), vm(D, ROWS),
            vm(D, ROWS), vm(*half_t), vm(*half_t), *sems(copies),
        ]

    outs = near(
        whole((KEYS, D), F32), whole(block, F32), whole(block, BF16), whole(block, BF16),
        whole(block, BF16), whole((1, D), F32),
        whole((2, 192, c_half), F32), whole((2, 192, c_half), BF16),
        whole((2, 96, f_half), F32), whole((2, 96, f_half), BF16),
    ) + far(whole((2, 96, e_half), BF16))
    (
        grad_source, res1, rows1, gatt1, gatt1_o, gg_b, c_keep, c_send, f_keep, f_send, e_recv,
    ) = fused_call(
        cross_kernel, 2,
        near(scal, q2, k2, v2, lse2, gatt, gatt_o, dots, dots_o, source, ck, cv, cq, so)
        + near(h1, gains, res2, rows2, a2) + far(e_send) + near(f_keep) + far(f_send),
        outs, scratch_2, 8, 40e9,
    )

    def scratch_3(copies):
        def two(width):
            return [vm(2, 96, width, dtype=F32), vm(2, 96, width), vm(2, 96, width)]

        return [
            vm(*pair), vm(D, TGT, dtype=F32), vm(*pair), vm(*pair), vm(D, ROWS), vm(D, ROWS),
            vm(*half_t), vm(*half_t), vm(1, D, dtype=F32),
            vm(HALF_D, 4 * D, dtype=F32), vm(HALF_D, 4 * D), vm(HALF_D, 4 * D),
            vm(4, 96, f_half // 2, dtype=F32), vm(2, 96, f_half),
            vm(2, 192, c_half), *two(c_half),
            vm(2, 192, c_half, dtype=F32), vm(2, 192, c_half), vm(2, 192, c_half),
            *two(c_half),
            vm(3, 96, f_half // 2), vm(3, 96, c_half // 2), vm(3, 96, c_half // 2),
            vm(5, 8, D, dtype=F32), vm(5, 8, D, dtype=F32), *sems(copies),
        ]

    def three(width):
        return whole((96, width), F32), whole((3, 96, width), BF16)

    grad_in, gain_sums, *threes = fused_call(
        self_kernel, 3,
        near(scal, q1, k1, v1, lse1, gatt1, gatt1_o, block_in, gains, sq, sk, sv)
        + near(res1, rows1, a1, gg_a, gg_b, f_keep) + far(f_send) + near(c_keep) + far(c_send),
        near(
            whole(block, F32), whole((8, D), F32),
            *three(f_half // 2), *three(c_half // 2), *three(c_half // 2),
        ),
        scratch_3, 32, 20e9,
    )
    wide, tall, ff_wide = whole((96, 192), F32), whole((192, 96), F32), whole((96, 512), F32)
    grad_embed, grad_in, *grads = pl.pallas_call(
        functools.partial(finish_kernel, vocab),
        out_shape=[
            whole((96, vocab), F32), whole(block, F32), wide, wide, wide, tall, wide, wide, wide, tall,
            ff_wide, ff_wide, ff_wide,
        ],
        scratch_shapes=[pltpu.VMEM((96, 192), F32)],
        compiler_params=pltpu.CompilerParams(vmem_limit_bytes=VMEM_LIMIT // 2),
    )(e_keep, e_recv, *threes, grad_in)
    grads[-1] = grads[-1].T
    grad_embed = grad_embed.T
    return grad_in, grad_source, gain_sums, grads, grad_embed


def logits_kernel(vocab, flat_ref, table_ref, target_ref, logits_ref, stats_ref):
    tile = pl.program_id(0)

    @pl.when(tile == 0)
    def _():
        row = lax.broadcasted_iota(jnp.int32, stats_ref.shape, 0)
        stats_ref[...] = jnp.where(row == 0, 2 * NEG, 0.0)

    logits = dot_nn(table_ref[...], flat_ref[...])
    entry = tile * HTILE + lax.broadcasted_iota(jnp.int32, logits.shape, 0)
    logits = jnp.where(entry < vocab, logits, 2 * NEG)
    logits_ref[...] = logits
    old = stats_ref[0:1, :]
    new = jnp.maximum(old, jnp.max(logits, axis=0, keepdims=True))
    stats_ref[1:2, :] = stats_ref[1:2, :] * jnp.exp(old - new) + jnp.sum(
        jnp.exp(logits - new), axis=0, keepdims=True
    )
    stats_ref[0:1, :] = new
    hit = jnp.where(entry == target_ref[...], logits, 0.0)
    stats_ref[2:3, :] += jnp.sum(hit, axis=0, keepdims=True)


def head_logits(flat, table, target):
    count = flat.shape[1]
    vocab = table.shape[0]
    tiles = pl.cdiv(vocab, HTILE)
    return pl.pallas_call(
        functools.partial(logits_kernel, vocab),
        grid=(tiles,),
        out_shape=[whole((tiles * HTILE, count), F32), whole((8, count), F32)],
        in_specs=[
            pl.BlockSpec((D, count), lambda i: (0, 0)),
            pl.BlockSpec((HTILE, D), lambda i: (i, 0)),
            pl.BlockSpec((1, count), lambda i: (0, 0)),
        ],
        out_specs=[
            pl.BlockSpec((HTILE, count), lambda i: (i, 0)),
            pl.BlockSpec((8, count), lambda i: (0, 0)),
        ],
        cost_estimate=pl.CostEstimate(
            flops=2 * count * vocab * D, bytes_accessed=vocab * (2 * D + 4 * count), transcendentals=0
        ),
        compiler_params=pltpu.CompilerParams(vmem_limit_bytes=VMEM_LIMIT // 2),
    )(flat, table, target)


def grads_kernel(vocab, logits_ref, table_ref, target_ref, lse_ref, live_ref, g_ref, gf_ref, acc_ref):
    tile = pl.program_id(0)

    @pl.when(tile == 0)
    def _():
        acc_ref[...] = jnp.zeros_like(acc_ref)

    entry = tile * HTILE + lax.broadcasted_iota(jnp.int32, logits_ref.shape, 0)
    hit = jnp.where(entry == target_ref[...], 1.0, 0.0)
    grad = jnp.where(live_ref[...] > 0, jnp.exp(logits_ref[...] - lse_ref[...]) - hit, 0.0)
    grad = grad.astype(BF16)
    g_ref[...] = grad
    entry = tile * HTILE + lax.broadcasted_iota(jnp.int32, (HTILE, D), 0)
    table = jnp.where(entry < vocab, table_ref[...], jnp.zeros_like(table_ref[...]))
    acc_ref[...] += lax.dot_general(
        grad, table, (((0,), (0,)), ((), ())), preferred_element_type=F32
    )

    @pl.when(tile == pl.num_programs(0) - 1)
    def _():
        gf_ref[...] = acc_ref[...].astype(gf_ref.dtype)


def head_grads(logits, table, target, lse, live, dtype):
    count = logits.shape[1]
    vocab = table.shape[0]
    tiles = pl.cdiv(vocab, HTILE)
    row = pl.BlockSpec((1, count), lambda i: (0, 0))
    return pl.pallas_call(
        functools.partial(grads_kernel, vocab),
        grid=(tiles,),
        out_shape=[whole((tiles * HTILE, count), BF16), whole((count, D), dtype)],
        in_specs=[
            pl.BlockSpec((HTILE, count), lambda i: (i, 0)),
            pl.BlockSpec((HTILE, D), lambda i: (i, 0)),
            row,
            row,
            row,
        ],
        out_specs=[
            pl.BlockSpec((HTILE, count), lambda i: (i, 0)),
            pl.BlockSpec((count, D), lambda i: (0, 0)),
        ],
        scratch_shapes=[pltpu.VMEM((count, D), F32)],
        cost_estimate=pl.CostEstimate(
            flops=2 * count * vocab * D, bytes_accessed=vocab * (2 * D + 6 * count), transcendentals=0
        ),
        compiler_params=pltpu.CompilerParams(vmem_limit_bytes=VMEM_LIMIT // 2),
    )(logits, table, target, lse, live)


def table_kernel(fm_a, fm_b, fs_a, fs_b, g_a, g_b, mine_ref, send_ref):
    first, second = g_a[...], g_b[...]
    mine_ref[...] = dot_nt(fm_a[...], first) + dot_nt(fm_b[...], second)
    send_ref[...] = (dot_nt(fs_a[...], first) + dot_nt(fs_b[...], second)).astype(BF16)


def table_grads(flat_a, flat_b, g_a, g_b):
    width, count = g_a.shape
    left = pl.BlockSpec((HALF_D, count), lambda i: (0, 0))
    right = pl.BlockSpec((HTILE, count), lambda i: (i, 0))
    out = pl.BlockSpec((HALF_D, HTILE), lambda i: (0, i))
    return pl.pallas_call(
        table_kernel,
        grid=(width // HTILE,),
        out_shape=[whole((HALF_D, width), F32), whole((HALF_D, width), BF16)],
        in_specs=[left] * 4 + [right] * 2,
        out_specs=[out] * 2,
        cost_estimate=pl.CostEstimate(
            flops=4 * count * width * D, bytes_accessed=width * (4 * count + 6 * HALF_D), transcendentals=0
        ),
        compiler_params=pltpu.CompilerParams(vmem_limit_bytes=VMEM_LIMIT),
    )(flat_a[0], flat_b[0], flat_a[1], flat_b[1], g_a, g_b)


def make(mesh):
    dp_size = mesh.shape["dp"]
    split = dp_size == 8

    def on_device(
        block_in,
        source,
        target_len,
        source_len,
        targets,
        gain_self,
        gain_cross,
        gain_ff,
        gain_final,
        self_q,
        self_k,
        self_v,
        self_o,
        cross_q,
        cross_k,
        cross_v,
        cross_o,
        ff_gate,
        ff_up,
        ff_down,
        embed_table,
    ):
        z = lax.axis_index("tensor")
        dp = lax.axis_index("dp")
        half = lax.rem(z, 2)
        seq = z // 2
        core = lax.rem(dp, 2)
        gains = jnp.stack([gain_self, gain_cross, gain_ff, gain_final])
        gain_self, gain_cross, gain_ff, gain_final = (gains[i : i + 1] for i in range(4))

        def pair_swap(value):
            return swap(value, "tensor", 4, 1)

        scal = jnp.stack(
            [
                half,
                lax.dynamic_index_in_dim(target_len, seq, keepdims=False),
                lax.dynamic_index_in_dim(source_len, seq, keepdims=False),
                core,
            ]
        ).astype(jnp.int32)

        def vm(shape, dtype):
            return pltpu.VMEM(shape, dtype)

        pair = (TGT, D)
        weights = (
            self_q.T, self_k.T, self_v.T, self_o, cross_q.T, cross_k.T, cross_v.T, cross_o,
            ff_gate, ff_up, ff_down,
        )
        vocab = embed_table.shape[0]
        if split:
            lens = jnp.concatenate([target_len, source_len])
            results = forward(True, lens, block_in, source, gains, weights)
            q1, k1, v1, lse1, a1, h1, q2, k2, v2, block_out, fin_t, h2, att_t, a2, lse2 = results[:15]
            g_a, g_b, gf_sum, gf_3, losses, fin_a, fin_b = fused_head(
                lens, fin_t, embed_table, targets.reshape(4, ROWS)
            )
            saved = (q1, k1, v1, lse1, a1, h1, q2, k2, v2, block_out, h2, att_t, a2, lse2)
            grad_block_in, grad_source, gain_sums, grads, grad_embed = fused_backward(
                lens, fin_a, fin_b, g_a, g_b, gf_sum, gf_3, saved, results[15:], gains,
                block_in, source, vocab,
            )
            return (
                block_out, losses.reshape(-1), grad_block_in, grad_source,
                gain_sums[3], gain_sums[2], gain_sums[1], gain_sums[0], *grads, grad_embed,
            )

        wide = [gather_wide(w.T if i in (8, 9) else w, dp_size) for i, w in enumerate(weights)]
        sq, sk, sv, so, cq, ck, cv, co, wg, wu, wd = wide
        weights = jnp.stack([sq, sk, sv, so]), jnp.stack([cq, ck, cv, co]), wg, wu, wd
        results = forward(False, scal, block_in, source, gains, weights)
        q1, k1, v1, lse1, a1, h1, q2, k2, v2, block_out, fin, h2, att_t, a2, lse2 = results
        fin = fin.T

        vocab = embed_table.shape[0]

        def block(by_block, j, axis=0):
            return lax.dynamic_index_in_dim(by_block, z ^ j, axis, keepdims=False)

        tgt_local = targets - z * vocab
        tgt_local = jnp.where((tgt_local >= 0) & (tgt_local < vocab), tgt_local, -1)
        tgt_blocks = tgt_local.reshape(4, ROWS)
        position = lax.rem(jnp.arange(4 * ROWS), TGT)
        live = position < jnp.repeat(target_len, TGT, total_repeat_length=4 * ROWS)
        live_blocks = live.astype(jnp.int32).reshape(4, ROWS)
        fin_1, fin_2, fin_3 = (swap(fin, "tensor", 4, j) for j in (1, 2, 3))
        fin_a = jnp.concatenate([fin_2, fin_3], 0).T
        fin_b = jnp.concatenate([fin, fin_1], 0).T

        def columns(by_block, order):
            return jnp.concatenate([block(by_block, j) for j in order], 0)[None, :]

        tgt_a, tgt_b = columns(tgt_blocks, (2, 3)), columns(tgt_blocks, (0, 1))
        logits_b, stats_b = head_logits(fin_b, embed_table, tgt_b)
        logits_a, stats_a = head_logits(fin_a, embed_table, tgt_a)
        stats = [stats_b[:, :ROWS], stats_b[:, ROWS:], stats_a[:, :ROWS], stats_a[:, ROWS:]]
        stats = jnp.stack(stats, 0)
        stats = jnp.stack([block(stats, j) for j in range(4)], 0)
        others = [stats] + [swap(stats, "tensor", 4, j) for j in (1, 2, 3)]

        def over_z(values, op):
            return op(op(values[0], values[1]), op(values[2], values[3]))

        top = over_z([s[:, 0] for s in others], jnp.maximum)
        total = over_z([s[:, 1] * jnp.exp(s[:, 0] - top) for s in others], jnp.add)
        picked = over_z([s[:, 2] for s in others], jnp.add)
        g_lse = top + jnp.log(total)
        token_loss = jnp.where(live, (g_lse - picked).reshape(-1), 0.0)
        g_a, gf_a = head_grads(
            logits_a, embed_table, tgt_a, columns(g_lse, (2, 3)), columns(live_blocks, (2, 3)), BF16
        )
        gf_2 = swap(gf_a[:ROWS], "tensor", 4, 2)
        g_b, gf_b = head_grads(
            logits_b, embed_table, tgt_b, columns(g_lse, (0, 1)), columns(live_blocks, (0, 1)), F32
        )
        g_b, gf_b, gf_2, gf_a = lax.optimization_barrier((g_b, gf_b, gf_2, gf_a))
        def halves(flat):
            return flat[:HALF_D], flat[HALF_D:]

        gf_3 = swap(gf_a[ROWS:], "tensor", 4, 3)
        gf_1 = swap(gf_b[ROWS:].astype(BF16), "tensor", 4, 1)
        e_mine, e_send = table_grads(halves(fin_a), halves(fin_b), g_a, g_b)
        e_sum = WideReduction(z, e_mine[:, :vocab], e_send[:, :vocab])

        half_t = (HALF_D, ROWS)
        ff_mine, ff_send, res2, rows2, gatt, dots, gg_a = local_call(
            functools.partial(ff_backward, False),
            [whole((HALF_D, 3 * FF), F32), whole((HALF_D, 3 * FF), BF16), whole((ROWS, D), F32)]
            + [whole((ROWS, D), BF16)] * 2
            + [whole((16, ROWS), F32), whole((2, D), F32)],
            [vm((D, ROWS), BF16)] * 2 + [vm(half_t, BF16)] * 4
            + [vm((ROWS, D), F32)],
            10e9,
            scal, gf_b[:ROWS], gf_1, gf_2, gf_3, block_out, h2,
            gain_ff, gain_final, wg, wu, wd, co, att_t,
        )
        ff_sum = WideReduction(z, ff_mine, ff_send)
        gatt_other, dots_other = pair_swap(gatt), pair_swap(dots)
        dk2, dv2, dq_own, dq_send = local_call(
            functools.partial(cross_backward, split),
            [whole((KEYS, D), BF16)] * 2 + [whole((D, ROWS), F32), whole((D, ROWS), BF16)],
            [vm(pair, BF16), vm((16, TGT), F32), vm((D, TGT), F32)],
            20e9,
            scal, q2, k2, v2, lse2, gatt, gatt_other, dots, dots_other,
        )
        dq_other = pair_swap(dq_send)
        grad_source, kv_mine, kv_send = local_call(
            functools.partial(source_backward, split),
            [whole((KEYS, D), F32), whole((HALF_D, 2 * D), F32), whole((HALF_D, 2 * D), BF16)],
            [vm((D, KEYS), BF16)] + [vm((HALF_D, KEYS), BF16)] * 2,
            5e9,
            scal, dk2, dv2, source, ck, cv,
        )
        c_mine, c_send, res1, rows1, gatt1, gg_b = local_call(
            functools.partial(query_backward, split),
            [whole((HALF_D, 4 * D), F32), whole((HALF_D, 4 * D), BF16), whole((ROWS, D), F32)]
            + [whole((ROWS, D), BF16)] * 2 + [whole((1, D), F32)],
            [vm((D, ROWS), BF16)] * 2 + [vm(half_t, BF16)] * 2 + [vm((D, ROWS), F32)],
            2e9,
            scal, dq_own, dq_other, h1, gain_cross, cq, res2, rows2, a2, so,
            kv_mine, kv_send,
        )
        c_sum = WideReduction(z, c_mine, c_send)
        gatt1_other = pair_swap(gatt1)
        s_mine, s_send, grad_block_in, gg_c = local_call(
            functools.partial(self_backward, split),
            [whole((HALF_D, 4 * D), F32), whole((HALF_D, 4 * D), BF16)]
            + [whole((ROWS, D), F32), whole((1, D), F32)],
            [vm(pair, BF16), vm((D, TGT), F32), vm(pair, BF16), vm(pair, BF16)]
            + [vm((D, ROWS), BF16)] * 2 + [vm(half_t, BF16)] * 2,
            12e9,
            scal, q1, k1, v1, lse1, gatt1, gatt1_other, block_in, gain_self, sq, sk, sv,
            res1, rows1, a1,
        )
        s_sum = WideReduction(z, s_mine, s_send)
        gains = jnp.concatenate([gg_a, gg_b, gg_c], 0)
        gains = lax.psum(gains, ("dp", "tensor"))
        grad_embed = e_sum.table(vocab)
        ff_grads = ff_sum.last(3, (2,))
        c_grads = c_sum.last(4, (3,))
        s_grads = s_sum.last(4, (3,))

        return (
            block_out,
            token_loss,
            grad_block_in,
            grad_source,
            gains[3],
            gains[2],
            gains[1],
            gains[0],
            *s_grads,
            *c_grads,
            *ff_grads,
            grad_embed,
        )

    return on_device


def solution(mesh):
    rows = P(("dp", "tensor"), None)
    wide, tall = P(None, "tensor"), P("tensor", None)
    in_specs = (rows, rows) + (P("dp"),) * 3 + (P(),) * 4
    in_specs += (wide, wide, wide, tall) * 2 + (wide, wide, tall, tall)
    g_in, g_out = P("dp", "tensor"), P("tensor", "dp")
    out_specs = (rows, P("dp"), rows, rows) + (P(),) * 4
    out_specs += (g_in, g_in, g_in, g_out) * 2 + (g_in, g_in, g_out, g_out)
    return jax.shard_map(
        make(mesh), mesh=mesh, in_specs=in_specs, out_specs=out_specs, check_vma=False
    )
```

```python
import functools
import math

import jax
import jax.numpy as jnp
from jax import lax
from jax.sharding import PartitionSpec as P
from jax.experimental import pallas as pl
from jax.experimental.pallas import tpu as pltpu

D = 768
HDIM = 64
NHEAD = D // HDIM
PAIRS = NHEAD // 2
FF = 2048
TGT = 512
ROWS = 256
KEYS = 1024
CHUNK = 256
HALF_D = D // 2
VTILE = 512
HTILE = 1024
F32 = jnp.float32
BF16 = jnp.bfloat16
MESH_ID = pl.DeviceIdType.MESH
VMEM_LIMIT = 56 * 2**20
FUSED_LIMIT = 62 * 2**20
NEG = -1000000000.0
SCALE = HDIM ** (-0.5)
EPS = 1e-06


def dot_nt(left, right):
    return lax.dot_general(left, right, (((1,), (1,)), ((), ())), preferred_element_type=F32)


def dot_nn(left, right):
    return lax.dot_general(left, right, (((1,), (0,)), ((), ())), preferred_element_type=F32)


def swap(value, axis_name, size, bit):
    return lax.ppermute(value, axis_name, [(i, i ^ bit) for i in range(size)])


class Gather:
    def __init__(self, links, refs, used):
        self.links, self.refs, self.used = links, refs, used
        self.last = []

    def piece(self, ref, shard, owner, part=None):
        if len(ref.shape) == 2:
            rows = ref.shape[0] // 32
            base = shard * 8 * rows + owner * rows
        else:
            rows = ref.shape[1] // 8
            base = shard * 2 * rows + lax.rem(owner, 2) * rows
        start, count = (0, rows) if part is None else (part * rows // 2, rows // 2)
        where = pl.ds(pl.multiple_of(base + start, 16), count)
        return ref.at[where] if len(ref.shape) == 2 else ref.at[owner // 2, where]

    def send(self, part, peer):
        send_sem, recv_sem = self.links["sems"]
        sem = self.used[0]
        self.used[0] += 1
        copy = pltpu.make_async_remote_copy(
            src_ref=part,
            dst_ref=part,
            send_sem=send_sem.at[sem],
            recv_sem=recv_sem.at[sem],
            device_id={"dp": peer[0], "tensor": peer[1]},
            device_id_type=MESH_ID,
        )
        copy.start()
        return copy

    def along_z(self):
        links = self.links
        self.z_copies = [
            self.send(self.piece(ref, links["z"], links["dp"]), peer)
            for ref in self.refs
            for peer in links["z_peers"]
        ]

    def along_xy(self):
        links = self.links
        for copy in self.z_copies:
            copy.wait()
        self.x_copies, self.y_copies = [], []
        for ref in self.refs:
            for _, shard in links["z_peers"]:
                part = self.piece(ref, shard, links["dp"])
                self.x_copies.append(self.send(part, links["x"]))
                self.y_copies.append(self.send(part, links["y"]))
                self.last.append(self.send(part, links["core"]))

    def diagonal(self):
        links = self.links
        self.d_copies = []
        at = 0
        for ref in self.refs:
            for _, shard in links["z_peers"]:
                self.x_copies[at].wait()
                self.d_copies.append(self.send(self.piece(ref, shard, links["x"][0], 0), links["y"]))
                self.y_copies[at].wait()
                self.d_copies.append(self.send(self.piece(ref, shard, links["y"][0], 1), links["x"]))
                for owner in (links["x"][0], links["y"][0]):
                    self.last.append(self.send(self.piece(ref, shard, owner), links["core"]))
                at += 1

    def finish(self):
        links = self.links
        for copy in self.d_copies:
            copy.wait()
        for ref in self.refs:
            for _, shard in links["z_peers"]:
                self.last.append(self.send(self.piece(ref, shard, links["xy"]), links["core"]))
        for copy in self.last:
            copy.wait()


def gather_wide(shard, dp_size):
    rows = shard.shape[0] // dp_size
    part = lax.dynamic_slice_in_dim(shard, lax.axis_index("dp") * rows, rows, 0)
    return lax.all_gather(part, ("tensor", "dp"), axis=0, tiled=True)


def block_rows(index):
    return pl.ds(pl.multiple_of(index * 96, 96), 96)


class Comm:
    def __init__(self, send_sem, recv_sem):
        self.send_sem, self.recv_sem, self.used = send_sem, recv_sem, 0
        dp, z = lax.axis_index("dp"), lax.axis_index("tensor")
        self.z = z
        self.c, self.x, self.y = lax.rem(dp, 2), lax.rem(dp // 2, 2), dp // 4
        low, high = lax.rem(z, 2), z // 2
        self.core_peer = (dp + 1 - 2 * self.c, z)
        self.x_peer = (dp + 2 - 4 * self.x, z)
        self.y_peer = (dp + 4 - 8 * self.y, z)
        self.z_shards = (high * 2 + 1 - low, (1 - high) * 2 + low, (1 - high) * 2 + 1 - low)
        self.z_peers = [(dp, shard) for shard in self.z_shards]

    def barrier(self):
        barrier = pltpu.get_barrier_semaphore()
        peers = [self.core_peer, self.x_peer, self.y_peer] + self.z_peers
        for peer in peers:
            pl.semaphore_signal(
                barrier, inc=1, device_id={"dp": peer[0], "tensor": peer[1]}, device_id_type=MESH_ID
            )
        pl.semaphore_wait(barrier, len(peers))

    def copy(self, src, dst, peer, index):
        return pltpu.make_async_remote_copy(
            src_ref=src,
            dst_ref=dst,
            send_sem=self.send_sem.at[index],
            recv_sem=self.recv_sem.at[index],
            device_id={"dp": peer[0], "tensor": peer[1]},
            device_id_type=MESH_ID,
        )

    def reserve(self, count):
        self.used += count
        return self.used - count

    def send(self, src, dst, peer):
        copy = self.copy(src, dst, peer, self.reserve(1))
        copy.start()
        return copy


def fold_one(comm, mine, got, keep, send, is_right):
    for other in range(2):
        rows = slice(other * 96, (other + 1) * 96)
        along_x, along_y = 2 * other + comm.x, 2 * comm.y + other
        stay = along_x * (1 - is_right) + along_y * is_right
        along_x, along_y = 2 * other + 1 - comm.x, 2 * (1 - comm.y) + other
        leave = along_x * (1 - is_right) + along_y * is_right
        stay, leave = block_rows(stay), block_rows(leave)
        keep[rows, :] = mine[stay, :] + got[stay, :].astype(F32)
        send[rows, :] = (mine[leave, :] + got[leave, :].astype(F32)).astype(BF16)


def fold_two(comm, mine, got, keep, send):
    for side, bit in enumerate((comm.y, comm.x)):
        stay, leave = block_rows(bit), block_rows(1 - bit)
        keep[side] = mine[side, stay, :] + got[side, stay, :].astype(F32)
        send[side] = (mine[side, leave, :] + got[side, leave, :].astype(F32)).astype(BF16)


class Flow:
    def __init__(self, comm, one, two, three):
        self.comm, self.one, self.two, self.three = comm, one, two, three
        self.copies = []

    def wait(self):
        for copy in self.copies:
            copy.wait()

    def from_core(self, mine, send, got):
        comm = self.comm
        self.copies = [comm.send(send, got, comm.core_peer)]
        self.mine, self.got = mine, got

    def fold_first(self):
        self.wait()
        keep, send, _ = self.one
        width = keep.shape[2]
        for side in range(2):
            cols = pl.ds(side * width, width)
            fold_one(
                self.comm, self.mine.at[:, cols], self.got.at[:, cols], keep.at[side], send.at[side], side
            )

    def send_first(self):
        comm = self.comm
        _, send, recv = self.one
        self.copies = [
            comm.send(send.at[0], recv.at[0], comm.x_peer),
            comm.send(send.at[1], recv.at[1], comm.y_peer),
        ]

    def fold_second(self):
        self.wait()
        fold_two(self.comm, self.one[0], self.one[2], self.two[0], self.two[1])

    def send_second(self):
        comm = self.comm
        _, send, recv = self.two
        self.copies = [
            comm.send(send.at[0], recv.at[0], comm.y_peer),
            comm.send(send.at[1], recv.at[1], comm.x_peer),
        ]

    def fold_third(self, shard_ref):
        self.wait()
        comm = self.comm
        (keep, _, recv), (keep3, send3, _) = self.two, self.three
        width = keep3.shape[1]
        for side in range(2):
            total = keep[side] + recv[side].astype(F32)
            shard_ref[2 * side, :, :width] = total[:, :width]
            shard_ref[2 * side + 1, :, :width] = total[:, width:]
        keep3[...] = shard_ref[comm.z, :, :width]
        for j, shard in enumerate(comm.z_shards):
            send3[j] = shard_ref[shard, :, :width].astype(BF16)

    def send_third(self):
        _, send3, recv3 = self.three
        peers = self.comm.z_peers
        self.copies = [self.comm.send(send3.at[j], recv3.at[j], peers[j]) for j in range(3)]


def finish_kernel(vocab, *refs):
    sources, (e_out, gin_out), refs = refs[:9], refs[9:11], refs[11:]
    refs, held, (sem, turn_ref) = refs[:11], refs[11:20], refs[20:]
    copies = [pltpu.make_async_copy(src, dst, sem.at[i]) for i, (src, dst) in enumerate(zip(sources, held))]
    for copy in copies:
        copy.start()
    for copy in copies:
        copy.wait()
    e_keep, e_recv, f_keep, f_recv, c_keep, c_recv, s_keep, s_recv, gin = held
    gin_out[...] = gin[...]
    width = e_keep.shape[2]
    for side in range(2):
        count = min(width, vocab - side * width)
        e_out[:, side * width : side * width + count] = e_keep[side, :, :count] + e_recv[
            side, :, :count
        ].astype(F32)
    for keep, recv, outs in ((f_keep, f_recv, refs[8:]), (c_keep, c_recv, refs[4:8]), (s_keep, s_recv, refs[:4])):
        width = keep.shape[1] // len(outs)
        for m, out in enumerate(outs):
            cols = slice(m * width, (m + 1) * width)
            part = keep[:, cols] + recv[0, :, cols].astype(F32)
            part = part + (recv[1, :, cols].astype(F32) + recv[2, :, cols].astype(F32))
            if out.shape[0] == 96:
                out[...] = part
            else:
                turn_ref[...] = part
                out[...] = turn_ref[...].T


class WideReduction:
    def __init__(self, z, mine, send):
        both = jnp.concatenate([mine, send.astype(F32)], 0)
        self.part = lax.psum_scatter(both, "dp", scatter_dimension=0, tiled=True)

    def last(self, count, flips):
        rows = self.part.shape[0]
        by_z = self.part.reshape(rows, 4, -1)
        total = lax.psum_scatter(by_z, "tensor", scatter_dimension=1, tiled=True)[:, 0]
        parts = jnp.split(total, count, axis=1)
        return [p.T if m in flips else p for m, p in enumerate(parts)]

    def table(self, vocab):
        return self.part.T


def rms_scale(values):
    return lax.rsqrt(jnp.mean(values * values, axis=-1, keepdims=True) + EPS)


def spots(scal, split):
    if split:
        z = lax.axis_index("tensor")
        half, core = lax.rem(z, 2), lax.rem(lax.axis_index("dp"), 2)
        return half, scal[z // 2], scal[2 + z // 2] - half * KEYS, core
    half, core = scal[0], scal[3]
    return half, scal[1], scal[2] - half * KEYS, core


def norm_back(values, inv_scale, gain, grad_out):
    weighted = gain * grad_out
    grad_gain = jnp.sum(grad_out * values * inv_scale, axis=0, keepdims=True)
    grad_values = inv_scale * weighted - values * inv_scale * inv_scale * inv_scale * jnp.mean(
        weighted * values, axis=-1, keepdims=True
    )
    return grad_values, grad_gain


def flip(value):
    return value.astype(F32).T


def lane_half(rows, which):
    lane = lax.broadcasted_iota(jnp.int32, (rows, 2 * HDIM), 1)
    return (lane >= HDIM) if which else (lane < HDIM)


def only(value, which):
    return jnp.where(lane_half(value.shape[0], which), value, jnp.zeros_like(value))


def split_rows(flat_ref, mine_ref, send_ref, core, split):
    for block in range(4):
        if split:
            first = pl.multiple_of((2 * block + core) * 96, 96)
            second = pl.multiple_of((2 * block + 1 - core) * 96, 96)
        else:
            first, second = block * 96, HALF_D + block * 96
        mine_ref[block * 96 : (block + 1) * 96, :] = flat_ref[pl.ds(first, 96), :]
        send_ref[block * 96 : (block + 1) * 96, :] = flat_ref[pl.ds(second, 96), :]


def by_shard(left_ref, rights, out_ref, first, per_shard):
    width = 192 * len(rights)
    for z in range(4):
        part = [right[:, z * 192 : (z + 1) * 192] for right in rights]
        right = jnp.concatenate(part, axis=1) if len(part) > 1 else part[0]
        start = z * per_shard + first
        out_ref[:, start : start + width] = dot_nn(left_ref[...], right).astype(out_ref.dtype)


def whole(shape, dtype):
    return jax.ShapeDtypeStruct(shape, dtype)


def local_call(body, outs, scratch, flops, *args):
    smem = pl.BlockSpec(memory_space=pltpu.SMEM)
    vmem = pl.BlockSpec(memory_space=pltpu.VMEM)
    bytes_all = sum(a.size * a.dtype.itemsize for a in args)
    bytes_all += sum(o.size * jnp.dtype(o.dtype).itemsize for o in outs)
    held = sum(math.prod(s.shape) * jnp.dtype(s.dtype).itemsize for s in scratch)
    return pl.pallas_call(
        body,
        out_shape=outs,
        in_specs=[smem] + [vmem] * (len(args) - 1),
        out_specs=[vmem] * len(outs),
        scratch_shapes=scratch,
        cost_estimate=pl.CostEstimate(
            flops=int(flops), bytes_accessed=int(bytes_all), transcendentals=0
        ),
        compiler_params=pltpu.CompilerParams(
            vmem_limit_bytes=min(VMEM_LIMIT, int(bytes_all + held + 16 * 2**20))
        ),
    )(*args)


def forward_kernel(split, *refs):
    (scal, x_own, source, gains), refs = refs[:4], refs[4:]
    gain_self, gain_cross, gain_ff, gain_final = (gains.at[i : i + 1] for i in range(4))
    shards, refs = refs[: 11 if split else 5], refs[11 if split else 5 :]
    (q1, k1, v1, lse1, att1, h1_out, q2, k2, v2), refs = refs[:9], refs[9:]
    (out_ref, fin_ref, h2_ref, att_t_ref, att2, lse2), refs = refs[:6], refs[6:]
    if split:
        copies_out, refs = refs[:11], refs[11:]
        (ws, wc, wg, wu, wd), refs = refs[:5], refs[5:]
    else:
        ws, wc, wg, wu, wd = shards
    (x_other, x_ref, n_ref, vt_ref, ot_ref, s_ref, o_send, o_other, lse_own, lse_other, mix_ref), refs = (
        refs[:11],
        refs[11:],
    )
    pair_send, pair_recv = refs[:2]
    dp = lax.axis_index("dp")
    z = lax.axis_index("tensor")
    low, high = lax.rem(z, 2), z // 2
    half = low
    live = scal[high] if split else scal[1]
    live_src = (scal[2 + high] if split else scal[2]) - low * KEYS
    z_peers = [(dp, high * 2 + 1 - low)]
    peers = z_peers
    if split:
        z_peers = z_peers + [(dp, (1 - high) * 2 + low), (dp, (1 - high) * 2 + 1 - low)]
        x_peer = dp + 2 - 4 * lax.rem(dp // 2, 2)
        y_peer = dp + 4 - 8 * (dp // 4)
        links = dict(
            dp=dp,
            z=z,
            z_peers=z_peers,
            x=(x_peer, z),
            y=(y_peer, z),
            xy=x_peer + y_peer - dp,
            core=(dp + 1 - 2 * lax.rem(dp, 2), z),
            sems=refs[2:4],
        )
        out_sem = refs[4]
        peers = z_peers + [links["x"], links["y"], links["core"]]
    barrier = pltpu.get_barrier_semaphore()
    for peer in peers:
        pl.semaphore_signal(
            barrier, inc=1, device_id={"dp": peer[0], "tensor": peer[1]}, device_id_type=MESH_ID
        )

    def exchange(index, src, dst):
        copy = pltpu.make_async_remote_copy(
            src_ref=src,
            dst_ref=dst,
            send_sem=pair_send.at[index],
            recv_sem=pair_recv.at[index],
            device_id={"dp": z_peers[0][0], "tensor": z_peers[0][1]},
            device_id_type=MESH_ID,
        )
        copy.start()
        return copy

    leaving = []
    if split:
        used = [0]
        groups = [Gather(links, refs_of, used) for refs_of in ([ws], [wc], [wg], [wu], [wd])]
        of_self, of_cross, of_gate, of_up, of_down = groups
        hid, fhid = D // 4, FF // 4

        def place_block(target, first):
            rows = pl.ds(pl.multiple_of(z * hid, 16), hid)
            for m in range(3):
                target[m, rows, :] = shards[first + m][...]
            target[3, rows, :] = shards[first + 3][...]

        def place_wide(target, shard, flipped):
            rows = pl.ds(pl.multiple_of(z * fhid, 16), fhid)
            target[rows, :] = flip(shard[...]).astype(BF16) if flipped else shard[...]

        def leave(first, parts):
            for i, part in enumerate(parts):
                copy = pltpu.make_async_copy(part, copies_out[first + i], out_sem.at[first + i])
                copy.start()
                leaving.append(copy)

        place_block(ws, 0)
        pl.semaphore_wait(barrier, len(peers))
        of_self.along_z()
    else:
        pl.semaphore_wait(barrier, len(peers))
    x_copy = exchange(0, x_own, x_other)
    if split:
        place_block(wc, 4)
        place_wide(wg, shards[8], True)
        place_wide(wu, shards[9], True)
        place_wide(wd, shards[10], False)
        of_self.along_xy()
        of_cross.along_z()
        of_self.diagonal()
        of_cross.along_xy()
        of_gate.along_z()
    x_copy.wait()
    own = pl.multiple_of(half * ROWS, ROWS)
    other = pl.multiple_of((1 - half) * ROWS, ROWS)
    x_ref[pl.ds(own, ROWS), :] = x_own[...].astype(F32)
    x_ref[pl.ds(other, ROWS), :] = x_other[...].astype(F32)
    lse1[...] = jnp.zeros_like(lse1)
    lse_own[...] = jnp.zeros_like(lse_own)
    if split:
        of_self.finish()
        leave(0, [ws.at[m] for m in range(4)])
    for i in range(2):
        rows = slice(i * ROWS, (i + 1) * ROWS)
        x = x_ref[rows, :]
        n = (x * rms_scale(x) * gain_self[...]).astype(BF16)
        n_ref[rows, :] = n
        q1[rows, :] = dot_nt(n, ws[0]).astype(BF16)
        k1[rows, :] = dot_nt(n, ws[1]).astype(BF16)
        v1[rows, :] = dot_nt(n, ws[2]).astype(BF16)
    vt_ref[:, :TGT] = dot_nt(ws[2], n_ref[...]).astype(BF16)
    if split:
        of_gate.along_xy()
        of_up.along_z()
    key = lax.broadcasted_iota(jnp.int32, (TGT, TGT), 0)
    query = lax.broadcasted_iota(jnp.int32, (TGT, TGT), 1)
    seen = (key <= query) & (key < live)

    def self_pairs(first, last):
        @pl.loop(first, last)
        def _(pair):
            lanes = pl.ds(pl.multiple_of(pair * 128, 128), 128)
            q_pair, k_pair = q1[:, lanes], k1[:, lanes]
            for which in range(2):
                head = 2 * pair + which
                feats = pl.ds(pl.multiple_of(head * HDIM, HDIM), HDIM)
                scores = jnp.where(seen, dot_nt(k_pair, only(q_pair, which)) * SCALE, NEG)
                top = jnp.max(scores, axis=0, keepdims=True)
                probs = jnp.exp(scores - top)
                total = jnp.sum(probs, axis=0, keepdims=True)
                lse1[pl.ds(head, 1), :] = top + jnp.log(total)
                ot_ref[feats, :] = dot_nn(vt_ref[feats, :TGT], probs.astype(BF16)) / total

    self_pairs(0, PAIRS // 2)
    if split:
        of_cross.diagonal()
    self_pairs(PAIRS // 2, PAIRS)
    if split:
        of_up.along_xy()
        of_down.along_z()
        of_gate.diagonal()
    for i in range(2):
        rows = slice(i * ROWS, (i + 1) * ROWS)
        att = flip(ot_ref[:, rows]).astype(BF16)
        n_ref[rows, :] = att
        x_ref[rows, :] = x_ref[rows, :] + dot_nn(att, ws[3])
    att1[...] = n_ref[pl.ds(own, ROWS), :]
    h1_out[...] = x_ref[pl.ds(own, ROWS), :]
    if split:
        of_cross.finish()
        leave(4, [wc.at[m] for m in range(4)])
    for i in range(2):
        rows = slice(i * ROWS, (i + 1) * ROWS)
        h1 = x_ref[rows, :]
        n = (h1 * rms_scale(h1) * gain_cross[...]).astype(BF16)
        q2[rows, :] = dot_nt(n, wc[0]).astype(BF16)
    for i in range(KEYS // CHUNK):
        rows = slice(i * CHUNK, (i + 1) * CHUNK)
        src = source[rows, :]
        k2[rows, :] = dot_nt(src, wc[1]).astype(BF16)
        v2[rows, :] = dot_nt(src, wc[2]).astype(BF16)
        vt_ref[:, rows] = dot_nt(wc[2], src).astype(BF16)
    if split:
        of_down.along_xy()
        of_up.diagonal()
        of_gate.finish()
        leave(8, [wg])
    chunk_key = lax.broadcasted_iota(jnp.int32, (CHUNK, TGT), 0)

    def cross_pairs(first, last):
        @pl.loop(first, last)
        def _(pair):
            lanes = pl.ds(pl.multiple_of(pair * 128, 128), 128)
            q_pair = q2[:, lanes]
            for which in range(2):
                head = 2 * pair + which
                feats = pl.ds(pl.multiple_of(head * HDIM, HDIM), HDIM)
                q_one = only(q_pair, which)
                top = jnp.full((1, TGT), 2 * NEG, F32)
                for i in range(KEYS // CHUNK):
                    rows = slice(i * CHUNK, (i + 1) * CHUNK)
                    scores = dot_nt(k2[rows, lanes], q_one) * SCALE
                    scores = jnp.where(chunk_key < live_src - i * CHUNK, scores, NEG)
                    s_ref[rows, :] = scores
                    top = jnp.maximum(top, jnp.max(scores, axis=0, keepdims=True))
                total = jnp.zeros((1, TGT), F32)
                out = jnp.zeros((HDIM, TGT), F32)
                for i in range(KEYS // CHUNK):
                    rows = slice(i * CHUNK, (i + 1) * CHUNK)
                    probs = jnp.exp(s_ref[rows, :] - top)
                    total = total + jnp.sum(probs, axis=0, keepdims=True)
                    out = out + dot_nn(vt_ref[feats, rows], probs.astype(BF16))
                lse_own[pl.ds(head, 1), :] = top + jnp.log(total)
                ot_ref[feats, :] = out / total

    cross_pairs(0, PAIRS // 2)
    o_send[: D // 2, :] = ot_ref[: D // 2, pl.ds(other, ROWS)].astype(BF16)
    pair_copies = [exchange(1, o_send.at[: D // 2], o_other.at[: D // 2])]
    if split:
        of_down.diagonal()
        of_up.finish()
        leave(9, [wu])
    cross_pairs(PAIRS // 2, PAIRS)
    o_send[D // 2 :, :] = ot_ref[D // 2 :, pl.ds(other, ROWS)].astype(BF16)
    pair_copies.append(exchange(2, o_send.at[D // 2 :], o_other.at[D // 2 :]))
    pair_copies.append(exchange(3, lse_own, lse_other))
    if split:
        of_down.finish()
        leave(10, [wd])
    for copy in pair_copies:
        copy.wait()

    first, second = lse_own[...], lse_other[...]
    top = jnp.maximum(first, second)
    lse2[...] = top + jnp.log(jnp.exp(first - top) + jnp.exp(second - top))
    lse = lse2[:, pl.ds(own, ROWS)]
    w_first = jnp.exp(lse_own[:, pl.ds(own, ROWS)] - lse)
    w_second = jnp.exp(lse_other[:, pl.ds(own, ROWS)] - lse)
    for head in range(NHEAD):
        feats = slice(head * HDIM, (head + 1) * HDIM)
        att_t_ref[feats, :] = (
            ot_ref[feats, pl.ds(own, ROWS)] * w_first[head : head + 1, :]
            + o_other[feats, :].astype(F32) * w_second[head : head + 1, :]
        )
    att = flip(att_t_ref[...]).astype(BF16)
    att2[...] = att
    h2 = h1_out[...] + dot_nn(att, wc[3])
    h2_ref[...] = h2
    n3 = (h2 * rms_scale(h2) * gain_ff[...]).astype(BF16)

    @pl.loop(0, FF // 512)
    def _(i):
        rows = pl.ds(pl.multiple_of(i * 512, 512), 512)
        gate = dot_nt(n3, wg[rows, :])
        up = dot_nt(n3, wu[rows, :])
        mix_ref[:, rows] = (jax.nn.gelu(gate, approximate=True) * up).astype(BF16)

    out = h2 + dot_nn(mix_ref[...], wd[...])
    out_ref[...] = out
    x_ref[:ROWS, :] = out * rms_scale(out) * gain_final[...] * D ** (-0.5)
    fin_ref[...] = x_ref[:ROWS, :].T.astype(BF16)
    for copy in leaving:
        copy.wait()


def forward(split, scal, x_own, source, gains, weights):
    pair = (TGT, D)
    block = (ROWS, D)
    outs = [whole(pair, BF16)] * 3 + [whole((16, TGT), F32), whole(block, BF16), whole(block, F32)]
    outs += [whole(pair, BF16)] + [whole((KEYS, D), BF16)] * 2
    outs += [whole(block, F32), whole((D, ROWS), BF16), whole(block, F32), whole((D, ROWS), F32)]
    outs += [whole(block, BF16), whole((16, TGT), F32)]
    vmem = pl.BlockSpec(memory_space=pltpu.VMEM)
    out_specs = [vmem] * len(outs)
    scratch = []
    if split:
        outs += [whole((D, D), BF16)] * 8 + [whole((FF, D), BF16)] * 3
        out_specs += [pl.BlockSpec(memory_space=pl.ANY)] * 11
        scratch += [pltpu.VMEM((4, D, D), BF16)] * 2 + [pltpu.VMEM((FF, D), BF16)] * 3
    scratch += [
        pltpu.VMEM(block, BF16),
        pltpu.VMEM(pair, F32),
        pltpu.VMEM(pair, BF16),
        pltpu.VMEM((D, KEYS), BF16),
        pltpu.VMEM((D, TGT), F32),
        pltpu.VMEM((KEYS, TGT), F32),
        pltpu.VMEM((D, ROWS), BF16),
        pltpu.VMEM((D, ROWS), BF16),
        pltpu.VMEM((16, TGT), F32),
        pltpu.VMEM((16, TGT), F32),
        pltpu.VMEM((ROWS, FF), BF16),
        pltpu.SemaphoreType.DMA((4,)),
        pltpu.SemaphoreType.DMA((4,)),
    ]
    if split:
        scratch += [pltpu.SemaphoreType.DMA((27 * 5,))] * 2 + [pltpu.SemaphoreType.DMA((11,))]
    args = (scal, x_own, source, gains, *weights)
    return pl.pallas_call(
        functools.partial(forward_kernel, split),
        out_shape=outs,
        in_specs=[pl.BlockSpec(memory_space=pltpu.SMEM)] + [vmem] * (len(args) - 1),
        out_specs=out_specs,
        scratch_shapes=scratch,
        cost_estimate=pl.CostEstimate(
            flops=int(80e9), bytes_accessed=int(6e7), transcendentals=0
        ),
        compiler_params=pltpu.CompilerParams(
            collective_id=0, has_side_effects=True, vmem_limit_bytes=VMEM_LIMIT
        ),
    )(*args)


def ff_backward(
    split, scal, gf_own, gf_1, gf_2, gf_3, block_out, h2_in, gain_ff, gain_final, wg, wu, wd,
    w_co, att_t, mine_ref, send_ref, res_ref, rows_ref, gatt_ref, dot_ref, gg_ref,
    flat_ref, flat_2, nm_ref, ns_ref, gm_ref, gs_ref, gn_ref,
):
    core = scal[3]
    grad = gf_own[...] + gf_1[...].astype(F32)
    grad = grad + (gf_2[...].astype(F32) + gf_3[...].astype(F32))
    out = block_out[...]
    res, gg_final = norm_back(out, rms_scale(out), gain_final[...], grad * D ** (-0.5))
    gg_ref[0:1, :] = gg_final
    rows_b = res.astype(BF16)
    res_ref[...] = res
    rows_ref[...] = rows_b
    flat_ref[...] = flip(rows_ref[...]).astype(BF16)
    split_rows(flat_ref, gm_ref, gs_ref, core, split)
    h2 = h2_in[...]
    scale3 = rms_scale(h2)
    n3 = (h2 * scale3 * gain_ff[...]).astype(BF16)
    rows_ref[...] = n3
    flat_2[...] = flip(rows_ref[...]).astype(BF16)
    split_rows(flat_2, nm_ref, ns_ref, core, split)
    gn_ref[...] = jnp.zeros_like(gn_ref)
    const = (2.0 / 3.141592653589793) ** 0.5

    @pl.loop(0, FF // 512)
    def _(i):
        start = pl.multiple_of(i * 512, 512)
        rows = pl.ds(start, 512)
        gate = dot_nt(n3, wg[rows, :])
        up = dot_nt(n3, wu[rows, :])
        square = gate * gate
        tanh = jnp.tanh(const * (gate + 0.044715 * gate * square))
        gelu = 0.5 * gate * (1.0 + tanh)
        slope = 0.5 * (1.0 + tanh) + 0.5 * gate * (1.0 - tanh * tanh) * const * (
            1.0 + 3.0 * 0.044715 * square
        )
        grad_mixed = dot_nt(rows_b, wd[rows, :])
        g_gate = (grad_mixed * up * slope).astype(BF16)
        g_up = (grad_mixed * gelu).astype(BF16)
        mixed = (gelu * up).astype(BF16)
        gn_ref[...] += dot_nn(g_gate, wg[rows, :]) + dot_nn(g_up, wu[rows, :])
        for m, (mine, send, right) in enumerate(
            ((nm_ref, ns_ref, g_gate), (nm_ref, ns_ref, g_up), (gm_ref, gs_ref, mixed))
        ):
            cols = pl.ds(pl.multiple_of(3 * start + m * 512, 512), 512)
            mine_ref[:, cols] = dot_nn(mine[...], right)
            send_ref[:, cols] = dot_nn(send[...], right).astype(BF16)

    step, gg_ff = norm_back(h2, scale3, gain_ff[...], gn_ref[...])
    gg_ref[1:2, :] = gg_ff
    res = res_ref[...] + step
    res_ref[...] = res
    rows_b = res.astype(BF16)
    rows_ref[...] = rows_b
    gatt_ref[...] = dot_nt(rows_b, w_co[...]).astype(BF16)
    gatt_t = dot_nt(w_co[...], rows_b).astype(BF16).astype(F32)
    dot_ref[...] = jnp.zeros_like(dot_ref)
    for head in range(NHEAD):
        feats = slice(head * HDIM, (head + 1) * HDIM)
        dot_ref[head : head + 1, :] = jnp.sum(gatt_t[feats, :] * att_t[feats, :], 0, keepdims=True)


def both_halves(half, own, other, target):
    target[pl.ds(pl.multiple_of(half * ROWS, ROWS), ROWS), :] = own[...]
    target[pl.ds(pl.multiple_of((1 - half) * ROWS, ROWS), ROWS), :] = other[...]


def cross_backward(
    split, scal, q2, k2, v2, lse, g_own, g_other, dot_own, dot_other,
    dk_ref, dv_ref, own_out, send_out, g_ref, dot_ref, dq_ref,
):
    half, _, live, _ = spots(scal, split)
    own = pl.multiple_of(half * ROWS, ROWS)
    other = pl.multiple_of((1 - half) * ROWS, ROWS)
    both_halves(half, g_own, g_other, g_ref)
    dot_ref[:, pl.ds(own, ROWS)] = dot_own[...]
    dot_ref[:, pl.ds(other, ROWS)] = dot_other[...]
    key = lax.broadcasted_iota(jnp.int32, (CHUNK, TGT), 0)

    @pl.loop(0, PAIRS)
    def _(pair):
        lanes = pl.ds(pl.multiple_of(pair * 128, 128), 128)
        q_pair, g_pair = q2[:, lanes], g_ref[:, lanes]
        for i in range(KEYS // CHUNK):
            rows = slice(i * CHUNK, (i + 1) * CHUNK)
            k_part, v_part = k2[rows, lanes], v2[rows, lanes]
            k_flip = flip(k_part).astype(BF16)
            grad_k = jnp.zeros((CHUNK, 128), F32)
            grad_v = jnp.zeros((CHUNK, 128), F32)
            for which in range(2):
                head = 2 * pair + which
                feats = pl.ds(pl.multiple_of(head * HDIM, HDIM), HDIM)
                q_one, g_one = only(q_pair, which), only(g_pair, which)
                scores = dot_nt(k_part, q_one) * SCALE
                scores = jnp.where(key < live - i * CHUNK, scores, NEG)
                probs = jnp.exp(scores - lse[pl.ds(head, 1), :])
                grad_p = dot_nt(v_part, g_one)
                grad_s = (probs * (grad_p - dot_ref[pl.ds(head, 1), :])).astype(BF16)
                grad_k = grad_k + dot_nn(grad_s, q_one)
                grad_v = grad_v + dot_nn(probs.astype(BF16), g_one)
                grad_q = dot_nn(k_flip[which * HDIM : (which + 1) * HDIM, :], grad_s)
                if i == 0:
                    dq_ref[feats, :] = grad_q
                else:
                    dq_ref[feats, :] += grad_q
            dk_ref[rows, lanes] = (grad_k * SCALE).astype(BF16)
            dv_ref[rows, lanes] = grad_v.astype(BF16)

    own_out[...] = dq_ref[:, pl.ds(own, ROWS)]
    send_out[...] = dq_ref[:, pl.ds(other, ROWS)].astype(BF16)


def source_backward(
    split, scal, dk, dv, source, w_ck, w_cv, gsrc_ref, mine_ref, send_ref, flat_ref, sm_ref, ss_ref
):
    for i in range(KEYS // CHUNK):
        rows = slice(i * CHUNK, (i + 1) * CHUNK)
        gsrc_ref[rows, :] = dot_nn(dk[rows, :], w_ck[...]) + dot_nn(dv[rows, :], w_cv[...])
        flat_ref[:, rows] = flip(source[rows, :]).astype(BF16)
    split_rows(flat_ref, sm_ref, ss_ref, spots(scal, split)[3], split)
    rights = (dk[...], dv[...])
    first, per_shard = (192, D) if split else (0, 384)
    by_shard(sm_ref, rights, mine_ref, first, per_shard)
    by_shard(ss_ref, rights, send_ref, first, per_shard)


def query_backward(
    split, scal, dq_own, dq_other, h1_in, gain_cross, w_cq, res_in, rows_in, att, w_so,
    kv_mine, kv_send, mine_ref, send_ref, res_ref, rows_ref, gatt_ref, gg_ref, flat_ref, flat_2, a_ref, b_ref, turn_ref,
):
    core = spots(scal, split)[3]
    turn_ref[...] = dq_own[...] + dq_other[...].astype(F32)
    dq = (turn_ref[...].T * SCALE).astype(BF16)
    h1 = h1_in[...]
    scale2 = rms_scale(h1)
    rows_ref[...] = (h1 * scale2 * gain_cross[...]).astype(BF16)
    flat_ref[...] = flip(rows_ref[...]).astype(BF16)
    split_rows(flat_ref, a_ref, b_ref, core, split)
    by_shard(a_ref, (dq,), mine_ref, 0, D)
    by_shard(b_ref, (dq,), send_ref, 0, D)
    step, gg = norm_back(h1, scale2, gain_cross[...], dot_nn(dq, w_cq[...]))
    gg_ref[...] = gg
    res = res_in[...] + step
    res_ref[...] = res
    rows_b = res.astype(BF16)
    rows_ref[...] = rows_b
    gatt_ref[...] = dot_nt(rows_b, w_so[...]).astype(BF16)
    flat_2[...] = flip(rows_in[...]).astype(BF16)
    split_rows(flat_2, a_ref, b_ref, core, split)
    by_shard(a_ref, (att[...],), mine_ref, 576, D)
    by_shard(b_ref, (att[...],), send_ref, 576, D)
    for z in range(0 if split else 4):
        cols = slice(z * D + 192, z * D + 576)
        mine_ref[:, cols] = kv_mine[:, z * 384 : (z + 1) * 384]
        send_ref[:, cols] = kv_send[:, z * 384 : (z + 1) * 384]


def self_backward(
    split, scal, q1, k1, v1, lse, g_own, g_other, x_own, gain_self, w_q, w_k, w_v, res_in, rows_in, att,
    mine_ref, send_ref, gin_ref, gg_ref,
    g_ref, dq_ref, dk_ref, dv_ref, flat_ref, flat_2, a_ref, b_ref, midway=None,
):
    half, live, _, core = spots(scal, split)
    own = pl.multiple_of(half * ROWS, ROWS)
    both_halves(half, g_own, g_other, g_ref)
    key = lax.broadcasted_iota(jnp.int32, (TGT, TGT), 0)
    query = lax.broadcasted_iota(jnp.int32, (TGT, TGT), 1)
    seen = (key <= query) & (key < live)

    @pl.loop(0, PAIRS)
    def _(pair):
        lanes = pl.ds(pl.multiple_of(pair * 128, 128), 128)
        q_pair, g_pair = q1[:, lanes], g_ref[:, lanes]
        k_pair, v_pair = k1[:, lanes], v1[:, lanes]
        k_flip = flip(k_pair).astype(BF16)
        grad_k = jnp.zeros((TGT, 128), F32)
        grad_v = jnp.zeros((TGT, 128), F32)
        for which in range(2):
            head = 2 * pair + which
            feats = pl.ds(pl.multiple_of(head * HDIM, HDIM), HDIM)
            q_one, g_one = only(q_pair, which), only(g_pair, which)
            scores = jnp.where(seen, dot_nt(k_pair, q_one) * SCALE, NEG)
            probs = jnp.exp(scores - lse[pl.ds(head, 1), :])
            grad_p = dot_nt(v_pair, g_one)
            row_dot = jnp.sum(probs * grad_p, axis=0, keepdims=True)
            grad_s = (probs * (grad_p - row_dot)).astype(BF16)
            grad_k = grad_k + dot_nn(grad_s, q_one)
            grad_v = grad_v + dot_nn(probs.astype(BF16), g_one)
            dq_ref[feats, :] = dot_nn(k_flip[which * HDIM : (which + 1) * HDIM, :], grad_s)
        dk_ref[:, lanes] = (grad_k * SCALE).astype(BF16)
        dv_ref[:, lanes] = grad_v.astype(BF16)

    if midway is not None:
        midway()
    dq = (flip(dq_ref[:, pl.ds(own, ROWS)]) * SCALE).astype(BF16)
    dk = dk_ref[pl.ds(own, ROWS), :]
    dv = dv_ref[pl.ds(own, ROWS), :]
    x = x_own[...].astype(F32)
    scale1 = rms_scale(x)
    grad_n = dot_nn(dq, w_q[...]) + dot_nn(dk, w_k[...]) + dot_nn(dv, w_v[...])
    step, gg = norm_back(x, scale1, gain_self[...], grad_n)
    gg_ref[...] = gg
    gin_ref[...] = res_in[...] + step
    g_ref[:ROWS, :] = (x * scale1 * gain_self[...]).astype(BF16)
    flat_ref[...] = flip(g_ref[:ROWS, :]).astype(BF16)
    split_rows(flat_ref, a_ref, b_ref, core, split)
    by_shard(a_ref, (dq, dk, dv), mine_ref, 0, D)
    by_shard(b_ref, (dq, dk, dv), send_ref, 0, D)
    flat_2[...] = flip(rows_in[...]).astype(BF16)
    split_rows(flat_2, a_ref, b_ref, core, split)
    by_shard(a_ref, (att[...],), mine_ref, 576, D)
    by_shard(b_ref, (att[...],), send_ref, 576, D)


def table_ff_kernel(*refs):
    (scal, g_a, g_b, fin_a, fin_b, gf_sum, gf_3), refs = refs[:7], refs[7:]
    (block_out, h2_in, gains, wg, wu, wd, w_co, att_t), refs = refs[:8], refs[8:]
    gain_ff, gain_final = gains.at[2:3], gains.at[3:4]
    (e_keep, e_send, f_keep, f_send, res_ref, rows_ref), refs = refs[:6], refs[6:]
    (gatt_ref, gatt_other, dot_ref, dot_other, gg_ref), refs = refs[:5], refs[5:]
    (ga_ring, gb_ring, w_ring, mine_ring, send_ring, got, e_keep1, e_send1, e_recv1), refs = (
        refs[:9],
        refs[9:],
    )
    (flat_ref, flat_2, nm_ref, ns_ref, gm_ref, gs_ref, gn_ref, gf_recv), refs = refs[:8], refs[8:]
    (fm_a, fm_b, fs_a, fs_b), refs = refs[:4], refs[4:]
    send_sem, recv_sem, load_sem, w_sem = refs
    comm = Comm(send_sem, recv_sem)
    core = comm.c

    def load(step):
        tile = lax.rem(step, 2) * 4 + step // 2
        rows = pl.ds(pl.multiple_of(tile * HTILE, HTILE), HTILE)
        slot = lax.rem(step, 2)
        return [
            pltpu.make_async_copy(src.at[rows], dst.at[slot], load_sem.at[slot, i])
            for i, (src, dst) in enumerate(((g_a, ga_ring), (g_b, gb_ring)))
        ]

    def load_weights(step):
        shard = lax.rem(step, 2) * 2 + step // 2
        rows = pl.ds(pl.multiple_of(shard * 512, 512), 512)
        slot = lax.rem(step, 2)
        return [
            pltpu.make_async_copy(src.at[rows], w_ring.at[slot, i], w_sem.at[slot, i])
            for i, src in enumerate((wg, wu, wd))
        ]

    for copy in load(0) + load_weights(0):
        copy.start()
    comm.barrier()
    gf_copies = [comm.send(gf_3, gf_recv, comm.z_peers[2])]
    split_rows(fin_a, fm_a, fs_a, core, True)
    split_rows(fin_b, fm_b, fs_b, core, True)
    e_core, e_line, f_core = comm.reserve(8), comm.reserve(8), comm.reserve(4)

    def core_copy(step):
        tile = lax.rem(step, 2) * 4 + step // 2
        return comm.copy(
            send_ring.at[lax.rem(step, 2), pl.ds(0, 2)],
            got.at[pl.ds(2 * tile, 2)],
            comm.core_peer,
            e_core + step,
        )

    def line_copy(step):
        side, column = lax.rem(step, 2), step // 2
        cols = pl.ds(pl.multiple_of(column * HTILE, HTILE), HTILE)
        peer = comm.x_peer[0] * (1 - side) + comm.y_peer[0] * side
        return comm.copy(
            e_send1.at[side, :, cols], e_recv1.at[side, :, cols], (peer, comm.z), e_line + step
        )

    @pl.loop(0, 9)
    def _(step):
        @pl.when(step < 8)
        def _():
            slot = lax.rem(step, 2)
            for copy in load(step):
                copy.wait()

            @pl.when(step < 7)
            def _():
                for copy in load(step + 1):
                    copy.start()

            @pl.when(step >= 2)
            def _():
                core_copy(step - 2).wait_send()

            for part in range(2):
                rows = slice(part * 512, (part + 1) * 512)
                first, second = ga_ring[slot, rows, :], gb_ring[slot, rows, :]
                mine_ring[slot, part] = dot_nt(fm_a[...], first) + dot_nt(fm_b[...], second)
                send_ring[slot, part] = (
                    dot_nt(fs_a[...], first) + dot_nt(fs_b[...], second)
                ).astype(BF16)
            core_copy(step).start()

        @pl.when(step > 0)
        def _():
            last = step - 1
            slot, side = lax.rem(last, 2), lax.rem(last, 2)
            tile = side * 4 + last // 2
            core_copy(last).wait_recv()
            for part in range(2):
                start = pl.multiple_of((last // 2) * HTILE + part * 512, 512)
                cols = pl.ds(start, 512)
                fold_one(
                    comm,
                    mine_ring.at[slot, part],
                    got.at[2 * tile + part],
                    e_keep1.at[side, :, cols],
                    e_send1.at[side, :, cols],
                    side,
                )
            line_copy(last).start()

    for step in (6, 7):
        core_copy(step).wait_send()
    for copy in gf_copies:
        copy.wait()

    grad = gf_sum[...] + gf_recv[...].astype(F32)
    out = block_out[...]
    res, gg_final = norm_back(out, rms_scale(out), gain_final[...], grad * D ** (-0.5))
    gg_ref[0:1, :] = gg_final
    res_ref[...] = res
    gatt_ref[...] = res.astype(BF16)
    flat_ref[...] = flip(gatt_ref[...]).astype(BF16)
    split_rows(flat_ref, gm_ref, gs_ref, core, True)
    h2 = h2_in[...]
    rows_ref[...] = (h2 * rms_scale(h2) * gain_ff[...]).astype(BF16)
    flat_2[...] = flip(rows_ref[...]).astype(BF16)
    split_rows(flat_2, nm_ref, ns_ref, core, True)
    gn_ref[...] = jnp.zeros_like(gn_ref)

    def ff_copy(step):
        return comm.copy(
            send_ring.at[lax.rem(step, 2)],
            got.at[pl.ds(3 * step, 3)],
            comm.core_peer,
            f_core + step,
        )

    @pl.loop(0, 5)
    def _(step):
        @pl.when(step < 4)
        def _():
            slot = lax.rem(step, 2)
            for copy in load_weights(step):
                copy.wait()

            @pl.when(step < 3)
            def _():
                for copy in load_weights(step + 1):
                    copy.start()

            @pl.when(step >= 2)
            def _():
                ff_copy(step - 2).wait_send()

            g_gate, g_up, mixed = ff_block(rows_ref, gatt_ref, gn_ref, w_ring.at[slot])
            for m, (mine, send, right) in enumerate(
                ((nm_ref, ns_ref, g_gate), (nm_ref, ns_ref, g_up), (gm_ref, gs_ref, mixed))
            ):
                mine_ring[slot, m] = dot_nn(mine[...], right)
                send_ring[slot, m] = dot_nn(send[...], right).astype(BF16)
            ff_copy(step).start()

        @pl.when(step > 0)
        def _():
            last = step - 1
            slot, side = lax.rem(last, 2), lax.rem(last, 2)
            ff_copy(last).wait_recv()
            for m in range(3):
                cols = pl.ds(pl.multiple_of((last // 2) * 1536 + m * 512, 512), 512)
                fold_one(
                    comm,
                    mine_ring.at[slot, m],
                    got.at[3 * last + m],
                    f_keep.at[side, :, cols],
                    f_send.at[side, :, cols],
                    side,
                )

    step, gg_ff = norm_back(h2_in[...], rms_scale(h2_in[...]), gain_ff[...], gn_ref[...])
    gg_ref[1:2, :] = gg_ff
    res = res_ref[...] + step
    res_ref[...] = res
    rows_b = res.astype(BF16)
    rows_ref[...] = rows_b
    gatt_ref[...] = dot_nt(rows_b, w_co[...]).astype(BF16)
    gatt_t = dot_nt(w_co[...], rows_b).astype(BF16).astype(F32)
    dot_ref[...] = jnp.zeros_like(dot_ref)
    for head in range(NHEAD):
        feats = slice(head * HDIM, (head + 1) * HDIM)
        dot_ref[head : head + 1, :] = jnp.sum(gatt_t[feats, :] * att_t[feats, :], 0, keepdims=True)
    pair_copies = [
        comm.send(gatt_ref, gatt_other, comm.z_peers[0]),
        comm.send(dot_ref, dot_other, comm.z_peers[0]),
    ]
    for step in (2, 3):
        ff_copy(step).wait_send()
    for step in range(8):
        line_copy(step).wait()
    fold_two(comm, e_keep1, e_recv1, e_keep, e_send)
    for copy in pair_copies:
        copy.wait()


def ff_block(n3_ref, grad_ref, gn_ref, weights):
    const = (2.0 / 3.141592653589793) ** 0.5
    wg, wu, wd = weights[0], weights[1], weights[2]
    n3 = n3_ref[...]
    gate = dot_nt(n3, wg)
    up = dot_nt(n3, wu)
    square = gate * gate
    tanh = jnp.tanh(const * (gate + 0.044715 * gate * square))
    gelu = 0.5 * gate * (1.0 + tanh)
    slope = 0.5 * (1.0 + tanh) + 0.5 * gate * (1.0 - tanh * tanh) * const * (
        1.0 + 3.0 * 0.044715 * square
    )
    grad_mixed = dot_nt(grad_ref[...], wd)
    g_gate = (grad_mixed * up * slope).astype(BF16)
    g_up = (grad_mixed * gelu).astype(BF16)
    gn_ref[...] += dot_nn(g_gate, wg) + dot_nn(g_up, wu)
    return g_gate, g_up, (gelu * up).astype(BF16)


def cross_kernel(*refs):
    (scal, q2, k2, v2, lse2, g_own, g_other, dot_own, dot_oth, source), refs = refs[:10], refs[10:]
    (w_ck, w_cv, w_cq, w_so, h1, gains, res_in, rows_in, att), refs = refs[:9], refs[9:]
    gain_cross = gains.at[1:2]
    (f_keep, f_send), refs = refs[:2], refs[2:]
    (gsrc, res_ref, rows_ref, gatt1, gatt1_other, gg_ref), refs = refs[:6], refs[6:]
    (c_keep, c_send, f_keep3, f_send3), refs = refs[:4], refs[4:]
    (g_ref, dot_ref, dq_ref, dk_ref, dv_ref, flat_ref, sm_ref, ss_ref), refs = refs[:8], refs[8:]
    (mine, send, got, f_recv, own_ref, go_ref, come_ref, flat2, a_ref, b_ref), refs = (
        refs[:10],
        refs[10:],
    )
    f_two, shard_ref, refs = refs[:3], refs[3], refs[4:]
    comm = Comm(*refs)
    comm.barrier()
    ff = Flow(comm, (f_keep, f_send, f_recv), f_two, (f_keep3, f_send3, None))
    ff.send_first()
    cross_backward(
        True, scal, q2, k2, v2, lse2, g_own, g_other, dot_own, dot_oth,
        dk_ref, dv_ref, own_ref, go_ref, g_ref, dot_ref, dq_ref,
    )
    dq_copy = comm.send(go_ref, come_ref, comm.z_peers[0])
    ff.fold_second()
    ff.send_second()
    source_backward(
        True, scal, dk_ref, dv_ref, source, w_ck, w_cv, gsrc, mine, send, flat_ref, sm_ref, ss_ref
    )
    dq_copy.wait()
    query_backward(
        True, scal, own_ref, come_ref, h1, gain_cross, w_cq, res_in, rows_in, att, w_so,
        None, None, mine, send, res_ref, rows_ref, gatt1, gg_ref, flat2, go_ref, a_ref, b_ref, dq_ref.at[:, :ROWS],
    )
    pair_copy = comm.send(gatt1, gatt1_other, comm.z_peers[0])
    cross = Flow(comm, (c_keep, c_send, None), None, None)
    cross.from_core(mine, send, got)
    cross.fold_first()
    ff.fold_third(shard_ref)
    pair_copy.wait()


def self_kernel(*refs):
    (scal, q1, k1, v1, lse1, g_own, g_other, x_own, gains, w_q, w_k, w_v), refs = (
        refs[:12],
        refs[12:],
    )
    gain_self = gains.at[0:1]
    (res_in, rows_in, att, gg_a, gg_b), refs = refs[:5], refs[5:]
    (f_send3, e_send, c_keep, c_send), refs = refs[:4], refs[4:]
    (gin_ref, gains_ref, f_recv3, c_keep3, c_recv3, s_keep3, s_recv3, e_recv), refs = refs[:8], refs[8:]
    (g_ref, dq_ref, dk_ref, dv_ref, flat_ref, flat_2, a_ref, b_ref, gain_ref), refs = refs[:9], refs[9:]
    (mine, send, got, shard_ref, shard_2), refs = refs[:5], refs[5:]
    (c_recv1, c_keep2, c_send2, c_recv2), refs = refs[:4], refs[4:]
    s_one, s_two, refs = refs[:3], refs[3:6], refs[6:]
    (c_send3, s_send3, gain_send, gain_recv), refs = refs[:4], refs[4:]
    c_three = c_keep3, c_send3, c_recv3
    s_three = s_keep3, s_send3, s_recv3
    comm = Comm(*refs)
    comm.barrier()
    cross = Flow(comm, (c_keep, c_send, c_recv1), (c_keep2, c_send2, c_recv2), c_three)
    ff = Flow(comm, None, None, (None, f_send3, f_recv3))
    own = Flow(comm, s_one, s_two, s_three)
    cross.send_first()
    ff.send_third()

    def midway():
        cross.fold_second()
        cross.send_second()

    self_backward(
        True, scal, q1, k1, v1, lse1, g_own, g_other, x_own, gain_self, w_q, w_k, w_v,
        res_in, rows_in, att, mine, send, gin_ref, gain_ref,
        g_ref, dq_ref, dk_ref, dv_ref, flat_ref, flat_2, a_ref, b_ref, midway,
    )
    own.from_core(mine, send, got)
    gains_ref[...] = jnp.zeros_like(gains_ref)
    gains_ref[0:2, :] = gg_a[...]
    gains_ref[2:3, :] = gg_b[...]
    gains_ref[3:4, :] = gain_ref[...]

    def gain_step(step, peer):
        gain_send[step] = gains_ref[...]
        return comm.send(gain_send.at[step], gain_recv.at[step], peer)

    def gain_done(step, copy):
        copy.wait()
        gains_ref[...] = gains_ref[...] + gain_recv[step]

    copy = gain_step(0, comm.core_peer)
    own.fold_first()
    own.send_first()
    gain_done(0, copy)
    copy = gain_step(1, comm.z_peers[0])
    cross.fold_third(shard_ref)
    cross.send_third()
    gain_done(1, copy)
    copy = gain_step(2, comm.x_peer)
    own.fold_second()
    own.send_second()
    e_copies = [
        comm.send(e_send.at[0], e_recv.at[0], comm.y_peer),
        comm.send(e_send.at[1], e_recv.at[1], comm.x_peer),
    ]
    gain_done(2, copy)
    copy = gain_step(3, comm.y_peer)
    own.fold_third(shard_2)
    own.send_third()
    gain_done(3, copy)
    copy = gain_step(4, comm.z_peers[1])
    ff.wait()
    cross.wait()
    gain_done(4, copy)
    own.wait()
    for copy in e_copies:
        copy.wait()


def head_kernel(vocab, *refs):
    (lens, fin_own, table, targets), refs = refs[:4], refs[4:]
    (g_a, g_b, gf_sum, gf_3, loss_ref, fin_a, fin_b), refs = refs[:7], refs[7:]
    (e_ref, l_ref, fin_recv, stats, stats_recv, ring, acc_ref, gf_send, gf_recv), refs = (
        refs[:9],
        refs[9:],
    )
    send_sem, recv_sem, e_sem, ring_sem = refs
    comm = Comm(send_sem, recv_sem)
    z = comm.z
    shards = (z,) + comm.z_shards
    load = pltpu.make_async_copy(table, e_ref.at[:vocab], e_sem.at[0])
    load.start()
    barrier = pltpu.get_barrier_semaphore()
    for peer in comm.z_peers:
        pl.semaphore_signal(
            barrier, inc=1, device_id={"dp": peer[0], "tensor": peer[1]}, device_id_type=MESH_ID
        )
    pl.semaphore_wait(barrier, 3)
    fin_copies = [comm.send(fin_own, fin_recv.at[j], comm.z_peers[j]) for j in range(3)]
    padded = e_ref.shape[0]
    if padded > vocab:
        e_ref[vocab:, :] = jnp.zeros((padded - vocab, D), BF16)
    load.wait()
    tiles = padded // HTILE
    local = []
    for shard in shards:
        target = targets[pl.ds(shard, 1), :] - z * vocab
        local.append(jnp.where(target < vocab, target, -1))
    entry = lax.broadcasted_iota(jnp.int32, (HTILE, ROWS), 0)

    for i in range(4):
        if i > 0:
            fin_copies[i - 1].wait()
        fin = fin_own if i == 0 else fin_recv.at[i - 1]
        lanes = slice((i % 2) * ROWS, (i % 2 + 1) * ROWS)
        (fin_b if i < 2 else fin_a)[:, lanes] = fin[...]
        row = lax.broadcasted_iota(jnp.int32, (8, ROWS), 0)
        stats[i] = jnp.where(row == 0, 2 * NEG, 0.0)

        @pl.loop(0, tiles)
        def _(tile):
            start = pl.multiple_of(tile * HTILE, HTILE)
            logits = dot_nn(e_ref[pl.ds(start, HTILE), :], fin[...])
            logits = jnp.where(entry < vocab - start, logits, 2 * NEG)
            l_ref[i, pl.ds(start, HTILE), :] = logits
            old = stats[i, 0:1, :]
            new = jnp.maximum(old, jnp.max(logits, axis=0, keepdims=True))
            stats[i, 1:2, :] = stats[i, 1:2, :] * jnp.exp(old - new) + jnp.sum(
                jnp.exp(logits - new), axis=0, keepdims=True
            )
            stats[i, 0:1, :] = new
            hit = jnp.where(entry == local[i] - start, logits, 0.0)
            stats[i, 2:3, :] += jnp.sum(hit, axis=0, keepdims=True)

    copies = [comm.send(stats, stats_recv.at[j], comm.z_peers[j]) for j in range(3)]
    for copy in copies:
        copy.wait()

    def over_z(values, op):
        return op(op(values[0], values[1]), op(values[2], values[3]))

    lse, live = [], []
    for i in range(4):
        parts = [stats.at[i]] + [stats_recv.at[k - 1, i ^ k] for k in (1, 2, 3)]
        top = over_z([p[0:1, :] for p in parts], jnp.maximum)
        total = over_z([p[1:2, :] * jnp.exp(p[0:1, :] - top) for p in parts], jnp.add)
        picked = over_z([p[2:3, :] for p in parts], jnp.add)
        lse.append(top + jnp.log(total))
        lane = lax.broadcasted_iota(jnp.int32, (1, ROWS), 1)
        live.append(lax.rem(shards[i], 2) * ROWS + lane < lens[shards[i] // 2])
        loss_ref[pl.ds(shards[i], 1), :] = jnp.where(live[i], lse[i] - picked, 0.0)

    gf_copies = []
    for i in (2, 1, 3, 0):
        target = g_b if i < 2 else g_a
        acc_ref[...] = jnp.zeros_like(acc_ref)

        def leave(tile):
            rows = pl.ds(pl.multiple_of(tile * HTILE, HTILE), HTILE)
            slot = lax.rem(tile, 2)
            return pltpu.make_async_copy(
                ring.at[slot], target.at[rows, pl.ds((i % 2) * ROWS, ROWS)], ring_sem.at[slot]
            )

        @pl.loop(0, tiles)
        def _(tile):
            start = pl.multiple_of(tile * HTILE, HTILE)

            @pl.when(tile >= 2)
            def _():
                leave(tile - 2).wait()

            hit = jnp.where(entry == local[i] - start, 1.0, 0.0)
            grad = jnp.exp(l_ref[i, pl.ds(start, HTILE), :] - lse[i]) - hit
            grad = jnp.where(live[i], grad, 0.0).astype(BF16)
            ring[lax.rem(tile, 2)] = grad
            leave(tile).start()
            acc_ref[...] += lax.dot_general(
                grad, e_ref[pl.ds(start, HTILE), :], (((0,), (0,)), ((), ())), preferred_element_type=F32
            )

        for tile in (tiles - 2, tiles - 1):
            leave(tile).wait()
        if i == 3:
            gf_3[...] = acc_ref[...].astype(BF16)
        elif i > 0:
            gf_send[i - 1] = acc_ref[...].astype(BF16)
            gf_copies.append(comm.send(gf_send.at[i - 1], gf_recv.at[i - 1], comm.z_peers[i - 1]))
    for copy in gf_copies:
        copy.wait()
    gf_sum[...] = acc_ref[...] + (gf_recv[0].astype(F32) + gf_recv[1].astype(F32))


def fused_head(lens, fin_t, table, targets):
    vocab = table.shape[0]
    padded = pl.cdiv(vocab, HTILE) * HTILE
    hbm, vmem = pl.BlockSpec(memory_space=pl.ANY), pl.BlockSpec(memory_space=pltpu.VMEM)
    grad = whole((padded, TGT), BF16)
    block = (ROWS, D)
    return pl.pallas_call(
        functools.partial(head_kernel, vocab),
        out_shape=[
            grad, grad, whole(block, F32), whole(block, BF16), whole((4, ROWS), F32),
            whole((D, TGT), BF16), whole((D, TGT), BF16),
        ],
        in_specs=[pl.BlockSpec(memory_space=pltpu.SMEM), vmem, hbm, vmem],
        out_specs=[hbm, hbm] + [vmem] * 5,
        scratch_shapes=[
            pltpu.VMEM((padded, D), BF16),
            pltpu.VMEM((4, padded, ROWS), F32),
            pltpu.VMEM((3, D, ROWS), BF16),
            pltpu.VMEM((4, 8, ROWS), F32),
            pltpu.VMEM((3, 4, 8, ROWS), F32),
            pltpu.VMEM((2, HTILE, ROWS), BF16),
            pltpu.VMEM(block, F32),
            pltpu.VMEM((2,) + block, BF16),
            pltpu.VMEM((2,) + block, BF16),
            pltpu.SemaphoreType.DMA((8,)),
            pltpu.SemaphoreType.DMA((8,)),
            pltpu.SemaphoreType.DMA((1,)),
            pltpu.SemaphoreType.DMA((2,)),
        ],
        compiler_params=pltpu.CompilerParams(
            collective_id=4, has_side_effects=True, vmem_limit_bytes=FUSED_LIMIT
        ),
    )(lens, fin_t, table, targets)


def fused_call(body, collective_id, ins, outs, scratch, copies, flops):
    hbm, vmem = pl.BlockSpec(memory_space=pl.ANY), pl.BlockSpec(memory_space=pltpu.VMEM)
    moved = sum(a.size * a.dtype.itemsize for a, _ in ins)
    return pl.pallas_call(
        body,
        out_shape=[shape for shape, _ in outs],
        in_specs=[pl.BlockSpec(memory_space=pltpu.SMEM)] + [hbm if far else vmem for _, far in ins[1:]],
        out_specs=[hbm if far else vmem for _, far in outs],
        scratch_shapes=scratch(copies),
        cost_estimate=pl.CostEstimate(
            flops=int(flops), bytes_accessed=int(moved), transcendentals=0
        ),
        compiler_params=pltpu.CompilerParams(
            collective_id=collective_id, has_side_effects=True, vmem_limit_bytes=FUSED_LIMIT
        ),
    )(*[a for a, _ in ins])


def fused_backward(
    scal, fin_a, fin_b, g_a, g_b, gf_sum, gf_3, saved, weights, gains, block_in, source, vocab
):
    (q1, k1, v1, lse1, a1, h1, q2, k2, v2, block_out, h2, att_t, a2, lse2) = saved
    (sq, sk, sv, so, cq, ck, cv, co, wg, wu, wd) = weights

    def vm(*shape, dtype=BF16):
        return pltpu.VMEM(shape, dtype)

    def sems(copies):
        return [pltpu.SemaphoreType.DMA((copies,))] * 2

    def near(*arrays):
        return [(a, False) for a in arrays]

    def far(*arrays):
        return [(a, True) for a in arrays]

    block, pair = (ROWS, D), (TGT, D)
    half_t = (HALF_D, ROWS)
    e_half, f_half, c_half = 4096, 3 * FF // 2, 2 * D

    def scratch_1(copies):
        return [
            vm(2, HTILE, TGT), vm(2, HTILE, TGT), vm(2, 3, 512, D), vm(2, 3, HALF_D, 512, dtype=F32),
            vm(2, 3, HALF_D, 512), vm(16, HALF_D, 512), vm(2, 192, e_half, dtype=F32),
            vm(2, 192, e_half), vm(2, 192, e_half), vm(D, ROWS), vm(D, ROWS),
            vm(*half_t), vm(*half_t), vm(*half_t), vm(*half_t), vm(*block, dtype=F32),
            vm(*block), *[vm(HALF_D, TGT)] * 4, *sems(copies),
            pltpu.SemaphoreType.DMA((2, 2)), pltpu.SemaphoreType.DMA((2, 3)),
        ]

    outs = near(
        whole((2, 96, e_half), F32), whole((2, 96, e_half), BF16),
        whole((2, 192, f_half), F32), whole((2, 192, f_half), BF16),
        whole(block, F32), whole(block, BF16), whole(block, BF16), whole(block, BF16),
        whole((16, ROWS), F32), whole((16, ROWS), F32), whole((2, D), F32),
    )
    e_keep, e_send, f_keep, f_send, res2, rows2, gatt, gatt_o, dots, dots_o, gg_a = fused_call(
        table_ff_kernel, 1,
        near(scal) + far(g_a, g_b) + near(fin_a, fin_b, gf_sum, gf_3)
        + near(block_out, h2, gains) + far(wg, wu, wd) + near(co, att_t),
        outs, scratch_1, 24, 40e9,
    )

    def scratch_2(copies):
        return [
            vm(*pair), vm(16, TGT, dtype=F32), vm(D, TGT, dtype=F32), vm(KEYS, D), vm(KEYS, D),
            vm(D, KEYS), vm(HALF_D, KEYS), vm(HALF_D, KEYS),
            vm(HALF_D, 4 * D, dtype=F32), vm(HALF_D, 4 * D), vm(HALF_D, 4 * D),
            vm(2, 192, f_half), vm(D, ROWS, dtype=F32), vm(D, ROWS), vm(D, ROWS),
            vm(D, ROWS), vm(*half_t), vm(*half_t),
            vm(2, 96, f_half, dtype=F32), vm(2, 96, f_half), vm(2, 96, f_half),
            vm(4, 96, f_half // 2, dtype=F32), *sems(copies),
        ]

    outs = near(
        whole((KEYS, D), F32), whole(block, F32), whole(block, BF16), whole(block, BF16),
        whole(block, BF16), whole((1, D), F32),
        whole((2, 192, c_half), F32), whole((2, 192, c_half), BF16),
        whole((96, f_half // 2), F32), whole((3, 96, f_half // 2), BF16),
    )
    (
        grad_source, res1, rows1, gatt1, gatt1_o, gg_b, c_keep, c_send, f_keep, f_send,
    ) = fused_call(
        cross_kernel, 2,
        near(scal, q2, k2, v2, lse2, gatt, gatt_o, dots, dots_o, source, ck, cv, cq, so)
        + near(h1, gains, res2, rows2, a2) + near(f_keep) + far(f_send),
        outs, scratch_2, 8, 40e9,
    )

    def scratch_3(copies):
        def two(width):
            return [vm(2, 96, width, dtype=F32), vm(2, 96, width), vm(2, 96, width)]

        return [
            vm(*pair), vm(D, TGT, dtype=F32), vm(*pair), vm(*pair), vm(D, ROWS), vm(D, ROWS),
            vm(*half_t), vm(*half_t), vm(1, D, dtype=F32),
            vm(HALF_D, 4 * D, dtype=F32), vm(HALF_D, 4 * D), vm(HALF_D, 4 * D),
            vm(4, 96, c_half // 2, dtype=F32), vm(4, 96, c_half // 2, dtype=F32),
            vm(2, 192, c_half), *two(c_half),
            vm(2, 192, c_half, dtype=F32), vm(2, 192, c_half), vm(2, 192, c_half),
            *two(c_half),
            vm(3, 96, c_half // 2), vm(3, 96, c_half // 2),
            vm(5, 8, D, dtype=F32), vm(5, 8, D, dtype=F32), *sems(copies),
        ]

    def three(width):
        return whole((96, width), F32), whole((3, 96, width), BF16)

    grad_in, gain_sums, f_recv, c_keep, c_recv, s_keep, s_recv, e_recv = fused_call(
        self_kernel, 3,
        near(scal, q1, k1, v1, lse1, gatt1, gatt1_o, block_in, gains, sq, sk, sv)
        + near(res1, rows1, a1, gg_a, gg_b) + far(f_send, e_send) + near(c_keep) + far(c_send),
        near(
            whole(block, F32), whole((8, D), F32), whole((3, 96, f_half // 2), BF16),
            *three(c_half // 2), *three(c_half // 2),
        )
        + far(whole((2, 96, e_half), BF16)),
        scratch_3, 32, 20e9,
    )
    parts = e_keep, e_recv, f_keep, f_recv, c_keep, c_recv, s_keep, s_recv, grad_in
    wide, tall, ff_wide = whole((96, 192), F32), whole((192, 96), F32), whole((96, 512), F32)
    grad_embed, grad_in, *grads = pl.pallas_call(
        functools.partial(finish_kernel, vocab),
        out_shape=[
            whole((96, vocab), F32), whole(block, F32), wide, wide, wide, tall, wide, wide, wide, tall,
            ff_wide, ff_wide, ff_wide,
        ],
        in_specs=[pl.BlockSpec(memory_space=pl.ANY)] * 9,
        scratch_shapes=[pltpu.VMEM(part.shape, part.dtype) for part in parts]
        + [pltpu.SemaphoreType.DMA((9,)), pltpu.VMEM((96, 192), F32)],
        compiler_params=pltpu.CompilerParams(vmem_limit_bytes=FUSED_LIMIT),
    )(*parts)
    grads[-1] = grads[-1].T
    grad_embed = grad_embed.T
    return grad_in, grad_source, gain_sums, grads, grad_embed


def logits_kernel(vocab, flat_ref, table_ref, target_ref, logits_ref, stats_ref):
    tile = pl.program_id(0)

    @pl.when(tile == 0)
    def _():
        row = lax.broadcasted_iota(jnp.int32, stats_ref.shape, 0)
        stats_ref[...] = jnp.where(row == 0, 2 * NEG, 0.0)

    logits = dot_nn(table_ref[...], flat_ref[...])
    entry = tile * HTILE + lax.broadcasted_iota(jnp.int32, logits.shape, 0)
    logits = jnp.where(entry < vocab, logits, 2 * NEG)
    logits_ref[...] = logits
    old = stats_ref[0:1, :]
    new = jnp.maximum(old, jnp.max(logits, axis=0, keepdims=True))
    stats_ref[1:2, :] = stats_ref[1:2, :] * jnp.exp(old - new) + jnp.sum(
        jnp.exp(logits - new), axis=0, keepdims=True
    )
    stats_ref[0:1, :] = new
    hit = jnp.where(entry == target_ref[...], logits, 0.0)
    stats_ref[2:3, :] += jnp.sum(hit, axis=0, keepdims=True)


def head_logits(flat, table, target):
    count = flat.shape[1]
    vocab = table.shape[0]
    tiles = pl.cdiv(vocab, HTILE)
    return pl.pallas_call(
        functools.partial(logits_kernel, vocab),
        grid=(tiles,),
        out_shape=[whole((tiles * HTILE, count), F32), whole((8, count), F32)],
        in_specs=[
            pl.BlockSpec((D, count), lambda i: (0, 0)),
            pl.BlockSpec((HTILE, D), lambda i: (i, 0)),
            pl.BlockSpec((1, count), lambda i: (0, 0)),
        ],
        out_specs=[
            pl.BlockSpec((HTILE, count), lambda i: (i, 0)),
            pl.BlockSpec((8, count), lambda i: (0, 0)),
        ],
        cost_estimate=pl.CostEstimate(
            flops=2 * count * vocab * D, bytes_accessed=vocab * (2 * D + 4 * count), transcendentals=0
        ),
        compiler_params=pltpu.CompilerParams(vmem_limit_bytes=VMEM_LIMIT // 2),
    )(flat, table, target)


def grads_kernel(vocab, logits_ref, table_ref, target_ref, lse_ref, live_ref, g_ref, gf_ref, acc_ref):
    tile = pl.program_id(0)

    @pl.when(tile == 0)
    def _():
        acc_ref[...] = jnp.zeros_like(acc_ref)

    entry = tile * HTILE + lax.broadcasted_iota(jnp.int32, logits_ref.shape, 0)
    hit = jnp.where(entry == target_ref[...], 1.0, 0.0)
    grad = jnp.where(live_ref[...] > 0, jnp.exp(logits_ref[...] - lse_ref[...]) - hit, 0.0)
    grad = grad.astype(BF16)
    g_ref[...] = grad
    entry = tile * HTILE + lax.broadcasted_iota(jnp.int32, (HTILE, D), 0)
    table = jnp.where(entry < vocab, table_ref[...], jnp.zeros_like(table_ref[...]))
    acc_ref[...] += lax.dot_general(
        grad, table, (((0,), (0,)), ((), ())), preferred_element_type=F32
    )

    @pl.when(tile == pl.num_programs(0) - 1)
    def _():
        gf_ref[...] = acc_ref[...].astype(gf_ref.dtype)


def head_grads(logits, table, target, lse, live, dtype):
    count = logits.shape[1]
    vocab = table.shape[0]
    tiles = pl.cdiv(vocab, HTILE)
    row = pl.BlockSpec((1, count), lambda i: (0, 0))
    return pl.pallas_call(
        functools.partial(grads_kernel, vocab),
        grid=(tiles,),
        out_shape=[whole((tiles * HTILE, count), BF16), whole((count, D), dtype)],
        in_specs=[
            pl.BlockSpec((HTILE, count), lambda i: (i, 0)),
            pl.BlockSpec((HTILE, D), lambda i: (i, 0)),
            row,
            row,
            row,
        ],
        out_specs=[
            pl.BlockSpec((HTILE, count), lambda i: (i, 0)),
            pl.BlockSpec((count, D), lambda i: (0, 0)),
        ],
        scratch_shapes=[pltpu.VMEM((count, D), F32)],
        cost_estimate=pl.CostEstimate(
            flops=2 * count * vocab * D, bytes_accessed=vocab * (2 * D + 6 * count), transcendentals=0
        ),
        compiler_params=pltpu.CompilerParams(vmem_limit_bytes=VMEM_LIMIT // 2),
    )(logits, table, target, lse, live)


def table_kernel(fm_a, fm_b, fs_a, fs_b, g_a, g_b, mine_ref, send_ref):
    first, second = g_a[...], g_b[...]
    mine_ref[...] = dot_nt(fm_a[...], first) + dot_nt(fm_b[...], second)
    send_ref[...] = (dot_nt(fs_a[...], first) + dot_nt(fs_b[...], second)).astype(BF16)


def table_grads(flat_a, flat_b, g_a, g_b):
    width, count = g_a.shape
    left = pl.BlockSpec((HALF_D, count), lambda i: (0, 0))
    right = pl.BlockSpec((HTILE, count), lambda i: (i, 0))
    out = pl.BlockSpec((HALF_D, HTILE), lambda i: (0, i))
    return pl.pallas_call(
        table_kernel,
        grid=(width // HTILE,),
        out_shape=[whole((HALF_D, width), F32), whole((HALF_D, width), BF16)],
        in_specs=[left] * 4 + [right] * 2,
        out_specs=[out] * 2,
        cost_estimate=pl.CostEstimate(
            flops=4 * count * width * D, bytes_accessed=width * (4 * count + 6 * HALF_D), transcendentals=0
        ),
        compiler_params=pltpu.CompilerParams(vmem_limit_bytes=VMEM_LIMIT),
    )(flat_a[0], flat_b[0], flat_a[1], flat_b[1], g_a, g_b)


def make(mesh):
    dp_size = mesh.shape["dp"]
    split = dp_size == 8

    def on_device(
        block_in,
        source,
        target_len,
        source_len,
        targets,
        gain_self,
        gain_cross,
        gain_ff,
        gain_final,
        self_q,
        self_k,
        self_v,
        self_o,
        cross_q,
        cross_k,
        cross_v,
        cross_o,
        ff_gate,
        ff_up,
        ff_down,
        embed_table,
    ):
        z = lax.axis_index("tensor")
        dp = lax.axis_index("dp")
        half = lax.rem(z, 2)
        seq = z // 2
        core = lax.rem(dp, 2)
        gains = jnp.stack([gain_self, gain_cross, gain_ff, gain_final])
        gain_self, gain_cross, gain_ff, gain_final = (gains[i : i + 1] for i in range(4))

        def pair_swap(value):
            return swap(value, "tensor", 4, 1)

        scal = jnp.stack(
            [
                half,
                lax.dynamic_index_in_dim(target_len, seq, keepdims=False),
                lax.dynamic_index_in_dim(source_len, seq, keepdims=False),
                core,
            ]
        ).astype(jnp.int32)

        def vm(shape, dtype):
            return pltpu.VMEM(shape, dtype)

        pair = (TGT, D)
        weights = (
            self_q.T, self_k.T, self_v.T, self_o, cross_q.T, cross_k.T, cross_v.T, cross_o,
            ff_gate, ff_up, ff_down,
        )
        vocab = embed_table.shape[0]
        if split:
            lens = jnp.concatenate([target_len, source_len])
            results = forward(True, lens, block_in, source, gains, weights)
            q1, k1, v1, lse1, a1, h1, q2, k2, v2, block_out, fin_t, h2, att_t, a2, lse2 = results[:15]
            g_a, g_b, gf_sum, gf_3, losses, fin_a, fin_b = fused_head(
                lens, fin_t, embed_table, targets.reshape(4, ROWS)
            )
            saved = (q1, k1, v1, lse1, a1, h1, q2, k2, v2, block_out, h2, att_t, a2, lse2)
            grad_block_in, grad_source, gain_sums, grads, grad_embed = fused_backward(
                lens, fin_a, fin_b, g_a, g_b, gf_sum, gf_3, saved, results[15:], gains,
                block_in, source, vocab,
            )
            return (
                block_out, losses.reshape(-1), grad_block_in, grad_source,
                gain_sums[3], gain_sums[2], gain_sums[1], gain_sums[0], *grads, grad_embed,
            )

        wide = [gather_wide(w.T if i in (8, 9) else w, dp_size) for i, w in enumerate(weights)]
        sq, sk, sv, so, cq, ck, cv, co, wg, wu, wd = wide
        weights = jnp.stack([sq, sk, sv, so]), jnp.stack([cq, ck, cv, co]), wg, wu, wd
        results = forward(False, scal, block_in, source, gains, weights)
        q1, k1, v1, lse1, a1, h1, q2, k2, v2, block_out, fin, h2, att_t, a2, lse2 = results
        fin = fin.T

        vocab = embed_table.shape[0]

        def block(by_block, j, axis=0):
            return lax.dynamic_index_in_dim(by_block, z ^ j, axis, keepdims=False)

        tgt_local = targets - z * vocab
        tgt_local = jnp.where((tgt_local >= 0) & (tgt_local < vocab), tgt_local, -1)
        tgt_blocks = tgt_local.reshape(4, ROWS)
        position = lax.rem(jnp.arange(4 * ROWS), TGT)
        live = position < jnp.repeat(target_len, TGT, total_repeat_length=4 * ROWS)
        live_blocks = live.astype(jnp.int32).reshape(4, ROWS)
        fin_1, fin_2, fin_3 = (swap(fin, "tensor", 4, j) for j in (1, 2, 3))
        fin_a = jnp.concatenate([fin_2, fin_3], 0).T
        fin_b = jnp.concatenate([fin, fin_1], 0).T

        def columns(by_block, order):
            return jnp.concatenate([block(by_block, j) for j in order], 0)[None, :]

        tgt_a, tgt_b = columns(tgt_blocks, (2, 3)), columns(tgt_blocks, (0, 1))
        logits_b, stats_b = head_logits(fin_b, embed_table, tgt_b)
        logits_a, stats_a = head_logits(fin_a, embed_table, tgt_a)
        stats = [stats_b[:, :ROWS], stats_b[:, ROWS:], stats_a[:, :ROWS], stats_a[:, ROWS:]]
        stats = jnp.stack(stats, 0)
        stats = jnp.stack([block(stats, j) for j in range(4)], 0)
        others = [stats] + [swap(stats, "tensor", 4, j) for j in (1, 2, 3)]

        def over_z(values, op):
            return op(op(values[0], values[1]), op(values[2], values[3]))

        top = over_z([s[:, 0] for s in others], jnp.maximum)
        total = over_z([s[:, 1] * jnp.exp(s[:, 0] - top) for s in others], jnp.add)
        picked = over_z([s[:, 2] for s in others], jnp.add)
        g_lse = top + jnp.log(total)
        token_loss = jnp.where(live, (g_lse - picked).reshape(-1), 0.0)
        g_a, gf_a = head_grads(
            logits_a, embed_table, tgt_a, columns(g_lse, (2, 3)), columns(live_blocks, (2, 3)), BF16
        )
        gf_2 = swap(gf_a[:ROWS], "tensor", 4, 2)
        g_b, gf_b = head_grads(
            logits_b, embed_table, tgt_b, columns(g_lse, (0, 1)), columns(live_blocks, (0, 1)), F32
        )
        g_b, gf_b, gf_2, gf_a = lax.optimization_barrier((g_b, gf_b, gf_2, gf_a))
        def halves(flat):
            return flat[:HALF_D], flat[HALF_D:]

        gf_3 = swap(gf_a[ROWS:], "tensor", 4, 3)
        gf_1 = swap(gf_b[ROWS:].astype(BF16), "tensor", 4, 1)
        e_mine, e_send = table_grads(halves(fin_a), halves(fin_b), g_a, g_b)
        e_sum = WideReduction(z, e_mine[:, :vocab], e_send[:, :vocab])

        half_t = (HALF_D, ROWS)
        ff_mine, ff_send, res2, rows2, gatt, dots, gg_a = local_call(
            functools.partial(ff_backward, False),
            [whole((HALF_D, 3 * FF), F32), whole((HALF_D, 3 * FF), BF16), whole((ROWS, D), F32)]
            + [whole((ROWS, D), BF16)] * 2
            + [whole((16, ROWS), F32), whole((2, D), F32)],
            [vm((D, ROWS), BF16)] * 2 + [vm(half_t, BF16)] * 4
            + [vm((ROWS, D), F32)],
            10e9,
            scal, gf_b[:ROWS], gf_1, gf_2, gf_3, block_out, h2,
            gain_ff, gain_final, wg, wu, wd, co, att_t,
        )
        ff_sum = WideReduction(z, ff_mine, ff_send)
        gatt_other, dots_other = pair_swap(gatt), pair_swap(dots)
        dk2, dv2, dq_own, dq_send = local_call(
            functools.partial(cross_backward, split),
            [whole((KEYS, D), BF16)] * 2 + [whole((D, ROWS), F32), whole((D, ROWS), BF16)],
            [vm(pair, BF16), vm((16, TGT), F32), vm((D, TGT), F32)],
            20e9,
            scal, q2, k2, v2, lse2, gatt, gatt_other, dots, dots_other,
        )
        dq_other = pair_swap(dq_send)
        grad_source, kv_mine, kv_send = local_call(
            functools.partial(source_backward, split),
            [whole((KEYS, D), F32), whole((HALF_D, 2 * D), F32), whole((HALF_D, 2 * D), BF16)],
            [vm((D, KEYS), BF16)] + [vm((HALF_D, KEYS), BF16)] * 2,
            5e9,
            scal, dk2, dv2, source, ck, cv,
        )
        c_mine, c_send, res1, rows1, gatt1, gg_b = local_call(
            functools.partial(query_backward, split),
            [whole((HALF_D, 4 * D), F32), whole((HALF_D, 4 * D), BF16), whole((ROWS, D), F32)]
            + [whole((ROWS, D), BF16)] * 2 + [whole((1, D), F32)],
            [vm((D, ROWS), BF16)] * 2 + [vm(half_t, BF16)] * 2 + [vm((D, ROWS), F32)],
            2e9,
            scal, dq_own, dq_other, h1, gain_cross, cq, res2, rows2, a2, so,
            kv_mine, kv_send,
        )
        c_sum = WideReduction(z, c_mine, c_send)
        gatt1_other = pair_swap(gatt1)
        s_mine, s_send, grad_block_in, gg_c = local_call(
            functools.partial(self_backward, split),
            [whole((HALF_D, 4 * D), F32), whole((HALF_D, 4 * D), BF16)]
            + [whole((ROWS, D), F32), whole((1, D), F32)],
            [vm(pair, BF16), vm((D, TGT), F32), vm(pair, BF16), vm(pair, BF16)]
            + [vm((D, ROWS), BF16)] * 2 + [vm(half_t, BF16)] * 2,
            12e9,
            scal, q1, k1, v1, lse1, gatt1, gatt1_other, block_in, gain_self, sq, sk, sv,
            res1, rows1, a1,
        )
        s_sum = WideReduction(z, s_mine, s_send)
        gains = jnp.concatenate([gg_a, gg_b, gg_c], 0)
        gains = lax.psum(gains, ("dp", "tensor"))
        grad_embed = e_sum.table(vocab)
        ff_grads = ff_sum.last(3, (2,))
        c_grads = c_sum.last(4, (3,))
        s_grads = s_sum.last(4, (3,))

        return (
            block_out,
            token_loss,
            grad_block_in,
            grad_source,
            gains[3],
            gains[2],
            gains[1],
            gains[0],
            *s_grads,
            *c_grads,
            *ff_grads,
            grad_embed,
        )

    return on_device


def solution(mesh):
    rows = P(("dp", "tensor"), None)
    wide, tall = P(None, "tensor"), P("tensor", None)
    in_specs = (rows, rows) + (P("dp"),) * 3 + (P(),) * 4
    in_specs += (wide, wide, wide, tall) * 2 + (wide, wide, tall, tall)
    g_in, g_out = P("dp", "tensor"), P("tensor", "dp")
    out_specs = (rows, P("dp"), rows, rows) + (P(),) * 4
    out_specs += (g_in, g_in, g_in, g_out) * 2 + (g_in, g_in, g_out, g_out)
    return jax.shard_map(
        make(mesh), mesh=mesh, in_specs=in_specs, out_specs=out_specs, check_vma=False
    )
```

```python
import functools
import math

import jax
import jax.numpy as jnp
from jax import lax
from jax.sharding import PartitionSpec as P
from jax.experimental import pallas as pl
from jax.experimental.pallas import tpu as pltpu

D = 768
HDIM = 64
NHEAD = D // HDIM
PAIRS = NHEAD // 2
FF = 2048
TGT = 512
ROWS = 256
KEYS = 1024
CHUNK = 256
HALF_D = D // 2
VTILE = 512
HTILE = 1024
F32 = jnp.float32
BF16 = jnp.bfloat16
MESH_ID = pl.DeviceIdType.MESH
VMEM_LIMIT = 56 * 2**20
FUSED_LIMIT = 62 * 2**20
NEG = -1000000000.0
SCALE = HDIM ** (-0.5)
EPS = 1e-06


def dot_nt(left, right):
    return lax.dot_general(left, right, (((1,), (1,)), ((), ())), preferred_element_type=F32)


def dot_nn(left, right):
    return lax.dot_general(left, right, (((1,), (0,)), ((), ())), preferred_element_type=F32)


def swap(value, axis_name, size, bit):
    return lax.ppermute(value, axis_name, [(i, i ^ bit) for i in range(size)])


class Gather:
    def __init__(self, links, refs, used):
        self.links, self.refs, self.used = links, refs, used
        self.last = []

    def piece(self, ref, shard, owner, part=None):
        if len(ref.shape) == 2:
            rows = ref.shape[0] // 32
            base = shard * 8 * rows + owner * rows
        else:
            rows = ref.shape[1] // 8
            base = shard * 2 * rows + lax.rem(owner, 2) * rows
        start, count = (0, rows) if part is None else (part * rows // 2, rows // 2)
        where = pl.ds(pl.multiple_of(base + start, 16), count)
        return ref.at[where] if len(ref.shape) == 2 else ref.at[owner // 2, where]

    def send(self, part, peer):
        send_sem, recv_sem = self.links["sems"]
        sem = self.used[0]
        self.used[0] += 1
        copy = pltpu.make_async_remote_copy(
            src_ref=part,
            dst_ref=part,
            send_sem=send_sem.at[sem],
            recv_sem=recv_sem.at[sem],
            device_id={"dp": peer[0], "tensor": peer[1]},
            device_id_type=MESH_ID,
        )
        copy.start()
        return copy

    def along_z(self):
        links = self.links
        self.z_copies = [
            self.send(self.piece(ref, links["z"], links["dp"]), peer)
            for ref in self.refs
            for peer in links["z_peers"]
        ]

    def along_xy(self):
        links = self.links
        for copy in self.z_copies:
            copy.wait()
        self.x_copies, self.y_copies = [], []
        for ref in self.refs:
            for _, shard in links["z_peers"]:
                part = self.piece(ref, shard, links["dp"])
                self.x_copies.append(self.send(part, links["x"]))
                self.y_copies.append(self.send(part, links["y"]))
                self.last.append(self.send(part, links["core"]))

    def diagonal(self):
        links = self.links
        self.d_copies = []
        at = 0
        for ref in self.refs:
            for _, shard in links["z_peers"]:
                self.x_copies[at].wait()
                self.d_copies.append(self.send(self.piece(ref, shard, links["x"][0], 0), links["y"]))
                self.y_copies[at].wait()
                self.d_copies.append(self.send(self.piece(ref, shard, links["y"][0], 1), links["x"]))
                for owner in (links["x"][0], links["y"][0]):
                    self.last.append(self.send(self.piece(ref, shard, owner), links["core"]))
                at += 1

    def finish(self):
        links = self.links
        for copy in self.d_copies:
            copy.wait()
        for ref in self.refs:
            for _, shard in links["z_peers"]:
                self.last.append(self.send(self.piece(ref, shard, links["xy"]), links["core"]))
        for copy in self.last:
            copy.wait()


def gather_wide(shard, dp_size):
    rows = shard.shape[0] // dp_size
    part = lax.dynamic_slice_in_dim(shard, lax.axis_index("dp") * rows, rows, 0)
    return lax.all_gather(part, ("tensor", "dp"), axis=0, tiled=True)


def block_rows(index):
    return pl.ds(pl.multiple_of(index * 96, 96), 96)


class Comm:
    def __init__(self, send_sem, recv_sem):
        self.send_sem, self.recv_sem, self.used = send_sem, recv_sem, 0
        dp, z = lax.axis_index("dp"), lax.axis_index("tensor")
        self.z = z
        self.c, self.x, self.y = lax.rem(dp, 2), lax.rem(dp // 2, 2), dp // 4
        low, high = lax.rem(z, 2), z // 2
        self.core_peer = (dp + 1 - 2 * self.c, z)
        self.x_peer = (dp + 2 - 4 * self.x, z)
        self.y_peer = (dp + 4 - 8 * self.y, z)
        self.z_shards = (high * 2 + 1 - low, (1 - high) * 2 + low, (1 - high) * 2 + 1 - low)
        self.z_peers = [(dp, shard) for shard in self.z_shards]

    def barrier(self):
        barrier = pltpu.get_barrier_semaphore()
        peers = [self.core_peer, self.x_peer, self.y_peer] + self.z_peers
        for peer in peers:
            pl.semaphore_signal(
                barrier, inc=1, device_id={"dp": peer[0], "tensor": peer[1]}, device_id_type=MESH_ID
            )
        pl.semaphore_wait(barrier, len(peers))

    def copy(self, src, dst, peer, index):
        return pltpu.make_async_remote_copy(
            src_ref=src,
            dst_ref=dst,
            send_sem=self.send_sem.at[index],
            recv_sem=self.recv_sem.at[index],
            device_id={"dp": peer[0], "tensor": peer[1]},
            device_id_type=MESH_ID,
        )

    def reserve(self, count):
        self.used += count
        return self.used - count

    def send(self, src, dst, peer):
        copy = self.copy(src, dst, peer, self.reserve(1))
        copy.start()
        return copy


def fold_one(comm, mine, got, keep, send, is_right):
    for other in range(2):
        rows = slice(other * 96, (other + 1) * 96)
        along_x, along_y = 2 * other + comm.x, 2 * comm.y + other
        stay = along_x * (1 - is_right) + along_y * is_right
        along_x, along_y = 2 * other + 1 - comm.x, 2 * (1 - comm.y) + other
        leave = along_x * (1 - is_right) + along_y * is_right
        stay, leave = block_rows(stay), block_rows(leave)
        keep[rows, :] = mine[stay, :] + got[stay, :].astype(F32)
        send[rows, :] = (mine[leave, :] + got[leave, :].astype(F32)).astype(BF16)


def fold_two(comm, mine, got, keep, send):
    for side, bit in enumerate((comm.y, comm.x)):
        stay, leave = block_rows(bit), block_rows(1 - bit)
        keep[side] = mine[side, stay, :] + got[side, stay, :].astype(F32)
        send[side] = (mine[side, leave, :] + got[side, leave, :].astype(F32)).astype(BF16)


class Flow:
    def __init__(self, comm, one, two, three):
        self.comm, self.one, self.two, self.three = comm, one, two, three
        self.copies = []

    def wait(self):
        for copy in self.copies:
            copy.wait()

    def from_core(self, mine, send, got):
        comm = self.comm
        self.copies = [comm.send(send, got, comm.core_peer)]
        self.mine, self.got = mine, got

    def fold_first(self):
        self.wait()
        keep, send, _ = self.one
        width = keep.shape[2]
        for side in range(2):
            cols = pl.ds(side * width, width)
            fold_one(
                self.comm, self.mine.at[:, cols], self.got.at[:, cols], keep.at[side], send.at[side], side
            )

    def send_first(self):
        comm = self.comm
        _, send, recv = self.one
        self.copies = [
            comm.send(send.at[0], recv.at[0], comm.x_peer),
            comm.send(send.at[1], recv.at[1], comm.y_peer),
        ]

    def fold_second(self):
        self.wait()
        fold_two(self.comm, self.one[0], self.one[2], self.two[0], self.two[1])

    def send_second(self):
        comm = self.comm
        _, send, recv = self.two
        self.copies = [
            comm.send(send.at[0], recv.at[0], comm.y_peer),
            comm.send(send.at[1], recv.at[1], comm.x_peer),
        ]

    def fold_third(self, shard_ref):
        self.wait()
        comm = self.comm
        (keep, _, recv), (keep3, send3, _) = self.two, self.three
        width = keep3.shape[1]
        for side in range(2):
            total = keep[side] + recv[side].astype(F32)
            shard_ref[2 * side, :, :width] = total[:, :width]
            shard_ref[2 * side + 1, :, :width] = total[:, width:]
        keep3[...] = shard_ref[comm.z, :, :width]
        for j, shard in enumerate(comm.z_shards):
            send3[j] = shard_ref[shard, :, :width].astype(BF16)

    def send_third(self):
        _, send3, recv3 = self.three
        peers = self.comm.z_peers
        self.copies = [self.comm.send(send3.at[j], recv3.at[j], peers[j]) for j in range(3)]


def finish_kernel(vocab, *refs):
    sources, (e_out, gin_out, gsrc_out, block_ref), refs = refs[:11], refs[11:15], refs[15:]
    refs, held, (sem, turn_ref) = refs[:11], refs[11:20], refs[20:]
    held = held + (gsrc_out, block_ref)
    copies = [pltpu.make_async_copy(src, dst, sem.at[i]) for i, (src, dst) in enumerate(zip(sources, held))]
    for copy in copies:
        copy.start()
    for copy in copies:
        copy.wait()
    e_keep, e_recv, f_keep, f_recv, c_keep, c_recv, s_keep, s_recv, gin = held[:9]
    gin_out[...] = gin[...]
    width = e_keep.shape[2]
    for side in range(2):
        count = min(width, vocab - side * width)
        e_out[:, side * width : side * width + count] = e_keep[side, :, :count] + e_recv[
            side, :, :count
        ].astype(F32)
    for keep, recv, outs in ((f_keep, f_recv, refs[8:]), (c_keep, c_recv, refs[4:8]), (s_keep, s_recv, refs[:4])):
        width = keep.shape[1] // len(outs)
        for m, out in enumerate(outs):
            cols = slice(m * width, (m + 1) * width)
            part = keep[:, cols] + recv[0, :, cols].astype(F32)
            part = part + (recv[1, :, cols].astype(F32) + recv[2, :, cols].astype(F32))
            if out.shape[0] == 96:
                out[...] = part
            else:
                turn_ref[...] = part
                out[...] = turn_ref[...].T


class WideReduction:
    def __init__(self, z, mine, send):
        both = jnp.concatenate([mine, send.astype(F32)], 0)
        self.part = lax.psum_scatter(both, "dp", scatter_dimension=0, tiled=True)

    def last(self, count, flips):
        rows = self.part.shape[0]
        by_z = self.part.reshape(rows, 4, -1)
        total = lax.psum_scatter(by_z, "tensor", scatter_dimension=1, tiled=True)[:, 0]
        parts = jnp.split(total, count, axis=1)
        return [p.T if m in flips else p for m, p in enumerate(parts)]

    def table(self, vocab):
        return self.part.T


def rms_scale(values):
    return lax.rsqrt(jnp.mean(values * values, axis=-1, keepdims=True) + EPS)


def spots(scal, split):
    if split:
        z = lax.axis_index("tensor")
        half, core = lax.rem(z, 2), lax.rem(lax.axis_index("dp"), 2)
        return half, scal[z // 2], scal[2 + z // 2] - half * KEYS, core
    half, core = scal[0], scal[3]
    return half, scal[1], scal[2] - half * KEYS, core


def norm_back(values, inv_scale, gain, grad_out):
    weighted = gain * grad_out
    grad_gain = jnp.sum(grad_out * values * inv_scale, axis=0, keepdims=True)
    grad_values = inv_scale * weighted - values * inv_scale * inv_scale * inv_scale * jnp.mean(
        weighted * values, axis=-1, keepdims=True
    )
    return grad_values, grad_gain


def flip(value):
    return value.astype(F32).T


def lane_half(rows, which):
    lane = lax.broadcasted_iota(jnp.int32, (rows, 2 * HDIM), 1)
    return (lane >= HDIM) if which else (lane < HDIM)


def only(value, which):
    return jnp.where(lane_half(value.shape[0], which), value, jnp.zeros_like(value))


def split_rows(flat_ref, mine_ref, send_ref, core, split):
    for block in range(4):
        if split:
            first = pl.multiple_of((2 * block + core) * 96, 96)
            second = pl.multiple_of((2 * block + 1 - core) * 96, 96)
        else:
            first, second = block * 96, HALF_D + block * 96
        mine_ref[block * 96 : (block + 1) * 96, :] = flat_ref[pl.ds(first, 96), :]
        send_ref[block * 96 : (block + 1) * 96, :] = flat_ref[pl.ds(second, 96), :]


def by_shard(left_ref, rights, out_ref, first, per_shard):
    width = 192 * len(rights)
    for z in range(4):
        part = [right[:, z * 192 : (z + 1) * 192] for right in rights]
        right = jnp.concatenate(part, axis=1) if len(part) > 1 else part[0]
        start = z * per_shard + first
        out_ref[:, start : start + width] = dot_nn(left_ref[...], right).astype(out_ref.dtype)


def whole(shape, dtype):
    return jax.ShapeDtypeStruct(shape, dtype)


def local_call(body, outs, scratch, flops, *args):
    smem = pl.BlockSpec(memory_space=pltpu.SMEM)
    vmem = pl.BlockSpec(memory_space=pltpu.VMEM)
    bytes_all = sum(a.size * a.dtype.itemsize for a in args)
    bytes_all += sum(o.size * jnp.dtype(o.dtype).itemsize for o in outs)
    held = sum(math.prod(s.shape) * jnp.dtype(s.dtype).itemsize for s in scratch)
    return pl.pallas_call(
        body,
        out_shape=outs,
        in_specs=[smem] + [vmem] * (len(args) - 1),
        out_specs=[vmem] * len(outs),
        scratch_shapes=scratch,
        cost_estimate=pl.CostEstimate(
            flops=int(flops), bytes_accessed=int(bytes_all), transcendentals=0
        ),
        compiler_params=pltpu.CompilerParams(
            vmem_limit_bytes=min(VMEM_LIMIT, int(bytes_all + held + 16 * 2**20))
        ),
    )(*args)


def forward_kernel(split, *refs):
    (scal, x_own, source, gains), refs = refs[:4], refs[4:]
    gain_self, gain_cross, gain_ff, gain_final = (gains.at[i : i + 1] for i in range(4))
    shards, refs = refs[: 11 if split else 5], refs[11 if split else 5 :]
    (q1, k1, v1, lse1, att1, h1_out, q2, k2, v2), refs = refs[:9], refs[9:]
    (out_ref, fin_ref, h2_ref, att_t_ref, att2, lse2), refs = refs[:6], refs[6:]
    if split:
        copies_out, refs = refs[:11], refs[11:]
        (ws, wc, wg, wu, wd), refs = refs[:5], refs[5:]
    else:
        ws, wc, wg, wu, wd = shards
    (x_other, x_ref, n_ref, vt_ref, ot_ref, s_ref, o_send, o_other, lse_own, lse_other, mix_ref), refs = (
        refs[:11],
        refs[11:],
    )
    pair_send, pair_recv = refs[:2]
    dp = lax.axis_index("dp")
    z = lax.axis_index("tensor")
    low, high = lax.rem(z, 2), z // 2
    half = low
    live = scal[high] if split else scal[1]
    live_src = (scal[2 + high] if split else scal[2]) - low * KEYS
    z_peers = [(dp, high * 2 + 1 - low)]
    peers = z_peers
    if split:
        z_peers = z_peers + [(dp, (1 - high) * 2 + low), (dp, (1 - high) * 2 + 1 - low)]
        x_peer = dp + 2 - 4 * lax.rem(dp // 2, 2)
        y_peer = dp + 4 - 8 * (dp // 4)
        links = dict(
            dp=dp,
            z=z,
            z_peers=z_peers,
            x=(x_peer, z),
            y=(y_peer, z),
            xy=x_peer + y_peer - dp,
            core=(dp + 1 - 2 * lax.rem(dp, 2), z),
            sems=refs[2:4],
        )
        out_sem = refs[4]
        peers = z_peers + [links["x"], links["y"], links["core"]]
    barrier = pltpu.get_barrier_semaphore()
    for peer in peers:
        pl.semaphore_signal(
            barrier, inc=1, device_id={"dp": peer[0], "tensor": peer[1]}, device_id_type=MESH_ID
        )

    def exchange(index, src, dst):
        copy = pltpu.make_async_remote_copy(
            src_ref=src,
            dst_ref=dst,
            send_sem=pair_send.at[index],
            recv_sem=pair_recv.at[index],
            device_id={"dp": z_peers[0][0], "tensor": z_peers[0][1]},
            device_id_type=MESH_ID,
        )
        copy.start()
        return copy

    leaving = []
    if split:
        used = [0]
        groups = [Gather(links, refs_of, used) for refs_of in ([ws], [wc], [wg], [wu], [wd])]
        of_self, of_cross, of_gate, of_up, of_down = groups
        hid, fhid = D // 4, FF // 4

        def place_block(target, first):
            rows = pl.ds(pl.multiple_of(z * hid, 16), hid)
            for m in range(3):
                target[m, rows, :] = shards[first + m][...]
            target[3, rows, :] = shards[first + 3][...]

        def place_wide(target, shard, flipped):
            rows = pl.ds(pl.multiple_of(z * fhid, 16), fhid)
            target[rows, :] = flip(shard[...]).astype(BF16) if flipped else shard[...]

        def leave(first, parts):
            for i, part in enumerate(parts):
                copy = pltpu.make_async_copy(part, copies_out[first + i], out_sem.at[first + i])
                copy.start()
                leaving.append(copy)

        place_block(ws, 0)
        pl.semaphore_wait(barrier, len(peers))
        of_self.along_z()
    else:
        pl.semaphore_wait(barrier, len(peers))
    x_copy = exchange(0, x_own, x_other)
    if split:
        place_block(wc, 4)
        place_wide(wg, shards[8], True)
        place_wide(wu, shards[9], True)
        place_wide(wd, shards[10], False)
        of_self.along_xy()
        of_cross.along_z()
        of_self.diagonal()
        of_cross.along_xy()
        of_gate.along_z()
    x_copy.wait()
    own = pl.multiple_of(half * ROWS, ROWS)
    other = pl.multiple_of((1 - half) * ROWS, ROWS)
    x_ref[pl.ds(own, ROWS), :] = x_own[...].astype(F32)
    x_ref[pl.ds(other, ROWS), :] = x_other[...].astype(F32)
    lse1[...] = jnp.zeros_like(lse1)
    lse_own[...] = jnp.zeros_like(lse_own)
    if split:
        of_self.finish()
        leave(0, [ws.at[m] for m in range(4)])
    for i in range(2):
        rows = slice(i * ROWS, (i + 1) * ROWS)
        x = x_ref[rows, :]
        n = (x * rms_scale(x) * gain_self[...]).astype(BF16)
        n_ref[rows, :] = n
        q1[rows, :] = dot_nt(n, ws[0]).astype(BF16)
        k1[rows, :] = dot_nt(n, ws[1]).astype(BF16)
        v1[rows, :] = dot_nt(n, ws[2]).astype(BF16)
    vt_ref[:, :TGT] = dot_nt(ws[2], n_ref[...]).astype(BF16)
    if split:
        of_gate.along_xy()
        of_up.along_z()
    key = lax.broadcasted_iota(jnp.int32, (TGT, TGT), 0)
    query = lax.broadcasted_iota(jnp.int32, (TGT, TGT), 1)
    seen = (key <= query) & (key < live)

    def self_pairs(first, last):
        @pl.loop(first, last)
        def _(pair):
            lanes = pl.ds(pl.multiple_of(pair * 128, 128), 128)
            q_pair, k_pair = q1[:, lanes], k1[:, lanes]
            for which in range(2):
                head = 2 * pair + which
                feats = pl.ds(pl.multiple_of(head * HDIM, HDIM), HDIM)
                scores = jnp.where(seen, dot_nt(k_pair, only(q_pair, which)) * SCALE, NEG)
                top = jnp.max(scores, axis=0, keepdims=True)
                probs = jnp.exp(scores - top)
                total = jnp.sum(probs, axis=0, keepdims=True)
                lse1[pl.ds(head, 1), :] = top + jnp.log(total)
                ot_ref[feats, :] = dot_nn(vt_ref[feats, :TGT], probs.astype(BF16)) / total

    self_pairs(0, PAIRS // 2)
    if split:
        of_cross.diagonal()
    self_pairs(PAIRS // 2, PAIRS)
    if split:
        of_up.along_xy()
        of_down.along_z()
        of_gate.diagonal()
    for i in range(2):
        rows = slice(i * ROWS, (i + 1) * ROWS)
        att = flip(ot_ref[:, rows]).astype(BF16)
        n_ref[rows, :] = att
        x_ref[rows, :] = x_ref[rows, :] + dot_nn(att, ws[3])
    att1[...] = n_ref[pl.ds(own, ROWS), :]
    h1_out[...] = x_ref[pl.ds(own, ROWS), :]
    if split:
        of_cross.finish()
        leave(4, [wc.at[m] for m in range(4)])
    for i in range(2):
        rows = slice(i * ROWS, (i + 1) * ROWS)
        h1 = x_ref[rows, :]
        n = (h1 * rms_scale(h1) * gain_cross[...]).astype(BF16)
        q2[rows, :] = dot_nt(n, wc[0]).astype(BF16)
    for i in range(KEYS // CHUNK):
        rows = slice(i * CHUNK, (i + 1) * CHUNK)
        src = source[rows, :]
        k2[rows, :] = dot_nt(src, wc[1]).astype(BF16)
        v2[rows, :] = dot_nt(src, wc[2]).astype(BF16)
        vt_ref[:, rows] = dot_nt(wc[2], src).astype(BF16)
    if split:
        of_up.diagonal()
        of_gate.finish()
        leave(8, [wg])
    chunk_key = lax.broadcasted_iota(jnp.int32, (CHUNK, TGT), 0)

    def cross_pairs(first, last):
        @pl.loop(first, last)
        def _(pair):
            lanes = pl.ds(pl.multiple_of(pair * 128, 128), 128)
            q_pair = q2[:, lanes]
            for which in range(2):
                head = 2 * pair + which
                feats = pl.ds(pl.multiple_of(head * HDIM, HDIM), HDIM)
                q_one = only(q_pair, which)
                top = jnp.full((1, TGT), 2 * NEG, F32)
                for i in range(KEYS // CHUNK):
                    rows = slice(i * CHUNK, (i + 1) * CHUNK)
                    scores = dot_nt(k2[rows, lanes], q_one) * SCALE
                    scores = jnp.where(chunk_key < live_src - i * CHUNK, scores, NEG)
                    s_ref[rows, :] = scores
                    top = jnp.maximum(top, jnp.max(scores, axis=0, keepdims=True))
                total = jnp.zeros((1, TGT), F32)
                out = jnp.zeros((HDIM, TGT), F32)
                for i in range(KEYS // CHUNK):
                    rows = slice(i * CHUNK, (i + 1) * CHUNK)
                    probs = jnp.exp(s_ref[rows, :] - top)
                    total = total + jnp.sum(probs, axis=0, keepdims=True)
                    out = out + dot_nn(vt_ref[feats, rows], probs.astype(BF16))
                lse_own[pl.ds(head, 1), :] = top + jnp.log(total)
                ot_ref[feats, :] = out / total

    cross_pairs(0, PAIRS // 2)
    o_send[: D // 2, :] = ot_ref[: D // 2, pl.ds(other, ROWS)].astype(BF16)
    pair_copies = [exchange(1, o_send.at[: D // 2], o_other.at[: D // 2])]
    if split:
        of_down.along_xy()
        of_up.finish()
        leave(9, [wu])
    cross_pairs(PAIRS // 2, PAIRS)
    o_send[D // 2 :, :] = ot_ref[D // 2 :, pl.ds(other, ROWS)].astype(BF16)
    pair_copies.append(exchange(2, o_send.at[D // 2 :], o_other.at[D // 2 :]))
    pair_copies.append(exchange(3, lse_own, lse_other))
    if split:
        of_down.diagonal()
    for copy in pair_copies:
        copy.wait()

    first, second = lse_own[...], lse_other[...]
    top = jnp.maximum(first, second)
    lse2[...] = top + jnp.log(jnp.exp(first - top) + jnp.exp(second - top))
    lse = lse2[:, pl.ds(own, ROWS)]
    w_first = jnp.exp(lse_own[:, pl.ds(own, ROWS)] - lse)
    w_second = jnp.exp(lse_other[:, pl.ds(own, ROWS)] - lse)
    for head in range(NHEAD):
        feats = slice(head * HDIM, (head + 1) * HDIM)
        att_t_ref[feats, :] = (
            ot_ref[feats, pl.ds(own, ROWS)] * w_first[head : head + 1, :]
            + o_other[feats, :].astype(F32) * w_second[head : head + 1, :]
        )
    att = flip(att_t_ref[...]).astype(BF16)
    att2[...] = att
    h2 = h1_out[...] + dot_nn(att, wc[3])
    h2_ref[...] = h2
    n3 = (h2 * rms_scale(h2) * gain_ff[...]).astype(BF16)

    @pl.loop(0, FF // 512)
    def _(i):
        rows = pl.ds(pl.multiple_of(i * 512, 512), 512)
        gate = dot_nt(n3, wg[rows, :])
        up = dot_nt(n3, wu[rows, :])
        mix_ref[:, rows] = (jax.nn.gelu(gate, approximate=True) * up).astype(BF16)

    if split:
        of_down.finish()
        leave(10, [wd])
    out = h2_ref[...] + dot_nn(mix_ref[...], wd[...])
    out_ref[...] = out
    x_ref[:ROWS, :] = out * rms_scale(out) * gain_final[...] * D ** (-0.5)
    fin_ref[...] = x_ref[:ROWS, :].T.astype(BF16)
    for copy in leaving:
        copy.wait()


def forward(split, scal, x_own, source, gains, weights):
    pair = (TGT, D)
    block = (ROWS, D)
    outs = [whole(pair, BF16)] * 3 + [whole((16, TGT), F32), whole(block, BF16), whole(block, F32)]
    outs += [whole(pair, BF16)] + [whole((KEYS, D), BF16)] * 2
    outs += [whole(block, F32), whole((D, ROWS), BF16), whole(block, F32), whole((D, ROWS), F32)]
    outs += [whole(block, BF16), whole((16, TGT), F32)]
    vmem = pl.BlockSpec(memory_space=pltpu.VMEM)
    out_specs = [vmem] * len(outs)
    scratch = []
    if split:
        outs += [whole((D, D), BF16)] * 8 + [whole((FF, D), BF16)] * 3
        out_specs += [pl.BlockSpec(memory_space=pl.ANY)] * 11
        scratch += [pltpu.VMEM((4, D, D), BF16)] * 2 + [pltpu.VMEM((FF, D), BF16)] * 3
    scratch += [
        pltpu.VMEM(block, BF16),
        pltpu.VMEM(pair, F32),
        pltpu.VMEM(pair, BF16),
        pltpu.VMEM((D, KEYS), BF16),
        pltpu.VMEM((D, TGT), F32),
        pltpu.VMEM((KEYS, TGT), F32),
        pltpu.VMEM((D, ROWS), BF16),
        pltpu.VMEM((D, ROWS), BF16),
        pltpu.VMEM((16, TGT), F32),
        pltpu.VMEM((16, TGT), F32),
        pltpu.VMEM((ROWS, FF), BF16),
        pltpu.SemaphoreType.DMA((4,)),
        pltpu.SemaphoreType.DMA((4,)),
    ]
    if split:
        scratch += [pltpu.SemaphoreType.DMA((27 * 5,))] * 2 + [pltpu.SemaphoreType.DMA((11,))]
    args = (scal, x_own, source, gains, *weights)
    return pl.pallas_call(
        functools.partial(forward_kernel, split),
        out_shape=outs,
        in_specs=[pl.BlockSpec(memory_space=pltpu.SMEM)] + [vmem] * (len(args) - 1),
        out_specs=out_specs,
        scratch_shapes=scratch,
        cost_estimate=pl.CostEstimate(
            flops=int(80e9), bytes_accessed=int(6e7), transcendentals=0
        ),
        compiler_params=pltpu.CompilerParams(
            collective_id=0, has_side_effects=True, vmem_limit_bytes=VMEM_LIMIT
        ),
    )(*args)


def ff_backward(
    split, scal, gf_own, gf_1, gf_2, gf_3, block_out, h2_in, gain_ff, gain_final, wg, wu, wd,
    w_co, att_t, mine_ref, send_ref, res_ref, rows_ref, gatt_ref, dot_ref, gg_ref,
    flat_ref, flat_2, nm_ref, ns_ref, gm_ref, gs_ref, gn_ref,
):
    core = scal[3]
    grad = gf_own[...] + gf_1[...].astype(F32)
    grad = grad + (gf_2[...].astype(F32) + gf_3[...].astype(F32))
    out = block_out[...]
    res, gg_final = norm_back(out, rms_scale(out), gain_final[...], grad * D ** (-0.5))
    gg_ref[0:1, :] = gg_final
    rows_b = res.astype(BF16)
    res_ref[...] = res
    rows_ref[...] = rows_b
    flat_ref[...] = flip(rows_ref[...]).astype(BF16)
    split_rows(flat_ref, gm_ref, gs_ref, core, split)
    h2 = h2_in[...]
    scale3 = rms_scale(h2)
    n3 = (h2 * scale3 * gain_ff[...]).astype(BF16)
    rows_ref[...] = n3
    flat_2[...] = flip(rows_ref[...]).astype(BF16)
    split_rows(flat_2, nm_ref, ns_ref, core, split)
    gn_ref[...] = jnp.zeros_like(gn_ref)
    const = (2.0 / 3.141592653589793) ** 0.5

    @pl.loop(0, FF // 512)
    def _(i):
        start = pl.multiple_of(i * 512, 512)
        rows = pl.ds(start, 512)
        gate = dot_nt(n3, wg[rows, :])
        up = dot_nt(n3, wu[rows, :])
        square = gate * gate
        tanh = jnp.tanh(const * (gate + 0.044715 * gate * square))
        gelu = 0.5 * gate * (1.0 + tanh)
        slope = 0.5 * (1.0 + tanh) + 0.5 * gate * (1.0 - tanh * tanh) * const * (
            1.0 + 3.0 * 0.044715 * square
        )
        grad_mixed = dot_nt(rows_b, wd[rows, :])
        g_gate = (grad_mixed * up * slope).astype(BF16)
        g_up = (grad_mixed * gelu).astype(BF16)
        mixed = (gelu * up).astype(BF16)
        gn_ref[...] += dot_nn(g_gate, wg[rows, :]) + dot_nn(g_up, wu[rows, :])
        for m, (mine, send, right) in enumerate(
            ((nm_ref, ns_ref, g_gate), (nm_ref, ns_ref, g_up), (gm_ref, gs_ref, mixed))
        ):
            cols = pl.ds(pl.multiple_of(3 * start + m * 512, 512), 512)
            mine_ref[:, cols] = dot_nn(mine[...], right)
            send_ref[:, cols] = dot_nn(send[...], right).astype(BF16)

    step, gg_ff = norm_back(h2, scale3, gain_ff[...], gn_ref[...])
    gg_ref[1:2, :] = gg_ff
    res = res_ref[...] + step
    res_ref[...] = res
    rows_b = res.astype(BF16)
    rows_ref[...] = rows_b
    gatt_ref[...] = dot_nt(rows_b, w_co[...]).astype(BF16)
    gatt_t = dot_nt(w_co[...], rows_b).astype(BF16).astype(F32)
    dot_ref[...] = jnp.zeros_like(dot_ref)
    for head in range(NHEAD):
        feats = slice(head * HDIM, (head + 1) * HDIM)
        dot_ref[head : head + 1, :] = jnp.sum(gatt_t[feats, :] * att_t[feats, :], 0, keepdims=True)


def both_halves(half, own, other, target):
    target[pl.ds(pl.multiple_of(half * ROWS, ROWS), ROWS), :] = own[...]
    target[pl.ds(pl.multiple_of((1 - half) * ROWS, ROWS), ROWS), :] = other[...]


def cross_backward(
    split, scal, q2, k2, v2, lse, g_own, g_other, dot_own, dot_other,
    dk_ref, dv_ref, own_out, send_out, g_ref, dot_ref, dq_ref,
):
    half, _, live, _ = spots(scal, split)
    own = pl.multiple_of(half * ROWS, ROWS)
    other = pl.multiple_of((1 - half) * ROWS, ROWS)
    both_halves(half, g_own, g_other, g_ref)
    dot_ref[:, pl.ds(own, ROWS)] = dot_own[...]
    dot_ref[:, pl.ds(other, ROWS)] = dot_other[...]
    key = lax.broadcasted_iota(jnp.int32, (CHUNK, TGT), 0)

    @pl.loop(0, PAIRS)
    def _(pair):
        lanes = pl.ds(pl.multiple_of(pair * 128, 128), 128)
        q_pair, g_pair = q2[:, lanes], g_ref[:, lanes]
        for i in range(KEYS // CHUNK):
            rows = slice(i * CHUNK, (i + 1) * CHUNK)
            k_part, v_part = k2[rows, lanes], v2[rows, lanes]
            k_flip = flip(k_part).astype(BF16)
            grad_k = jnp.zeros((CHUNK, 128), F32)
            grad_v = jnp.zeros((CHUNK, 128), F32)
            for which in range(2):
                head = 2 * pair + which
                feats = pl.ds(pl.multiple_of(head * HDIM, HDIM), HDIM)
                q_one, g_one = only(q_pair, which), only(g_pair, which)
                scores = dot_nt(k_part, q_one) * SCALE
                scores = jnp.where(key < live - i * CHUNK, scores, NEG)
                probs = jnp.exp(scores - lse[pl.ds(head, 1), :])
                grad_p = dot_nt(v_part, g_one)
                grad_s = (probs * (grad_p - dot_ref[pl.ds(head, 1), :])).astype(BF16)
                grad_k = grad_k + dot_nn(grad_s, q_one)
                grad_v = grad_v + dot_nn(probs.astype(BF16), g_one)
                grad_q = dot_nn(k_flip[which * HDIM : (which + 1) * HDIM, :], grad_s)
                if i == 0:
                    dq_ref[feats, :] = grad_q
                else:
                    dq_ref[feats, :] += grad_q
            dk_ref[rows, lanes] = (grad_k * SCALE).astype(BF16)
            dv_ref[rows, lanes] = grad_v.astype(BF16)

    own_out[...] = dq_ref[:, pl.ds(own, ROWS)]
    send_out[...] = dq_ref[:, pl.ds(other, ROWS)].astype(BF16)


def source_backward(
    split, scal, dk, dv, source, w_ck, w_cv, gsrc_ref, mine_ref, send_ref, flat_ref, sm_ref, ss_ref
):
    for i in range(KEYS // CHUNK):
        rows = slice(i * CHUNK, (i + 1) * CHUNK)
        gsrc_ref[rows, :] = dot_nn(dk[rows, :], w_ck[...]) + dot_nn(dv[rows, :], w_cv[...])
        flat_ref[:, rows] = flip(source[rows, :]).astype(BF16)
    split_rows(flat_ref, sm_ref, ss_ref, spots(scal, split)[3], split)
    rights = (dk[...], dv[...])
    first, per_shard = (192, D) if split else (0, 384)
    by_shard(sm_ref, rights, mine_ref, first, per_shard)
    by_shard(ss_ref, rights, send_ref, first, per_shard)


def query_backward(
    split, scal, dq_own, dq_other, h1_in, gain_cross, w_cq, res_in, rows_in, att, w_so,
    kv_mine, kv_send, mine_ref, send_ref, res_ref, rows_ref, gatt_ref, gg_ref, flat_ref, flat_2, a_ref, b_ref, turn_ref,
):
    core = spots(scal, split)[3]
    turn_ref[...] = dq_own[...] + dq_other[...].astype(F32)
    dq = (turn_ref[...].T * SCALE).astype(BF16)
    h1 = h1_in[...]
    scale2 = rms_scale(h1)
    rows_ref[...] = (h1 * scale2 * gain_cross[...]).astype(BF16)
    flat_ref[...] = flip(rows_ref[...]).astype(BF16)
    split_rows(flat_ref, a_ref, b_ref, core, split)
    by_shard(a_ref, (dq,), mine_ref, 0, D)
    by_shard(b_ref, (dq,), send_ref, 0, D)
    step, gg = norm_back(h1, scale2, gain_cross[...], dot_nn(dq, w_cq[...]))
    gg_ref[...] = gg
    res = res_in[...] + step
    res_ref[...] = res
    rows_b = res.astype(BF16)
    rows_ref[...] = rows_b
    gatt_ref[...] = dot_nt(rows_b, w_so[...]).astype(BF16)
    flat_2[...] = flip(rows_in[...]).astype(BF16)
    split_rows(flat_2, a_ref, b_ref, core, split)
    by_shard(a_ref, (att[...],), mine_ref, 576, D)
    by_shard(b_ref, (att[...],), send_ref, 576, D)
    for z in range(0 if split else 4):
        cols = slice(z * D + 192, z * D + 576)
        mine_ref[:, cols] = kv_mine[:, z * 384 : (z + 1) * 384]
        send_ref[:, cols] = kv_send[:, z * 384 : (z + 1) * 384]


def self_backward(
    split, scal, q1, k1, v1, lse, g_own, g_other, x_own, gain_self, w_q, w_k, w_v, res_in, rows_in, att,
    mine_ref, send_ref, gin_ref, gg_ref,
    g_ref, dq_ref, dk_ref, dv_ref, flat_ref, flat_2, a_ref, b_ref, midway=None,
):
    half, live, _, core = spots(scal, split)
    own = pl.multiple_of(half * ROWS, ROWS)
    both_halves(half, g_own, g_other, g_ref)
    key = lax.broadcasted_iota(jnp.int32, (TGT, TGT), 0)
    query = lax.broadcasted_iota(jnp.int32, (TGT, TGT), 1)
    seen = (key <= query) & (key < live)

    @pl.loop(0, PAIRS)
    def _(pair):
        lanes = pl.ds(pl.multiple_of(pair * 128, 128), 128)
        q_pair, g_pair = q1[:, lanes], g_ref[:, lanes]
        k_pair, v_pair = k1[:, lanes], v1[:, lanes]
        k_flip = flip(k_pair).astype(BF16)
        grad_k = jnp.zeros((TGT, 128), F32)
        grad_v = jnp.zeros((TGT, 128), F32)
        for which in range(2):
            head = 2 * pair + which
            feats = pl.ds(pl.multiple_of(head * HDIM, HDIM), HDIM)
            q_one, g_one = only(q_pair, which), only(g_pair, which)
            scores = jnp.where(seen, dot_nt(k_pair, q_one) * SCALE, NEG)
            probs = jnp.exp(scores - lse[pl.ds(head, 1), :])
            grad_p = dot_nt(v_pair, g_one)
            row_dot = jnp.sum(probs * grad_p, axis=0, keepdims=True)
            grad_s = (probs * (grad_p - row_dot)).astype(BF16)
            grad_k = grad_k + dot_nn(grad_s, q_one)
            grad_v = grad_v + dot_nn(probs.astype(BF16), g_one)
            dq_ref[feats, :] = dot_nn(k_flip[which * HDIM : (which + 1) * HDIM, :], grad_s)
        dk_ref[:, lanes] = (grad_k * SCALE).astype(BF16)
        dv_ref[:, lanes] = grad_v.astype(BF16)

    if midway is not None:
        midway()
    dq = (flip(dq_ref[:, pl.ds(own, ROWS)]) * SCALE).astype(BF16)
    dk = dk_ref[pl.ds(own, ROWS), :]
    dv = dv_ref[pl.ds(own, ROWS), :]
    x = x_own[...].astype(F32)
    scale1 = rms_scale(x)
    grad_n = dot_nn(dq, w_q[...]) + dot_nn(dk, w_k[...]) + dot_nn(dv, w_v[...])
    step, gg = norm_back(x, scale1, gain_self[...], grad_n)
    gg_ref[...] = gg
    gin_ref[...] = res_in[...] + step
    g_ref[:ROWS, :] = (x * scale1 * gain_self[...]).astype(BF16)
    flat_ref[...] = flip(g_ref[:ROWS, :]).astype(BF16)
    split_rows(flat_ref, a_ref, b_ref, core, split)
    by_shard(a_ref, (dq, dk, dv), mine_ref, 0, D)
    by_shard(b_ref, (dq, dk, dv), send_ref, 0, D)
    flat_2[...] = flip(rows_in[...]).astype(BF16)
    split_rows(flat_2, a_ref, b_ref, core, split)
    by_shard(a_ref, (att[...],), mine_ref, 576, D)
    by_shard(b_ref, (att[...],), send_ref, 576, D)


def table_ff_kernel(*refs):
    (scal, g_a, g_b, fin_a, fin_b, gf_sum, gf_3), refs = refs[:7], refs[7:]
    (block_out, h2_in, gains, wg, wu, wd, w_co, att_t), refs = refs[:8], refs[8:]
    gain_ff, gain_final = gains.at[2:3], gains.at[3:4]
    (e_keep, e_send, f_keep, f_send, res_ref, rows_ref), refs = refs[:6], refs[6:]
    (gatt_ref, gatt_other, dot_ref, dot_other, gg_ref), refs = refs[:5], refs[5:]
    (ga_ring, gb_ring, w_ring, mine_ring, send_ring, got, e_keep1, e_send1, e_recv1), refs = (
        refs[:9],
        refs[9:],
    )
    (flat_ref, flat_2, nm_ref, ns_ref, gm_ref, gs_ref, gn_ref, gf_recv), refs = refs[:8], refs[8:]
    (fm_a, fm_b, fs_a, fs_b), refs = refs[:4], refs[4:]
    send_sem, recv_sem, load_sem, w_sem = refs
    comm = Comm(send_sem, recv_sem)
    core = comm.c

    def load(step):
        tile = lax.rem(step, 2) * 4 + step // 2
        rows = pl.ds(pl.multiple_of(tile * HTILE, HTILE), HTILE)
        slot = lax.rem(step, 2)
        return [
            pltpu.make_async_copy(src.at[rows], dst.at[slot], load_sem.at[slot, i])
            for i, (src, dst) in enumerate(((g_a, ga_ring), (g_b, gb_ring)))
        ]

    def load_weights(step):
        shard = lax.rem(step, 2) * 2 + step // 2
        rows = pl.ds(pl.multiple_of(shard * 512, 512), 512)
        slot = lax.rem(step, 2)
        return [
            pltpu.make_async_copy(src.at[rows], w_ring.at[slot, i], w_sem.at[slot, i])
            for i, src in enumerate((wg, wu, wd))
        ]

    for copy in load(0) + load_weights(0):
        copy.start()
    comm.barrier()
    gf_copies = [comm.send(gf_3, gf_recv, comm.z_peers[2])]
    split_rows(fin_a, fm_a, fs_a, core, True)
    split_rows(fin_b, fm_b, fs_b, core, True)
    e_core, e_line, f_core = comm.reserve(8), comm.reserve(8), comm.reserve(4)

    def core_copy(step):
        tile = lax.rem(step, 2) * 4 + step // 2
        return comm.copy(
            send_ring.at[lax.rem(step, 2), pl.ds(0, 2)],
            got.at[pl.ds(2 * tile, 2)],
            comm.core_peer,
            e_core + step,
        )

    def line_copy(step):
        side, column = lax.rem(step, 2), step // 2
        cols = pl.ds(pl.multiple_of(column * HTILE, HTILE), HTILE)
        peer = comm.x_peer[0] * (1 - side) + comm.y_peer[0] * side
        return comm.copy(
            e_send1.at[side, :, cols], e_recv1.at[side, :, cols], (peer, comm.z), e_line + step
        )

    @pl.loop(0, 9)
    def _(step):
        @pl.when(step < 8)
        def _():
            slot = lax.rem(step, 2)
            for copy in load(step):
                copy.wait()

            @pl.when(step < 7)
            def _():
                for copy in load(step + 1):
                    copy.start()

            @pl.when(step >= 2)
            def _():
                core_copy(step - 2).wait_send()

            for part in range(2):
                rows = slice(part * 512, (part + 1) * 512)
                first, second = ga_ring[slot, rows, :], gb_ring[slot, rows, :]
                mine_ring[slot, part] = dot_nt(fm_a[...], first) + dot_nt(fm_b[...], second)
                send_ring[slot, part] = (
                    dot_nt(fs_a[...], first) + dot_nt(fs_b[...], second)
                ).astype(BF16)
            core_copy(step).start()

        @pl.when(step > 0)
        def _():
            last = step - 1
            slot, side = lax.rem(last, 2), lax.rem(last, 2)
            tile = side * 4 + last // 2
            core_copy(last).wait_recv()
            for part in range(2):
                start = pl.multiple_of((last // 2) * HTILE + part * 512, 512)
                cols = pl.ds(start, 512)
                fold_one(
                    comm,
                    mine_ring.at[slot, part],
                    got.at[2 * tile + part],
                    e_keep1.at[side, :, cols],
                    e_send1.at[side, :, cols],
                    side,
                )
            line_copy(last).start()

    for step in (6, 7):
        core_copy(step).wait_send()
    for copy in gf_copies:
        copy.wait()

    grad = gf_sum[...] + gf_recv[...].astype(F32)
    out = block_out[...]
    res, gg_final = norm_back(out, rms_scale(out), gain_final[...], grad * D ** (-0.5))
    gg_ref[0:1, :] = gg_final
    res_ref[...] = res
    gatt_ref[...] = res.astype(BF16)
    flat_ref[...] = flip(gatt_ref[...]).astype(BF16)
    split_rows(flat_ref, gm_ref, gs_ref, core, True)
    h2 = h2_in[...]
    rows_ref[...] = (h2 * rms_scale(h2) * gain_ff[...]).astype(BF16)
    flat_2[...] = flip(rows_ref[...]).astype(BF16)
    split_rows(flat_2, nm_ref, ns_ref, core, True)
    gn_ref[...] = jnp.zeros_like(gn_ref)

    def ff_copy(step):
        return comm.copy(
            send_ring.at[lax.rem(step, 2)],
            got.at[pl.ds(3 * step, 3)],
            comm.core_peer,
            f_core + step,
        )

    @pl.loop(0, 5)
    def _(step):
        @pl.when(step < 4)
        def _():
            slot = lax.rem(step, 2)
            for copy in load_weights(step):
                copy.wait()

            @pl.when(step < 3)
            def _():
                for copy in load_weights(step + 1):
                    copy.start()

            @pl.when(step >= 2)
            def _():
                ff_copy(step - 2).wait_send()

            g_gate, g_up, mixed = ff_block(rows_ref, gatt_ref, gn_ref, w_ring.at[slot])
            for m, (mine, send, right) in enumerate(
                ((nm_ref, ns_ref, g_gate), (nm_ref, ns_ref, g_up), (gm_ref, gs_ref, mixed))
            ):
                mine_ring[slot, m] = dot_nn(mine[...], right)
                send_ring[slot, m] = dot_nn(send[...], right).astype(BF16)
            ff_copy(step).start()

        @pl.when(step > 0)
        def _():
            last = step - 1
            slot, side = lax.rem(last, 2), lax.rem(last, 2)
            ff_copy(last).wait_recv()
            for m in range(3):
                cols = pl.ds(pl.multiple_of((last // 2) * 1536 + m * 512, 512), 512)
                fold_one(
                    comm,
                    mine_ring.at[slot, m],
                    got.at[3 * last + m],
                    f_keep.at[side, :, cols],
                    f_send.at[side, :, cols],
                    side,
                )

    step, gg_ff = norm_back(h2_in[...], rms_scale(h2_in[...]), gain_ff[...], gn_ref[...])
    gg_ref[1:2, :] = gg_ff
    res = res_ref[...] + step
    res_ref[...] = res
    rows_b = res.astype(BF16)
    rows_ref[...] = rows_b
    gatt_ref[...] = dot_nt(rows_b, w_co[...]).astype(BF16)
    gatt_t = dot_nt(w_co[...], rows_b).astype(BF16).astype(F32)
    dot_ref[...] = jnp.zeros_like(dot_ref)
    for head in range(NHEAD):
        feats = slice(head * HDIM, (head + 1) * HDIM)
        dot_ref[head : head + 1, :] = jnp.sum(gatt_t[feats, :] * att_t[feats, :], 0, keepdims=True)
    pair_copies = [
        comm.send(gatt_ref, gatt_other, comm.z_peers[0]),
        comm.send(dot_ref, dot_other, comm.z_peers[0]),
    ]
    for step in (2, 3):
        ff_copy(step).wait_send()
    for step in range(8):
        line_copy(step).wait()
    fold_two(comm, e_keep1, e_recv1, e_keep, e_send)
    for copy in pair_copies:
        copy.wait()


def ff_block(n3_ref, grad_ref, gn_ref, weights):
    const = (2.0 / 3.141592653589793) ** 0.5
    wg, wu, wd = weights[0], weights[1], weights[2]
    n3 = n3_ref[...]
    gate = dot_nt(n3, wg)
    up = dot_nt(n3, wu)
    square = gate * gate
    tanh = jnp.tanh(const * (gate + 0.044715 * gate * square))
    gelu = 0.5 * gate * (1.0 + tanh)
    slope = 0.5 * (1.0 + tanh) + 0.5 * gate * (1.0 - tanh * tanh) * const * (
        1.0 + 3.0 * 0.044715 * square
    )
    grad_mixed = dot_nt(grad_ref[...], wd)
    g_gate = (grad_mixed * up * slope).astype(BF16)
    g_up = (grad_mixed * gelu).astype(BF16)
    gn_ref[...] += dot_nn(g_gate, wg) + dot_nn(g_up, wu)
    return g_gate, g_up, (gelu * up).astype(BF16)


def cross_kernel(*refs):
    (scal, q2, k2, v2, lse2, g_own, g_other, dot_own, dot_oth, source), refs = refs[:10], refs[10:]
    (w_ck, w_cv, w_cq, w_so, h1, gains, res_in, rows_in, att), refs = refs[:9], refs[9:]
    gain_cross = gains.at[1:2]
    (f_keep, f_send), refs = refs[:2], refs[2:]
    (gsrc, res_ref, rows_ref, gatt1, gatt1_other, gg_ref), refs = refs[:6], refs[6:]
    (c_keep, c_send, f_keep3, f_send3), refs = refs[:4], refs[4:]
    (g_ref, dot_ref, dq_ref, dk_ref, dv_ref, flat_ref, sm_ref, ss_ref), refs = refs[:8], refs[8:]
    (mine, send, got, f_recv, own_ref, go_ref, come_ref, flat2, a_ref, b_ref), refs = (
        refs[:10],
        refs[10:],
    )
    f_two, shard_ref, refs = refs[:3], refs[3], refs[4:]
    comm = Comm(*refs)
    comm.barrier()
    ff = Flow(comm, (f_keep, f_send, f_recv), f_two, (f_keep3, f_send3, None))
    ff.send_first()
    cross_backward(
        True, scal, q2, k2, v2, lse2, g_own, g_other, dot_own, dot_oth,
        dk_ref, dv_ref, own_ref, go_ref, g_ref, dot_ref, dq_ref,
    )
    dq_copy = comm.send(go_ref, come_ref, comm.z_peers[0])
    ff.fold_second()
    ff.send_second()
    source_backward(
        True, scal, dk_ref, dv_ref, source, w_ck, w_cv, gsrc, mine, send, flat_ref, sm_ref, ss_ref
    )
    dq_copy.wait()
    query_backward(
        True, scal, own_ref, come_ref, h1, gain_cross, w_cq, res_in, rows_in, att, w_so,
        None, None, mine, send, res_ref, rows_ref, gatt1, gg_ref, flat2, go_ref, a_ref, b_ref, dq_ref.at[:, :ROWS],
    )
    pair_copy = comm.send(gatt1, gatt1_other, comm.z_peers[0])
    cross = Flow(comm, (c_keep, c_send, None), None, None)
    cross.from_core(mine, send, got)
    cross.fold_first()
    ff.fold_third(shard_ref)
    pair_copy.wait()


def self_kernel(*refs):
    (scal, q1, k1, v1, lse1, g_own, g_other, x_own, gains, w_q, w_k, w_v), refs = (
        refs[:12],
        refs[12:],
    )
    gain_self = gains.at[0:1]
    (res_in, rows_in, att, gg_a, gg_b), refs = refs[:5], refs[5:]
    (f_send3, e_send, c_keep, c_send), refs = refs[:4], refs[4:]
    (gin_ref, gains_ref, f_recv3, c_keep3, c_recv3, s_keep3, s_recv3, e_recv), refs = refs[:8], refs[8:]
    (g_ref, dq_ref, dk_ref, dv_ref, flat_ref, flat_2, a_ref, b_ref, gain_ref), refs = refs[:9], refs[9:]
    (mine, send, got, shard_ref, shard_2), refs = refs[:5], refs[5:]
    (c_recv1, c_keep2, c_send2, c_recv2), refs = refs[:4], refs[4:]
    s_one, s_two, refs = refs[:3], refs[3:6], refs[6:]
    (c_send3, s_send3, gain_send, gain_recv), refs = refs[:4], refs[4:]
    c_three = c_keep3, c_send3, c_recv3
    s_three = s_keep3, s_send3, s_recv3
    comm = Comm(*refs)
    comm.barrier()
    cross = Flow(comm, (c_keep, c_send, c_recv1), (c_keep2, c_send2, c_recv2), c_three)
    ff = Flow(comm, None, None, (None, f_send3, f_recv3))
    own = Flow(comm, s_one, s_two, s_three)
    cross.send_first()
    ff.send_third()

    def midway():
        cross.fold_second()
        cross.send_second()

    self_backward(
        True, scal, q1, k1, v1, lse1, g_own, g_other, x_own, gain_self, w_q, w_k, w_v,
        res_in, rows_in, att, mine, send, gin_ref, gain_ref,
        g_ref, dq_ref, dk_ref, dv_ref, flat_ref, flat_2, a_ref, b_ref, midway,
    )
    own.from_core(mine, send, got)
    gains_ref[...] = jnp.zeros_like(gains_ref)
    gains_ref[0:2, :] = gg_a[...]
    gains_ref[2:3, :] = gg_b[...]
    gains_ref[3:4, :] = gain_ref[...]

    def gain_step(step, peer):
        gain_send[step] = gains_ref[...]
        return comm.send(gain_send.at[step], gain_recv.at[step], peer)

    def gain_done(step, copy):
        copy.wait()
        gains_ref[...] = gains_ref[...] + gain_recv[step]

    copy = gain_step(0, comm.core_peer)
    own.fold_first()
    own.send_first()
    gain_done(0, copy)
    copy = gain_step(1, comm.z_peers[0])
    cross.fold_third(shard_ref)
    cross.send_third()
    gain_done(1, copy)
    copy = gain_step(2, comm.x_peer)
    own.fold_second()
    own.send_second()
    e_copies = [
        comm.send(e_send.at[0], e_recv.at[0], comm.y_peer),
        comm.send(e_send.at[1], e_recv.at[1], comm.x_peer),
    ]
    gain_done(2, copy)
    copy = gain_step(3, comm.y_peer)
    own.fold_third(shard_2)
    own.send_third()
    gain_done(3, copy)
    copy = gain_step(4, comm.z_peers[1])
    ff.wait()
    cross.wait()
    gain_done(4, copy)
    own.wait()
    for copy in e_copies:
        copy.wait()


def head_kernel(vocab, *refs):
    (lens, fin_own, table, targets), refs = refs[:4], refs[4:]
    (g_a, g_b, gf_sum, gf_3, loss_ref, fin_a, fin_b), refs = refs[:7], refs[7:]
    (e_ref, l_ref, fin_recv, stats, stats_recv, ring, acc_ref, gf_send, gf_recv), refs = (
        refs[:9],
        refs[9:],
    )
    send_sem, recv_sem, e_sem, ring_sem = refs
    comm = Comm(send_sem, recv_sem)
    z = comm.z
    shards = (z,) + comm.z_shards
    load = pltpu.make_async_copy(table, e_ref.at[:vocab], e_sem.at[0])
    load.start()
    barrier = pltpu.get_barrier_semaphore()
    for peer in comm.z_peers:
        pl.semaphore_signal(
            barrier, inc=1, device_id={"dp": peer[0], "tensor": peer[1]}, device_id_type=MESH_ID
        )
    pl.semaphore_wait(barrier, 3)
    fin_copies = [comm.send(fin_own, fin_recv.at[j], comm.z_peers[j]) for j in range(3)]
    padded = e_ref.shape[0]
    if padded > vocab:
        e_ref[vocab:, :] = jnp.zeros((padded - vocab, D), BF16)
    load.wait()
    tiles = padded // HTILE
    local = []
    for shard in shards:
        target = targets[pl.ds(shard, 1), :] - z * vocab
        local.append(jnp.where(target < vocab, target, -1))
    entry = lax.broadcasted_iota(jnp.int32, (HTILE, ROWS), 0)

    for i in range(4):
        if i > 0:
            fin_copies[i - 1].wait()
        fin = fin_own if i == 0 else fin_recv.at[i - 1]
        lanes = slice((i % 2) * ROWS, (i % 2 + 1) * ROWS)
        (fin_b if i < 2 else fin_a)[:, lanes] = fin[...]
        row = lax.broadcasted_iota(jnp.int32, (8, ROWS), 0)
        stats[i] = jnp.where(row == 0, 2 * NEG, 0.0)

        @pl.loop(0, tiles)
        def _(tile):
            start = pl.multiple_of(tile * HTILE, HTILE)
            logits = dot_nn(e_ref[pl.ds(start, HTILE), :], fin[...])
            logits = jnp.where(entry < vocab - start, logits, 2 * NEG)
            l_ref[i, pl.ds(start, HTILE), :] = logits
            old = stats[i, 0:1, :]
            new = jnp.maximum(old, jnp.max(logits, axis=0, keepdims=True))
            stats[i, 1:2, :] = stats[i, 1:2, :] * jnp.exp(old - new) + jnp.sum(
                jnp.exp(logits - new), axis=0, keepdims=True
            )
            stats[i, 0:1, :] = new
            hit = jnp.where(entry == local[i] - start, logits, 0.0)
            stats[i, 2:3, :] += jnp.sum(hit, axis=0, keepdims=True)

    copies = [comm.send(stats, stats_recv.at[j], comm.z_peers[j]) for j in range(3)]
    for copy in copies:
        copy.wait()

    def over_z(values, op):
        return op(op(values[0], values[1]), op(values[2], values[3]))

    lse, live = [], []
    for i in range(4):
        parts = [stats.at[i]] + [stats_recv.at[k - 1, i ^ k] for k in (1, 2, 3)]
        top = over_z([p[0:1, :] for p in parts], jnp.maximum)
        total = over_z([p[1:2, :] * jnp.exp(p[0:1, :] - top) for p in parts], jnp.add)
        picked = over_z([p[2:3, :] for p in parts], jnp.add)
        lse.append(top + jnp.log(total))
        lane = lax.broadcasted_iota(jnp.int32, (1, ROWS), 1)
        live.append(lax.rem(shards[i], 2) * ROWS + lane < lens[shards[i] // 2])
        loss_ref[pl.ds(shards[i], 1), :] = jnp.where(live[i], lse[i] - picked, 0.0)

    gf_copies = []
    for i in (2, 1, 3, 0):
        target = g_b if i < 2 else g_a
        acc_ref[...] = jnp.zeros_like(acc_ref)

        def leave(tile):
            rows = pl.ds(pl.multiple_of(tile * HTILE, HTILE), HTILE)
            slot = lax.rem(tile, 2)
            return pltpu.make_async_copy(
                ring.at[slot], target.at[rows, pl.ds((i % 2) * ROWS, ROWS)], ring_sem.at[slot]
            )

        @pl.loop(0, tiles)
        def _(tile):
            start = pl.multiple_of(tile * HTILE, HTILE)

            @pl.when(tile >= 2)
            def _():
                leave(tile - 2).wait()

            hit = jnp.where(entry == local[i] - start, 1.0, 0.0)
            grad = jnp.exp(l_ref[i, pl.ds(start, HTILE), :] - lse[i]) - hit
            grad = jnp.where(live[i], grad, 0.0).astype(BF16)
            ring[lax.rem(tile, 2)] = grad
            leave(tile).start()
            acc_ref[...] += lax.dot_general(
                grad, e_ref[pl.ds(start, HTILE), :], (((0,), (0,)), ((), ())), preferred_element_type=F32
            )

        for tile in (tiles - 2, tiles - 1):
            leave(tile).wait()
        if i == 3:
            gf_3[...] = acc_ref[...].astype(BF16)
        elif i > 0:
            gf_send[i - 1] = acc_ref[...].astype(BF16)
            gf_copies.append(comm.send(gf_send.at[i - 1], gf_recv.at[i - 1], comm.z_peers[i - 1]))
    for copy in gf_copies:
        copy.wait()
    gf_sum[...] = acc_ref[...] + (gf_recv[0].astype(F32) + gf_recv[1].astype(F32))


def fused_head(lens, fin_t, table, targets):
    vocab = table.shape[0]
    padded = pl.cdiv(vocab, HTILE) * HTILE
    hbm, vmem = pl.BlockSpec(memory_space=pl.ANY), pl.BlockSpec(memory_space=pltpu.VMEM)
    grad = whole((padded, TGT), BF16)
    block = (ROWS, D)
    return pl.pallas_call(
        functools.partial(head_kernel, vocab),
        out_shape=[
            grad, grad, whole(block, F32), whole(block, BF16), whole((4, ROWS), F32),
            whole((D, TGT), BF16), whole((D, TGT), BF16),
        ],
        in_specs=[pl.BlockSpec(memory_space=pltpu.SMEM), vmem, hbm, vmem],
        out_specs=[hbm, hbm] + [vmem] * 5,
        scratch_shapes=[
            pltpu.VMEM((padded, D), BF16),
            pltpu.VMEM((4, padded, ROWS), F32),
            pltpu.VMEM((3, D, ROWS), BF16),
            pltpu.VMEM((4, 8, ROWS), F32),
            pltpu.VMEM((3, 4, 8, ROWS), F32),
            pltpu.VMEM((2, HTILE, ROWS), BF16),
            pltpu.VMEM(block, F32),
            pltpu.VMEM((2,) + block, BF16),
            pltpu.VMEM((2,) + block, BF16),
            pltpu.SemaphoreType.DMA((8,)),
            pltpu.SemaphoreType.DMA((8,)),
            pltpu.SemaphoreType.DMA((1,)),
            pltpu.SemaphoreType.DMA((2,)),
        ],
        compiler_params=pltpu.CompilerParams(
            collective_id=4, has_side_effects=True, vmem_limit_bytes=FUSED_LIMIT
        ),
    )(lens, fin_t, table, targets)


def fused_call(body, collective_id, ins, outs, scratch, copies, flops):
    hbm, vmem = pl.BlockSpec(memory_space=pl.ANY), pl.BlockSpec(memory_space=pltpu.VMEM)
    moved = sum(a.size * a.dtype.itemsize for a, _ in ins)
    return pl.pallas_call(
        body,
        out_shape=[shape for shape, _ in outs],
        in_specs=[pl.BlockSpec(memory_space=pltpu.SMEM)] + [hbm if far else vmem for _, far in ins[1:]],
        out_specs=[hbm if far else vmem for _, far in outs],
        scratch_shapes=scratch(copies),
        cost_estimate=pl.CostEstimate(
            flops=int(flops), bytes_accessed=int(moved), transcendentals=0
        ),
        compiler_params=pltpu.CompilerParams(
            collective_id=collective_id, has_side_effects=True, vmem_limit_bytes=FUSED_LIMIT
        ),
    )(*[a for a, _ in ins])


def fused_backward(
    scal, fin_a, fin_b, g_a, g_b, gf_sum, gf_3, saved, weights, gains, block_in, source, vocab
):
    (q1, k1, v1, lse1, a1, h1, q2, k2, v2, block_out, h2, att_t, a2, lse2) = saved
    (sq, sk, sv, so, cq, ck, cv, co, wg, wu, wd) = weights

    def vm(*shape, dtype=BF16):
        return pltpu.VMEM(shape, dtype)

    def sems(copies):
        return [pltpu.SemaphoreType.DMA((copies,))] * 2

    def near(*arrays):
        return [(a, False) for a in arrays]

    def far(*arrays):
        return [(a, True) for a in arrays]

    block, pair = (ROWS, D), (TGT, D)
    half_t = (HALF_D, ROWS)
    e_half, f_half, c_half = 4096, 3 * FF // 2, 2 * D

    def scratch_1(copies):
        return [
            vm(2, HTILE, TGT), vm(2, HTILE, TGT), vm(2, 3, 512, D), vm(2, 3, HALF_D, 512, dtype=F32),
            vm(2, 3, HALF_D, 512), vm(16, HALF_D, 512), vm(2, 192, e_half, dtype=F32),
            vm(2, 192, e_half), vm(2, 192, e_half), vm(D, ROWS), vm(D, ROWS),
            vm(*half_t), vm(*half_t), vm(*half_t), vm(*half_t), vm(*block, dtype=F32),
            vm(*block), *[vm(HALF_D, TGT)] * 4, *sems(copies),
            pltpu.SemaphoreType.DMA((2, 2)), pltpu.SemaphoreType.DMA((2, 3)),
        ]

    outs = near(
        whole((2, 96, e_half), F32), whole((2, 96, e_half), BF16),
        whole((2, 192, f_half), F32), whole((2, 192, f_half), BF16),
        whole(block, F32), whole(block, BF16), whole(block, BF16), whole(block, BF16),
        whole((16, ROWS), F32), whole((16, ROWS), F32), whole((2, D), F32),
    )
    e_keep, e_send, f_keep, f_send, res2, rows2, gatt, gatt_o, dots, dots_o, gg_a = fused_call(
        table_ff_kernel, 1,
        near(scal) + far(g_a, g_b) + near(fin_a, fin_b, gf_sum, gf_3)
        + near(block_out, h2, gains) + far(wg, wu, wd) + near(co, att_t),
        outs, scratch_1, 24, 40e9,
    )

    def scratch_2(copies):
        return [
            vm(*pair), vm(16, TGT, dtype=F32), vm(D, TGT, dtype=F32), vm(KEYS, D), vm(KEYS, D),
            vm(D, KEYS), vm(HALF_D, KEYS), vm(HALF_D, KEYS),
            vm(HALF_D, 4 * D, dtype=F32), vm(HALF_D, 4 * D), vm(HALF_D, 4 * D),
            vm(2, 192, f_half), vm(D, ROWS, dtype=F32), vm(D, ROWS), vm(D, ROWS),
            vm(D, ROWS), vm(*half_t), vm(*half_t),
            vm(2, 96, f_half, dtype=F32), vm(2, 96, f_half), vm(2, 96, f_half),
            vm(4, 96, f_half // 2, dtype=F32), *sems(copies),
        ]

    outs = near(
        whole((KEYS, D), F32), whole(block, F32), whole(block, BF16), whole(block, BF16),
        whole(block, BF16), whole((1, D), F32),
        whole((2, 192, c_half), F32), whole((2, 192, c_half), BF16),
        whole((96, f_half // 2), F32), whole((3, 96, f_half // 2), BF16),
    )
    (
        grad_source, res1, rows1, gatt1, gatt1_o, gg_b, c_keep, c_send, f_keep, f_send,
    ) = fused_call(
        cross_kernel, 2,
        near(scal, q2, k2, v2, lse2, gatt, gatt_o, dots, dots_o, source, ck, cv, cq, so)
        + near(h1, gains, res2, rows2, a2) + near(f_keep) + far(f_send),
        outs, scratch_2, 8, 40e9,
    )

    def scratch_3(copies):
        def two(width):
            return [vm(2, 96, width, dtype=F32), vm(2, 96, width), vm(2, 96, width)]

        return [
            vm(*pair), vm(D, TGT, dtype=F32), vm(*pair), vm(*pair), vm(D, ROWS), vm(D, ROWS),
            vm(*half_t), vm(*half_t), vm(1, D, dtype=F32),
            vm(HALF_D, 4 * D, dtype=F32), vm(HALF_D, 4 * D), vm(HALF_D, 4 * D),
            vm(4, 96, c_half // 2, dtype=F32), vm(4, 96, c_half // 2, dtype=F32),
            vm(2, 192, c_half), *two(c_half),
            vm(2, 192, c_half, dtype=F32), vm(2, 192, c_half), vm(2, 192, c_half),
            *two(c_half),
            vm(3, 96, c_half // 2), vm(3, 96, c_half // 2),
            vm(5, 8, D, dtype=F32), vm(5, 8, D, dtype=F32), *sems(copies),
        ]

    def three(width):
        return whole((96, width), F32), whole((3, 96, width), BF16)

    grad_in, gain_sums, f_recv, c_keep, c_recv, s_keep, s_recv, e_recv = fused_call(
        self_kernel, 3,
        near(scal, q1, k1, v1, lse1, gatt1, gatt1_o, block_in, gains, sq, sk, sv)
        + near(res1, rows1, a1, gg_a, gg_b) + far(f_send, e_send) + near(c_keep) + far(c_send),
        near(
            whole(block, F32), whole((8, D), F32), whole((3, 96, f_half // 2), BF16),
            *three(c_half // 2), *three(c_half // 2),
        )
        + far(whole((2, 96, e_half), BF16)),
        scratch_3, 32, 20e9,
    )
    parts = e_keep, e_recv, f_keep, f_recv, c_keep, c_recv, s_keep, s_recv, grad_in
    through = grad_source, block_out
    wide, tall, ff_wide = whole((96, 192), F32), whole((192, 96), F32), whole((96, 512), F32)
    grad_embed, grad_in, grad_source, block_out, *grads = pl.pallas_call(
        functools.partial(finish_kernel, vocab),
        out_shape=[
            whole((96, vocab), F32), whole(block, F32), whole((KEYS, D), F32), whole(block, F32),
            wide, wide, wide, tall, wide, wide, wide, tall,
            ff_wide, ff_wide, ff_wide,
        ],
        in_specs=[pl.BlockSpec(memory_space=pl.ANY)] * 11,
        scratch_shapes=[pltpu.VMEM(part.shape, part.dtype) for part in parts]
        + [pltpu.SemaphoreType.DMA((11,)), pltpu.VMEM((96, 192), F32)],
        compiler_params=pltpu.CompilerParams(vmem_limit_bytes=FUSED_LIMIT),
    )(*parts, *through)
    grads[-1] = grads[-1].T
    grad_embed = grad_embed.T
    return block_out, grad_in, grad_source, gain_sums, grads, grad_embed


def logits_kernel(vocab, flat_ref, table_ref, target_ref, logits_ref, stats_ref):
    tile = pl.program_id(0)

    @pl.when(tile == 0)
    def _():
        row = lax.broadcasted_iota(jnp.int32, stats_ref.shape, 0)
        stats_ref[...] = jnp.where(row == 0, 2 * NEG, 0.0)

    logits = dot_nn(table_ref[...], flat_ref[...])
    entry = tile * HTILE + lax.broadcasted_iota(jnp.int32, logits.shape, 0)
    logits = jnp.where(entry < vocab, logits, 2 * NEG)
    logits_ref[...] = logits
    old = stats_ref[0:1, :]
    new = jnp.maximum(old, jnp.max(logits, axis=0, keepdims=True))
    stats_ref[1:2, :] = stats_ref[1:2, :] * jnp.exp(old - new) + jnp.sum(
        jnp.exp(logits - new), axis=0, keepdims=True
    )
    stats_ref[0:1, :] = new
    hit = jnp.where(entry == target_ref[...], logits, 0.0)
    stats_ref[2:3, :] += jnp.sum(hit, axis=0, keepdims=True)


def head_logits(flat, table, target):
    count = flat.shape[1]
    vocab = table.shape[0]
    tiles = pl.cdiv(vocab, HTILE)
    return pl.pallas_call(
        functools.partial(logits_kernel, vocab),
        grid=(tiles,),
        out_shape=[whole((tiles * HTILE, count), F32), whole((8, count), F32)],
        in_specs=[
            pl.BlockSpec((D, count), lambda i: (0, 0)),
            pl.BlockSpec((HTILE, D), lambda i: (i, 0)),
            pl.BlockSpec((1, count), lambda i: (0, 0)),
        ],
        out_specs=[
            pl.BlockSpec((HTILE, count), lambda i: (i, 0)),
            pl.BlockSpec((8, count), lambda i: (0, 0)),
        ],
        cost_estimate=pl.CostEstimate(
            flops=2 * count * vocab * D, bytes_accessed=vocab * (2 * D + 4 * count), transcendentals=0
        ),
        compiler_params=pltpu.CompilerParams(vmem_limit_bytes=VMEM_LIMIT // 2),
    )(flat, table, target)


def grads_kernel(vocab, logits_ref, table_ref, target_ref, lse_ref, live_ref, g_ref, gf_ref, acc_ref):
    tile = pl.program_id(0)

    @pl.when(tile == 0)
    def _():
        acc_ref[...] = jnp.zeros_like(acc_ref)

    entry = tile * HTILE + lax.broadcasted_iota(jnp.int32, logits_ref.shape, 0)
    hit = jnp.where(entry == target_ref[...], 1.0, 0.0)
    grad = jnp.where(live_ref[...] > 0, jnp.exp(logits_ref[...] - lse_ref[...]) - hit, 0.0)
    grad = grad.astype(BF16)
    g_ref[...] = grad
    entry = tile * HTILE + lax.broadcasted_iota(jnp.int32, (HTILE, D), 0)
    table = jnp.where(entry < vocab, table_ref[...], jnp.zeros_like(table_ref[...]))
    acc_ref[...] += lax.dot_general(
        grad, table, (((0,), (0,)), ((), ())), preferred_element_type=F32
    )

    @pl.when(tile == pl.num_programs(0) - 1)
    def _():
        gf_ref[...] = acc_ref[...].astype(gf_ref.dtype)


def head_grads(logits, table, target, lse, live, dtype):
    count = logits.shape[1]
    vocab = table.shape[0]
    tiles = pl.cdiv(vocab, HTILE)
    row = pl.BlockSpec((1, count), lambda i: (0, 0))
    return pl.pallas_call(
        functools.partial(grads_kernel, vocab),
        grid=(tiles,),
        out_shape=[whole((tiles * HTILE, count), BF16), whole((count, D), dtype)],
        in_specs=[
            pl.BlockSpec((HTILE, count), lambda i: (i, 0)),
            pl.BlockSpec((HTILE, D), lambda i: (i, 0)),
            row,
            row,
            row,
        ],
        out_specs=[
            pl.BlockSpec((HTILE, count), lambda i: (i, 0)),
            pl.BlockSpec((count, D), lambda i: (0, 0)),
        ],
        scratch_shapes=[pltpu.VMEM((count, D), F32)],
        cost_estimate=pl.CostEstimate(
            flops=2 * count * vocab * D, bytes_accessed=vocab * (2 * D + 6 * count), transcendentals=0
        ),
        compiler_params=pltpu.CompilerParams(vmem_limit_bytes=VMEM_LIMIT // 2),
    )(logits, table, target, lse, live)


def table_kernel(fm_a, fm_b, fs_a, fs_b, g_a, g_b, mine_ref, send_ref):
    first, second = g_a[...], g_b[...]
    mine_ref[...] = dot_nt(fm_a[...], first) + dot_nt(fm_b[...], second)
    send_ref[...] = (dot_nt(fs_a[...], first) + dot_nt(fs_b[...], second)).astype(BF16)


def table_grads(flat_a, flat_b, g_a, g_b):
    width, count = g_a.shape
    left = pl.BlockSpec((HALF_D, count), lambda i: (0, 0))
    right = pl.BlockSpec((HTILE, count), lambda i: (i, 0))
    out = pl.BlockSpec((HALF_D, HTILE), lambda i: (0, i))
    return pl.pallas_call(
        table_kernel,
        grid=(width // HTILE,),
        out_shape=[whole((HALF_D, width), F32), whole((HALF_D, width), BF16)],
        in_specs=[left] * 4 + [right] * 2,
        out_specs=[out] * 2,
        cost_estimate=pl.CostEstimate(
            flops=4 * count * width * D, bytes_accessed=width * (4 * count + 6 * HALF_D), transcendentals=0
        ),
        compiler_params=pltpu.CompilerParams(vmem_limit_bytes=VMEM_LIMIT),
    )(flat_a[0], flat_b[0], flat_a[1], flat_b[1], g_a, g_b)


def make(mesh):
    dp_size = mesh.shape["dp"]
    split = dp_size == 8

    def on_device(
        block_in,
        source,
        target_len,
        source_len,
        targets,
        gain_self,
        gain_cross,
        gain_ff,
        gain_final,
        self_q,
        self_k,
        self_v,
        self_o,
        cross_q,
        cross_k,
        cross_v,
        cross_o,
        ff_gate,
        ff_up,
        ff_down,
        embed_table,
    ):
        z = lax.axis_index("tensor")
        dp = lax.axis_index("dp")
        half = lax.rem(z, 2)
        seq = z // 2
        core = lax.rem(dp, 2)
        gains = jnp.concatenate([gain_self, gain_cross, gain_ff, gain_final]).reshape(4, D)
        gain_self, gain_cross, gain_ff, gain_final = (gains[i : i + 1] for i in range(4))

        def pair_swap(value):
            return swap(value, "tensor", 4, 1)

        scal = jnp.stack(
            [
                half,
                lax.dynamic_index_in_dim(target_len, seq, keepdims=False),
                lax.dynamic_index_in_dim(source_len, seq, keepdims=False),
                core,
            ]
        ).astype(jnp.int32)

        def vm(shape, dtype):
            return pltpu.VMEM(shape, dtype)

        pair = (TGT, D)
        weights = (
            self_q.T, self_k.T, self_v.T, self_o, cross_q.T, cross_k.T, cross_v.T, cross_o,
            ff_gate, ff_up, ff_down,
        )
        vocab = embed_table.shape[0]
        if split:
            lens = jnp.concatenate([target_len, source_len])
            results = forward(True, lens, block_in, source, gains, weights)
            q1, k1, v1, lse1, a1, h1, q2, k2, v2, block_out, fin_t, h2, att_t, a2, lse2 = results[:15]
            g_a, g_b, gf_sum, gf_3, losses, fin_a, fin_b = fused_head(
                lens, fin_t, embed_table, targets.reshape(4, ROWS)
            )
            saved = (q1, k1, v1, lse1, a1, h1, q2, k2, v2, block_out, h2, att_t, a2, lse2)
            block_out, grad_block_in, grad_source, gain_sums, grads, grad_embed = fused_backward(
                lens, fin_a, fin_b, g_a, g_b, gf_sum, gf_3, saved, results[15:], gains,
                block_in, source, vocab,
            )
            return (
                block_out, losses.reshape(-1), grad_block_in, grad_source,
                gain_sums[3], gain_sums[2], gain_sums[1], gain_sums[0], *grads, grad_embed,
            )

        wide = [gather_wide(w.T if i in (8, 9) else w, dp_size) for i, w in enumerate(weights)]
        sq, sk, sv, so, cq, ck, cv, co, wg, wu, wd = wide
        weights = jnp.stack([sq, sk, sv, so]), jnp.stack([cq, ck, cv, co]), wg, wu, wd
        results = forward(False, scal, block_in, source, gains, weights)
        q1, k1, v1, lse1, a1, h1, q2, k2, v2, block_out, fin, h2, att_t, a2, lse2 = results
        fin = fin.T

        vocab = embed_table.shape[0]

        def block(by_block, j, axis=0):
            return lax.dynamic_index_in_dim(by_block, z ^ j, axis, keepdims=False)

        tgt_local = targets - z * vocab
        tgt_local = jnp.where((tgt_local >= 0) & (tgt_local < vocab), tgt_local, -1)
        tgt_blocks = tgt_local.reshape(4, ROWS)
        position = lax.rem(jnp.arange(4 * ROWS), TGT)
        live = position < jnp.repeat(target_len, TGT, total_repeat_length=4 * ROWS)
        live_blocks = live.astype(jnp.int32).reshape(4, ROWS)
        fin_1, fin_2, fin_3 = (swap(fin, "tensor", 4, j) for j in (1, 2, 3))
        fin_a = jnp.concatenate([fin_2, fin_3], 0).T
        fin_b = jnp.concatenate([fin, fin_1], 0).T

        def columns(by_block, order):
            return jnp.concatenate([block(by_block, j) for j in order], 0)[None, :]

        tgt_a, tgt_b = columns(tgt_blocks, (2, 3)), columns(tgt_blocks, (0, 1))
        logits_b, stats_b = head_logits(fin_b, embed_table, tgt_b)
        logits_a, stats_a = head_logits(fin_a, embed_table, tgt_a)
        stats = [stats_b[:, :ROWS], stats_b[:, ROWS:], stats_a[:, :ROWS], stats_a[:, ROWS:]]
        stats = jnp.stack(stats, 0)
        stats = jnp.stack([block(stats, j) for j in range(4)], 0)
        others = [stats] + [swap(stats, "tensor", 4, j) for j in (1, 2, 3)]

        def over_z(values, op):
            return op(op(values[0], values[1]), op(values[2], values[3]))

        top = over_z([s[:, 0] for s in others], jnp.maximum)
        total = over_z([s[:, 1] * jnp.exp(s[:, 0] - top) for s in others], jnp.add)
        picked = over_z([s[:, 2] for s in others], jnp.add)
        g_lse = top + jnp.log(total)
        token_loss = jnp.where(live, (g_lse - picked).reshape(-1), 0.0)
        g_a, gf_a = head_grads(
            logits_a, embed_table, tgt_a, columns(g_lse, (2, 3)), columns(live_blocks, (2, 3)), BF16
        )
        gf_2 = swap(gf_a[:ROWS], "tensor", 4, 2)
        g_b, gf_b = head_grads(
            logits_b, embed_table, tgt_b, columns(g_lse, (0, 1)), columns(live_blocks, (0, 1)), F32
        )
        g_b, gf_b, gf_2, gf_a = lax.optimization_barrier((g_b, gf_b, gf_2, gf_a))
        def halves(flat):
            return flat[:HALF_D], flat[HALF_D:]

        gf_3 = swap(gf_a[ROWS:], "tensor", 4, 3)
        gf_1 = swap(gf_b[ROWS:].astype(BF16), "tensor", 4, 1)
        e_mine, e_send = table_grads(halves(fin_a), halves(fin_b), g_a, g_b)
        e_sum = WideReduction(z, e_mine[:, :vocab], e_send[:, :vocab])

        half_t = (HALF_D, ROWS)
        ff_mine, ff_send, res2, rows2, gatt, dots, gg_a = local_call(
            functools.partial(ff_backward, False),
            [whole((HALF_D, 3 * FF), F32), whole((HALF_D, 3 * FF), BF16), whole((ROWS, D), F32)]
            + [whole((ROWS, D), BF16)] * 2
            + [whole((16, ROWS), F32), whole((2, D), F32)],
            [vm((D, ROWS), BF16)] * 2 + [vm(half_t, BF16)] * 4
            + [vm((ROWS, D), F32)],
            10e9,
            scal, gf_b[:ROWS], gf_1, gf_2, gf_3, block_out, h2,
            gain_ff, gain_final, wg, wu, wd, co, att_t,
        )
        ff_sum = WideReduction(z, ff_mine, ff_send)
        gatt_other, dots_other = pair_swap(gatt), pair_swap(dots)
        dk2, dv2, dq_own, dq_send = local_call(
            functools.partial(cross_backward, split),
            [whole((KEYS, D), BF16)] * 2 + [whole((D, ROWS), F32), whole((D, ROWS), BF16)],
            [vm(pair, BF16), vm((16, TGT), F32), vm((D, TGT), F32)],
            20e9,
            scal, q2, k2, v2, lse2, gatt, gatt_other, dots, dots_other,
        )
        dq_other = pair_swap(dq_send)
        grad_source, kv_mine, kv_send = local_call(
            functools.partial(source_backward, split),
            [whole((KEYS, D), F32), whole((HALF_D, 2 * D), F32), whole((HALF_D, 2 * D), BF16)],
            [vm((D, KEYS), BF16)] + [vm((HALF_D, KEYS), BF16)] * 2,
            5e9,
            scal, dk2, dv2, source, ck, cv,
        )
        c_mine, c_send, res1, rows1, gatt1, gg_b = local_call(
            functools.partial(query_backward, split),
            [whole((HALF_D, 4 * D), F32), whole((HALF_D, 4 * D), BF16), whole((ROWS, D), F32)]
            + [whole((ROWS, D), BF16)] * 2 + [whole((1, D), F32)],
            [vm((D, ROWS), BF16)] * 2 + [vm(half_t, BF16)] * 2 + [vm((D, ROWS), F32)],
            2e9,
            scal, dq_own, dq_other, h1, gain_cross, cq, res2, rows2, a2, so,
            kv_mine, kv_send,
        )
        c_sum = WideReduction(z, c_mine, c_send)
        gatt1_other = pair_swap(gatt1)
        s_mine, s_send, grad_block_in, gg_c = local_call(
            functools.partial(self_backward, split),
            [whole((HALF_D, 4 * D), F32), whole((HALF_D, 4 * D), BF16)]
            + [whole((ROWS, D), F32), whole((1, D), F32)],
            [vm(pair, BF16), vm((D, TGT), F32), vm(pair, BF16), vm(pair, BF16)]
            + [vm((D, ROWS), BF16)] * 2 + [vm(half_t, BF16)] * 2,
            12e9,
            scal, q1, k1, v1, lse1, gatt1, gatt1_other, block_in, gain_self, sq, sk, sv,
            res1, rows1, a1,
        )
        s_sum = WideReduction(z, s_mine, s_send)
        gains = jnp.concatenate([gg_a, gg_b, gg_c], 0)
        gains = lax.psum(gains, ("dp", "tensor"))
        grad_embed = e_sum.table(vocab)
        ff_grads = ff_sum.last(3, (2,))
        c_grads = c_sum.last(4, (3,))
        s_grads = s_sum.last(4, (3,))

        return (
            block_out,
            token_loss,
            grad_block_in,
            grad_source,
            gains[3],
            gains[2],
            gains[1],
            gains[0],
            *s_grads,
            *c_grads,
            *ff_grads,
            grad_embed,
        )

    return on_device


def solution(mesh):
    rows = P(("dp", "tensor"), None)
    wide, tall = P(None, "tensor"), P("tensor", None)
    in_specs = (rows, rows) + (P("dp"),) * 3 + (P(),) * 4
    in_specs += (wide, wide, wide, tall) * 2 + (wide, wide, tall, tall)
    g_in, g_out = P("dp", "tensor"), P("tensor", "dp")
    out_specs = (rows, P("dp"), rows, rows) + (P(),) * 4
    out_specs += (g_in, g_in, g_in, g_out) * 2 + (g_in, g_in, g_out, g_out)
    return jax.shard_map(
        make(mesh), mesh=mesh, in_specs=in_specs, out_specs=out_specs, check_vma=False
    )
```
